32 devices in a mesh: loop: 2 (over x), fsdp: 16 (over z, y, core).
Axes of the slice: x: 2, y: 2, z: 4, core: 2. Of those that a mesh axis runs over, the one named last changes fastest.
Arguments:
- hidden_input: bfloat16 [2, 2048, 2048], P('loop', 'fsdp'), may hold values from -6 to 6
- sequence_lengths: int32 [2, 4], P('loop'), may hold values from 1 to 1024, 2048 in all within a row
- norm_gain_values: bfloat16 [2, 2048], replicated, may hold values from 0.5 to 1.5
- input_proj_weight: bfloat16 [2048, 2560], P('fsdp'), may hold values from -0.125 to 0.125
- output_proj_weight: bfloat16 [2048, 2048], P('fsdp'), may hold values from -2 to 2
- feedforward_weight: bfloat16 [16384, 3, 2048], P('fsdp'), may hold values from -0.09375 to 0.09375
- adapter_first: bfloat16 [2, 2048, 1536], P('loop'), may hold values from -0.125 to 0.125
- adapter_second: bfloat16 [2, 256, 39424], P('loop'), may hold values from -0.1875 to 0.1875
- adapter_down_first: bfloat16 [2, 16384, 256], P('loop'), may hold values from -0.046875 to 0.046875
- output_gradient: bfloat16 [2, 2048, 2048], P('loop', 'fsdp'), may hold values from -6 to 6
Outputs:
- hidden_out: bfloat16 [2, 2048, 2048], P('loop', 'fsdp')
- hidden_grad: float32 [2, 2048, 2048], P('loop', 'fsdp')
- norm_gain_grad: float32 [2, 2048], P(None, 'fsdp')
- attn_in_grad: float32 [2048, 2560], P('fsdp')
- attn_out_grad: float32 [2048, 2048], P('fsdp')
- ffn_grad: float32 [16384, 3, 2048], P('fsdp')
- lora_a_grad: float32 [2, 2048, 1536], P('loop', 'fsdp')
- lora_b_grad: float32 [2, 256, 39424], P('loop', None, 'fsdp')
- lora_down_grad: float32 [2, 16384, 256], P('loop', 'fsdp')
The draws below stay inside these ranges and needn't reach their ends.
Inputs may be any that keep to these rules, and one draw needn't show every extreme that they name: `sequence_lengths`: row l holds the lengths of the 4 sequences packed in order into loop group l's 2048 rows; they sum to 2048 and the longest has exactly 1024 tokens.
All inputs are finite; a program needn't handle non-finite values.
Results may differ from the reference program's by a relative error of at most 0.017.
Values may be sent and summed in bfloat16 or wider, within the bound.
A program may use at most 1.5625 GiB of HBM per device.

```python
import math
from functools import partial
import jax
import jax.numpy as jnp
import numpy as np
from jax import lax

MODEL_WIDTH = 2048
HEADS = 8
HEAD_WIDTH = 256
HIDDEN_COUNT = 16384
ADAPTER_RANK = 256
QUERY_WIDTH = 2048
PROJECT_COLUMNS = 2560
ADAPTER_COLUMNS = 39424
LOOP_COUNT = 2
TOK_DEV = 128
NSEQ = 4
TOKENS = 2048
MAXLEN = 1024


def with_spikes(result, rng, source, target, parts, factor):
    owner, partner = [(jnp.arange(result.shape[dim]) // (result.shape[dim] // parts)).reshape([-1 if axis == dim else 1 for axis in range(result.ndim)]) for dim in (source, target)]
    chosen = jax.random.permutation(rng, parts)[partner]
    strong = (owner == chosen) | (owner == (partner + parts // 2) % parts)
    return jnp.where(strong, factor * result, result)


def steps_of(rng, dims, pieces, low, largest):
    def one(dim, blocks):
        steps = jax.random.uniform(jax.random.fold_in(jax.random.fold_in(rng, 6), dim), (blocks,), jnp.float32, low / len(pieces), largest / len(pieces))
        return jnp.repeat(jnp.exp(steps), dims[dim] // blocks).reshape((-1,) + (1,) * (len(dims) - dim - 1))

    level = one(*pieces[0])
    for cut in pieces[1:]:
        level = level * one(*cut)
    return level


def split_up(count, total, bound, lean):
    weights = [(1 << 20) // math.isqrt(rank ** lean) + 1 for rank in range(2, count + 1)]
    spare, holding = total - bound - (count - 1), [1] * (count - 1)
    while spare > 0:
        movable = [i for i in range(count - 1) if holding[i] < bound]
        mass, remaining = sum([weights[i] for i in movable]), spare
        for i in movable:
            extra = min(bound - holding[i], max(1, remaining * weights[i] // mass), spare)
            holding[i] = holding[i] + extra
            spare = spare - extra
    return np.array([bound] + holding)


def ragged(key, amount, total, reach, slope):
    if amount == 2:
        one = jax.random.randint(key, (), max(1, total - reach), min(reach, total - 1) + 1)
        return jnp.stack([one, total - one])
    tallies = jnp.asarray(split_up(amount, total, reach, slope), jnp.int32)
    twos = (amount - 1) // 2
    giver, sink = tallies[1:1 + 2 * twos:2], tallies[2:2 + 2 * twos:2]
    margin = jnp.minimum(giver - 1, reach - sink)
    shifted = jax.random.randint(jax.random.fold_in(key, 1), (twos,), 0, 1 << 20) % (margin + 1)
    tallies = tallies.at[1:1 + 2 * twos:2].set(giver - shifted).at[2:2 + 2 * twos:2].set(sink + shifted)
    return tallies[jax.random.permutation(jax.random.fold_in(key, 2), amount)]


def normal_values(key, shape, deviation, limit, pieces=(), held_as=jnp.bfloat16):
    level = steps_of(key, shape, pieces, -0.22, 0.18) if pieces else 1.0
    values = jax.random.normal(key, shape, jnp.float32) * deviation * level
    return jnp.minimum(jnp.maximum(values, -limit), limit).astype(held_as)


def gaussian_with(stream_key, dims, scale, most, pieces, heavy, held_as=jnp.bfloat16):
    result = scale * jax.random.normal(stream_key, dims, jnp.float32)
    if pieces:
        result = result * steps_of(stream_key, dims, pieces, -0.22, 0.18)
    return jnp.clip(with_spikes(result, jax.random.fold_in(stream_key, 3), *heavy), -most, most).astype(held_as)


def setup_inputs(seed: int = 0) -> dict:
    key_of = jax.random.split(jax.random.key(seed), 11)
    hidden_input = gaussian_with(key_of[0], (LOOP_COUNT, TOKENS, MODEL_WIDTH), 1.0, 6.0, ((0, 2), (1, 16)), (1, 2, 16, 2.0))
    sequence_lengths = jax.vmap(lambda own: ragged(own, NSEQ, TOKENS, MAXLEN, 2))(jax.random.split(key_of[1], LOOP_COUNT)).reshape((LOOP_COUNT, NSEQ)).astype(jnp.int32)
    norm_gain_values = jnp.clip(1.0 + 0.1 * jax.random.normal(key_of[2], (2, MODEL_WIDTH), jnp.float32), 0.5, 1.5).astype(jnp.bfloat16)
    input_proj_weight = normal_values(key_of[3], (MODEL_WIDTH, PROJECT_COLUMNS), MODEL_WIDTH ** -0.5, 0.125, ((0, 16),))
    output_proj_weight = normal_values(key_of[4], (MODEL_WIDTH, QUERY_WIDTH), (max(QUERY_WIDTH // 256, 1)) ** -0.5, 2.0, ((0, 16),))
    feedforward_weight = normal_values(key_of[5], (HIDDEN_COUNT, 3, MODEL_WIDTH), (2 * MODEL_WIDTH) ** -0.5, 0.09375, ((0, 16),))
    adapter_first = normal_values(key_of[6], (LOOP_COUNT, MODEL_WIDTH, 6 * ADAPTER_RANK), MODEL_WIDTH ** -0.5, 0.125, ((0, 2),))
    adapter_second = normal_values(key_of[7], (LOOP_COUNT, ADAPTER_RANK, ADAPTER_COLUMNS), (4 * ADAPTER_RANK) ** -0.5, 0.1875, ((0, 2),))
    adapter_down_first = normal_values(key_of[8], (LOOP_COUNT, HIDDEN_COUNT, ADAPTER_RANK), HIDDEN_COUNT ** -0.5, 0.046875, ((0, 2),))
    output_gradient = gaussian_with(key_of[9], (LOOP_COUNT, TOKENS, MODEL_WIDTH), 1.0, 6.0, ((0, 2), (1, 16)), (1, 2, 16, 2.0))
    return dict(hidden_input=hidden_input, sequence_lengths=sequence_lengths, norm_gain_values=norm_gain_values, input_proj_weight=input_proj_weight, output_proj_weight=output_proj_weight, feedforward_weight=feedforward_weight, adapter_first=adapter_first, adapter_second=adapter_second, adapter_down_first=adapter_down_first, output_gradient=output_gradient)


epsilon = 1e-06

@jax.custom_vjp
def low_rank_rows(v):
    return lax.optimization_barrier(v.astype(jnp.bfloat16)).astype(jnp.float32)

@jax.custom_vjp
def low_rank_backward(v):
    return v

def low_keep(v):
    return (low_rank_rows(v), None)

def low_pass(kept, grad):
    return (grad,)

def back_keep(v):
    return (v, None)

def back_low(kept, grad):
    return (low_rank_rows(grad),)
low_rank_rows.defvjp(low_keep, low_pass)
low_rank_backward.defvjp(back_keep, back_low)

def matrix_product_exact(former, latter):
    return jnp.dot(former, latter, precision=lax.Precision.HIGHEST, preferred_element_type=jnp.float32)

def segment_info(lengths, row_count):
    row_ids = jnp.arange(row_count, dtype=jnp.int32)
    finish = jnp.cumsum(lengths).astype(jnp.int32)
    starts = (finish - lengths).astype(jnp.int32)
    segment = lax.optimization_barrier(jnp.sum((row_ids[:, None] >= finish[None, :]).astype(jnp.int32), axis=1)).astype(jnp.int32)
    labels = jnp.arange(lengths.shape[0], dtype=jnp.int32)
    opening = lax.optimization_barrier(jnp.sum(jnp.where(segment[:, None] == labels[None, :], starts[None, :], 0), axis=1)).astype(jnp.int32)
    return (segment, (row_ids - opening).astype(jnp.int32))

def rotate(values, position, direction):
    half_dim = HEAD_WIDTH // 2
    frequency = jnp.exp(jnp.arange(half_dim).astype(jnp.float32) * (-2.0 * math.log(10000.0) / HEAD_WIDTH))
    angles = position.astype(jnp.float32)[:, None] * frequency[None, :]
    cosine = jnp.cos(angles)[:, None, :]
    sine_val = direction * jnp.sin(angles)[:, None, :]
    shaped = values.reshape(values.shape[0], -1, HEAD_WIDTH)
    former = shaped[..., :half_dim]
    latter = shaped[..., half_dim:]
    turned = jnp.concatenate([former * cosine - latter * sine_val, latter * cosine + former * sine_val], axis=-1)
    return turned.reshape(values.shape)

def rms_norm(values, gain):
    return values * lax.rsqrt(lax.optimization_barrier(jnp.mean(values * values, axis=-1, keepdims=True)) + epsilon) * gain

def gelu_tanh(values):
    return jax.nn.gelu(values, approximate=True)

def attend_all(query_rot, key_rot, value_every, segment):
    row_count = query_rot.shape[0]
    block_rows = 4 * TOK_DEV
    blocks = row_count // block_rows
    row_ids = jnp.arange(row_count, dtype=jnp.int32)
    scaling = HEAD_WIDTH ** (-0.5)

    def one_block(inputs):
        queries, segment_rows, row_block = inputs
        product = jnp.einsum('thd,ud->thu', queries, key_rot, precision=lax.Precision.HIGHEST, preferred_element_type=jnp.float32) * scaling
        product = low_rank_backward(product)
        allowed = (segment_rows[:, None] == segment[None, :]) & (row_block[:, None] >= row_ids[None, :])
        product = jnp.where(allowed[:, None, :], product, -1e+30)
        weights = jax.nn.softmax(product, axis=-1)
        mixture = jnp.einsum('thu,ud->thd', low_rank_rows(weights), value_every, precision=lax.Precision.HIGHEST, preferred_element_type=jnp.float32)
        return mixture.reshape(block_rows, QUERY_WIDTH)
    queries = query_rot.reshape(blocks, block_rows, HEADS, HEAD_WIDTH)
    mixture = lax.map(jax.checkpoint(one_block), (queries, segment.reshape(blocks, block_rows), row_ids.reshape(blocks, block_rows)))
    return mixture.reshape(row_count, QUERY_WIDTH)

def layer_forward(hidden_state, gains, attention_input_proj, attention_output_proj, feedforward, first_factor, second_factor, down_factor, segment, position):
    normalized = low_rank_rows(rms_norm(hidden_state, gains[0]))
    adapter_projection = low_rank_backward(low_rank_rows(matrix_product_exact(normalized, first_factor[:, :3 * ADAPTER_RANK])))
    projected_rows = matrix_product_exact(normalized, attention_input_proj)
    query_unrotated = low_rank_backward(projected_rows[:, :QUERY_WIDTH] + matrix_product_exact(adapter_projection[:, :ADAPTER_RANK], second_factor[:, :QUERY_WIDTH]))
    key_unrotated = low_rank_backward(projected_rows[:, QUERY_WIDTH:QUERY_WIDTH + HEAD_WIDTH] + matrix_product_exact(adapter_projection[:, ADAPTER_RANK:2 * ADAPTER_RANK], second_factor[:, QUERY_WIDTH:QUERY_WIDTH + HEAD_WIDTH]))
    value_every = low_rank_backward(low_rank_rows(projected_rows[:, QUERY_WIDTH + HEAD_WIDTH:] + matrix_product_exact(adapter_projection[:, 2 * ADAPTER_RANK:], second_factor[:, QUERY_WIDTH + HEAD_WIDTH:PROJECT_COLUMNS])))
    query_rot = low_rank_rows(rotate(query_unrotated, position, 1.0))
    key_rot = low_rank_rows(rotate(key_unrotated, position, 1.0))
    attention_output = low_rank_backward(low_rank_rows(attend_all(query_rot, key_rot, value_every, segment)))
    adapter_output = low_rank_backward(low_rank_rows(matrix_product_exact(attention_output, first_factor[:, 3 * ADAPTER_RANK:4 * ADAPTER_RANK])))
    middle_state = hidden_state + low_rank_backward(matrix_product_exact(attention_output, attention_output_proj.T) + matrix_product_exact(adapter_output, second_factor[:, PROJECT_COLUMNS:PROJECT_COLUMNS + MODEL_WIDTH]))
    normalized_second = low_rank_rows(rms_norm(middle_state, gains[1]))
    adapter_feedforward = low_rank_backward(low_rank_rows(matrix_product_exact(normalized_second, first_factor[:, 4 * ADAPTER_RANK:])))
    gate_column_start = PROJECT_COLUMNS + MODEL_WIDTH
    gate_activation = low_rank_backward(matrix_product_exact(normalized_second, feedforward[:, 0, :].T) + matrix_product_exact(adapter_feedforward[:, :ADAPTER_RANK], second_factor[:, gate_column_start:gate_column_start + HIDDEN_COUNT]))
    upward_activation = low_rank_backward(matrix_product_exact(normalized_second, feedforward[:, 1, :].T) + matrix_product_exact(adapter_feedforward[:, ADAPTER_RANK:], second_factor[:, gate_column_start + HIDDEN_COUNT:gate_column_start + 2 * HIDDEN_COUNT]))
    hidden_unit_rows = low_rank_rows(gelu_tanh(gate_activation) * upward_activation)
    adapter_hidden = low_rank_backward(low_rank_rows(matrix_product_exact(hidden_unit_rows, down_factor)))
    feedforward_branch = low_rank_backward(matrix_product_exact(hidden_unit_rows, feedforward[:, 2, :]) + matrix_product_exact(adapter_hidden, second_factor[:, gate_column_start + 2 * HIDDEN_COUNT:]))
    return middle_state + feedforward_branch

def reference(hidden_input, sequence_lengths, norm_gain_values, input_proj_weight, output_proj_weight, feedforward_weight, adapter_first, adapter_second, adapter_down_first, output_gradient):
    norm_gain_pair = norm_gain_values.astype(jnp.float32)
    attention_input_proj = input_proj_weight.astype(jnp.float32)
    attention_output_proj = output_proj_weight.astype(jnp.float32)
    feedforward_rows = feedforward_weight.astype(jnp.float32)
    gain_total = jnp.zeros_like(norm_gain_pair)
    in_total = jnp.zeros_like(attention_input_proj)
    out_total = jnp.zeros_like(attention_output_proj)
    ffn_total = jnp.zeros_like(feedforward_rows)
    outputs = []
    input_grads = []
    first_grads = []
    second_grads = []
    down_grads = []
    for loop_group_index in range(LOOP_COUNT):
        segment, position = segment_info(sequence_lengths[loop_group_index], TOKENS)
        forward_apply = partial(layer_forward, segment=segment, position=position)
        result_value, pullback_function = jax.vjp(forward_apply, hidden_input[loop_group_index].astype(jnp.float32), norm_gain_pair, attention_input_proj, attention_output_proj, feedforward_rows, adapter_first[loop_group_index].astype(jnp.float32), adapter_second[loop_group_index].astype(jnp.float32), adapter_down_first[loop_group_index].astype(jnp.float32))
        grads = pullback_function(output_gradient[loop_group_index].astype(jnp.float32))
        outputs.append(result_value.astype(jnp.bfloat16))
        input_grads.append(grads[0])
        gain_total = gain_total + grads[1]
        in_total = in_total + grads[2]
        out_total = out_total + grads[3]
        ffn_total = ffn_total + grads[4]
        first_grads.append(grads[5])
        second_grads.append(grads[6])
        down_grads.append(grads[7])
    return (jnp.stack(outputs), jnp.stack(input_grads), gain_total, in_total, out_total, ffn_total, jnp.stack(first_grads), jnp.stack(second_grads), jnp.stack(down_grads))
```

```python
import math

import jax
import jax.numpy as jnp
from jax import lax
from jax.sharding import PartitionSpec as P

MODEL_WIDTH = 2048
HEADS = 8
HEAD_WIDTH = 256
HIDDEN_COUNT = 16384
ADAPTER_RANK = 256
QUERY_WIDTH = 2048
PROJECT_COLUMNS = 2560
ADAPTER_COLUMNS = 39424
GATE_START = PROJECT_COLUMNS + MODEL_WIDTH

epsilon = 1e-06
bf16 = jnp.bfloat16
f32 = jnp.float32


def matrix_product(former, latter):
    return jnp.dot(former, latter, preferred_element_type=f32)


def times_transposed(former, latter):
    return lax.dot_general(former, latter, (((1,), (1,)), ((), ())), preferred_element_type=f32)


def outer_product_rows(former, latter):
    return lax.dot_general(former, latter, (((0,), (0,)), ((), ())), preferred_element_type=f32)


def segment_info(lengths, row_count):
    row_ids = jnp.arange(row_count, dtype=jnp.int32)
    count = lengths.shape[0]
    labels = jnp.arange(count, dtype=jnp.int32)
    finish = jnp.sum(jnp.where(labels[:, None] <= labels[None, :], lengths[:, None], 0), axis=0)
    starts = finish - lengths
    segment = jnp.sum((row_ids[:, None] >= finish[None, :]).astype(jnp.int32), axis=1)
    opening = jnp.sum(jnp.where(segment[:, None] == labels[None, :], starts[None, :], 0), axis=1)
    return (segment, row_ids - opening)


def rotate(values, position, direction):
    half_dim = HEAD_WIDTH // 2
    frequency = jnp.exp(
        jnp.arange(half_dim).astype(f32) * (-2.0 * math.log(10000.0) / HEAD_WIDTH)
    )
    angles = position.astype(f32)[:, None] * frequency[None, :]
    cosine = jnp.cos(angles)[:, None, :]
    sine_val = direction * jnp.sin(angles)[:, None, :]
    shaped = values.reshape(values.shape[0], -1, HEAD_WIDTH)
    former = shaped[..., :half_dim]
    latter = shaped[..., half_dim:]
    turned = jnp.concatenate(
        [former * cosine - latter * sine_val, latter * cosine + former * sine_val], axis=-1
    )
    return turned.reshape(values.shape)


def rms_scale(values):
    return lax.rsqrt(jnp.mean(values * values, axis=-1, keepdims=True) + epsilon)


def gelu_tanh(values):
    return jax.nn.gelu(values, approximate=True)


def unit_backward(gate_value, upward_activation, hidden_unit_gradient):
    activated, pullback_function = jax.vjp(gelu_tanh, gate_value)
    gate_grad = pullback_function(hidden_unit_gradient * upward_activation)[0]
    return (gate_grad.astype(bf16), (hidden_unit_gradient * activated).astype(bf16))


def scores_of(query_heads, key_rows, allowed, scaling):
    product = (
        jnp.einsum("thd,ud->thu", query_heads, key_rows, preferred_element_type=f32) * scaling
    )
    return jnp.where(allowed[:, None, :], product, -1e30)


def gather_rows(block):
    return lax.all_gather(block, "fsdp", axis=0, tiled=True)


def scatter_rows(partial):
    return lax.psum_scatter(partial.astype(bf16), "fsdp", scatter_dimension=0, tiled=True).astype(f32)


def turn(block):
    return lax.all_to_all(block, "fsdp", split_axis=1, concat_axis=0, tiled=True)


def per_device(
    hidden_input,
    sequence_lengths,
    norm_gain_values,
    input_proj_weight,
    output_proj_weight,
    feedforward_weight,
    adapter_first,
    adapter_second,
    adapter_down_first,
    output_gradient,
):
    size = lax.axis_size("fsdp")
    place = lax.axis_index("fsdp")
    tokens_dev = hidden_input.shape[1]
    all_rows = tokens_dev * size
    hidden_own = HIDDEN_COUNT // size
    width_own = MODEL_WIDTH // size
    columns_own = ADAPTER_COLUMNS // size
    offset = place * tokens_dev
    segment_all, position_all = segment_info(sequence_lengths[0], all_rows)
    segment_own = lax.dynamic_slice_in_dim(segment_all, offset, tokens_dev)
    position_own = lax.dynamic_slice_in_dim(position_all, offset, tokens_dev)
    row_all = jnp.arange(all_rows, dtype=jnp.int32)
    row_own = offset + jnp.arange(tokens_dev, dtype=jnp.int32)
    allowed = (segment_own[:, None] == segment_all[None, :]) & (
        row_own[:, None] >= row_all[None, :]
    )
    gains = norm_gain_values.astype(f32)
    first_factor = adapter_first[0]
    second_factor = adapter_second[0]
    rank = ADAPTER_RANK
    narrow_projection = first_factor[:, : 3 * rank]
    narrow_output = first_factor[:, 3 * rank : 4 * rank]
    squeeze_gate = first_factor[:, 4 * rank : 5 * rank]
    squeeze_up = first_factor[:, 5 * rank :]
    narrow_down = lax.dynamic_slice_in_dim(adapter_down_first[0], place * hidden_own, hidden_own, 0)
    widen_query = second_factor[:, :QUERY_WIDTH]
    widen_key = second_factor[:, QUERY_WIDTH : QUERY_WIDTH + HEAD_WIDTH]
    widen_value = second_factor[:, QUERY_WIDTH + HEAD_WIDTH : PROJECT_COLUMNS]
    widen_output = second_factor[:, PROJECT_COLUMNS:GATE_START]
    widen_gate = lax.dynamic_slice_in_dim(
        second_factor, GATE_START + place * hidden_own, hidden_own, 1
    )
    widen_up = lax.dynamic_slice_in_dim(
        second_factor, GATE_START + HIDDEN_COUNT + place * hidden_own, hidden_own, 1
    )
    widen_down = second_factor[:, GATE_START + 2 * HIDDEN_COUNT :]
    scaling = HEAD_WIDTH ** (-0.5)

    hidden_state = hidden_input[0].astype(f32)
    scale_one = rms_scale(hidden_state)
    normalized = (hidden_state * scale_one * gains[0]).astype(bf16)
    proj_in = gather_rows(input_proj_weight)
    proj_out = gather_rows(output_proj_weight)
    lora_qkv = matrix_product(normalized, narrow_projection).astype(bf16)
    projected = matrix_product(normalized, proj_in)
    query_pre = projected[:, :QUERY_WIDTH] + matrix_product(lora_qkv[:, :rank], widen_query)
    key_pre = projected[:, QUERY_WIDTH : QUERY_WIDTH + HEAD_WIDTH] + matrix_product(
        lora_qkv[:, rank : 2 * rank], widen_key
    )
    value_local = (
        projected[:, QUERY_WIDTH + HEAD_WIDTH :]
        + matrix_product(lora_qkv[:, 2 * rank :], widen_value)
    ).astype(bf16)
    query_rot = rotate(query_pre, position_own, 1.0).astype(bf16)
    key_rot = rotate(key_pre, position_own, 1.0).astype(bf16)
    keys_all = gather_rows(jnp.concatenate([key_rot, value_local], axis=1))
    key_rows, value_rows = keys_all[:, :HEAD_WIDTH], keys_all[:, HEAD_WIDTH:]
    query_heads = query_rot.reshape(tokens_dev, HEADS, HEAD_WIDTH)
    scores = scores_of(query_heads, key_rows, allowed, scaling)
    row_max = jnp.max(scores, axis=-1, keepdims=True)
    powered = jnp.exp(scores - row_max)
    row_sum = jnp.sum(powered, axis=-1, keepdims=True)
    probs = powered / row_sum
    probs_low = probs.astype(bf16)
    attended = (
        jnp.einsum("thu,ud->thd", probs_low, value_rows, preferred_element_type=f32)
        .reshape(tokens_dev, QUERY_WIDTH)
        .astype(bf16)
    )
    lora_out = matrix_product(attended, narrow_output).astype(bf16)
    middle = (
        hidden_state
        + times_transposed(attended, proj_out)
        + matrix_product(lora_out, widen_output)
    )
    scale_two = rms_scale(middle)
    normed_two = (middle * scale_two * gains[1]).astype(bf16)

    grad_all = gather_rows(output_gradient[0])
    two_all = gather_rows(normed_two)
    weight_gate = feedforward_weight[:, 0, :]
    weight_up = feedforward_weight[:, 1, :]
    weight_down = feedforward_weight[:, 2, :]
    lora_gate = matrix_product(two_all, squeeze_gate).astype(bf16)
    lora_up = matrix_product(two_all, squeeze_up).astype(bf16)
    hd_grad = times_transposed(grad_all, widen_down).astype(bf16)
    gate = times_transposed(two_all, weight_gate) + matrix_product(lora_gate, widen_gate)
    upward = times_transposed(two_all, weight_up) + matrix_product(lora_up, widen_up)
    units = (gelu_tanh(gate) * upward).astype(bf16)
    units_grad = times_transposed(grad_all, weight_down) + times_transposed(hd_grad, narrow_down)
    gate_grad, up_grad = unit_backward(gate, upward, units_grad)
    back_part = jnp.concatenate(
        [
            matrix_product(gate_grad, weight_gate) + matrix_product(up_grad, weight_up),
            times_transposed(gate_grad, widen_gate),
            times_transposed(up_grad, widen_up),
        ],
        axis=1,
    )
    back_own = scatter_rows(back_part)
    out_part = jnp.concatenate(
        [matrix_product(units, weight_down), matrix_product(units, narrow_down)], axis=1
    )
    out_own = scatter_rows(out_part)
    ffn_grad = jnp.stack(
        [
            outer_product_rows(gate_grad, two_all),
            outer_product_rows(up_grad, two_all),
            outer_product_rows(units, grad_all),
        ],
        axis=1,
    ).astype(bf16)
    ffn_sum = lax.psum(ffn_grad, "loop").astype(f32)
    down_own = outer_product_rows(units, hd_grad)
    gate_piece = outer_product_rows(lora_gate, gate_grad)
    up_piece = outer_product_rows(lora_up, up_grad)

    lora_hd = out_own[:, MODEL_WIDTH:].astype(bf16)
    hidden_out = (middle + out_own[:, :MODEL_WIDTH] + matrix_product(lora_hd, widen_down)).astype(bf16)

    gate_low = back_own[:, MODEL_WIDTH : MODEL_WIDTH + rank].astype(bf16)
    up_low = back_own[:, MODEL_WIDTH + rank :].astype(bf16)
    two_grad = (
        back_own[:, :MODEL_WIDTH]
        + times_transposed(gate_low, squeeze_gate)
        + times_transposed(up_low, squeeze_up)
    )
    weighted_two = gains[1] * two_grad
    middle_grad = (
        output_gradient[0].astype(f32)
        + scale_two * weighted_two
        - middle * scale_two**3 * jnp.mean(middle * weighted_two, axis=-1, keepdims=True)
    )
    gain_two = jnp.sum(two_grad * middle * scale_two, axis=0)

    branch_grad = middle_grad.astype(bf16)
    lora_out_grad = times_transposed(branch_grad, widen_output).astype(bf16)
    attended_grad = (
        matrix_product(branch_grad, proj_out) + times_transposed(lora_out_grad, narrow_output)
    ).astype(bf16)
    heads_grad = attended_grad.reshape(tokens_dev, HEADS, HEAD_WIDTH)
    prob_grad = jnp.einsum("thd,ud->thu", heads_grad, value_rows, preferred_element_type=f32)
    row_dot = jnp.sum(probs * prob_grad, axis=-1, keepdims=True)
    score_grad = (probs * (prob_grad - row_dot)).astype(bf16)
    query_rot_grad = (
        jnp.einsum("thu,ud->thd", score_grad, key_rows, preferred_element_type=f32) * scaling
    )
    key_part = (
        jnp.einsum("thu,thd->ud", score_grad, query_heads, preferred_element_type=f32) * scaling
    )
    value_part = jnp.einsum("thu,thd->ud", probs_low, heads_grad, preferred_element_type=f32)
    pair_grad = scatter_rows(jnp.concatenate([key_part, value_part], axis=1))
    query_grad = rotate(
        query_rot_grad.reshape(tokens_dev, QUERY_WIDTH), position_own, -1.0
    ).astype(bf16)
    key_grad = rotate(pair_grad[:, :HEAD_WIDTH], position_own, -1.0).astype(bf16)
    value_grad = pair_grad[:, HEAD_WIDTH:].astype(bf16)
    proj_grad = jnp.concatenate([query_grad, key_grad, value_grad], axis=1)
    lora_qkv_grad = jnp.concatenate(
        [
            times_transposed(query_grad, widen_query),
            times_transposed(key_grad, widen_key),
            times_transposed(value_grad, widen_value),
        ],
        axis=1,
    ).astype(bf16)
    normed_grad = times_transposed(proj_grad, proj_in) + times_transposed(
        lora_qkv_grad, narrow_projection
    )
    weighted_one = gains[0] * normed_grad
    input_grad = (
        middle_grad
        + scale_one * weighted_one
        - hidden_state
        * scale_one**3
        * jnp.mean(hidden_state * weighted_one, axis=-1, keepdims=True)
    )
    gain_one = jnp.sum(normed_grad * hidden_state * scale_one, axis=0)
    gain_sum = lax.psum(
        lax.psum_scatter(
            jnp.stack([gain_one, gain_two]), "fsdp", scatter_dimension=1, tiled=True
        ).astype(bf16),
        "loop",
    ).astype(f32)

    attended_all = gather_rows(jnp.concatenate([attended, lora_qkv], axis=1))
    lora_qkv_all = attended_all[:, QUERY_WIDTH:]
    attended_all = attended_all[:, :QUERY_WIDTH]
    lora_out_all = matrix_product(attended_all, narrow_output).astype(bf16)
    low_all = gather_rows(
        jnp.concatenate([lora_out_grad, gate_low, up_low, lora_hd], axis=1)
    )
    proj_all = gather_rows(jnp.concatenate([proj_grad, lora_qkv_grad], axis=1))
    qkv_low_all = proj_all[:, PROJECT_COLUMNS:]
    proj_all = proj_all[:, :PROJECT_COLUMNS]
    normed_turn = turn(normalized)
    branch_turn = turn(branch_grad)
    column = place * width_own
    attended_turn = lax.dynamic_slice_in_dim(attended_all, column, width_own, 1)
    two_turn = lax.dynamic_slice_in_dim(two_all, column, width_own, 1)
    attn_part = jnp.concatenate(
        [outer_product_rows(normed_turn, proj_all), outer_product_rows(branch_turn, attended_all)],
        axis=1,
    ).astype(bf16)
    attn_sum = lax.psum(attn_part, "loop").astype(f32)
    squeeze_own = jnp.concatenate(
        [
            outer_product_rows(normed_turn, qkv_low_all),
            outer_product_rows(attended_turn, low_all[:, :rank]),
            outer_product_rows(two_turn, low_all[:, rank : 3 * rank]),
        ],
        axis=1,
    )
    out_piece = outer_product_rows(lora_out_all, branch_turn)
    down_piece = outer_product_rows(low_all[:, 3 * rank :], grad_all)
    pieces = lax.all_gather(
        jnp.concatenate([out_piece, gate_piece, up_piece], axis=1).astype(bf16), "fsdp", axis=0
    )

    def laid(first, last):
        return pieces[:, :, first:last].transpose(1, 0, 2).reshape(rank, -1)

    expand_all = jnp.concatenate(
        [
            outer_product_rows(lora_qkv_all[:, :rank], proj_all[:, :QUERY_WIDTH]).astype(bf16),
            outer_product_rows(
                lora_qkv_all[:, rank : 2 * rank], proj_all[:, QUERY_WIDTH : QUERY_WIDTH + HEAD_WIDTH]
            ).astype(bf16),
            outer_product_rows(
                lora_qkv_all[:, 2 * rank :], proj_all[:, QUERY_WIDTH + HEAD_WIDTH :]
            ).astype(bf16),
            laid(0, width_own),
            laid(width_own, width_own + hidden_own),
            laid(width_own + hidden_own, width_own + 2 * hidden_own),
            down_piece.astype(bf16),
        ],
        axis=1,
    )
    expand_own = lax.dynamic_slice_in_dim(expand_all, place * columns_own, columns_own, 1).astype(f32)
    return (
        hidden_out[None],
        input_grad[None],
        gain_sum,
        attn_sum[:, :PROJECT_COLUMNS],
        attn_sum[:, PROJECT_COLUMNS:],
        ffn_sum,
        squeeze_own[None],
        expand_own[None],
        down_own[None],
    )


def solution(mesh):
    return jax.shard_map(
        per_device,
        mesh=mesh,
        in_specs=(
            P("loop", "fsdp", None),
            P("loop", None),
            P(),
            P("fsdp", None),
            P("fsdp", None),
            P("fsdp", None, None),
            P("loop", None, None),
            P("loop", None, None),
            P("loop", None, None),
            P("loop", "fsdp", None),
        ),
        out_specs=(
            P("loop", "fsdp", None),
            P("loop", "fsdp", None),
            P(None, "fsdp"),
            P("fsdp", None),
            P("fsdp", None),
            P("fsdp", None, None),
            P("loop", "fsdp", None),
            P("loop", None, "fsdp"),
            P("loop", "fsdp", None),
        ),
        check_vma=False,
    )
```

```python
import functools
import math

import jax
import jax.numpy as jnp
from jax import lax
from jax.experimental import pallas as pl
from jax.experimental.pallas import tpu as pltpu
from jax.sharding import PartitionSpec as P

MODEL_WIDTH = 2048
HEADS = 8
HEAD_WIDTH = 256
HIDDEN_COUNT = 16384
ADAPTER_RANK = 256
QUERY_WIDTH = 2048
PROJECT_COLUMNS = 2560
ADAPTER_COLUMNS = 39424
GATE_START = PROJECT_COLUMNS + MODEL_WIDTH

epsilon = 1e-06
bf16 = jnp.bfloat16
f32 = jnp.float32
MESH = pl.DeviceIdType.MESH


def matrix_product(former, latter):
    return jnp.dot(former, latter, preferred_element_type=f32)


def times_transposed(former, latter):
    return lax.dot_general(former, latter, (((1,), (1,)), ((), ())), preferred_element_type=f32)


def outer_product_rows(former, latter):
    return lax.dot_general(former, latter, (((0,), (0,)), ((), ())), preferred_element_type=f32)


def segment_info(lengths, row_count):
    row_ids = jnp.arange(row_count, dtype=jnp.int32)
    count = lengths.shape[0]
    labels = jnp.arange(count, dtype=jnp.int32)
    finish = jnp.sum(jnp.where(labels[:, None] <= labels[None, :], lengths[:, None], 0), axis=0)
    starts = finish - lengths
    segment = jnp.sum((row_ids[:, None] >= finish[None, :]).astype(jnp.int32), axis=1)
    opening = jnp.sum(jnp.where(segment[:, None] == labels[None, :], starts[None, :], 0), axis=1)
    return (segment, row_ids - opening)


def rotate(values, position, direction):
    half_dim = HEAD_WIDTH // 2
    frequency = jnp.exp(
        jnp.arange(half_dim).astype(f32) * (-2.0 * math.log(10000.0) / HEAD_WIDTH)
    )
    angles = position.astype(f32)[:, None] * frequency[None, :]
    cosine = jnp.cos(angles)[:, None, :]
    sine_val = direction * jnp.sin(angles)[:, None, :]
    shaped = values.reshape(values.shape[0], -1, HEAD_WIDTH)
    former = shaped[..., :half_dim]
    latter = shaped[..., half_dim:]
    turned = jnp.concatenate(
        [former * cosine - latter * sine_val, latter * cosine + former * sine_val], axis=-1
    )
    return turned.reshape(values.shape)


def rms_scale(values):
    return lax.rsqrt(jnp.mean(values * values, axis=-1, keepdims=True) + epsilon)


def gelu_tanh(values):
    return jax.nn.gelu(values, approximate=True)


def unit_backward(gate_value, upward_activation, hidden_unit_gradient):
    activated, pullback_function = jax.vjp(gelu_tanh, gate_value)
    gate_grad = pullback_function(hidden_unit_gradient * upward_activation)[0]
    return (gate_grad.astype(bf16), (hidden_unit_gradient * activated).astype(bf16))


def scores_of(query_heads, key_rows, allowed, scaling):
    product = (
        jnp.einsum("thd,ud->thu", query_heads, key_rows, preferred_element_type=f32) * scaling
    )
    return jnp.where(allowed[:, None, :], product, -1e30)


def gather_rows(block):
    return lax.all_gather(block, "fsdp", axis=0, tiled=True)


def scatter_rows(partial):
    return lax.psum_scatter(partial.astype(bf16), "fsdp", scatter_dimension=0, tiled=True).astype(f32)


def both_loops(partial):
    shares = lax.all_gather(partial.astype(bf16), "loop", axis=0)
    return shares[0].astype(f32) + shares[1].astype(f32)


def turn(block):
    return lax.all_to_all(block, "fsdp", split_axis=1, concat_axis=0, tiled=True)


def chip_at(q, chips):
    return jnp.where(q < 4, 2 * q, 15 - 2 * q) if chips == 8 else q

def ring_place(chip, chips):
    return jnp.where(chip % 2 == 0, chip // 2, 7 - chip // 2) if chips == 8 else chip

def ring_neighbours(chips):
    me = lax.axis_index("fsdp")
    core = me % 2
    p = ring_place(me // 2, chips)
    def device(shift, c):
        return chip_at((p + shift + chips) % chips, chips) * 2 + c
    return core, device

def meet(devices):
    barrier = pltpu.get_barrier_semaphore()
    for d in devices:
        pl.semaphore_signal(barrier, inc=1, device_id={"fsdp": d}, device_id_type=MESH)
    pl.semaphore_wait(barrier, len(devices))

def gather_kernel(chips, x_ref, o_ref, own_sem, ring_send, ring_recv, side_send, side_recv):
    core, device = ring_neighbours(chips)
    rows = x_ref.shape[0]
    reach = chips // 2
    ways = (device(1, core), device(-1, core))
    side = device(0, 1 - core)
    meet((*ways, side))

    def span(way, hops):
        return (way * (rows // 2), rows // 2) if hops == reach else (0, rows)

    def at(way, hops, c, part):
        origin = device(-hops if way == 0 else hops, c)
        return o_ref.at[pl.ds(pl.multiple_of(origin * rows + part[0], 8), part[1])]

    def hop(way, hops):
        part = span(way, hops)
        here = at(way, hops - 1, core, part)
        src = x_ref.at[pl.ds(part[0], part[1])] if hops == 1 else here
        return pltpu.make_async_remote_copy(src, here, ring_send.at[way, hops - 1], ring_recv.at[way, hops - 1], device_id={"fsdp": ways[way]}, device_id_type=MESH)

    def arriving(way, hops):
        here = at(way, hops, core, span(way, hops))
        return pltpu.make_async_remote_copy(here, here, ring_send.at[way, hops - 1], ring_recv.at[way, hops - 1], device_id={"fsdp": ways[way]}, device_id_type=MESH)

    def across(way, hops, c):
        part = span(way, hops) if hops else (0, rows)
        there = at(way, hops, c, part)
        src = there if hops else x_ref
        return pltpu.make_async_remote_copy(src, there, side_send.at[way, hops], side_recv.at[way, hops], device_id={"fsdp": side}, device_id_type=MESH)

    for way in (0, 1):
        hop(way, 1).start()
    across(0, 0, core).start()
    own = pltpu.make_async_copy(x_ref, at(0, 0, core, (0, rows)), own_sem)
    own.start()
    for hops in range(1, reach + 1):
        for way in (0, 1):
            arriving(way, hops).wait_recv()
            if hops < reach:
                hop(way, hops + 1).start()
            across(way, hops, core).start()
    across(0, 0, 1 - core).wait_recv()
    across(0, 0, core).wait_send()
    for hops in range(1, reach + 1):
        for way in (0, 1):
            across(way, hops, 1 - core).wait_recv()
            across(way, hops, core).wait_send()
            hop(way, hops).wait_send()
    own.wait()

def busy(us):
    return pl.CostEstimate(flops=0, bytes_accessed=int(us * 3.0e6), transcendentals=0)


def ring_gather(block, ident):
    size = lax.axis_size("fsdp")
    chips = size // 2
    rows, columns = block.shape
    pair = pltpu.SemaphoreType.DMA((2, chips // 2))
    sides = pltpu.SemaphoreType.DMA((2, chips // 2 + 1))
    return pl.pallas_call(
        functools.partial(gather_kernel, chips),
        out_shape=jax.ShapeDtypeStruct((size * rows, columns), block.dtype),
        in_specs=[pl.BlockSpec(memory_space=pl.ANY)],
        out_specs=pl.BlockSpec(memory_space=pl.ANY),
        scratch_shapes=[pltpu.SemaphoreType.DMA, pair, pair, sides, sides],
        compiler_params=pltpu.CompilerParams(collective_id=ident, has_side_effects=True),
        cost_estimate=busy(size * rows * columns * 2 / 180e3 + 10),
        name="ring_gather",
    )(block)

def scatter_kernel(chips, x_ref, o_ref, side_buf, ring_buf, send_buf, side_send, side_recv, ring_send, ring_recv):
    core, device = ring_neighbours(chips)
    rows, columns = o_ref.shape
    reach = chips // 2
    half = columns // 2
    ways = (device(1, core), device(-1, core))
    side = device(0, 1 - core)
    meet((*ways, side))

    def shift(way, hops):
        return (hops if way == 0 else chips - hops) % chips

    def across(target, c):
        there = pl.ds(pl.multiple_of(device(target, c) * rows, 16), rows)
        return pltpu.make_async_remote_copy(x_ref.at[there], side_buf.at[target], side_send.at[target], side_recv.at[target], device_id={"fsdp": side}, device_id_type=MESH)

    def hop(way, step):
        cols = pl.ds(way * half, half) if step == 0 else pl.ds(0, columns)
        return pltpu.make_async_remote_copy(send_buf.at[way, step, :, cols], ring_buf.at[way, step, :, cols], ring_send.at[way, step], ring_recv.at[way, step], device_id={"fsdp": ways[way]}, device_id_type=MESH)

    order = [reach] + [shift(way, hops) for hops in range(reach - 1, 0, -1) for way in (0, 1)] + [0]
    for target in order:
        across(target, 1 - core).start()
    tile = 16

    def add(target, incoming, store):
        first = pl.multiple_of(device(target, core) * rows, 16)
        @pl.loop(0, rows // tile)
        def _(i):
            here = pl.ds(pl.multiple_of(i * tile, tile), tile)
            total = x_ref[pl.ds(pl.multiple_of(first + i * tile, tile), tile), :].astype(f32) + side_buf[target, here, :].astype(f32)
            store(here, total, [(way, step, ring_buf[way, step, here, pl.ds(way * half, half) if step == 0 else pl.ds(0, columns)].astype(f32)) for way, step in incoming])

    for step in range(reach):
        hops = reach - step
        for way in (0, 1):
            target = shift(way, hops)
            if step or way == 0:
                across(target, core).wait_recv()
            if step:
                hop(way, step - 1).wait_recv()

            def store(here, total, more, way=way, step=step):
                if step == 0:
                    send_buf[way, step, here, pl.ds(way * half, half)] = total[:, way * half:(way + 1) * half].astype(bf16)
                elif step == 1:
                    other = total[:, (1 - way) * half:(2 - way) * half]
                    send_buf[way, step, here, pl.ds((1 - way) * half, half)] = other.astype(bf16)
                    send_buf[way, step, here, pl.ds(way * half, half)] = (total[:, way * half:(way + 1) * half] + more[0][2]).astype(bf16)
                else:
                    send_buf[way, step, here, :] = (total + more[0][2]).astype(bf16)
            add(target, [(way, step - 1)] if step else [], store)
            hop(way, step).start()
    across(0, core).wait_recv()
    for way in (0, 1):
        hop(way, reach - 1).wait_recv()

    def last(here, total, more):
        o_ref[here, :] = total + (more[0][2] + more[1][2])
    add(0, [(0, reach - 1), (1, reach - 1)], last)
    for target in order:
        across(target, 1 - core).wait_send()
    for step in range(reach):
        for way in (0, 1):
            hop(way, step).wait_send()

def ring_scatter(partial, ident):
    size = lax.axis_size("fsdp")
    if size != 16:
        return scatter_rows(partial)
    partial = partial.astype(bf16)
    chips = size // 2
    rows, columns = partial.shape[0] // size, partial.shape[1]
    pair = pltpu.SemaphoreType.DMA((2, chips // 2))
    sides = pltpu.SemaphoreType.DMA((chips,))
    return pl.pallas_call(
        functools.partial(scatter_kernel, chips),
        out_shape=jax.ShapeDtypeStruct((rows, columns), f32),
        in_specs=[pl.BlockSpec(memory_space=pltpu.VMEM)],
        out_specs=pl.BlockSpec(memory_space=pltpu.VMEM),
        scratch_shapes=[
            pltpu.VMEM((chips, rows, columns), bf16),
            pltpu.VMEM((2, chips // 2, rows, columns), bf16),
            pltpu.VMEM((2, chips // 2, rows, columns), bf16),
            sides, sides, pair, pair],
        compiler_params=pltpu.CompilerParams(collective_id=ident, has_side_effects=True, vmem_limit_bytes=48 << 20),
        cost_estimate=busy(size * rows * columns * 2 / 180e3 + 10),
        name="ring_scatter",
    )(partial)


def place_kernel(size, chunk, own_count, mid_ref, near_ref, far_ref, o_ref, send_sem, recv_sem, own_sem):
    me = lax.axis_index("fsdp")
    hidden = HIDDEN_COUNT // size
    width = MODEL_WIDTH // size
    sections = (
        (0, PROJECT_COLUMNS, width),
        (width, GATE_START, hidden),
        (width + hidden, GATE_START + HIDDEN_COUNT, hidden),
    )
    barrier = pltpu.get_barrier_semaphore()

    def greet(i, carry):
        other = (me + i) % size
        pl.semaphore_signal(barrier, inc=1, device_id={"fsdp": other}, device_id_type=MESH)
        return carry

    lax.fori_loop(1, size, greet, 0)
    pl.semaphore_wait(barrier, size - 1)

    def rows(ref, first):
        return ref.at[pl.ds(pl.multiple_of(first, 8), chunk)]

    def remote(source, first, owner, sent=0):
        return pltpu.make_async_remote_copy(
            source,
            rows(o_ref, first),
            send_sem.at[sent],
            recv_sem.at[first // chunk],
            device_id={"fsdp": owner},
            device_id_type=MESH,
        )

    def local(source, first):
        return pltpu.make_async_copy(source, rows(o_ref, first), own_sem.at[first // chunk])

    for base, start, length in sections:

        def send(j, carry, base=base, start=start, length=length):
            column = start + me * length + j * chunk
            owner = column // own_count
            first = column - owner * own_count
            source = rows(mid_ref, base + j * chunk)

            @pl.when(owner != me)
            def _():
                remote(source, first, owner, base // chunk + j).start()

            @pl.when(owner == me)
            def _():
                local(source, first).start()

            return carry

        lax.fori_loop(0, length // chunk, send, 0)

    def fill(j, carry):
        column = me * own_count + j * chunk

        @pl.when(column < PROJECT_COLUMNS)
        def _():
            local(rows(near_ref, column), j * chunk).start()

        @pl.when(column >= GATE_START + 2 * HIDDEN_COUNT)
        def _():
            local(rows(far_ref, column - (GATE_START + 2 * HIDDEN_COUNT)), j * chunk).start()

        return carry

    lax.fori_loop(0, own_count // chunk, fill, 0)

    def arrive(j, carry):
        column = me * own_count + j * chunk
        here = rows(o_ref, j * chunk)
        away = 0
        for _, start, length in sections:
            inside = (column >= start) & (column < start + length * size)
            away = away + (inside & ((column - start) // length != me)).astype(jnp.int32)

        @pl.when(away > 0)
        def _():
            remote(here, j * chunk, (me + 1) % size).wait_recv()

        @pl.when(away == 0)
        def _():
            local(rows(near_ref, 0), j * chunk).wait()

        return carry

    lax.fori_loop(0, own_count // chunk, arrive, 0)
    for base, start, length in sections:

        def sent(j, carry, base=base, start=start, length=length):
            column = start + me * length + j * chunk
            owner = column // own_count

            @pl.when(owner != me)
            def _():
                remote(
                    rows(mid_ref, base + j * chunk),
                    column - owner * own_count,
                    owner,
                    base // chunk + j,
                ).wait_send()

            return carry

        lax.fori_loop(0, length // chunk, sent, 0)


def place_columns(middle, near, far, ident):
    size = lax.axis_size("fsdp")
    own_count = ADAPTER_COLUMNS // size
    chunk = math.gcd(own_count, MODEL_WIDTH // size, HIDDEN_COUNT // size, PROJECT_COLUMNS, GATE_START)
    anywhere = pl.BlockSpec(memory_space=pl.ANY)
    return pl.pallas_call(
        functools.partial(place_kernel, size, chunk, own_count),
        out_shape=jax.ShapeDtypeStruct((own_count, ADAPTER_RANK), f32),
        in_specs=[anywhere] * 3,
        out_specs=anywhere,
        scratch_shapes=[
            pltpu.SemaphoreType.DMA((middle.shape[0] // chunk,)),
            pltpu.SemaphoreType.DMA((own_count // chunk,)),
            pltpu.SemaphoreType.DMA((own_count // chunk,)),
        ],
        compiler_params=pltpu.CompilerParams(collective_id=ident, has_side_effects=True),
        cost_estimate=busy(30),
        name="place_columns",
    )(middle, near, far)


def per_device(
    hidden_input,
    sequence_lengths,
    norm_gain_values,
    input_proj_weight,
    output_proj_weight,
    feedforward_weight,
    adapter_first,
    adapter_second,
    adapter_down_first,
    output_gradient,
):
    size = lax.axis_size("fsdp")
    place = lax.axis_index("fsdp")
    tokens_dev = hidden_input.shape[1]
    all_rows = tokens_dev * size
    hidden_own = HIDDEN_COUNT // size
    width_own = MODEL_WIDTH // size
    columns_own = ADAPTER_COLUMNS // size
    offset = place * tokens_dev
    segment_all, position_all = segment_info(sequence_lengths[0], all_rows)
    segment_own = lax.dynamic_slice_in_dim(segment_all, offset, tokens_dev)
    position_own = lax.dynamic_slice_in_dim(position_all, offset, tokens_dev)
    row_all = jnp.arange(all_rows, dtype=jnp.int32)
    row_own = offset + jnp.arange(tokens_dev, dtype=jnp.int32)
    allowed = (segment_own[:, None] == segment_all[None, :]) & (
        row_own[:, None] >= row_all[None, :]
    )
    gains = norm_gain_values.astype(f32)
    first_factor = adapter_first[0]
    second_factor = adapter_second[0]
    rank = ADAPTER_RANK
    narrow_projection = first_factor[:, : 3 * rank]
    narrow_output = first_factor[:, 3 * rank : 4 * rank]
    squeeze_gate = first_factor[:, 4 * rank : 5 * rank]
    squeeze_up = first_factor[:, 5 * rank :]
    narrow_down = lax.dynamic_slice_in_dim(adapter_down_first[0], place * hidden_own, hidden_own, 0)
    widen_query = second_factor[:, :QUERY_WIDTH]
    widen_key = second_factor[:, QUERY_WIDTH : QUERY_WIDTH + HEAD_WIDTH]
    widen_value = second_factor[:, QUERY_WIDTH + HEAD_WIDTH : PROJECT_COLUMNS]
    widen_output = second_factor[:, PROJECT_COLUMNS:GATE_START]
    widen_gate = lax.dynamic_slice_in_dim(
        second_factor, GATE_START + place * hidden_own, hidden_own, 1
    )
    widen_up = lax.dynamic_slice_in_dim(
        second_factor, GATE_START + HIDDEN_COUNT + place * hidden_own, hidden_own, 1
    )
    widen_down = second_factor[:, GATE_START + 2 * HIDDEN_COUNT :]
    scaling = HEAD_WIDTH ** (-0.5)

    hidden_state = hidden_input[0].astype(f32)
    scale_one = rms_scale(hidden_state)
    normalized = (hidden_state * scale_one * gains[0]).astype(bf16)
    proj_in = ring_gather(input_proj_weight, 0)
    proj_out = gather_rows(output_proj_weight)
    lora_qkv = matrix_product(normalized, narrow_projection).astype(bf16)
    projected = matrix_product(normalized, proj_in)
    query_pre = projected[:, :QUERY_WIDTH] + matrix_product(lora_qkv[:, :rank], widen_query)
    key_pre = projected[:, QUERY_WIDTH : QUERY_WIDTH + HEAD_WIDTH] + matrix_product(
        lora_qkv[:, rank : 2 * rank], widen_key
    )
    value_local = (
        projected[:, QUERY_WIDTH + HEAD_WIDTH :]
        + matrix_product(lora_qkv[:, 2 * rank :], widen_value)
    ).astype(bf16)
    query_rot = rotate(query_pre, position_own, 1.0).astype(bf16)
    key_rot = rotate(key_pre, position_own, 1.0).astype(bf16)
    keys_all = ring_gather(jnp.concatenate([key_rot, value_local], axis=1), 1)
    key_rows, value_rows = keys_all[:, :HEAD_WIDTH], keys_all[:, HEAD_WIDTH:]
    query_heads = query_rot.reshape(tokens_dev, HEADS, HEAD_WIDTH)
    scores = scores_of(query_heads, key_rows, allowed, scaling)
    row_max = jnp.max(scores, axis=-1, keepdims=True)
    powered = jnp.exp(scores - row_max)
    row_sum = jnp.sum(powered, axis=-1, keepdims=True)
    probs = powered / row_sum
    probs_low = probs.astype(bf16)
    attended = (
        jnp.einsum("thu,ud->thd", probs_low, value_rows, preferred_element_type=f32)
        .reshape(tokens_dev, QUERY_WIDTH)
        .astype(bf16)
    )
    lora_out = matrix_product(attended, narrow_output).astype(bf16)
    middle = (
        hidden_state
        + times_transposed(attended, proj_out)
        + matrix_product(lora_out, widen_output)
    )
    scale_two = rms_scale(middle)
    normed_two = (middle * scale_two * gains[1]).astype(bf16)

    grad_all = gather_rows(output_gradient[0])
    two_all = ring_gather(normed_two, 2)
    weight_gate = feedforward_weight[:, 0, :]
    weight_up = feedforward_weight[:, 1, :]
    weight_down = feedforward_weight[:, 2, :]
    lora_gate = matrix_product(two_all, squeeze_gate).astype(bf16)
    lora_up = matrix_product(two_all, squeeze_up).astype(bf16)
    hd_grad = times_transposed(grad_all, widen_down).astype(bf16)
    gate = times_transposed(two_all, weight_gate) + matrix_product(lora_gate, widen_gate)
    upward = times_transposed(two_all, weight_up) + matrix_product(lora_up, widen_up)
    units = (gelu_tanh(gate) * upward).astype(bf16)
    units_grad = times_transposed(grad_all, weight_down) + times_transposed(hd_grad, narrow_down)
    gate_grad, up_grad = unit_backward(gate, upward, units_grad)
    back_part = jnp.concatenate(
        [
            matrix_product(gate_grad, weight_gate) + matrix_product(up_grad, weight_up),
            times_transposed(gate_grad, widen_gate),
            times_transposed(up_grad, widen_up),
        ],
        axis=1,
    )
    ffn_shares = [
        outer_product_rows(former, latter).astype(bf16)
        for former, latter in ((units, grad_all), (gate_grad, two_all), (up_grad, two_all))
    ]
    out_part = jnp.concatenate(
        [matrix_product(units, weight_down), matrix_product(units, narrow_down)], axis=1
    )
    ffn_shares, out_part, back_part = lax.optimization_barrier(
        (ffn_shares, out_part.astype(bf16), back_part.astype(bf16))
    )
    down_total, gate_total, up_total = [both_loops(share) for share in ffn_shares]
    back_own = ring_scatter(back_part, 3)
    out_own = scatter_rows(out_part)
    ffn_sum = jnp.stack(
        [
            gate_total,
            up_total,
            down_total,
        ],
        axis=1,
    )
    down_own = outer_product_rows(units, hd_grad)
    gate_piece = outer_product_rows(gate_grad, lora_gate)
    up_piece = outer_product_rows(up_grad, lora_up)

    lora_hd = out_own[:, MODEL_WIDTH:].astype(bf16)
    hidden_out = (middle + out_own[:, :MODEL_WIDTH] + matrix_product(lora_hd, widen_down)).astype(bf16)

    gate_low = back_own[:, MODEL_WIDTH : MODEL_WIDTH + rank].astype(bf16)
    up_low = back_own[:, MODEL_WIDTH + rank :].astype(bf16)
    two_grad = (
        back_own[:, :MODEL_WIDTH]
        + times_transposed(gate_low, squeeze_gate)
        + times_transposed(up_low, squeeze_up)
    )
    weighted_two = gains[1] * two_grad
    middle_grad = (
        output_gradient[0].astype(f32)
        + scale_two * weighted_two
        - middle * scale_two**3 * jnp.mean(middle * weighted_two, axis=-1, keepdims=True)
    )
    gain_two = jnp.sum(two_grad * middle * scale_two, axis=0)

    branch_grad = middle_grad.astype(bf16)
    lora_out_grad = times_transposed(branch_grad, widen_output).astype(bf16)
    attended_grad = (
        matrix_product(branch_grad, proj_out) + times_transposed(lora_out_grad, narrow_output)
    ).astype(bf16)
    heads_grad = attended_grad.reshape(tokens_dev, HEADS, HEAD_WIDTH)
    prob_grad = jnp.einsum("thd,ud->thu", heads_grad, value_rows, preferred_element_type=f32)
    row_dot = jnp.sum(probs * prob_grad, axis=-1, keepdims=True)
    score_grad = (probs * (prob_grad - row_dot)).astype(bf16)
    query_rot_grad = (
        jnp.einsum("thu,ud->thd", score_grad, key_rows, preferred_element_type=f32) * scaling
    )
    key_part = (
        jnp.einsum("thu,thd->ud", score_grad, query_heads, preferred_element_type=f32) * scaling
    )
    value_part = jnp.einsum("thu,thd->ud", probs_low, heads_grad, preferred_element_type=f32)
    pair_grad = ring_scatter(jnp.concatenate([key_part, value_part], axis=1), 4)
    query_grad = rotate(
        query_rot_grad.reshape(tokens_dev, QUERY_WIDTH), position_own, -1.0
    ).astype(bf16)
    key_grad = rotate(pair_grad[:, :HEAD_WIDTH], position_own, -1.0).astype(bf16)
    value_grad = pair_grad[:, HEAD_WIDTH:].astype(bf16)
    proj_grad = jnp.concatenate([query_grad, key_grad, value_grad], axis=1)
    lora_qkv_grad = jnp.concatenate(
        [
            times_transposed(query_grad, widen_query),
            times_transposed(key_grad, widen_key),
            times_transposed(value_grad, widen_value),
        ],
        axis=1,
    ).astype(bf16)
    normed_grad = times_transposed(proj_grad, proj_in) + times_transposed(
        lora_qkv_grad, narrow_projection
    )
    weighted_one = gains[0] * normed_grad
    input_grad = (
        middle_grad
        + scale_one * weighted_one
        - hidden_state
        * scale_one**3
        * jnp.mean(hidden_state * weighted_one, axis=-1, keepdims=True)
    )
    gain_one = jnp.sum(normed_grad * hidden_state * scale_one, axis=0)
    gain_sum = lax.psum(
        lax.psum_scatter(
            jnp.stack([gain_one, gain_two]), "fsdp", scatter_dimension=1, tiled=True
        ).astype(bf16),
        "loop",
    ).astype(f32)

    attended_all = gather_rows(jnp.concatenate([attended, lora_qkv], axis=1))
    lora_qkv_all = attended_all[:, QUERY_WIDTH:]
    attended_all = attended_all[:, :QUERY_WIDTH]
    lora_out_all = matrix_product(attended_all, narrow_output).astype(bf16)
    proj_all = ring_gather(
        jnp.concatenate([proj_grad, lora_out_grad, gate_low, up_low, lora_hd], axis=1), 5
    )
    low_all = proj_all[:, PROJECT_COLUMNS:]
    proj_all = proj_all[:, :PROJECT_COLUMNS]
    qkv_low_all = jnp.concatenate(
        [
            times_transposed(proj_all[:, :QUERY_WIDTH], widen_query),
            times_transposed(proj_all[:, QUERY_WIDTH : QUERY_WIDTH + HEAD_WIDTH], widen_key),
            times_transposed(proj_all[:, QUERY_WIDTH + HEAD_WIDTH :], widen_value),
        ],
        axis=1,
    ).astype(bf16)
    normed_turn = turn(normalized)
    branch_turn = turn(branch_grad)
    column = place * width_own
    attended_turn = lax.dynamic_slice_in_dim(attended_all, column, width_own, 1)
    two_turn = lax.dynamic_slice_in_dim(two_all, column, width_own, 1)
    attn_part = jnp.concatenate(
        [outer_product_rows(normed_turn, proj_all), outer_product_rows(branch_turn, attended_all)],
        axis=1,
    )
    attn_sum = both_loops(attn_part)
    squeeze_own = jnp.concatenate(
        [
            outer_product_rows(normed_turn, qkv_low_all),
            outer_product_rows(attended_turn, low_all[:, :rank]),
            outer_product_rows(two_turn, low_all[:, rank : 3 * rank]),
        ],
        axis=1,
    )
    out_piece = outer_product_rows(branch_turn, lora_out_all)
    near = jnp.concatenate(
        [
            outer_product_rows(proj_all[:, :QUERY_WIDTH], lora_qkv_all[:, :rank]),
            outer_product_rows(
                proj_all[:, QUERY_WIDTH : QUERY_WIDTH + HEAD_WIDTH], lora_qkv_all[:, rank : 2 * rank]
            ),
            outer_product_rows(proj_all[:, QUERY_WIDTH + HEAD_WIDTH :], lora_qkv_all[:, 2 * rank :]),
        ],
        axis=0,
    )
    far = outer_product_rows(grad_all, low_all[:, 3 * rank :])
    expand_own = place_columns(
        jnp.concatenate([out_piece, gate_piece, up_piece], axis=0), near, far, 6
    ).T
    return (
        hidden_out[None],
        input_grad[None],
        gain_sum,
        attn_sum[:, :PROJECT_COLUMNS],
        attn_sum[:, PROJECT_COLUMNS:],
        ffn_sum,
        squeeze_own[None],
        expand_own[None],
        down_own[None],
    )


def solution(mesh):
    return jax.shard_map(
        per_device,
        mesh=mesh,
        in_specs=(
            P("loop", "fsdp", None),
            P("loop", None),
            P(),
            P("fsdp", None),
            P("fsdp", None),
            P("fsdp", None, None),
            P("loop", None, None),
            P("loop", None, None),
            P("loop", None, None),
            P("loop", "fsdp", None),
        ),
        out_specs=(
            P("loop", "fsdp", None),
            P("loop", "fsdp", None),
            P(None, "fsdp"),
            P("fsdp", None),
            P("fsdp", None),
            P("fsdp", None, None),
            P("loop", "fsdp", None),
            P("loop", None, "fsdp"),
            P("loop", "fsdp", None),
        ),
        check_vma=False,
    )
```

```python
import functools
import math

import jax
import jax.numpy as jnp
from jax import lax
from jax.experimental import pallas as pl
from jax.experimental.pallas import tpu as pltpu
from jax.sharding import PartitionSpec as P

MODEL_WIDTH = 2048
HEADS = 8
HEAD_WIDTH = 256
HIDDEN_COUNT = 16384
ADAPTER_RANK = 256
QUERY_WIDTH = 2048
PROJECT_COLUMNS = 2560
ADAPTER_COLUMNS = 39424
GATE_START = PROJECT_COLUMNS + MODEL_WIDTH

epsilon = 1e-06
bf16 = jnp.bfloat16
f32 = jnp.float32
MESH = pl.DeviceIdType.MESH


def matrix_product(former, latter):
    return jnp.dot(former, latter, preferred_element_type=f32)


def times_transposed(former, latter):
    return lax.dot_general(former, latter, (((1,), (1,)), ((), ())), preferred_element_type=f32)


def outer_product_rows(former, latter):
    return lax.dot_general(former, latter, (((0,), (0,)), ((), ())), preferred_element_type=f32)


def segment_info(lengths, row_count):
    row_ids = jnp.arange(row_count, dtype=jnp.int32)
    count = lengths.shape[0]
    labels = jnp.arange(count, dtype=jnp.int32)
    finish = jnp.sum(jnp.where(labels[:, None] <= labels[None, :], lengths[:, None], 0), axis=0)
    starts = finish - lengths
    segment = jnp.sum((row_ids[:, None] >= finish[None, :]).astype(jnp.int32), axis=1)
    opening = jnp.sum(jnp.where(segment[:, None] == labels[None, :], starts[None, :], 0), axis=1)
    return (segment, row_ids - opening)


def rotate(values, position, direction):
    half_dim = HEAD_WIDTH // 2
    frequency = jnp.exp(
        jnp.arange(half_dim).astype(f32) * (-2.0 * math.log(10000.0) / HEAD_WIDTH)
    )
    angles = position.astype(f32)[:, None] * frequency[None, :]
    cosine = jnp.cos(angles)[:, None, :]
    sine_val = direction * jnp.sin(angles)[:, None, :]
    shaped = values.reshape(values.shape[0], -1, HEAD_WIDTH)
    former = shaped[..., :half_dim]
    latter = shaped[..., half_dim:]
    turned = jnp.concatenate(
        [former * cosine - latter * sine_val, latter * cosine + former * sine_val], axis=-1
    )
    return turned.reshape(values.shape)


def rms_scale(values):
    return lax.rsqrt(jnp.mean(values * values, axis=-1, keepdims=True) + epsilon)


def gelu_tanh(values):
    return jax.nn.gelu(values, approximate=True)


def unit_backward(gate_value, upward_activation, hidden_unit_gradient):
    activated, pullback_function = jax.vjp(gelu_tanh, gate_value)
    gate_grad = pullback_function(hidden_unit_gradient * upward_activation)[0]
    return (gate_grad.astype(bf16), (hidden_unit_gradient * activated).astype(bf16))


def scores_of(query_heads, key_rows, allowed, scaling):
    product = (
        jnp.einsum("thd,ud->thu", query_heads, key_rows, preferred_element_type=f32) * scaling
    )
    return jnp.where(allowed[:, None, :], product, -1e30)


def gather_rows(block):
    return lax.all_gather(block, "fsdp", axis=0, tiled=True)


def scatter_rows(partial):
    return lax.psum_scatter(partial.astype(bf16), "fsdp", scatter_dimension=0, tiled=True).astype(f32)


def loop_shares(partial):
    return lax.all_gather(partial.astype(bf16), "loop", axis=0)


def both_loops(shares):
    return shares[0].astype(f32) + shares[1].astype(f32)


def turn(block):
    return lax.all_to_all(block, "fsdp", split_axis=1, concat_axis=0, tiled=True)


def chip_at(q, chips):
    return jnp.where(q < 4, 2 * q, 15 - 2 * q) if chips == 8 else q

def ring_place(chip, chips):
    return jnp.where(chip % 2 == 0, chip // 2, 7 - chip // 2) if chips == 8 else chip

def ring_neighbours(chips):
    me = lax.axis_index("fsdp")
    core = me % 2
    p = ring_place(me // 2, chips)
    def device(shift, c):
        return chip_at((p + shift + chips) % chips, chips) * 2 + c
    return core, device

def meet(devices):
    barrier = pltpu.get_barrier_semaphore()
    for d in devices:
        pl.semaphore_signal(barrier, inc=1, device_id={"fsdp": d}, device_id_type=MESH)
    pl.semaphore_wait(barrier, len(devices))

def gather_kernel(chips, x_ref, o_ref, own_sem, ring_send, ring_recv, side_send, side_recv):
    core, device = ring_neighbours(chips)
    rows = x_ref.shape[0]
    reach = chips // 2
    ways = (device(1, core), device(-1, core))
    side = device(0, 1 - core)
    meet((*ways, side))

    def span(way, hops):
        return (way * (rows // 2), rows // 2) if hops == reach else (0, rows)

    def at(way, hops, c, part):
        origin = device(-hops if way == 0 else hops, c)
        return o_ref.at[pl.ds(pl.multiple_of(origin * rows + part[0], 8), part[1])]

    def hop(way, hops):
        part = span(way, hops)
        here = at(way, hops - 1, core, part)
        src = x_ref.at[pl.ds(part[0], part[1])] if hops == 1 else here
        return pltpu.make_async_remote_copy(src, here, ring_send.at[way, hops - 1], ring_recv.at[way, hops - 1], device_id={"fsdp": ways[way]}, device_id_type=MESH)

    def arriving(way, hops):
        here = at(way, hops, core, span(way, hops))
        return pltpu.make_async_remote_copy(here, here, ring_send.at[way, hops - 1], ring_recv.at[way, hops - 1], device_id={"fsdp": ways[way]}, device_id_type=MESH)

    def across(way, hops, c):
        part = span(way, hops) if hops else (0, rows)
        there = at(way, hops, c, part)
        src = there if hops else x_ref
        return pltpu.make_async_remote_copy(src, there, side_send.at[way, hops], side_recv.at[way, hops], device_id={"fsdp": side}, device_id_type=MESH)

    for way in (0, 1):
        hop(way, 1).start()
    across(0, 0, core).start()
    own = pltpu.make_async_copy(x_ref, at(0, 0, core, (0, rows)), own_sem)
    own.start()
    for hops in range(1, reach + 1):
        for way in (0, 1):
            arriving(way, hops).wait_recv()
            if hops < reach:
                hop(way, hops + 1).start()
            across(way, hops, core).start()
    across(0, 0, 1 - core).wait_recv()
    across(0, 0, core).wait_send()
    for hops in range(1, reach + 1):
        for way in (0, 1):
            across(way, hops, 1 - core).wait_recv()
            across(way, hops, core).wait_send()
            hop(way, hops).wait_send()
    own.wait()

def busy(us):
    return pl.CostEstimate(flops=0, bytes_accessed=int(us * 3.0e6), transcendentals=0)


def ring_gather(block, ident):
    size = lax.axis_size("fsdp")
    chips = size // 2
    rows, columns = block.shape
    pair = pltpu.SemaphoreType.DMA((2, chips // 2))
    sides = pltpu.SemaphoreType.DMA((2, chips // 2 + 1))
    return pl.pallas_call(
        functools.partial(gather_kernel, chips),
        out_shape=jax.ShapeDtypeStruct((size * rows, columns), block.dtype),
        in_specs=[pl.BlockSpec(memory_space=pl.ANY)],
        out_specs=pl.BlockSpec(memory_space=pl.ANY),
        scratch_shapes=[pltpu.SemaphoreType.DMA, pair, pair, sides, sides],
        compiler_params=pltpu.CompilerParams(collective_id=ident, has_side_effects=True),
        cost_estimate=busy(1),
        name="ring_gather",
    )(block)

def scatter_kernel(chips, count, *refs):
    x_refs, o_ref = refs[:count], refs[count]
    side_buf, ring_buf, side_send, side_recv, ring_send, ring_recv = refs[count + 1 :]
    core, device = ring_neighbours(chips)
    rows, columns = o_ref.shape
    reach = chips // 2
    half = columns // 2
    tile = 16
    ways = (device(1, core), device(-1, core))
    side = device(0, 1 - core)
    meet((*ways, side))
    starts = [sum(x.shape[1] for x in x_refs[:i]) for i in range(count)]

    def shift(way, hops):
        return (hops if way == 0 else chips - hops) % chips

    def across(target, c, i):
        there = pl.ds(pl.multiple_of(device(target, c) * rows, tile), rows)
        return pltpu.make_async_remote_copy(
            x_refs[i].at[there],
            side_buf.at[target, :, pl.ds(starts[i], x_refs[i].shape[1])],
            side_send.at[target, i],
            side_recv.at[target, i],
            device_id={"fsdp": side},
            device_id_type=MESH,
        )

    def hop(way, step):
        cols = pl.ds(way * half, half) if step == 0 else pl.ds(0, columns)
        return pltpu.make_async_remote_copy(
            side_buf.at[shift(way, reach - step), :, cols],
            ring_buf.at[way, step, :, cols],
            ring_send.at[way, step],
            ring_recv.at[way, step],
            device_id={"fsdp": ways[way]},
            device_id_type=MESH,
        )

    order = [reach] + [shift(way, hops) for hops in range(reach - 1, 0, -1) for way in (0, 1)] + [0]
    for target in order:
        for i in range(count):
            across(target, 1 - core, i).start()

    def add(target, incoming, store):
        first = pl.multiple_of(device(target, core) * rows, tile)
        for i in range(count):
            across(target, core, i).wait_recv()

        @pl.loop(0, rows // tile)
        def _(j):
            here = pl.ds(pl.multiple_of(j * tile, tile), tile)
            mine = pl.ds(pl.multiple_of(first + j * tile, tile), tile)
            for i in range(count):
                cols = pl.ds(starts[i], x_refs[i].shape[1])
                total = x_refs[i][mine, :].astype(f32) + side_buf[target, here, cols].astype(f32)
                for way, step in incoming:
                    if step:
                        total = total + ring_buf[way, step, here, cols].astype(f32)
                store(here, cols, total)
            for way, step in incoming:
                if not step:
                    cols = pl.ds(way * half, half)
                    store(
                        here,
                        cols,
                        side_buf[target, here, cols].astype(f32) + ring_buf[way, 0, here, cols].astype(f32),
                    )

    for step in range(reach):
        for way in (0, 1):
            target = shift(way, reach - step)
            if step:
                hop(way, step - 1).wait_recv()

            def store(here, cols, total, target=target):
                side_buf[target, here, cols] = total.astype(bf16)

            if step or way == 0:
                add(target, [(way, step - 1)] if step else [], store)
            hop(way, step).start()
    for way in (0, 1):
        hop(way, reach - 1).wait_recv()

    def last(here, cols, total):
        o_ref[here, cols] = total

    add(0, [(0, reach - 1), (1, reach - 1)], last)
    for target in order:
        for i in range(count):
            across(target, 1 - core, i).wait_send()
    for step in range(reach):
        for way in (0, 1):
            hop(way, step).wait_send()


def ring_scatter(terms, ident):
    size = lax.axis_size("fsdp")
    terms = [term.astype(bf16) for term in terms]
    if size != 16:
        return scatter_rows(jnp.concatenate(terms, axis=1))
    chips, count = size // 2, len(terms)
    rows, columns = terms[0].shape[0] // size, sum(term.shape[1] for term in terms)
    pair = pltpu.SemaphoreType.DMA((2, chips // 2))
    sides = pltpu.SemaphoreType.DMA((chips, count))
    return pl.pallas_call(
        functools.partial(scatter_kernel, chips, count),
        out_shape=jax.ShapeDtypeStruct((rows, columns), f32),
        in_specs=[pl.BlockSpec(memory_space=pltpu.VMEM)] * count,
        out_specs=pl.BlockSpec(memory_space=pltpu.VMEM),
        scratch_shapes=[
            pltpu.VMEM((chips, rows, columns), bf16),
            pltpu.VMEM((2, chips // 2, rows, columns), bf16),
            sides,
            sides,
            pair,
            pair,
        ],
        compiler_params=pltpu.CompilerParams(
            collective_id=ident, has_side_effects=True, vmem_limit_bytes=56 << 20
        ),
        cost_estimate=busy(1),
        name="ring_scatter",
    )(*terms)


def place_kernel(size, chunk, own_count, mid_ref, near_ref, far_ref, o_ref, send_sem, recv_sem, own_sem):
    me = lax.axis_index("fsdp")
    hidden = HIDDEN_COUNT // size
    width = MODEL_WIDTH // size
    sections = (
        (0, PROJECT_COLUMNS, width),
        (width, GATE_START, hidden),
        (width + hidden, GATE_START + HIDDEN_COUNT, hidden),
    )
    barrier = pltpu.get_barrier_semaphore()

    def greet(i, carry):
        other = (me + i) % size
        pl.semaphore_signal(barrier, inc=1, device_id={"fsdp": other}, device_id_type=MESH)
        return carry

    lax.fori_loop(1, size, greet, 0)
    pl.semaphore_wait(barrier, size - 1)

    def rows(ref, first):
        return ref.at[pl.ds(pl.multiple_of(first, 8), chunk)]

    def aim(start, length):
        owner = (start + me * length) // own_count
        return owner, start + me * length - owner * own_count

    def remote(source, first, owner, sent=0):
        return pltpu.make_async_remote_copy(
            source,
            rows(o_ref, first),
            send_sem.at[sent],
            recv_sem.at[first // chunk],
            device_id={"fsdp": owner},
            device_id_type=MESH,
        )

    def local(source, first):
        return pltpu.make_async_copy(source, rows(o_ref, first), own_sem.at[first // chunk])

    for base, start, length in sections:

        def send(j, carry, base=base, aimed=aim(start, length)):
            over = (aimed[1] + j * chunk >= own_count).astype(jnp.int32)
            owner = aimed[0] + over
            first = aimed[1] + j * chunk - over * own_count
            source = rows(mid_ref, base + j * chunk)

            @pl.when(owner != me)
            def _():
                remote(source, first, owner, base // chunk + j).start()

            @pl.when(owner == me)
            def _():
                local(source, first).start()

            return carry

        lax.fori_loop(0, length // chunk, send, 0)

    def fill(j, carry):
        column = me * own_count + j * chunk

        @pl.when(column < PROJECT_COLUMNS)
        def _():
            local(rows(near_ref, column), j * chunk).start()

        @pl.when(column >= GATE_START + 2 * HIDDEN_COUNT)
        def _():
            local(rows(far_ref, column - (GATE_START + 2 * HIDDEN_COUNT)), j * chunk).start()

        return carry

    lax.fori_loop(0, own_count // chunk, fill, 0)

    def arrive(j, carry):
        column = me * own_count + j * chunk
        here = rows(o_ref, j * chunk)
        away = 0
        for _, start, length in sections:
            mine = start + me * length
            inside = (column >= start) & (column < start + length * size)
            outside = (column < mine) | (column >= mine + length)
            away = away + (inside & outside).astype(jnp.int32)

        @pl.when(away > 0)
        def _():
            remote(here, j * chunk, (me + 1) % size).wait_recv()

        @pl.when(away == 0)
        def _():
            local(rows(near_ref, 0), j * chunk).wait()

        return carry

    lax.fori_loop(0, own_count // chunk, arrive, 0)
    for base, start, length in sections:

        def sent(j, carry, base=base, aimed=aim(start, length)):
            over = (aimed[1] + j * chunk >= own_count).astype(jnp.int32)
            owner = aimed[0] + over
            first = aimed[1] + j * chunk - over * own_count

            @pl.when(owner != me)
            def _():
                remote(rows(mid_ref, base + j * chunk), first, owner, base // chunk + j).wait_send()

            return carry

        lax.fori_loop(0, length // chunk, sent, 0)


def place_columns(middle, near, far, ident):
    size = lax.axis_size("fsdp")
    own_count = ADAPTER_COLUMNS // size
    chunk = math.gcd(own_count, MODEL_WIDTH // size, HIDDEN_COUNT // size, PROJECT_COLUMNS, GATE_START)
    anywhere = pl.BlockSpec(memory_space=pl.ANY)
    return pl.pallas_call(
        functools.partial(place_kernel, size, chunk, own_count),
        out_shape=jax.ShapeDtypeStruct((own_count, ADAPTER_RANK), bf16),
        in_specs=[anywhere] * 3,
        out_specs=anywhere,
        scratch_shapes=[
            pltpu.SemaphoreType.DMA((middle.shape[0] // chunk,)),
            pltpu.SemaphoreType.DMA((own_count // chunk,)),
            pltpu.SemaphoreType.DMA((own_count // chunk,)),
        ],
        compiler_params=pltpu.CompilerParams(collective_id=ident, has_side_effects=True),
        cost_estimate=busy(30),
        name="place_columns",
    )(middle, near, far)


def per_device(
    hidden_input,
    sequence_lengths,
    norm_gain_values,
    input_proj_weight,
    output_proj_weight,
    feedforward_weight,
    adapter_first,
    adapter_second,
    adapter_down_first,
    output_gradient,
):
    size = lax.axis_size("fsdp")
    place = lax.axis_index("fsdp")
    tokens_dev = hidden_input.shape[1]
    all_rows = tokens_dev * size
    hidden_own = HIDDEN_COUNT // size
    width_own = MODEL_WIDTH // size
    columns_own = ADAPTER_COLUMNS // size
    offset = place * tokens_dev
    segment_all, position_all = segment_info(sequence_lengths[0], all_rows)
    segment_own = lax.dynamic_slice_in_dim(segment_all, offset, tokens_dev)
    position_own = lax.dynamic_slice_in_dim(position_all, offset, tokens_dev)
    row_all = jnp.arange(all_rows, dtype=jnp.int32)
    row_own = offset + jnp.arange(tokens_dev, dtype=jnp.int32)
    allowed = (segment_own[:, None] == segment_all[None, :]) & (
        row_own[:, None] >= row_all[None, :]
    )
    gains = norm_gain_values.astype(f32)
    first_factor = adapter_first[0]
    second_factor = adapter_second[0]
    rank = ADAPTER_RANK
    narrow_projection = first_factor[:, : 3 * rank]
    narrow_output = first_factor[:, 3 * rank : 4 * rank]
    squeeze_gate = first_factor[:, 4 * rank : 5 * rank]
    squeeze_up = first_factor[:, 5 * rank :]
    narrow_down = lax.dynamic_slice_in_dim(adapter_down_first[0], place * hidden_own, hidden_own, 0)
    widen_query = second_factor[:, :QUERY_WIDTH]
    widen_key = second_factor[:, QUERY_WIDTH : QUERY_WIDTH + HEAD_WIDTH]
    widen_value = second_factor[:, QUERY_WIDTH + HEAD_WIDTH : PROJECT_COLUMNS]
    widen_output = second_factor[:, PROJECT_COLUMNS:GATE_START]
    widen_gate = lax.dynamic_slice_in_dim(
        second_factor, GATE_START + place * hidden_own, hidden_own, 1
    )
    widen_up = lax.dynamic_slice_in_dim(
        second_factor, GATE_START + HIDDEN_COUNT + place * hidden_own, hidden_own, 1
    )
    widen_down = second_factor[:, GATE_START + 2 * HIDDEN_COUNT :]
    scaling = HEAD_WIDTH ** (-0.5)

    hidden_state = hidden_input[0].astype(f32)
    scale_one = rms_scale(hidden_state)
    normalized = (hidden_state * scale_one * gains[0]).astype(bf16)
    proj_in = ring_gather(input_proj_weight, 0)
    proj_in, proj_out, grad_rows = lax.optimization_barrier(
        (proj_in, output_proj_weight, output_gradient[0])
    )
    proj_out = gather_rows(proj_out)
    lora_qkv = matrix_product(normalized, narrow_projection).astype(bf16)
    projected = matrix_product(normalized, proj_in)
    query_pre = projected[:, :QUERY_WIDTH] + matrix_product(lora_qkv[:, :rank], widen_query)
    key_pre = projected[:, QUERY_WIDTH : QUERY_WIDTH + HEAD_WIDTH] + matrix_product(
        lora_qkv[:, rank : 2 * rank], widen_key
    )
    value_local = (
        projected[:, QUERY_WIDTH + HEAD_WIDTH :]
        + matrix_product(lora_qkv[:, 2 * rank :], widen_value)
    ).astype(bf16)
    query_rot = rotate(query_pre, position_own, 1.0).astype(bf16)
    key_rot = rotate(key_pre, position_own, 1.0).astype(bf16)
    keys_all = ring_gather(jnp.concatenate([key_rot, value_local], axis=1), 1)
    key_rows, value_rows = keys_all[:, :HEAD_WIDTH], keys_all[:, HEAD_WIDTH:]
    query_heads = query_rot.reshape(tokens_dev, HEADS, HEAD_WIDTH)
    scores = scores_of(query_heads, key_rows, allowed, scaling)
    row_max = jnp.max(scores, axis=-1, keepdims=True)
    powered = jnp.exp(scores - row_max)
    row_sum = jnp.sum(powered, axis=-1, keepdims=True)
    probs = powered / row_sum
    probs_low = probs.astype(bf16)
    attended = (
        jnp.einsum("thu,ud->thd", probs_low, value_rows, preferred_element_type=f32)
        .reshape(tokens_dev, QUERY_WIDTH)
        .astype(bf16)
    )
    lora_out = matrix_product(attended, narrow_output).astype(bf16)
    middle = (
        hidden_state
        + times_transposed(attended, proj_out)
        + matrix_product(lora_out, widen_output)
    )
    scale_two = rms_scale(middle)
    normed_two = (middle * scale_two * gains[1]).astype(bf16)

    two_all = ring_gather(normed_two, 2)
    two_all, grad_rows = lax.optimization_barrier((two_all, grad_rows))
    grad_all = gather_rows(grad_rows)
    weight_gate = feedforward_weight[:, 0, :]
    weight_up = feedforward_weight[:, 1, :]
    weight_down = feedforward_weight[:, 2, :]
    lora_gate = matrix_product(two_all, squeeze_gate).astype(bf16)
    lora_up = matrix_product(two_all, squeeze_up).astype(bf16)
    hd_grad = times_transposed(grad_all, widen_down).astype(bf16)
    gate = times_transposed(two_all, weight_gate) + matrix_product(lora_gate, widen_gate)
    upward = times_transposed(two_all, weight_up) + matrix_product(lora_up, widen_up)
    units = (gelu_tanh(gate) * upward).astype(bf16)
    units_grad = times_transposed(grad_all, weight_down) + times_transposed(hd_grad, narrow_down)
    gate_grad, up_grad = unit_backward(gate, upward, units_grad)
    back_terms = [
        (matrix_product(gate_grad, weight_gate) + matrix_product(up_grad, weight_up)).astype(bf16),
        times_transposed(gate_grad, widen_gate).astype(bf16),
        times_transposed(up_grad, widen_up).astype(bf16),
        matrix_product(units, weight_down).astype(bf16),
        matrix_product(units, narrow_down).astype(bf16),
    ]
    ffn_shares = jnp.stack(
        [
            outer_product_rows(former, latter).astype(bf16)
            for former, latter in ((gate_grad, two_all), (up_grad, two_all), (units, grad_all))
        ]
    )
    attended_all = gather_rows(jnp.concatenate([attended, lora_qkv], axis=1))
    ffn_shares, back_terms, attended_all = lax.optimization_barrier(
        (ffn_shares, back_terms, attended_all)
    )
    ffn_both = loop_shares(ffn_shares)
    rows_sum = ring_scatter(back_terms, 3)
    back_own, out_own = rows_sum[:, : MODEL_WIDTH + 2 * rank], rows_sum[:, MODEL_WIDTH + 2 * rank :]
    down_own = outer_product_rows(units, hd_grad)
    gate_piece = outer_product_rows(gate_grad, lora_gate)
    up_piece = outer_product_rows(up_grad, lora_up)

    lora_hd = out_own[:, MODEL_WIDTH:].astype(bf16)
    hidden_out = (middle + out_own[:, :MODEL_WIDTH] + matrix_product(lora_hd, widen_down)).astype(bf16)

    gate_low = back_own[:, MODEL_WIDTH : MODEL_WIDTH + rank].astype(bf16)
    up_low = back_own[:, MODEL_WIDTH + rank :].astype(bf16)
    two_grad = (
        back_own[:, :MODEL_WIDTH]
        + times_transposed(gate_low, squeeze_gate)
        + times_transposed(up_low, squeeze_up)
    )
    weighted_two = gains[1] * two_grad
    middle_grad = (
        output_gradient[0].astype(f32)
        + scale_two * weighted_two
        - middle * scale_two**3 * jnp.mean(middle * weighted_two, axis=-1, keepdims=True)
    )
    gain_two = jnp.sum(two_grad * middle * scale_two, axis=0)

    branch_grad = middle_grad.astype(bf16)
    lora_out_grad = times_transposed(branch_grad, widen_output).astype(bf16)
    attended_grad = (
        matrix_product(branch_grad, proj_out) + times_transposed(lora_out_grad, narrow_output)
    ).astype(bf16)
    heads_grad = attended_grad.reshape(tokens_dev, HEADS, HEAD_WIDTH)
    prob_grad = jnp.einsum("thd,ud->thu", heads_grad, value_rows, preferred_element_type=f32)
    row_dot = jnp.sum(probs * prob_grad, axis=-1, keepdims=True)
    score_grad = (probs * (prob_grad - row_dot)).astype(bf16)
    query_rot_grad = (
        jnp.einsum("thu,ud->thd", score_grad, key_rows, preferred_element_type=f32) * scaling
    )
    key_part = (
        jnp.einsum("thu,thd->ud", score_grad, query_heads, preferred_element_type=f32) * scaling
    )
    value_part = jnp.einsum("thu,thd->ud", probs_low, heads_grad, preferred_element_type=f32)
    pair_grad = ring_scatter([key_part, value_part], 4)
    query_grad = rotate(
        query_rot_grad.reshape(tokens_dev, QUERY_WIDTH), position_own, -1.0
    ).astype(bf16)
    key_grad = rotate(pair_grad[:, :HEAD_WIDTH], position_own, -1.0).astype(bf16)
    value_grad = pair_grad[:, HEAD_WIDTH:].astype(bf16)
    proj_grad = jnp.concatenate([query_grad, key_grad, value_grad], axis=1)
    lora_qkv_grad = jnp.concatenate(
        [
            times_transposed(query_grad, widen_query),
            times_transposed(key_grad, widen_key),
            times_transposed(value_grad, widen_value),
        ],
        axis=1,
    ).astype(bf16)
    normed_grad = times_transposed(proj_grad, proj_in) + times_transposed(
        lora_qkv_grad, narrow_projection
    )
    weighted_one = gains[0] * normed_grad
    input_grad = (
        middle_grad
        + scale_one * weighted_one
        - hidden_state
        * scale_one**3
        * jnp.mean(hidden_state * weighted_one, axis=-1, keepdims=True)
    )
    gain_one = jnp.sum(normed_grad * hidden_state * scale_one, axis=0)

    lora_qkv_all = attended_all[:, QUERY_WIDTH:]
    attended_all = attended_all[:, :QUERY_WIDTH]
    lora_out_all = matrix_product(attended_all, narrow_output).astype(bf16)
    gain_rows = jnp.stack([gain_one, gain_two]).astype(bf16).reshape(tokens_dev, -1)
    gain_count = gain_rows.shape[1]
    gain_rows = jnp.pad(gain_rows, ((0, 0), (0, -gain_count % 128)))
    proj_rows = jnp.concatenate(
        [proj_grad, lora_out_grad, gate_low, up_low, lora_hd, gain_rows], axis=1
    )
    proj_all = ring_gather(proj_rows, 5)
    low_all = proj_all[:, PROJECT_COLUMNS : PROJECT_COLUMNS + 4 * rank]
    gain_all = proj_all[:, PROJECT_COLUMNS + 4 * rank :][:, :gain_count].reshape(size, 2, MODEL_WIDTH)
    gain_all = jnp.sum(gain_all.astype(f32), axis=0)
    gain_own = lax.dynamic_slice_in_dim(gain_all, place * width_own, width_own, 1)
    proj_all = proj_all[:, :PROJECT_COLUMNS]
    qkv_low_all = jnp.concatenate(
        [
            times_transposed(proj_all[:, :QUERY_WIDTH], widen_query),
            times_transposed(proj_all[:, QUERY_WIDTH : QUERY_WIDTH + HEAD_WIDTH], widen_key),
            times_transposed(proj_all[:, QUERY_WIDTH + HEAD_WIDTH :], widen_value),
        ],
        axis=1,
    ).astype(bf16)
    normed_turn = turn(normalized)
    branch_turn = turn(branch_grad)
    column = place * width_own
    attended_turn = lax.dynamic_slice_in_dim(attended_all, column, width_own, 1)
    two_turn = lax.dynamic_slice_in_dim(two_all, column, width_own, 1)
    attn_part = jnp.concatenate(
        [outer_product_rows(normed_turn, proj_all), outer_product_rows(branch_turn, attended_all)],
        axis=1,
    )
    gain_part = jnp.pad(gain_own, ((0, width_own - 2), (0, -width_own % 128)))
    attn_part, ffn_both = lax.optimization_barrier(
        (jnp.concatenate([attn_part, gain_part], axis=1).astype(bf16), ffn_both)
    )
    attn_sum = both_loops(loop_shares(attn_part))
    gain_column = PROJECT_COLUMNS + QUERY_WIDTH
    gain_sum = attn_sum[:2, gain_column : gain_column + width_own]
    squeeze_own = jnp.concatenate(
        [
            outer_product_rows(normed_turn, qkv_low_all),
            outer_product_rows(attended_turn, low_all[:, :rank]),
            outer_product_rows(two_turn, low_all[:, rank : 3 * rank]),
        ],
        axis=1,
    )
    out_piece = outer_product_rows(branch_turn, lora_out_all)
    near = jnp.concatenate(
        [
            outer_product_rows(proj_all[:, :QUERY_WIDTH], lora_qkv_all[:, :rank]),
            outer_product_rows(
                proj_all[:, QUERY_WIDTH : QUERY_WIDTH + HEAD_WIDTH], lora_qkv_all[:, rank : 2 * rank]
            ),
            outer_product_rows(proj_all[:, QUERY_WIDTH + HEAD_WIDTH :], lora_qkv_all[:, 2 * rank :]),
        ],
        axis=0,
    )
    far = outer_product_rows(grad_all, low_all[:, 3 * rank :])
    expand_own = place_columns(
        jnp.concatenate([out_piece, gate_piece, up_piece], axis=0).astype(bf16),
        near.astype(bf16),
        far.astype(bf16),
        6,
    )
    expand_own = expand_own.T.astype(f32)
    ffn_sum = both_loops(ffn_both).transpose(1, 0, 2)
    return (
        hidden_out[None],
        input_grad[None],
        gain_sum,
        attn_sum[:, :PROJECT_COLUMNS],
        attn_sum[:, PROJECT_COLUMNS:gain_column],
        ffn_sum,
        squeeze_own[None],
        expand_own[None],
        down_own[None],
    )


def solution(mesh):
    return jax.shard_map(
        per_device,
        mesh=mesh,
        in_specs=(
            P("loop", "fsdp", None),
            P("loop", None),
            P(),
            P("fsdp", None),
            P("fsdp", None),
            P("fsdp", None, None),
            P("loop", None, None),
            P("loop", None, None),
            P("loop", None, None),
            P("loop", "fsdp", None),
        ),
        out_specs=(
            P("loop", "fsdp", None),
            P("loop", "fsdp", None),
            P(None, "fsdp"),
            P("fsdp", None),
            P("fsdp", None),
            P("fsdp", None, None),
            P("loop", "fsdp", None),
            P("loop", None, "fsdp"),
            P("loop", "fsdp", None),
        ),
        check_vma=False,
    )
```

```python
import functools
import math

import jax
import jax.numpy as jnp
from jax import lax
from jax.experimental import pallas as pl
from jax.experimental.pallas import tpu as pltpu
from jax.sharding import PartitionSpec as P

MODEL_WIDTH = 2048
HEADS = 8
HEAD_WIDTH = 256
HIDDEN_COUNT = 16384
ADAPTER_RANK = 256
QUERY_WIDTH = 2048
PROJECT_COLUMNS = 2560
ADAPTER_COLUMNS = 39424
GATE_START = PROJECT_COLUMNS + MODEL_WIDTH

epsilon = 1e-06
bf16 = jnp.bfloat16
f32 = jnp.float32
MESH = pl.DeviceIdType.MESH


def matrix_product(former, latter):
    return jnp.dot(former, latter, preferred_element_type=f32)


def times_transposed(former, latter):
    return lax.dot_general(former, latter, (((1,), (1,)), ((), ())), preferred_element_type=f32)


def outer_product_rows(former, latter):
    return lax.dot_general(former, latter, (((0,), (0,)), ((), ())), preferred_element_type=f32)


def segment_info(lengths, row_count):
    row_ids = jnp.arange(row_count, dtype=jnp.int32)
    count = lengths.shape[0]
    labels = jnp.arange(count, dtype=jnp.int32)
    finish = jnp.sum(jnp.where(labels[:, None] <= labels[None, :], lengths[:, None], 0), axis=0)
    starts = finish - lengths
    segment = jnp.sum((row_ids[:, None] >= finish[None, :]).astype(jnp.int32), axis=1)
    opening = jnp.sum(jnp.where(segment[:, None] == labels[None, :], starts[None, :], 0), axis=1)
    return (segment, row_ids - opening)


def rotate(values, position, direction):
    half_dim = HEAD_WIDTH // 2
    frequency = jnp.exp(
        jnp.arange(half_dim).astype(f32) * (-2.0 * math.log(10000.0) / HEAD_WIDTH)
    )
    angles = position.astype(f32)[:, None] * frequency[None, :]
    cosine = jnp.cos(angles)[:, None, :]
    sine_val = direction * jnp.sin(angles)[:, None, :]
    shaped = values.reshape(values.shape[0], -1, HEAD_WIDTH)
    former = shaped[..., :half_dim]
    latter = shaped[..., half_dim:]
    turned = jnp.concatenate(
        [former * cosine - latter * sine_val, latter * cosine + former * sine_val], axis=-1
    )
    return turned.reshape(values.shape)


def rms_scale(values):
    return lax.rsqrt(jnp.mean(values * values, axis=-1, keepdims=True) + epsilon)


def gelu_tanh(values):
    return jax.nn.gelu(values, approximate=True)


def unit_backward(gate_value, upward_activation, hidden_unit_gradient):
    activated, pullback_function = jax.vjp(gelu_tanh, gate_value)
    gate_grad = pullback_function(hidden_unit_gradient * upward_activation)[0]
    return (gate_grad.astype(bf16), (hidden_unit_gradient * activated).astype(bf16))


def scores_of(query_heads, key_rows, allowed, scaling):
    product = (
        jnp.einsum("thd,ud->thu", query_heads, key_rows, preferred_element_type=f32) * scaling
    )
    return jnp.where(allowed[:, None, :], product, -1e30)


def gather_rows(block):
    return lax.all_gather(block, "fsdp", axis=0, tiled=True)


def scatter_rows(partial):
    return lax.psum_scatter(partial.astype(bf16), "fsdp", scatter_dimension=0, tiled=True).astype(f32)


def loop_shares(partial):
    return lax.all_gather(partial.astype(bf16), "loop", axis=0)


def both_loops(shares):
    return shares[0].astype(f32) + shares[1].astype(f32)


def turn(block):
    return lax.all_to_all(block, "fsdp", split_axis=1, concat_axis=0, tiled=True)


def chip_at(q, chips):
    return jnp.where(q < 4, 2 * q, 15 - 2 * q) if chips == 8 else q

def ring_place(chip, chips):
    return jnp.where(chip % 2 == 0, chip // 2, 7 - chip // 2) if chips == 8 else chip

def ring_neighbours(chips):
    me = lax.axis_index("fsdp")
    core = me % 2
    p = ring_place(me // 2, chips)
    def device(shift, c):
        return chip_at((p + shift + chips) % chips, chips) * 2 + c
    return core, device

def meet(devices):
    barrier = pltpu.get_barrier_semaphore()
    for d in devices:
        pl.semaphore_signal(barrier, inc=1, device_id={"fsdp": d}, device_id_type=MESH)
    pl.semaphore_wait(barrier, len(devices))

def gather_kernel(chips, x_ref, o_ref, own_sem, ring_send, ring_recv, side_send, side_recv):
    core, device = ring_neighbours(chips)
    rows = x_ref.shape[0]
    reach = chips // 2
    ways = (device(1, core), device(-1, core))
    side = device(0, 1 - core)
    meet((*ways, side))

    def span(way, hops):
        return (way * (rows // 2), rows // 2) if hops == reach else (0, rows)

    def at(way, hops, c, part):
        origin = device(-hops if way == 0 else hops, c)
        return o_ref.at[pl.ds(pl.multiple_of(origin * rows + part[0], 8), part[1])]

    def hop(way, hops):
        part = span(way, hops)
        here = at(way, hops - 1, core, part)
        src = x_ref.at[pl.ds(part[0], part[1])] if hops == 1 else here
        return pltpu.make_async_remote_copy(src, here, ring_send.at[way, hops - 1], ring_recv.at[way, hops - 1], device_id={"fsdp": ways[way]}, device_id_type=MESH)

    def arriving(way, hops):
        here = at(way, hops, core, span(way, hops))
        return pltpu.make_async_remote_copy(here, here, ring_send.at[way, hops - 1], ring_recv.at[way, hops - 1], device_id={"fsdp": ways[way]}, device_id_type=MESH)

    def across(way, hops, c):
        part = span(way, hops) if hops else (0, rows)
        there = at(way, hops, c, part)
        src = there if hops else x_ref
        return pltpu.make_async_remote_copy(src, there, side_send.at[way, hops], side_recv.at[way, hops], device_id={"fsdp": side}, device_id_type=MESH)

    for way in (0, 1):
        hop(way, 1).start()
    across(0, 0, core).start()
    own = pltpu.make_async_copy(x_ref, at(0, 0, core, (0, rows)), own_sem)
    own.start()
    for hops in range(1, reach + 1):
        for way in (0, 1):
            arriving(way, hops).wait_recv()
            if hops < reach:
                hop(way, hops + 1).start()
            across(way, hops, core).start()
    across(0, 0, 1 - core).wait_recv()
    across(0, 0, core).wait_send()
    for hops in range(1, reach + 1):
        for way in (0, 1):
            across(way, hops, 1 - core).wait_recv()
            across(way, hops, core).wait_send()
            hop(way, hops).wait_send()
    own.wait()

def busy(us):
    return pl.CostEstimate(flops=0, bytes_accessed=int(us * 3.0e6), transcendentals=0)


def ring_gather(block, ident):
    size = lax.axis_size("fsdp")
    chips = size // 2
    rows, columns = block.shape
    pair = pltpu.SemaphoreType.DMA((2, chips // 2))
    sides = pltpu.SemaphoreType.DMA((2, chips // 2 + 1))
    return pl.pallas_call(
        functools.partial(gather_kernel, chips),
        out_shape=jax.ShapeDtypeStruct((size * rows, columns), block.dtype),
        in_specs=[pl.BlockSpec(memory_space=pl.ANY)],
        out_specs=pl.BlockSpec(memory_space=pl.ANY),
        scratch_shapes=[pltpu.SemaphoreType.DMA, pair, pair, sides, sides],
        compiler_params=pltpu.CompilerParams(collective_id=ident, has_side_effects=True),
        cost_estimate=busy(1),
        name="ring_gather",
    )(block)

def scatter_kernel(chips, count, *refs):
    x_refs, o_ref = refs[:count], refs[count]
    side_buf, ring_buf, side_send, side_recv, ring_send, ring_recv = refs[count + 1 :]
    core, device = ring_neighbours(chips)
    rows, columns = o_ref.shape
    reach = chips // 2
    half = columns // 2
    tile = 16
    ways = (device(1, core), device(-1, core))
    side = device(0, 1 - core)
    meet((*ways, side))
    starts = [sum(x.shape[1] for x in x_refs[:i]) for i in range(count)]

    def shift(way, hops):
        return (hops if way == 0 else chips - hops) % chips

    def across(target, c, i):
        there = pl.ds(pl.multiple_of(device(target, c) * rows, tile), rows)
        return pltpu.make_async_remote_copy(
            x_refs[i].at[there],
            side_buf.at[target, :, pl.ds(starts[i], x_refs[i].shape[1])],
            side_send.at[target, i],
            side_recv.at[target, i],
            device_id={"fsdp": side},
            device_id_type=MESH,
        )

    def hop(way, step):
        cols = pl.ds(way * half, half) if step == 0 else pl.ds(0, columns)
        return pltpu.make_async_remote_copy(
            side_buf.at[shift(way, reach - step), :, cols],
            ring_buf.at[way, step, :, cols],
            ring_send.at[way, step],
            ring_recv.at[way, step],
            device_id={"fsdp": ways[way]},
            device_id_type=MESH,
        )

    order = [reach] + [shift(way, hops) for hops in range(reach - 1, 0, -1) for way in (0, 1)] + [0]
    for target in order:
        for i in range(count):
            across(target, 1 - core, i).start()

    def add(target, incoming, store):
        first = pl.multiple_of(device(target, core) * rows, tile)
        for i in range(count):
            across(target, core, i).wait_recv()

        @pl.loop(0, rows // tile)
        def _(j):
            here = pl.ds(pl.multiple_of(j * tile, tile), tile)
            mine = pl.ds(pl.multiple_of(first + j * tile, tile), tile)
            for i in range(count):
                cols = pl.ds(starts[i], x_refs[i].shape[1])
                total = x_refs[i][mine, :].astype(f32) + side_buf[target, here, cols].astype(f32)
                for way, step in incoming:
                    if step:
                        total = total + ring_buf[way, step, here, cols].astype(f32)
                store(here, cols, total)
            for way, step in incoming:
                if not step:
                    cols = pl.ds(way * half, half)
                    store(
                        here,
                        cols,
                        side_buf[target, here, cols].astype(f32) + ring_buf[way, 0, here, cols].astype(f32),
                    )

    for step in range(reach):
        for way in (0, 1):
            target = shift(way, reach - step)
            if step:
                hop(way, step - 1).wait_recv()

            def store(here, cols, total, target=target):
                side_buf[target, here, cols] = total.astype(bf16)

            if step or way == 0:
                add(target, [(way, step - 1)] if step else [], store)
            hop(way, step).start()
    for way in (0, 1):
        hop(way, reach - 1).wait_recv()

    def last(here, cols, total):
        o_ref[here, cols] = total

    add(0, [(0, reach - 1), (1, reach - 1)], last)
    for target in order:
        for i in range(count):
            across(target, 1 - core, i).wait_send()
    for step in range(reach):
        for way in (0, 1):
            hop(way, step).wait_send()


def ring_scatter(terms, ident):
    size = lax.axis_size("fsdp")
    terms = [term.astype(bf16) for term in terms]
    if size != 16:
        return scatter_rows(jnp.concatenate(terms, axis=1))
    chips, count = size // 2, len(terms)
    rows, columns = terms[0].shape[0] // size, sum(term.shape[1] for term in terms)
    pair = pltpu.SemaphoreType.DMA((2, chips // 2))
    sides = pltpu.SemaphoreType.DMA((chips, count))
    return pl.pallas_call(
        functools.partial(scatter_kernel, chips, count),
        out_shape=jax.ShapeDtypeStruct((rows, columns), f32),
        in_specs=[pl.BlockSpec(memory_space=pltpu.VMEM)] * count,
        out_specs=pl.BlockSpec(memory_space=pltpu.VMEM),
        scratch_shapes=[
            pltpu.VMEM((chips, rows, columns), bf16),
            pltpu.VMEM((2, chips // 2, rows, columns), bf16),
            sides,
            sides,
            pair,
            pair,
        ],
        compiler_params=pltpu.CompilerParams(
            collective_id=ident, has_side_effects=True, vmem_limit_bytes=56 << 20
        ),
        cost_estimate=busy(1),
        name="ring_scatter",
    )(*terms)


def mix_kernel(chips, *refs):
    gate_ref, up_ref, unit_ref, gate_w, up_w, down_w, gate_b, up_b, down_a, o_ref = refs[:10]
    side_buf, ring_buf, stage, mine, side_send, side_recv, ring_send, ring_recv = refs[10:]
    core, device = ring_neighbours(chips)
    rows, columns = o_ref.shape
    reach = chips // 2
    half = columns // 2
    tile = 16
    wide = 256
    ways = (device(1, core), device(-1, core))
    side = device(0, 1 - core)
    meet((*ways, side))
    order = [(reach, 0, 0)]
    for step in range(1, reach):
        order += [(reach - step, 0, step), (chips - reach + step, 1, step)]
    order.append((0, 0, reach))

    def across(i):
        target = order[i][0]
        return pltpu.make_async_remote_copy(
            stage.at[i % 2],
            side_buf.at[target],
            side_send.at[target],
            side_recv.at[target],
            device_id={"fsdp": side},
            device_id_type=MESH,
        )

    def hop(way, step):
        target = (reach - step if way == 0 else chips - reach + step) % chips
        cols = pl.ds(way * half, half) if step == 0 else pl.ds(0, columns)
        return pltpu.make_async_remote_copy(
            side_buf.at[target, :, cols],
            ring_buf.at[way, step, :, cols],
            ring_send.at[way, step],
            ring_recv.at[way, step],
            device_id={"fsdp": ways[way]},
            device_id_type=MESH,
        )

    def make(i):
        target, slot = order[i][0], i % 2
        if i >= 2:
            across(i - 2).wait_send()
        theirs = pl.ds(pl.multiple_of(device(target, 1 - core) * rows, rows), rows)
        ours = pl.ds(pl.multiple_of(device(target, core) * rows, rows), rows)

        def block(ref):
            return jnp.concatenate([ref[theirs, :], ref[ours, :]], axis=0)

        def put(first, value):
            cols = pl.ds(pl.multiple_of(first, wide), wide)
            stage[slot, :, cols] = value[:rows].astype(bf16)
            mine[slot, :, cols] = value[rows:].astype(bf16)

        @pl.loop(0, MODEL_WIDTH // wide)
        def _(t):
            cols = pl.ds(pl.multiple_of(t * wide, wide), wide)
            put(
                t * wide,
                matrix_product(block(gate_ref), gate_w[:, cols])
                + matrix_product(block(up_ref), up_w[:, cols]),
            )
            put(
                MODEL_WIDTH + 2 * ADAPTER_RANK + t * wide,
                matrix_product(block(unit_ref), down_w[:, cols]),
            )

        put(MODEL_WIDTH, times_transposed(block(gate_ref), gate_b[...]))
        put(MODEL_WIDTH + ADAPTER_RANK, times_transposed(block(up_ref), up_b[...]))
        put(2 * MODEL_WIDTH + 2 * ADAPTER_RANK, matrix_product(block(unit_ref), down_a[...]))
        across(i).start()

    def add(i):
        target, way, step = order[i]
        last = target == 0
        incoming = [(w, step - 1) for w in ((0, 1) if last else (way,))] if step else []
        across(i).wait_recv()
        for w, s in incoming:
            hop(w, s).wait_recv()

        @pl.loop(0, rows // tile)
        def _(j):
            here = pl.ds(pl.multiple_of(j * tile, tile), tile)
            for part in (0, 1):
                cols = pl.ds(part * half, half)
                total = mine[i % 2, here, cols].astype(f32) + side_buf[target, here, cols].astype(f32)
                for w, s in incoming:
                    if s or w == part:
                        total = total + ring_buf[w, s, here, cols].astype(f32)
                if last:
                    o_ref[here, cols] = total
                else:
                    side_buf[target, here, cols] = total.astype(bf16)

        if not last:
            hop(way, step).start()
            if step == 0:
                hop(1, 0).start()

    make(0)
    for i in range(len(order)):
        if i + 1 < len(order):
            make(i + 1)
        add(i)
    for i in range(len(order) - 2, len(order)):
        across(i).wait_send()
    for step in range(reach):
        for way in (0, 1):
            hop(way, step).wait_send()


def mix_rows(gate_grad, up_grad, units, gate_w, up_w, down_w, gate_b, up_b, down_a, ident):
    size = lax.axis_size("fsdp")
    if size != 16:
        terms = [
            matrix_product(gate_grad, gate_w) + matrix_product(up_grad, up_w),
            times_transposed(gate_grad, gate_b),
            times_transposed(up_grad, up_b),
            matrix_product(units, down_w),
            matrix_product(units, down_a),
        ]
        return scatter_rows(jnp.concatenate(terms, axis=1))
    chips = size // 2
    rows, columns = units.shape[0] // size, 2 * MODEL_WIDTH + 3 * ADAPTER_RANK
    pair = pltpu.SemaphoreType.DMA((2, chips // 2))
    sides = pltpu.SemaphoreType.DMA((chips,))
    return pl.pallas_call(
        functools.partial(mix_kernel, chips),
        out_shape=jax.ShapeDtypeStruct((rows, columns), f32),
        in_specs=[pl.BlockSpec(memory_space=pltpu.VMEM)] * 9,
        out_specs=pl.BlockSpec(memory_space=pltpu.VMEM),
        scratch_shapes=[
            pltpu.VMEM((chips, rows, columns), bf16),
            pltpu.VMEM((2, chips // 2, rows, columns), bf16),
            pltpu.VMEM((2, rows, columns), bf16),
            pltpu.VMEM((2, rows, columns), bf16),
            sides,
            sides,
            pair,
            pair,
        ],
        compiler_params=pltpu.CompilerParams(
            collective_id=ident, has_side_effects=True, vmem_limit_bytes=60 << 20
        ),
        cost_estimate=busy(1),
        name="mix_rows",
    )(gate_grad, up_grad, units, gate_w, up_w, down_w, gate_b, up_b, down_a)


def place_kernel(size, chunk, own_count, mid_ref, near_ref, far_ref, o_ref, send_sem, recv_sem, own_sem):
    me = lax.axis_index("fsdp")
    hidden = HIDDEN_COUNT // size
    width = MODEL_WIDTH // size
    sections = (
        (0, PROJECT_COLUMNS, width),
        (width, GATE_START, hidden),
        (width + hidden, GATE_START + HIDDEN_COUNT, hidden),
    )
    barrier = pltpu.get_barrier_semaphore()

    def greet(i, carry):
        other = (me + i) % size
        pl.semaphore_signal(barrier, inc=1, device_id={"fsdp": other}, device_id_type=MESH)
        return carry

    lax.fori_loop(1, size, greet, 0)
    pl.semaphore_wait(barrier, size - 1)

    def rows(ref, first):
        return ref.at[pl.ds(pl.multiple_of(first, 8), chunk)]

    def aim(start, length):
        owner = (start + me * length) // own_count
        return owner, start + me * length - owner * own_count

    def remote(source, first, owner, sent=0):
        return pltpu.make_async_remote_copy(
            source,
            rows(o_ref, first),
            send_sem.at[sent],
            recv_sem.at[first // chunk],
            device_id={"fsdp": owner},
            device_id_type=MESH,
        )

    def local(source, first):
        return pltpu.make_async_copy(source, rows(o_ref, first), own_sem.at[first // chunk])

    for base, start, length in sections:

        def send(j, carry, base=base, aimed=aim(start, length)):
            over = (aimed[1] + j * chunk >= own_count).astype(jnp.int32)
            owner = aimed[0] + over
            first = aimed[1] + j * chunk - over * own_count
            source = rows(mid_ref, base + j * chunk)

            @pl.when(owner != me)
            def _():
                remote(source, first, owner, base // chunk + j).start()

            @pl.when(owner == me)
            def _():
                local(source, first).start()

            return carry

        lax.fori_loop(0, length // chunk, send, 0)

    def fill(j, carry):
        column = me * own_count + j * chunk

        @pl.when(column < PROJECT_COLUMNS)
        def _():
            local(rows(near_ref, column), j * chunk).start()

        @pl.when(column >= GATE_START + 2 * HIDDEN_COUNT)
        def _():
            local(rows(far_ref, column - (GATE_START + 2 * HIDDEN_COUNT)), j * chunk).start()

        return carry

    lax.fori_loop(0, own_count // chunk, fill, 0)

    def arrive(j, carry):
        column = me * own_count + j * chunk
        here = rows(o_ref, j * chunk)
        away = 0
        for _, start, length in sections:
            mine = start + me * length
            inside = (column >= start) & (column < start + length * size)
            outside = (column < mine) | (column >= mine + length)
            away = away + (inside & outside).astype(jnp.int32)

        @pl.when(away > 0)
        def _():
            remote(here, j * chunk, (me + 1) % size).wait_recv()

        @pl.when(away == 0)
        def _():
            local(rows(near_ref, 0), j * chunk).wait()

        return carry

    lax.fori_loop(0, own_count // chunk, arrive, 0)
    for base, start, length in sections:

        def sent(j, carry, base=base, aimed=aim(start, length)):
            over = (aimed[1] + j * chunk >= own_count).astype(jnp.int32)
            owner = aimed[0] + over
            first = aimed[1] + j * chunk - over * own_count

            @pl.when(owner != me)
            def _():
                remote(rows(mid_ref, base + j * chunk), first, owner, base // chunk + j).wait_send()

            return carry

        lax.fori_loop(0, length // chunk, sent, 0)


def place_columns(middle, near, far, ident):
    size = lax.axis_size("fsdp")
    own_count = ADAPTER_COLUMNS // size
    chunk = math.gcd(own_count, MODEL_WIDTH // size, HIDDEN_COUNT // size, PROJECT_COLUMNS, GATE_START)
    anywhere = pl.BlockSpec(memory_space=pl.ANY)
    return pl.pallas_call(
        functools.partial(place_kernel, size, chunk, own_count),
        out_shape=jax.ShapeDtypeStruct((own_count, ADAPTER_RANK), bf16),
        in_specs=[anywhere] * 3,
        out_specs=anywhere,
        scratch_shapes=[
            pltpu.SemaphoreType.DMA((middle.shape[0] // chunk,)),
            pltpu.SemaphoreType.DMA((own_count // chunk,)),
            pltpu.SemaphoreType.DMA((own_count // chunk,)),
        ],
        compiler_params=pltpu.CompilerParams(collective_id=ident, has_side_effects=True),
        cost_estimate=busy(30),
        name="place_columns",
    )(middle, near, far)


def per_device(
    hidden_input,
    sequence_lengths,
    norm_gain_values,
    input_proj_weight,
    output_proj_weight,
    feedforward_weight,
    adapter_first,
    adapter_second,
    adapter_down_first,
    output_gradient,
):
    size = lax.axis_size("fsdp")
    place = lax.axis_index("fsdp")
    tokens_dev = hidden_input.shape[1]
    all_rows = tokens_dev * size
    hidden_own = HIDDEN_COUNT // size
    width_own = MODEL_WIDTH // size
    columns_own = ADAPTER_COLUMNS // size
    offset = place * tokens_dev
    segment_all, position_all = segment_info(sequence_lengths[0], all_rows)
    segment_own = lax.dynamic_slice_in_dim(segment_all, offset, tokens_dev)
    position_own = lax.dynamic_slice_in_dim(position_all, offset, tokens_dev)
    row_all = jnp.arange(all_rows, dtype=jnp.int32)
    row_own = offset + jnp.arange(tokens_dev, dtype=jnp.int32)
    allowed = (segment_own[:, None] == segment_all[None, :]) & (
        row_own[:, None] >= row_all[None, :]
    )
    gains = norm_gain_values.astype(f32)
    first_factor = adapter_first[0]
    second_factor = adapter_second[0]
    rank = ADAPTER_RANK
    narrow_projection = first_factor[:, : 3 * rank]
    narrow_output = first_factor[:, 3 * rank : 4 * rank]
    squeeze_gate = first_factor[:, 4 * rank : 5 * rank]
    squeeze_up = first_factor[:, 5 * rank :]
    narrow_down = lax.dynamic_slice_in_dim(adapter_down_first[0], place * hidden_own, hidden_own, 0)
    widen_query = second_factor[:, :QUERY_WIDTH]
    widen_key = second_factor[:, QUERY_WIDTH : QUERY_WIDTH + HEAD_WIDTH]
    widen_value = second_factor[:, QUERY_WIDTH + HEAD_WIDTH : PROJECT_COLUMNS]
    widen_output = second_factor[:, PROJECT_COLUMNS:GATE_START]
    widen_gate = lax.dynamic_slice_in_dim(
        second_factor, GATE_START + place * hidden_own, hidden_own, 1
    )
    widen_up = lax.dynamic_slice_in_dim(
        second_factor, GATE_START + HIDDEN_COUNT + place * hidden_own, hidden_own, 1
    )
    widen_down = second_factor[:, GATE_START + 2 * HIDDEN_COUNT :]
    scaling = HEAD_WIDTH ** (-0.5)

    hidden_state = hidden_input[0].astype(f32)
    scale_one = rms_scale(hidden_state)
    normalized = (hidden_state * scale_one * gains[0]).astype(bf16)
    proj_in = ring_gather(input_proj_weight, 0)
    proj_in, proj_out, grad_rows = lax.optimization_barrier(
        (proj_in, output_proj_weight, output_gradient[0])
    )
    proj_out = gather_rows(proj_out)
    lora_qkv = matrix_product(normalized, narrow_projection).astype(bf16)
    projected = matrix_product(normalized, proj_in)
    query_pre = projected[:, :QUERY_WIDTH] + matrix_product(lora_qkv[:, :rank], widen_query)
    key_pre = projected[:, QUERY_WIDTH : QUERY_WIDTH + HEAD_WIDTH] + matrix_product(
        lora_qkv[:, rank : 2 * rank], widen_key
    )
    value_local = (
        projected[:, QUERY_WIDTH + HEAD_WIDTH :]
        + matrix_product(lora_qkv[:, 2 * rank :], widen_value)
    ).astype(bf16)
    query_rot = rotate(query_pre, position_own, 1.0).astype(bf16)
    key_rot = rotate(key_pre, position_own, 1.0).astype(bf16)
    keys_all = ring_gather(jnp.concatenate([key_rot, value_local], axis=1), 1)
    key_rows, value_rows = keys_all[:, :HEAD_WIDTH], keys_all[:, HEAD_WIDTH:]
    query_heads = query_rot.reshape(tokens_dev, HEADS, HEAD_WIDTH)
    scores = scores_of(query_heads, key_rows, allowed, scaling)
    row_max = jnp.max(scores, axis=-1, keepdims=True)
    powered = jnp.exp(scores - row_max)
    row_sum = jnp.sum(powered, axis=-1, keepdims=True)
    probs = powered / row_sum
    probs_low = probs.astype(bf16)
    attended = (
        jnp.einsum("thu,ud->thd", probs_low, value_rows, preferred_element_type=f32)
        .reshape(tokens_dev, QUERY_WIDTH)
        .astype(bf16)
    )
    lora_out = matrix_product(attended, narrow_output).astype(bf16)
    middle = (
        hidden_state
        + times_transposed(attended, proj_out)
        + matrix_product(lora_out, widen_output)
    )
    scale_two = rms_scale(middle)
    normed_two = (middle * scale_two * gains[1]).astype(bf16)

    two_all = ring_gather(normed_two, 2)
    two_all, grad_rows = lax.optimization_barrier((two_all, grad_rows))
    grad_all = gather_rows(grad_rows)
    weight_gate = feedforward_weight[:, 0, :]
    weight_up = feedforward_weight[:, 1, :]
    weight_down = feedforward_weight[:, 2, :]
    lora_gate = matrix_product(two_all, squeeze_gate).astype(bf16)
    lora_up = matrix_product(two_all, squeeze_up).astype(bf16)
    hd_grad = times_transposed(grad_all, widen_down).astype(bf16)
    gate = times_transposed(two_all, weight_gate) + matrix_product(lora_gate, widen_gate)
    upward = times_transposed(two_all, weight_up) + matrix_product(lora_up, widen_up)
    units = (gelu_tanh(gate) * upward).astype(bf16)
    units_grad = times_transposed(grad_all, weight_down) + times_transposed(hd_grad, narrow_down)
    gate_grad, up_grad = unit_backward(gate, upward, units_grad)
    ffn_shares = jnp.stack(
        [
            outer_product_rows(former, latter).astype(bf16)
            for former, latter in ((gate_grad, two_all), (up_grad, two_all), (units, grad_all))
        ]
    )
    attended_all = gather_rows(jnp.concatenate([attended, lora_qkv], axis=1))
    ffn_shares, gate_grad, attended_all = lax.optimization_barrier(
        (ffn_shares, gate_grad, attended_all)
    )
    ffn_both = loop_shares(ffn_shares)
    rows_sum = mix_rows(
        gate_grad, up_grad, units, weight_gate, weight_up, weight_down, widen_gate, widen_up, narrow_down, 3
    )
    back_own, out_own = rows_sum[:, : MODEL_WIDTH + 2 * rank], rows_sum[:, MODEL_WIDTH + 2 * rank :]
    down_own = outer_product_rows(units, hd_grad)
    gate_piece = outer_product_rows(gate_grad, lora_gate)
    up_piece = outer_product_rows(up_grad, lora_up)

    lora_hd = out_own[:, MODEL_WIDTH:].astype(bf16)
    hidden_out = (middle + out_own[:, :MODEL_WIDTH] + matrix_product(lora_hd, widen_down)).astype(bf16)

    gate_low = back_own[:, MODEL_WIDTH : MODEL_WIDTH + rank].astype(bf16)
    up_low = back_own[:, MODEL_WIDTH + rank :].astype(bf16)
    two_grad = (
        back_own[:, :MODEL_WIDTH]
        + times_transposed(gate_low, squeeze_gate)
        + times_transposed(up_low, squeeze_up)
    )
    weighted_two = gains[1] * two_grad
    middle_grad = (
        output_gradient[0].astype(f32)
        + scale_two * weighted_two
        - middle * scale_two**3 * jnp.mean(middle * weighted_two, axis=-1, keepdims=True)
    )
    gain_two = jnp.sum(two_grad * middle * scale_two, axis=0)

    branch_grad = middle_grad.astype(bf16)
    lora_out_grad = times_transposed(branch_grad, widen_output).astype(bf16)
    attended_grad = (
        matrix_product(branch_grad, proj_out) + times_transposed(lora_out_grad, narrow_output)
    ).astype(bf16)
    heads_grad = attended_grad.reshape(tokens_dev, HEADS, HEAD_WIDTH)
    prob_grad = jnp.einsum("thd,ud->thu", heads_grad, value_rows, preferred_element_type=f32)
    row_dot = jnp.sum(probs * prob_grad, axis=-1, keepdims=True)
    score_grad = (probs * (prob_grad - row_dot)).astype(bf16)
    query_rot_grad = (
        jnp.einsum("thu,ud->thd", score_grad, key_rows, preferred_element_type=f32) * scaling
    )
    key_part = (
        jnp.einsum("thu,thd->ud", score_grad, query_heads, preferred_element_type=f32) * scaling
    )
    value_part = jnp.einsum("thu,thd->ud", probs_low, heads_grad, preferred_element_type=f32)
    pair_grad = ring_scatter([key_part, value_part], 4)
    query_grad = rotate(
        query_rot_grad.reshape(tokens_dev, QUERY_WIDTH), position_own, -1.0
    ).astype(bf16)
    key_grad = rotate(pair_grad[:, :HEAD_WIDTH], position_own, -1.0).astype(bf16)
    value_grad = pair_grad[:, HEAD_WIDTH:].astype(bf16)
    proj_grad = jnp.concatenate([query_grad, key_grad, value_grad], axis=1)
    lora_qkv_grad = jnp.concatenate(
        [
            times_transposed(query_grad, widen_query),
            times_transposed(key_grad, widen_key),
            times_transposed(value_grad, widen_value),
        ],
        axis=1,
    ).astype(bf16)
    normed_grad = times_transposed(proj_grad, proj_in) + times_transposed(
        lora_qkv_grad, narrow_projection
    )
    weighted_one = gains[0] * normed_grad
    input_grad = (
        middle_grad
        + scale_one * weighted_one
        - hidden_state
        * scale_one**3
        * jnp.mean(hidden_state * weighted_one, axis=-1, keepdims=True)
    )
    gain_one = jnp.sum(normed_grad * hidden_state * scale_one, axis=0)

    lora_qkv_all = attended_all[:, QUERY_WIDTH:]
    attended_all = attended_all[:, :QUERY_WIDTH]
    lora_out_all = matrix_product(attended_all, narrow_output).astype(bf16)
    gain_rows = jnp.stack([gain_one, gain_two]).astype(bf16).reshape(tokens_dev, -1)
    gain_count = gain_rows.shape[1]
    gain_rows = jnp.pad(gain_rows, ((0, 0), (0, -gain_count % 128)))
    proj_rows = jnp.concatenate(
        [proj_grad, lora_out_grad, gate_low, up_low, lora_hd, gain_rows], axis=1
    )
    proj_all = ring_gather(proj_rows, 5)
    low_all = proj_all[:, PROJECT_COLUMNS : PROJECT_COLUMNS + 4 * rank]
    gain_all = proj_all[:, PROJECT_COLUMNS + 4 * rank :][:, :gain_count].reshape(size, 2, MODEL_WIDTH)
    gain_all = jnp.sum(gain_all.astype(f32), axis=0)
    gain_own = lax.dynamic_slice_in_dim(gain_all, place * width_own, width_own, 1)
    proj_all = proj_all[:, :PROJECT_COLUMNS]
    qkv_low_all = jnp.concatenate(
        [
            times_transposed(proj_all[:, :QUERY_WIDTH], widen_query),
            times_transposed(proj_all[:, QUERY_WIDTH : QUERY_WIDTH + HEAD_WIDTH], widen_key),
            times_transposed(proj_all[:, QUERY_WIDTH + HEAD_WIDTH :], widen_value),
        ],
        axis=1,
    ).astype(bf16)
    normed_turn = turn(normalized)
    branch_turn = turn(branch_grad)
    column = place * width_own
    attended_turn = lax.dynamic_slice_in_dim(attended_all, column, width_own, 1)
    two_turn = lax.dynamic_slice_in_dim(two_all, column, width_own, 1)
    attn_part = jnp.concatenate(
        [outer_product_rows(normed_turn, proj_all), outer_product_rows(branch_turn, attended_all)],
        axis=1,
    )
    gain_part = jnp.pad(gain_own, ((0, width_own - 2), (0, -width_own % 128)))
    attn_part, ffn_both = lax.optimization_barrier(
        (jnp.concatenate([attn_part, gain_part], axis=1).astype(bf16), ffn_both)
    )
    attn_sum = both_loops(loop_shares(attn_part))
    gain_column = PROJECT_COLUMNS + QUERY_WIDTH
    gain_sum = attn_sum[:2, gain_column : gain_column + width_own]
    squeeze_own = jnp.concatenate(
        [
            outer_product_rows(normed_turn, qkv_low_all),
            outer_product_rows(attended_turn, low_all[:, :rank]),
            outer_product_rows(two_turn, low_all[:, rank : 3 * rank]),
        ],
        axis=1,
    )
    out_piece = outer_product_rows(branch_turn, lora_out_all)
    near = jnp.concatenate(
        [
            outer_product_rows(proj_all[:, :QUERY_WIDTH], lora_qkv_all[:, :rank]),
            outer_product_rows(
                proj_all[:, QUERY_WIDTH : QUERY_WIDTH + HEAD_WIDTH], lora_qkv_all[:, rank : 2 * rank]
            ),
            outer_product_rows(proj_all[:, QUERY_WIDTH + HEAD_WIDTH :], lora_qkv_all[:, 2 * rank :]),
        ],
        axis=0,
    )
    far = outer_product_rows(grad_all, low_all[:, 3 * rank :])
    expand_own = place_columns(
        jnp.concatenate([out_piece, gate_piece, up_piece], axis=0).astype(bf16),
        near.astype(bf16),
        far.astype(bf16),
        6,
    )
    expand_own = expand_own.T.astype(f32)
    ffn_sum = both_loops(ffn_both).transpose(1, 0, 2)
    return (
        hidden_out[None],
        input_grad[None],
        gain_sum,
        attn_sum[:, :PROJECT_COLUMNS],
        attn_sum[:, PROJECT_COLUMNS:gain_column],
        ffn_sum,
        squeeze_own[None],
        expand_own[None],
        down_own[None],
    )


def solution(mesh):
    return jax.shard_map(
        per_device,
        mesh=mesh,
        in_specs=(
            P("loop", "fsdp", None),
            P("loop", None),
            P(),
            P("fsdp", None),
            P("fsdp", None),
            P("fsdp", None, None),
            P("loop", None, None),
            P("loop", None, None),
            P("loop", None, None),
            P("loop", "fsdp", None),
        ),
        out_specs=(
            P("loop", "fsdp", None),
            P("loop", "fsdp", None),
            P(None, "fsdp"),
            P("fsdp", None),
            P("fsdp", None),
            P("fsdp", None, None),
            P("loop", "fsdp", None),
            P("loop", None, "fsdp"),
            P("loop", "fsdp", None),
        ),
        check_vma=False,
    )
```

```python
import functools
import math

import jax
import jax.numpy as jnp
from jax import lax
from jax.experimental import pallas as pl
from jax.experimental.pallas import tpu as pltpu
from jax.sharding import PartitionSpec as P

MODEL_WIDTH = 2048
HEADS = 8
HEAD_WIDTH = 256
HIDDEN_COUNT = 16384
ADAPTER_RANK = 256
QUERY_WIDTH = 2048
PROJECT_COLUMNS = 2560
ADAPTER_COLUMNS = 39424
GATE_START = PROJECT_COLUMNS + MODEL_WIDTH

epsilon = 1e-06
bf16 = jnp.bfloat16
f32 = jnp.float32
MESH = pl.DeviceIdType.MESH


def matrix_product(former, latter):
    return jnp.dot(former, latter, preferred_element_type=f32)


def times_transposed(former, latter):
    return lax.dot_general(former, latter, (((1,), (1,)), ((), ())), preferred_element_type=f32)


def outer_product_rows(former, latter):
    return lax.dot_general(former, latter, (((0,), (0,)), ((), ())), preferred_element_type=f32)


def segment_info(lengths, row_count):
    row_ids = jnp.arange(row_count, dtype=jnp.int32)
    count = lengths.shape[0]
    labels = jnp.arange(count, dtype=jnp.int32)
    finish = jnp.sum(jnp.where(labels[:, None] <= labels[None, :], lengths[:, None], 0), axis=0)
    starts = finish - lengths
    segment = jnp.sum((row_ids[:, None] >= finish[None, :]).astype(jnp.int32), axis=1)
    opening = jnp.sum(jnp.where(segment[:, None] == labels[None, :], starts[None, :], 0), axis=1)
    return (segment, row_ids - opening)


def rotate(values, position, direction):
    half_dim = HEAD_WIDTH // 2
    frequency = jnp.exp(
        jnp.arange(half_dim).astype(f32) * (-2.0 * math.log(10000.0) / HEAD_WIDTH)
    )
    angles = position.astype(f32)[:, None] * frequency[None, :]
    cosine = jnp.cos(angles)[:, None, :]
    sine_val = direction * jnp.sin(angles)[:, None, :]
    shaped = values.reshape(values.shape[0], -1, HEAD_WIDTH)
    former = shaped[..., :half_dim]
    latter = shaped[..., half_dim:]
    turned = jnp.concatenate(
        [former * cosine - latter * sine_val, latter * cosine + former * sine_val], axis=-1
    )
    return turned.reshape(values.shape)


def rms_scale(values):
    return lax.rsqrt(jnp.mean(values * values, axis=-1, keepdims=True) + epsilon)


def gelu_tanh(values):
    return jax.nn.gelu(values, approximate=True)


def unit_backward(gate_value, upward_activation, hidden_unit_gradient):
    activated, pullback_function = jax.vjp(gelu_tanh, gate_value)
    gate_grad = pullback_function(hidden_unit_gradient * upward_activation)[0]
    return (gate_grad.astype(bf16), (hidden_unit_gradient * activated).astype(bf16))


def scores_of(query_heads, key_rows, allowed, scaling):
    product = (
        jnp.einsum("thd,ud->thu", query_heads, key_rows, preferred_element_type=f32) * scaling
    )
    return jnp.where(allowed[:, None, :], product, -1e30)


def gather_rows(block):
    return lax.all_gather(block, "fsdp", axis=0, tiled=True)


def scatter_rows(partial):
    return lax.psum_scatter(partial.astype(bf16), "fsdp", scatter_dimension=0, tiled=True).astype(f32)


def loop_shares(partial):
    return lax.all_gather(partial.astype(bf16), "loop", axis=0)


def both_loops(shares):
    return shares[0].astype(f32) + shares[1].astype(f32)


def turn(block):
    return lax.all_to_all(block, "fsdp", split_axis=1, concat_axis=0, tiled=True)


def chip_at(q, chips):
    return jnp.where(q < 4, 2 * q, 15 - 2 * q) if chips == 8 else q

def ring_place(chip, chips):
    return jnp.where(chip % 2 == 0, chip // 2, 7 - chip // 2) if chips == 8 else chip

def ring_neighbours(chips):
    me = lax.axis_index("fsdp")
    core = me % 2
    p = ring_place(me // 2, chips)
    def device(shift, c):
        return chip_at((p + shift + chips) % chips, chips) * 2 + c
    return core, device

def meet(devices):
    barrier = pltpu.get_barrier_semaphore()
    for d in devices:
        pl.semaphore_signal(barrier, inc=1, device_id={"fsdp": d}, device_id_type=MESH)
    pl.semaphore_wait(barrier, len(devices))

def gather_kernel(chips, x_ref, o_ref, own_sem, ring_send, ring_recv, side_send, side_recv, greet=None, also=None):
    core, device = ring_neighbours(chips)
    rows = x_ref.shape[0]
    reach = chips // 2
    ways = (device(1, core), device(-1, core))
    side = device(0, 1 - core)
    if greet is None:
        meet((*ways, side))
    else:
        greet()

    def span(way, hops):
        return (way * (rows // 2), rows // 2) if hops == reach else (0, rows)

    def at(way, hops, c, part):
        origin = device(-hops if way == 0 else hops, c)
        return o_ref.at[pl.ds(pl.multiple_of(origin * rows + part[0], 8), part[1])]

    def hop(way, hops):
        part = span(way, hops)
        here = at(way, hops - 1, core, part)
        src = x_ref.at[pl.ds(part[0], part[1])] if hops == 1 else here
        return pltpu.make_async_remote_copy(src, here, ring_send.at[way, hops - 1], ring_recv.at[way, hops - 1], device_id={"fsdp": ways[way]}, device_id_type=MESH)

    def arriving(way, hops):
        here = at(way, hops, core, span(way, hops))
        return pltpu.make_async_remote_copy(here, here, ring_send.at[way, hops - 1], ring_recv.at[way, hops - 1], device_id={"fsdp": ways[way]}, device_id_type=MESH)

    def across(way, hops, c):
        part = span(way, hops) if hops else (0, rows)
        there = at(way, hops, c, part)
        src = there if hops else x_ref
        return pltpu.make_async_remote_copy(src, there, side_send.at[way, hops], side_recv.at[way, hops], device_id={"fsdp": side}, device_id_type=MESH)

    for way in (0, 1):
        hop(way, 1).start()
    across(0, 0, core).start()
    own = pltpu.make_async_copy(x_ref, at(0, 0, core, (0, rows)), own_sem)
    own.start()
    if also is not None:
        also()
    for hops in range(1, reach + 1):
        for way in (0, 1):
            arriving(way, hops).wait_recv()
            if hops < reach:
                hop(way, hops + 1).start()
            across(way, hops, core).start()
    across(0, 0, 1 - core).wait_recv()
    across(0, 0, core).wait_send()
    for hops in range(1, reach + 1):
        for way in (0, 1):
            across(way, hops, 1 - core).wait_recv()
            across(way, hops, core).wait_send()
            hop(way, hops).wait_send()
    own.wait()

def busy(us):
    return pl.CostEstimate(flops=0, bytes_accessed=int(us * 3.0e6), transcendentals=0)


def ring_gather(block, ident):
    size = lax.axis_size("fsdp")
    chips = size // 2
    rows, columns = block.shape
    pair = pltpu.SemaphoreType.DMA((2, chips // 2))
    sides = pltpu.SemaphoreType.DMA((2, chips // 2 + 1))
    return pl.pallas_call(
        functools.partial(gather_kernel, chips),
        out_shape=jax.ShapeDtypeStruct((size * rows, columns), block.dtype),
        in_specs=[pl.BlockSpec(memory_space=pl.ANY)],
        out_specs=pl.BlockSpec(memory_space=pl.ANY),
        scratch_shapes=[pltpu.SemaphoreType.DMA, pair, pair, sides, sides],
        compiler_params=pltpu.CompilerParams(collective_id=ident, has_side_effects=True),
        cost_estimate=busy(1),
        name="ring_gather",
    )(block)

def scatter_kernel(chips, count, *refs):
    x_refs, o_ref = refs[:count], refs[count]
    side_buf, ring_buf, side_send, side_recv, ring_send, ring_recv = refs[count + 1 :]
    core, device = ring_neighbours(chips)
    rows, columns = o_ref.shape
    reach = chips // 2
    half = columns // 2
    tile = 16
    ways = (device(1, core), device(-1, core))
    side = device(0, 1 - core)
    meet((*ways, side))
    starts = [sum(x.shape[1] for x in x_refs[:i]) for i in range(count)]

    def shift(way, hops):
        return (hops if way == 0 else chips - hops) % chips

    def across(target, c, i):
        there = pl.ds(pl.multiple_of(device(target, c) * rows, tile), rows)
        return pltpu.make_async_remote_copy(
            x_refs[i].at[there],
            side_buf.at[target, :, pl.ds(starts[i], x_refs[i].shape[1])],
            side_send.at[target, i],
            side_recv.at[target, i],
            device_id={"fsdp": side},
            device_id_type=MESH,
        )

    def hop(way, step):
        cols = pl.ds(way * half, half) if step == 0 else pl.ds(0, columns)
        return pltpu.make_async_remote_copy(
            side_buf.at[shift(way, reach - step), :, cols],
            ring_buf.at[way, step, :, cols],
            ring_send.at[way, step],
            ring_recv.at[way, step],
            device_id={"fsdp": ways[way]},
            device_id_type=MESH,
        )

    order = [reach] + [shift(way, hops) for hops in range(reach - 1, 0, -1) for way in (0, 1)] + [0]
    for target in order:
        for i in range(count):
            across(target, 1 - core, i).start()

    def add(target, incoming, store):
        first = pl.multiple_of(device(target, core) * rows, tile)
        for i in range(count):
            across(target, core, i).wait_recv()

        @pl.loop(0, rows // tile)
        def _(j):
            here = pl.ds(pl.multiple_of(j * tile, tile), tile)
            mine = pl.ds(pl.multiple_of(first + j * tile, tile), tile)
            for i in range(count):
                cols = pl.ds(starts[i], x_refs[i].shape[1])
                total = x_refs[i][mine, :].astype(f32) + side_buf[target, here, cols].astype(f32)
                for way, step in incoming:
                    if step:
                        total = total + ring_buf[way, step, here, cols].astype(f32)
                store(here, cols, total)
            for way, step in incoming:
                if not step:
                    cols = pl.ds(way * half, half)
                    store(
                        here,
                        cols,
                        side_buf[target, here, cols].astype(f32) + ring_buf[way, 0, here, cols].astype(f32),
                    )

    for step in range(reach):
        for way in (0, 1):
            target = shift(way, reach - step)
            if step:
                hop(way, step - 1).wait_recv()

            def store(here, cols, total, target=target):
                side_buf[target, here, cols] = total.astype(bf16)

            if step or way == 0:
                add(target, [(way, step - 1)] if step else [], store)
            hop(way, step).start()
    for way in (0, 1):
        hop(way, reach - 1).wait_recv()

    def last(here, cols, total):
        o_ref[here, cols] = total

    add(0, [(0, reach - 1), (1, reach - 1)], last)
    for target in order:
        for i in range(count):
            across(target, 1 - core, i).wait_send()
    for step in range(reach):
        for way in (0, 1):
            hop(way, step).wait_send()


def ring_scatter(terms, ident):
    size = lax.axis_size("fsdp")
    terms = [term.astype(bf16) for term in terms]
    if size != 16:
        return scatter_rows(jnp.concatenate(terms, axis=1))
    chips, count = size // 2, len(terms)
    rows, columns = terms[0].shape[0] // size, sum(term.shape[1] for term in terms)
    pair = pltpu.SemaphoreType.DMA((2, chips // 2))
    sides = pltpu.SemaphoreType.DMA((chips, count))
    return pl.pallas_call(
        functools.partial(scatter_kernel, chips, count),
        out_shape=jax.ShapeDtypeStruct((rows, columns), f32),
        in_specs=[pl.BlockSpec(memory_space=pltpu.VMEM)] * count,
        out_specs=pl.BlockSpec(memory_space=pltpu.VMEM),
        scratch_shapes=[
            pltpu.VMEM((chips, rows, columns), bf16),
            pltpu.VMEM((2, chips // 2, rows, columns), bf16),
            sides,
            sides,
            pair,
            pair,
        ],
        compiler_params=pltpu.CompilerParams(
            collective_id=ident, has_side_effects=True, vmem_limit_bytes=56 << 20
        ),
        cost_estimate=busy(1),
        name="ring_scatter",
    )(*terms)


def mix_kernel(chips, *refs):
    gate_ref, up_ref, unit_ref, planes, gate_b, up_b, down_a, o_ref = refs[:8]
    held, side_buf, ring_buf, stage, mine, held_sem, side_send, side_recv, ring_send, ring_recv = refs[8:]
    fetches = [pltpu.make_async_copy(planes.at[i], held.at[i], held_sem.at[i]) for i in range(3)]
    for fetch in fetches:
        fetch.start()
    core, device = ring_neighbours(chips)
    rows, columns = o_ref.shape
    reach = chips // 2
    half = columns // 2
    tile = 16
    wide = 256
    ways = (device(1, core), device(-1, core))
    side = device(0, 1 - core)
    meet((*ways, side))
    order = [(reach, 0, 0)]
    for step in range(1, reach):
        order += [(reach - step, 0, step), (chips - reach + step, 1, step)]
    order.append((0, 0, reach))

    def across(i):
        target = order[i][0]
        return pltpu.make_async_remote_copy(
            stage.at[i % 2],
            side_buf.at[target],
            side_send.at[target],
            side_recv.at[target],
            device_id={"fsdp": side},
            device_id_type=MESH,
        )

    def hop(way, step):
        target = (reach - step if way == 0 else chips - reach + step) % chips
        cols = pl.ds(way * half, half) if step == 0 else pl.ds(0, columns)
        return pltpu.make_async_remote_copy(
            side_buf.at[target, :, cols],
            ring_buf.at[way, step, :, cols],
            ring_send.at[way, step],
            ring_recv.at[way, step],
            device_id={"fsdp": ways[way]},
            device_id_type=MESH,
        )

    def make(i):
        target, slot = order[i][0], i % 2
        if i >= 2:
            across(i - 2).wait_send()
        theirs = pl.ds(pl.multiple_of(device(target, 1 - core) * rows, rows), rows)
        ours = pl.ds(pl.multiple_of(device(target, core) * rows, rows), rows)

        def block(ref):
            return jnp.concatenate([ref[theirs, :], ref[ours, :]], axis=0)

        def put(first, value):
            cols = pl.ds(pl.multiple_of(first, wide), wide)
            stage[slot, :, cols] = value[:rows].astype(bf16)
            mine[slot, :, cols] = value[rows:].astype(bf16)

        @pl.loop(0, MODEL_WIDTH // wide)
        def _(t):
            cols = pl.ds(pl.multiple_of(t * wide, wide), wide)
            put(
                t * wide,
                matrix_product(block(gate_ref), held[0, :, cols])
                + matrix_product(block(up_ref), held[1, :, cols]),
            )
            put(
                MODEL_WIDTH + 2 * ADAPTER_RANK + t * wide,
                matrix_product(block(unit_ref), held[2, :, cols]),
            )

        put(MODEL_WIDTH, times_transposed(block(gate_ref), gate_b[...]))
        put(MODEL_WIDTH + ADAPTER_RANK, times_transposed(block(up_ref), up_b[...]))
        put(2 * MODEL_WIDTH + 2 * ADAPTER_RANK, matrix_product(block(unit_ref), down_a[...]))
        across(i).start()

    def add(i):
        target, way, step = order[i]
        last = target == 0
        incoming = [(w, step - 1) for w in ((0, 1) if last else (way,))] if step else []
        across(i).wait_recv()
        for w, s in incoming:
            hop(w, s).wait_recv()

        @pl.loop(0, rows // tile)
        def _(j):
            here = pl.ds(pl.multiple_of(j * tile, tile), tile)
            for part in (0, 1):
                cols = pl.ds(part * half, half)
                total = mine[i % 2, here, cols].astype(f32) + side_buf[target, here, cols].astype(f32)
                for w, s in incoming:
                    if s or w == part:
                        total = total + ring_buf[w, s, here, cols].astype(f32)
                if last:
                    o_ref[here, cols] = total
                else:
                    side_buf[target, here, cols] = total.astype(bf16)

        if not last:
            hop(way, step).start()
            if step == 0:
                hop(1, 0).start()

    for fetch in fetches:
        fetch.wait()
    make(0)
    for i in range(len(order)):
        if i + 1 < len(order):
            make(i + 1)
        add(i)
    for i in range(len(order) - 2, len(order)):
        across(i).wait_send()
    for step in range(reach):
        for way in (0, 1):
            hop(way, step).wait_send()


def mix_rows(gate_grad, up_grad, units, planes, gate_b, up_b, down_a, ident):
    size = lax.axis_size("fsdp")
    if size != 16:
        terms = [
            matrix_product(gate_grad, planes[0]) + matrix_product(up_grad, planes[1]),
            times_transposed(gate_grad, gate_b),
            times_transposed(up_grad, up_b),
            matrix_product(units, planes[2]),
            matrix_product(units, down_a),
        ]
        return scatter_rows(jnp.concatenate(terms, axis=1))
    chips = size // 2
    rows, columns = units.shape[0] // size, 2 * MODEL_WIDTH + 3 * ADAPTER_RANK
    pair = pltpu.SemaphoreType.DMA((2, chips // 2))
    sides = pltpu.SemaphoreType.DMA((chips,))
    return pl.pallas_call(
        functools.partial(mix_kernel, chips),
        out_shape=jax.ShapeDtypeStruct((rows, columns), f32),
        in_specs=[pl.BlockSpec(memory_space=pltpu.VMEM)] * 3
        + [pl.BlockSpec(memory_space=pl.ANY)]
        + [pl.BlockSpec(memory_space=pltpu.VMEM)] * 3,
        out_specs=pl.BlockSpec(memory_space=pltpu.VMEM),
        scratch_shapes=[
            pltpu.VMEM(planes.shape, bf16),
            pltpu.VMEM((chips, rows, columns), bf16),
            pltpu.VMEM((2, chips // 2, rows, columns), bf16),
            pltpu.VMEM((2, rows, columns), bf16),
            pltpu.VMEM((2, rows, columns), bf16),
            pltpu.SemaphoreType.DMA((3,)),
            sides,
            sides,
            pair,
            pair,
        ],
        compiler_params=pltpu.CompilerParams(
            collective_id=ident, has_side_effects=True, vmem_limit_bytes=60 << 20
        ),
        cost_estimate=busy(1),
        name="mix_rows",
    )(gate_grad, up_grad, units, planes, gate_b, up_b, down_a)


def share_kernel(size, chunk, own_count, x_ref, mid_ref, all_ref, o_ref, *sems):
    send_sem, recv_sem, own_sem = sems[5:]
    me = lax.axis_index("fsdp")
    hidden = HIDDEN_COUNT // size
    width = MODEL_WIDTH // size
    sections = (
        (0, PROJECT_COLUMNS, width),
        (width, GATE_START, hidden),
        (width + hidden, GATE_START + HIDDEN_COUNT, hidden),
    )

    def greet():
        barrier = pltpu.get_barrier_semaphore()

        def one(i, carry):
            pl.semaphore_signal(barrier, inc=1, device_id={"fsdp": (me + i) % size}, device_id_type=MESH)
            return carry

        lax.fori_loop(1, size, one, 0)
        pl.semaphore_wait(barrier, size - 1)

    def rows(ref, first):
        return ref.at[pl.ds(pl.multiple_of(first, 8), chunk)]

    def aim(start, length):
        owner = (start + me * length) // own_count
        return owner, start + me * length - owner * own_count

    def remote(source, first, owner, sent=0):
        return pltpu.make_async_remote_copy(
            source,
            rows(o_ref, first),
            send_sem.at[sent],
            recv_sem.at[first // chunk],
            device_id={"fsdp": owner},
            device_id_type=MESH,
        )

    def local(source, first):
        return pltpu.make_async_copy(source, rows(o_ref, first), own_sem.at[first // chunk])

    def send_all():
        for base, start, length in sections:

            def send(j, carry, base=base, aimed=aim(start, length)):
                over = (aimed[1] + j * chunk >= own_count).astype(jnp.int32)
                owner = aimed[0] + over
                first = aimed[1] + j * chunk - over * own_count
                source = rows(mid_ref, base + j * chunk)

                @pl.when(owner != me)
                def _():
                    remote(source, first, owner, base // chunk + j).start()

                @pl.when(owner == me)
                def _():
                    local(source, first).start()

                return carry

            lax.fori_loop(0, length // chunk, send, 0)

    gather_kernel(size // 2, x_ref, all_ref, *sems[:5], greet=greet, also=send_all)

    def arrive(j, carry):
        column = me * own_count + j * chunk
        here = rows(o_ref, j * chunk)
        away, kept = 0, 0
        for _, start, length in sections:
            mine = start + me * length
            inside = (column >= start) & (column < start + length * size)
            outside = (column < mine) | (column >= mine + length)
            away = away + (inside & outside).astype(jnp.int32)
            kept = kept + (inside & ~outside).astype(jnp.int32)

        @pl.when(away > 0)
        def _():
            remote(here, j * chunk, (me + 1) % size).wait_recv()

        @pl.when(kept > 0)
        def _():
            local(rows(mid_ref, 0), j * chunk).wait()

        return carry

    lax.fori_loop(0, own_count // chunk, arrive, 0)
    for base, start, length in sections:

        def sent(j, carry, base=base, aimed=aim(start, length)):
            over = (aimed[1] + j * chunk >= own_count).astype(jnp.int32)
            owner = aimed[0] + over
            first = aimed[1] + j * chunk - over * own_count

            @pl.when(owner != me)
            def _():
                remote(rows(mid_ref, base + j * chunk), first, owner, base // chunk + j).wait_send()

            return carry

        lax.fori_loop(0, length // chunk, sent, 0)


def share_rows(block, middle, ident):
    size = lax.axis_size("fsdp")
    rows, columns = block.shape
    own_count = ADAPTER_COLUMNS // size
    chunk = math.gcd(own_count, MODEL_WIDTH // size, HIDDEN_COUNT // size, PROJECT_COLUMNS, GATE_START)
    anywhere = pl.BlockSpec(memory_space=pl.ANY)
    pair = pltpu.SemaphoreType.DMA((2, size // 4))
    sides = pltpu.SemaphoreType.DMA((2, size // 4 + 1))
    return pl.pallas_call(
        functools.partial(share_kernel, size, chunk, own_count),
        out_shape=(
            jax.ShapeDtypeStruct((size * rows, columns), block.dtype),
            jax.ShapeDtypeStruct((own_count, ADAPTER_RANK), bf16),
        ),
        in_specs=[anywhere] * 2,
        out_specs=(anywhere, anywhere),
        scratch_shapes=[
            pltpu.SemaphoreType.DMA,
            pair,
            pair,
            sides,
            sides,
            pltpu.SemaphoreType.DMA((middle.shape[0] // chunk,)),
            pltpu.SemaphoreType.DMA((own_count // chunk,)),
            pltpu.SemaphoreType.DMA((own_count // chunk,)),
        ],
        compiler_params=pltpu.CompilerParams(collective_id=ident, has_side_effects=True),
        cost_estimate=busy(1),
        name="share_rows",
    )(block, middle)


def per_device(
    hidden_input,
    sequence_lengths,
    norm_gain_values,
    input_proj_weight,
    output_proj_weight,
    feedforward_weight,
    adapter_first,
    adapter_second,
    adapter_down_first,
    output_gradient,
):
    size = lax.axis_size("fsdp")
    place = lax.axis_index("fsdp")
    tokens_dev = hidden_input.shape[1]
    all_rows = tokens_dev * size
    hidden_own = HIDDEN_COUNT // size
    width_own = MODEL_WIDTH // size
    columns_own = ADAPTER_COLUMNS // size
    offset = place * tokens_dev
    segment_all, position_all = segment_info(sequence_lengths[0], all_rows)
    segment_own = lax.dynamic_slice_in_dim(segment_all, offset, tokens_dev)
    position_own = lax.dynamic_slice_in_dim(position_all, offset, tokens_dev)
    row_all = jnp.arange(all_rows, dtype=jnp.int32)
    row_own = offset + jnp.arange(tokens_dev, dtype=jnp.int32)
    allowed = (segment_own[:, None] == segment_all[None, :]) & (
        row_own[:, None] >= row_all[None, :]
    )
    gains = norm_gain_values.astype(f32)
    first_factor = adapter_first[0]
    second_factor = adapter_second[0]
    rank = ADAPTER_RANK
    narrow_projection = first_factor[:, : 3 * rank]
    narrow_output = first_factor[:, 3 * rank : 4 * rank]
    squeeze_gate = first_factor[:, 4 * rank : 5 * rank]
    squeeze_up = first_factor[:, 5 * rank :]
    narrow_down = lax.dynamic_slice_in_dim(adapter_down_first[0], place * hidden_own, hidden_own, 0)
    widen_query = second_factor[:, :QUERY_WIDTH]
    widen_key = second_factor[:, QUERY_WIDTH : QUERY_WIDTH + HEAD_WIDTH]
    widen_value = second_factor[:, QUERY_WIDTH + HEAD_WIDTH : PROJECT_COLUMNS]
    widen_output = second_factor[:, PROJECT_COLUMNS:GATE_START]
    widen_gate = lax.dynamic_slice_in_dim(
        second_factor, GATE_START + place * hidden_own, hidden_own, 1
    )
    widen_up = lax.dynamic_slice_in_dim(
        second_factor, GATE_START + HIDDEN_COUNT + place * hidden_own, hidden_own, 1
    )
    widen_down = second_factor[:, GATE_START + 2 * HIDDEN_COUNT :]
    scaling = HEAD_WIDTH ** (-0.5)

    hidden_state = hidden_input[0].astype(f32)
    scale_one = rms_scale(hidden_state)
    normalized = (hidden_state * scale_one * gains[0]).astype(bf16)
    proj_in = ring_gather(input_proj_weight, 0)
    proj_in, proj_out, grad_rows = lax.optimization_barrier(
        (proj_in, output_proj_weight, output_gradient[0])
    )
    proj_out = gather_rows(proj_out)
    lora_qkv = matrix_product(normalized, narrow_projection).astype(bf16)
    projected = matrix_product(normalized, proj_in)
    query_pre = projected[:, :QUERY_WIDTH] + matrix_product(lora_qkv[:, :rank], widen_query)
    key_pre = projected[:, QUERY_WIDTH : QUERY_WIDTH + HEAD_WIDTH] + matrix_product(
        lora_qkv[:, rank : 2 * rank], widen_key
    )
    value_local = (
        projected[:, QUERY_WIDTH + HEAD_WIDTH :]
        + matrix_product(lora_qkv[:, 2 * rank :], widen_value)
    ).astype(bf16)
    query_rot = rotate(query_pre, position_own, 1.0).astype(bf16)
    key_rot = rotate(key_pre, position_own, 1.0).astype(bf16)
    keys_all = ring_gather(jnp.concatenate([key_rot, value_local], axis=1), 1)
    key_rows, value_rows = keys_all[:, :HEAD_WIDTH], keys_all[:, HEAD_WIDTH:]
    query_heads = query_rot.reshape(tokens_dev, HEADS, HEAD_WIDTH)
    scores = scores_of(query_heads, key_rows, allowed, scaling)
    row_max = jnp.max(scores, axis=-1, keepdims=True)
    powered = jnp.exp(scores - row_max)
    row_sum = jnp.sum(powered, axis=-1, keepdims=True)
    probs = powered / row_sum
    probs_low = probs.astype(bf16)
    attended = (
        jnp.einsum("thu,ud->thd", probs_low, value_rows, preferred_element_type=f32)
        .reshape(tokens_dev, QUERY_WIDTH)
        .astype(bf16)
    )
    lora_out = matrix_product(attended, narrow_output).astype(bf16)
    middle = (
        hidden_state
        + times_transposed(attended, proj_out)
        + matrix_product(lora_out, widen_output)
    )
    scale_two = rms_scale(middle)
    normed_two = (middle * scale_two * gains[1]).astype(bf16)

    two_all = ring_gather(normed_two, 2)
    two_all, grad_rows = lax.optimization_barrier((two_all, grad_rows))
    grad_all = gather_rows(grad_rows)
    weight_planes = feedforward_weight.transpose(1, 0, 2)
    weight_gate, weight_up, weight_down = weight_planes[0], weight_planes[1], weight_planes[2]
    lora_gate = matrix_product(two_all, squeeze_gate).astype(bf16)
    lora_up = matrix_product(two_all, squeeze_up).astype(bf16)
    hd_grad = times_transposed(grad_all, widen_down).astype(bf16)
    gate = times_transposed(two_all, weight_gate) + matrix_product(lora_gate, widen_gate)
    upward = times_transposed(two_all, weight_up) + matrix_product(lora_up, widen_up)
    units = (gelu_tanh(gate) * upward).astype(bf16)
    units_grad = times_transposed(grad_all, weight_down) + times_transposed(hd_grad, narrow_down)
    gate_grad, up_grad = unit_backward(gate, upward, units_grad)
    ffn_shares = jnp.stack(
        [
            outer_product_rows(former, latter).astype(bf16)
            for former, latter in ((gate_grad, two_all), (up_grad, two_all), (units, grad_all))
        ]
    )
    attended_all = gather_rows(jnp.concatenate([attended, lora_qkv], axis=1))
    ffn_shares, gate_grad, attended_all = lax.optimization_barrier(
        (ffn_shares, gate_grad, attended_all)
    )
    ffn_both = loop_shares(ffn_shares)
    rows_sum = mix_rows(
        gate_grad, up_grad, units, weight_planes, widen_gate, widen_up, narrow_down, 3
    )
    back_own, out_own = rows_sum[:, : MODEL_WIDTH + 2 * rank], rows_sum[:, MODEL_WIDTH + 2 * rank :]
    down_own = outer_product_rows(units, hd_grad)
    gate_piece = outer_product_rows(gate_grad, lora_gate)
    up_piece = outer_product_rows(up_grad, lora_up)

    lora_hd = out_own[:, MODEL_WIDTH:].astype(bf16)
    hidden_out = (middle + out_own[:, :MODEL_WIDTH] + matrix_product(lora_hd, widen_down)).astype(bf16)

    gate_low = back_own[:, MODEL_WIDTH : MODEL_WIDTH + rank].astype(bf16)
    up_low = back_own[:, MODEL_WIDTH + rank :].astype(bf16)
    two_grad = (
        back_own[:, :MODEL_WIDTH]
        + times_transposed(gate_low, squeeze_gate)
        + times_transposed(up_low, squeeze_up)
    )
    weighted_two = gains[1] * two_grad
    middle_grad = (
        output_gradient[0].astype(f32)
        + scale_two * weighted_two
        - middle * scale_two**3 * jnp.mean(middle * weighted_two, axis=-1, keepdims=True)
    )
    gain_two = jnp.sum(two_grad * middle * scale_two, axis=0)

    branch_grad = middle_grad.astype(bf16)
    lora_out_grad = times_transposed(branch_grad, widen_output).astype(bf16)
    attended_grad = (
        matrix_product(branch_grad, proj_out) + times_transposed(lora_out_grad, narrow_output)
    ).astype(bf16)
    heads_grad = attended_grad.reshape(tokens_dev, HEADS, HEAD_WIDTH)
    prob_grad = jnp.einsum("thd,ud->thu", heads_grad, value_rows, preferred_element_type=f32)
    row_dot = jnp.sum(probs * prob_grad, axis=-1, keepdims=True)
    score_grad = (probs * (prob_grad - row_dot)).astype(bf16)
    query_rot_grad = (
        jnp.einsum("thu,ud->thd", score_grad, key_rows, preferred_element_type=f32) * scaling
    )
    key_part = (
        jnp.einsum("thu,thd->ud", score_grad, query_heads, preferred_element_type=f32) * scaling
    )
    value_part = jnp.einsum("thu,thd->ud", probs_low, heads_grad, preferred_element_type=f32)
    pair_grad = ring_scatter([key_part, value_part], 4)
    query_grad = rotate(
        query_rot_grad.reshape(tokens_dev, QUERY_WIDTH), position_own, -1.0
    ).astype(bf16)
    key_grad = rotate(pair_grad[:, :HEAD_WIDTH], position_own, -1.0).astype(bf16)
    value_grad = pair_grad[:, HEAD_WIDTH:].astype(bf16)
    proj_grad = jnp.concatenate([query_grad, key_grad, value_grad], axis=1)
    lora_qkv_grad = jnp.concatenate(
        [
            times_transposed(query_grad, widen_query),
            times_transposed(key_grad, widen_key),
            times_transposed(value_grad, widen_value),
        ],
        axis=1,
    ).astype(bf16)
    normed_grad = times_transposed(proj_grad, proj_in) + times_transposed(
        lora_qkv_grad, narrow_projection
    )
    weighted_one = gains[0] * normed_grad
    input_grad = (
        middle_grad
        + scale_one * weighted_one
        - hidden_state
        * scale_one**3
        * jnp.mean(hidden_state * weighted_one, axis=-1, keepdims=True)
    )
    gain_one = jnp.sum(normed_grad * hidden_state * scale_one, axis=0)

    lora_qkv_all = attended_all[:, QUERY_WIDTH:]
    lora_out_all = matrix_product(attended_all[:, :QUERY_WIDTH], narrow_output).astype(bf16)
    normed_turn, branch_turn = turn(normalized), turn(branch_grad)
    out_piece = outer_product_rows(branch_turn, lora_out_all)
    gain_rows = jnp.stack([gain_one, gain_two]).astype(bf16).reshape(tokens_dev, -1)
    gain_count = gain_rows.shape[1]
    gain_rows = jnp.pad(gain_rows, ((0, 0), (0, -gain_count % 128)))
    proj_rows = jnp.concatenate(
        [proj_grad, lora_out_grad, gate_low, up_low, lora_hd, gain_rows], axis=1
    )
    proj_rows, normed_turn, branch_turn = lax.optimization_barrier(
        (proj_rows, normed_turn, branch_turn)
    )
    proj_all, middle_own = share_rows(
        proj_rows, jnp.concatenate([out_piece, gate_piece, up_piece], axis=0).astype(bf16), 5
    )
    column = place * width_own
    gain_all = proj_all[:, PROJECT_COLUMNS + 4 * rank :][:, :gain_count].reshape(size, 2, MODEL_WIDTH)
    gain_all = jnp.sum(gain_all.astype(f32), axis=0)
    gain_own = lax.dynamic_slice_in_dim(gain_all, column, width_own, 1)
    gain_part = jnp.pad(gain_own, ((0, width_own - 2), (0, -width_own % 128)))
    attn_part = jnp.concatenate(
        [
            outer_product_rows(normed_turn, proj_all[:, :PROJECT_COLUMNS]),
            outer_product_rows(branch_turn, attended_all)[:, :QUERY_WIDTH],
            gain_part,
        ],
        axis=1,
    ).astype(bf16)
    attn_part, ffn_both, proj_all = lax.optimization_barrier((attn_part, ffn_both, proj_all))
    attn_sum = both_loops(loop_shares(attn_part))
    gain_column = PROJECT_COLUMNS + QUERY_WIDTH
    gain_sum = attn_sum[:2, gain_column : gain_column + width_own]
    low_all = proj_all[:, PROJECT_COLUMNS : PROJECT_COLUMNS + 4 * rank]
    proj_all = proj_all[:, :PROJECT_COLUMNS]
    qkv_low_all = jnp.concatenate(
        [
            times_transposed(proj_all[:, :QUERY_WIDTH], widen_query),
            times_transposed(proj_all[:, QUERY_WIDTH : QUERY_WIDTH + HEAD_WIDTH], widen_key),
            times_transposed(proj_all[:, QUERY_WIDTH + HEAD_WIDTH :], widen_value),
        ],
        axis=1,
    ).astype(bf16)
    attended_turn = lax.dynamic_slice_in_dim(attended_all, column, width_own, 1)
    two_turn = lax.dynamic_slice_in_dim(two_all, column, width_own, 1)
    squeeze_own = jnp.concatenate(
        [
            outer_product_rows(normed_turn, qkv_low_all),
            outer_product_rows(attended_turn, low_all[:, :rank]),
            outer_product_rows(two_turn, low_all[:, rank : 3 * rank]),
        ],
        axis=1,
    )
    near = jnp.concatenate(
        [
            outer_product_rows(proj_all[:, :QUERY_WIDTH], lora_qkv_all[:, :rank]),
            outer_product_rows(
                proj_all[:, QUERY_WIDTH : QUERY_WIDTH + HEAD_WIDTH], lora_qkv_all[:, rank : 2 * rank]
            ),
            outer_product_rows(proj_all[:, QUERY_WIDTH + HEAD_WIDTH :], lora_qkv_all[:, 2 * rank :]),
        ],
        axis=0,
    )
    far = outer_product_rows(grad_all, low_all[:, 3 * rank :])
    first = place * columns_own
    far_start = GATE_START + 2 * HIDDEN_COUNT
    near = lax.dynamic_slice_in_dim(
        jnp.pad(near.astype(bf16), ((0, columns_own), (0, 0))), jnp.minimum(first, PROJECT_COLUMNS), columns_own, 0
    )
    far = lax.dynamic_slice_in_dim(
        jnp.pad(far.astype(bf16), ((columns_own, 0), (0, 0))),
        jnp.maximum(first - far_start + columns_own, 0),
        columns_own,
        0,
    )
    owned = first + jnp.arange(columns_own, dtype=jnp.int32)[:, None]
    expand_own = jnp.where(
        owned < PROJECT_COLUMNS, near, jnp.where(owned < far_start, middle_own, far)
    ).T.astype(f32)
    ffn_sum = both_loops(ffn_both).transpose(1, 0, 2)
    return (
        hidden_out[None],
        input_grad[None],
        gain_sum,
        attn_sum[:, :PROJECT_COLUMNS],
        attn_sum[:, PROJECT_COLUMNS:gain_column],
        ffn_sum,
        squeeze_own[None],
        expand_own[None],
        down_own[None],
    )


def solution(mesh):
    return jax.shard_map(
        per_device,
        mesh=mesh,
        in_specs=(
            P("loop", "fsdp", None),
            P("loop", None),
            P(),
            P("fsdp", None),
            P("fsdp", None),
            P("fsdp", None, None),
            P("loop", None, None),
            P("loop", None, None),
            P("loop", None, None),
            P("loop", "fsdp", None),
        ),
        out_specs=(
            P("loop", "fsdp", None),
            P("loop", "fsdp", None),
            P(None, "fsdp"),
            P("fsdp", None),
            P("fsdp", None),
            P("fsdp", None, None),
            P("loop", "fsdp", None),
            P("loop", None, "fsdp"),
            P("loop", "fsdp", None),
        ),
        check_vma=False,
    )
```

```python
import functools
import math

import jax
import jax.numpy as jnp
from jax import lax
from jax.experimental import pallas as pl
from jax.experimental.pallas import tpu as pltpu
from jax.sharding import PartitionSpec as P

MODEL_WIDTH = 2048
HEADS = 8
HEAD_WIDTH = 256
HIDDEN_COUNT = 16384
ADAPTER_RANK = 256
QUERY_WIDTH = 2048
PROJECT_COLUMNS = 2560
ADAPTER_COLUMNS = 39424
GATE_START = PROJECT_COLUMNS + MODEL_WIDTH

epsilon = 1e-06
bf16 = jnp.bfloat16
f32 = jnp.float32
MESH = pl.DeviceIdType.MESH


def matrix_product(former, latter):
    return jnp.dot(former, latter, preferred_element_type=f32)


def times_transposed(former, latter):
    return lax.dot_general(former, latter, (((1,), (1,)), ((), ())), preferred_element_type=f32)


def outer_product_rows(former, latter):
    return lax.dot_general(former, latter, (((0,), (0,)), ((), ())), preferred_element_type=f32)


def segment_info(lengths, row_count):
    row_ids = jnp.arange(row_count, dtype=jnp.int32)
    count = lengths.shape[0]
    labels = jnp.arange(count, dtype=jnp.int32)
    finish = jnp.sum(jnp.where(labels[:, None] <= labels[None, :], lengths[:, None], 0), axis=0)
    starts = finish - lengths
    segment = jnp.sum((row_ids[:, None] >= finish[None, :]).astype(jnp.int32), axis=1)
    opening = jnp.sum(jnp.where(segment[:, None] == labels[None, :], starts[None, :], 0), axis=1)
    return (segment, row_ids - opening)


def rotate(values, position, direction):
    half_dim = HEAD_WIDTH // 2
    frequency = jnp.exp(
        jnp.arange(half_dim).astype(f32) * (-2.0 * math.log(10000.0) / HEAD_WIDTH)
    )
    angles = position.astype(f32)[:, None] * frequency[None, :]
    cosine = jnp.cos(angles)[:, None, :]
    sine_val = direction * jnp.sin(angles)[:, None, :]
    shaped = values.reshape(values.shape[0], -1, HEAD_WIDTH)
    former = shaped[..., :half_dim]
    latter = shaped[..., half_dim:]
    turned = jnp.concatenate(
        [former * cosine - latter * sine_val, latter * cosine + former * sine_val], axis=-1
    )
    return turned.reshape(values.shape)


def rms_scale(values):
    return lax.rsqrt(jnp.mean(values * values, axis=-1, keepdims=True) + epsilon)


def gelu_tanh(values):
    return jax.nn.gelu(values, approximate=True)


def unit_backward(gate_value, upward_activation, hidden_unit_gradient):
    activated, pullback_function = jax.vjp(gelu_tanh, gate_value)
    gate_grad = pullback_function(hidden_unit_gradient * upward_activation)[0]
    return (gate_grad.astype(bf16), (hidden_unit_gradient * activated).astype(bf16))


def scores_of(query_heads, key_rows, allowed, scaling):
    product = (
        jnp.einsum("thd,ud->thu", query_heads, key_rows, preferred_element_type=f32) * scaling
    )
    return jnp.where(allowed[:, None, :], product, -1e30)


def gather_rows(block):
    return lax.all_gather(block, "fsdp", axis=0, tiled=True)


def scatter_rows(partial):
    return lax.psum_scatter(partial.astype(bf16), "fsdp", scatter_dimension=0, tiled=True).astype(f32)


def loop_shares(partial):
    return lax.all_gather(partial.astype(bf16), "loop", axis=0)


def both_loops(shares):
    return shares[0].astype(f32) + shares[1].astype(f32)


def turn(block):
    return lax.all_to_all(block, "fsdp", split_axis=1, concat_axis=0, tiled=True)


def chip_at(q, chips):
    return jnp.where(q < 4, 2 * q, 15 - 2 * q) if chips == 8 else q

def ring_place(chip, chips):
    return jnp.where(chip % 2 == 0, chip // 2, 7 - chip // 2) if chips == 8 else chip

def ring_neighbours(chips):
    me = lax.axis_index("fsdp")
    core = me % 2
    p = ring_place(me // 2, chips)
    def device(shift, c):
        return chip_at((p + shift + chips) % chips, chips) * 2 + c
    return core, device

def meet(devices):
    barrier = pltpu.get_barrier_semaphore()
    for d in devices:
        pl.semaphore_signal(barrier, inc=1, device_id={"fsdp": d}, device_id_type=MESH)
    pl.semaphore_wait(barrier, len(devices))

def gather_kernel(chips, x_ref, o_ref, own_sem, ring_send, ring_recv, side_send, side_recv, greet=None, also=None):
    core, device = ring_neighbours(chips)
    rows = x_ref.shape[0]
    reach = chips // 2
    ways = (device(1, core), device(-1, core))
    side = device(0, 1 - core)
    if greet is None:
        meet((*ways, side))
    else:
        greet()

    def span(way, hops):
        return (way * (rows // 2), rows // 2) if hops == reach else (0, rows)

    def at(way, hops, c, part):
        origin = device(-hops if way == 0 else hops, c)
        return o_ref.at[pl.ds(pl.multiple_of(origin * rows + part[0], 8), part[1])]

    def hop(way, hops):
        part = span(way, hops)
        here = at(way, hops - 1, core, part)
        src = x_ref.at[pl.ds(part[0], part[1])] if hops == 1 else here
        return pltpu.make_async_remote_copy(src, here, ring_send.at[way, hops - 1], ring_recv.at[way, hops - 1], device_id={"fsdp": ways[way]}, device_id_type=MESH)

    def arriving(way, hops):
        here = at(way, hops, core, span(way, hops))
        return pltpu.make_async_remote_copy(here, here, ring_send.at[way, hops - 1], ring_recv.at[way, hops - 1], device_id={"fsdp": ways[way]}, device_id_type=MESH)

    def across(way, hops, c):
        part = span(way, hops) if hops else (0, rows)
        there = at(way, hops, c, part)
        src = there if hops else x_ref
        return pltpu.make_async_remote_copy(src, there, side_send.at[way, hops], side_recv.at[way, hops], device_id={"fsdp": side}, device_id_type=MESH)

    for way in (0, 1):
        hop(way, 1).start()
    across(0, 0, core).start()
    own = pltpu.make_async_copy(x_ref, at(0, 0, core, (0, rows)), own_sem)
    own.start()
    if also is not None:
        also()
    for hops in range(1, reach + 1):
        for way in (0, 1):
            arriving(way, hops).wait_recv()
            if hops < reach:
                hop(way, hops + 1).start()
            across(way, hops, core).start()
    across(0, 0, 1 - core).wait_recv()
    across(0, 0, core).wait_send()
    for hops in range(1, reach + 1):
        for way in (0, 1):
            across(way, hops, 1 - core).wait_recv()
            across(way, hops, core).wait_send()
            hop(way, hops).wait_send()
    own.wait()

def busy(us):
    return pl.CostEstimate(flops=0, bytes_accessed=int(us * 3.0e6), transcendentals=0)


def ring_gather(block, ident):
    size = lax.axis_size("fsdp")
    chips = size // 2
    rows, columns = block.shape
    pair = pltpu.SemaphoreType.DMA((2, chips // 2))
    sides = pltpu.SemaphoreType.DMA((2, chips // 2 + 1))
    return pl.pallas_call(
        functools.partial(gather_kernel, chips),
        out_shape=jax.ShapeDtypeStruct((size * rows, columns), block.dtype),
        in_specs=[pl.BlockSpec(memory_space=pl.ANY)],
        out_specs=pl.BlockSpec(memory_space=pl.ANY),
        scratch_shapes=[pltpu.SemaphoreType.DMA, pair, pair, sides, sides],
        compiler_params=pltpu.CompilerParams(collective_id=ident, has_side_effects=True),
        cost_estimate=busy(1),
        name="ring_gather",
    )(block)

def scatter_kernel(chips, count, *refs):
    x_refs, o_ref = refs[:count], refs[count]
    side_buf, ring_buf, side_send, side_recv, ring_send, ring_recv = refs[count + 1 :]
    core, device = ring_neighbours(chips)
    rows, columns = o_ref.shape
    reach = chips // 2
    half = columns // 2
    tile = 16
    ways = (device(1, core), device(-1, core))
    side = device(0, 1 - core)
    meet((*ways, side))
    starts = [sum(x.shape[1] for x in x_refs[:i]) for i in range(count)]

    def shift(way, hops):
        return (hops if way == 0 else chips - hops) % chips

    def across(target, c, i):
        there = pl.ds(pl.multiple_of(device(target, c) * rows, tile), rows)
        return pltpu.make_async_remote_copy(
            x_refs[i].at[there],
            side_buf.at[target, :, pl.ds(starts[i], x_refs[i].shape[1])],
            side_send.at[target, i],
            side_recv.at[target, i],
            device_id={"fsdp": side},
            device_id_type=MESH,
        )

    def hop(way, step):
        cols = pl.ds(way * half, half) if step == 0 else pl.ds(0, columns)
        return pltpu.make_async_remote_copy(
            side_buf.at[shift(way, reach - step), :, cols],
            ring_buf.at[way, step, :, cols],
            ring_send.at[way, step],
            ring_recv.at[way, step],
            device_id={"fsdp": ways[way]},
            device_id_type=MESH,
        )

    order = [reach] + [shift(way, hops) for hops in range(reach - 1, 0, -1) for way in (0, 1)] + [0]
    for target in order:
        for i in range(count):
            across(target, 1 - core, i).start()

    def add(target, incoming, store):
        first = pl.multiple_of(device(target, core) * rows, tile)
        for i in range(count):
            across(target, core, i).wait_recv()

        @pl.loop(0, rows // tile)
        def _(j):
            here = pl.ds(pl.multiple_of(j * tile, tile), tile)
            mine = pl.ds(pl.multiple_of(first + j * tile, tile), tile)
            for i in range(count):
                cols = pl.ds(starts[i], x_refs[i].shape[1])
                total = x_refs[i][mine, :].astype(f32) + side_buf[target, here, cols].astype(f32)
                for way, step in incoming:
                    if step:
                        total = total + ring_buf[way, step, here, cols].astype(f32)
                store(here, cols, total)
            for way, step in incoming:
                if not step:
                    cols = pl.ds(way * half, half)
                    store(
                        here,
                        cols,
                        side_buf[target, here, cols].astype(f32) + ring_buf[way, 0, here, cols].astype(f32),
                    )

    for step in range(reach):
        for way in (0, 1):
            target = shift(way, reach - step)
            if step:
                hop(way, step - 1).wait_recv()

            def store(here, cols, total, target=target):
                side_buf[target, here, cols] = total.astype(bf16)

            if step or way == 0:
                add(target, [(way, step - 1)] if step else [], store)
            hop(way, step).start()
    for way in (0, 1):
        hop(way, reach - 1).wait_recv()

    def last(here, cols, total):
        o_ref[here, cols] = total

    add(0, [(0, reach - 1), (1, reach - 1)], last)
    for target in order:
        for i in range(count):
            across(target, 1 - core, i).wait_send()
    for step in range(reach):
        for way in (0, 1):
            hop(way, step).wait_send()


def ring_scatter(terms, ident):
    size = lax.axis_size("fsdp")
    terms = [term.astype(bf16) for term in terms]
    if size != 16:
        return scatter_rows(jnp.concatenate(terms, axis=1))
    chips, count = size // 2, len(terms)
    rows, columns = terms[0].shape[0] // size, sum(term.shape[1] for term in terms)
    pair = pltpu.SemaphoreType.DMA((2, chips // 2))
    sides = pltpu.SemaphoreType.DMA((chips, count))
    return pl.pallas_call(
        functools.partial(scatter_kernel, chips, count),
        out_shape=jax.ShapeDtypeStruct((rows, columns), f32),
        in_specs=[pl.BlockSpec(memory_space=pltpu.VMEM)] * count,
        out_specs=pl.BlockSpec(memory_space=pltpu.VMEM),
        scratch_shapes=[
            pltpu.VMEM((chips, rows, columns), bf16),
            pltpu.VMEM((2, chips // 2, rows, columns), bf16),
            sides,
            sides,
            pair,
            pair,
        ],
        compiler_params=pltpu.CompilerParams(
            collective_id=ident, has_side_effects=True, vmem_limit_bytes=56 << 20
        ),
        cost_estimate=busy(1),
        name="ring_scatter",
    )(*terms)


def unit_kernel(chips, *refs):
    sources, (planes, squeeze, widen_down, widen_gate, widen_up, narrow) = refs[:2], refs[2:8]
    outs, (held, rows_v, acts, low) = refs[8:11], refs[11:15]
    held_sem, own_sem, ring_send, ring_recv, side_send, side_recv, out_sem = refs[15:]
    core, device = ring_neighbours(chips)
    rows = sources[0].shape[0]
    reach = chips // 2
    wide = 256
    ways = (device(1, core), device(-1, core))
    side = device(0, 1 - core)
    fetches = [pltpu.make_async_copy(planes.at[i], held.at[i], held_sem.at[i]) for i in range(3)]
    for fetch in fetches:
        fetch.start()
    meet((*ways, side))

    def span(way, hops):
        return (way * (rows // 2), rows // 2) if hops == reach else (0, rows)

    def at(i, way, hops, c, part):
        origin = device(-hops if way == 0 else hops, c)
        return rows_v.at[i, pl.ds(pl.multiple_of(origin * rows + part[0], 16), part[1])]

    def hop(i, way, hops):
        part = span(way, hops)
        here = at(i, way, hops - 1, core, part)
        src = sources[i].at[pl.ds(part[0], part[1])] if hops == 1 else here
        return pltpu.make_async_remote_copy(
            src,
            here,
            ring_send.at[i, way, hops - 1],
            ring_recv.at[i, way, hops - 1],
            device_id={"fsdp": ways[way]},
            device_id_type=MESH,
        )

    def arriving(i, way, hops):
        here = at(i, way, hops, core, span(way, hops))
        return pltpu.make_async_remote_copy(
            here,
            here,
            ring_send.at[i, way, hops - 1],
            ring_recv.at[i, way, hops - 1],
            device_id={"fsdp": ways[way]},
            device_id_type=MESH,
        )

    def across(i, way, hops, c):
        part = span(way, hops) if hops else (0, rows)
        there = at(i, way, hops, c, part)
        return pltpu.make_async_remote_copy(
            there if hops else sources[i],
            there,
            side_send.at[i, way, hops],
            side_recv.at[i, way, hops],
            device_id={"fsdp": side},
            device_id_type=MESH,
        )

    def leaving(n, first):
        mine = pl.ds(first, 2 * rows)
        pairs = [(rows_v.at[i, mine], outs[0].at[i, mine]) for i in (0, 1)]
        pairs += [(acts.at[i, mine], outs[1].at[i, mine]) for i in range(3)]
        pairs += [(low.at[mine], outs[2].at[mine])]
        return [pltpu.make_async_copy(a, b, out_sem.at[n, i]) for i, (a, b) in enumerate(pairs)]

    def first_row(shift):
        return pl.multiple_of(device(shift, 0) * rows, 2 * rows)

    def work(n, first):
        mine = pl.ds(first, 2 * rows)
        rank = ADAPTER_RANK
        low[mine, : 2 * rank] = matrix_product(rows_v[0, mine, :], squeeze[...]).astype(bf16)
        low[mine, 2 * rank :] = times_transposed(rows_v[1, mine, :], widen_down[...]).astype(bf16)

        @pl.loop(0, held.shape[1] // wide)
        def _(t):
            own = pl.ds(pl.multiple_of(t * wide, wide), wide)
            two = rows_v[0, mine, :]
            gate = times_transposed(two, held[0, own, :]) + matrix_product(
                low[mine, :rank], widen_gate[:, own]
            )
            upward = times_transposed(two, held[1, own, :]) + matrix_product(
                low[mine, rank : 2 * rank], widen_up[:, own]
            )
            pull = times_transposed(rows_v[1, mine, :], held[2, own, :]) + times_transposed(
                low[mine, 2 * rank :], narrow[own, :]
            )
            scale = math.sqrt(2.0 / math.pi)
            square = gate * gate
            bend = jnp.tanh(scale * gate * (1.0 + 0.044715 * square))
            rise = 0.5 * (1.0 + bend)
            active = gate * rise
            slope = rise + 0.5 * gate * (1.0 - bend * bend) * (scale * (1.0 + 3 * 0.044715 * square))
            acts[0, mine, own] = (pull * upward * slope).astype(bf16)
            acts[1, mine, own] = (pull * active).astype(bf16)
            acts[2, mine, own] = (active * upward).astype(bf16)

        for copy in leaving(n, first):
            copy.start()

    for i in (0, 1):
        for way in (0, 1):
            hop(i, way, 1).start()
        across(i, 0, 0, core).start()
    keeps = [
        pltpu.make_async_copy(sources[i], at(i, 0, 0, core, (0, rows)), own_sem.at[i]) for i in (0, 1)
    ]
    for keep in keeps:
        keep.start()
    for copy in keeps + fetches:
        copy.wait()
    for i in (0, 1):
        across(i, 0, 0, 1 - core).wait_recv()
    work(0, first_row(0))
    for hops in range(1, reach + 1):
        for i in (0, 1):
            for way in (0, 1):
                arriving(i, way, hops).wait_recv()
                if hops < reach:
                    hop(i, way, hops + 1).start()
                across(i, way, hops, core).start()
        if hops < reach:
            for way in (0, 1):
                for i in (0, 1):
                    across(i, way, hops, 1 - core).wait_recv()
                work(2 * hops - 1 + way, first_row(-hops if way == 0 else hops))
    for way in (0, 1):
        for i in (0, 1):
            across(i, way, reach, 1 - core).wait_recv()
    work(2 * reach - 1, first_row(reach))
    for i in (0, 1):
        across(i, 0, 0, core).wait_send()
        for hops in range(1, reach + 1):
            for way in (0, 1):
                across(i, way, hops, core).wait_send()
                hop(i, way, hops).wait_send()
    for n in range(chips):
        if n == 0:
            shift = 0
        elif n == 2 * reach - 1:
            shift = reach
        else:
            shift = (-1 if n % 2 else 1) * ((n + 1) // 2)
        for copy in leaving(n, first_row(shift)):
            copy.wait()


def unit_rows(two, grad, planes, squeeze, widen_down, widen_gate, widen_up, narrow, ident):
    size = lax.axis_size("fsdp")
    rank = ADAPTER_RANK
    if size != 16:
        two, grad = gather_rows(two), gather_rows(grad)
        low = matrix_product(two, squeeze).astype(bf16)
        pulled = times_transposed(grad, widen_down).astype(bf16)
        gate = times_transposed(two, planes[0]) + matrix_product(low[:, :rank], widen_gate)
        upward = times_transposed(two, planes[1]) + matrix_product(low[:, rank:], widen_up)
        units_grad = times_transposed(grad, planes[2]) + times_transposed(pulled, narrow)
        units = (gelu_tanh(gate) * upward).astype(bf16)
        gate_grad, up_grad = unit_backward(gate, upward, units_grad)
        return (
            jnp.stack([two, grad]),
            jnp.stack([gate_grad, up_grad, units]),
            jnp.concatenate([low, pulled], axis=1),
        )
    chips = size // 2
    rows, columns = two.shape
    all_rows, hidden = size * rows, planes.shape[1]
    anywhere, inside = pl.BlockSpec(memory_space=pl.ANY), pl.BlockSpec(memory_space=pltpu.VMEM)
    pair = pltpu.SemaphoreType.DMA((2, 2, chips // 2))
    sides = pltpu.SemaphoreType.DMA((2, 2, chips // 2 + 1))
    return pl.pallas_call(
        functools.partial(unit_kernel, chips),
        out_shape=(
            jax.ShapeDtypeStruct((2, all_rows, columns), bf16),
            jax.ShapeDtypeStruct((3, all_rows, hidden), bf16),
            jax.ShapeDtypeStruct((all_rows, 3 * rank), bf16),
        ),
        in_specs=[anywhere] * 3 + [inside] * 5,
        out_specs=(anywhere,) * 3,
        scratch_shapes=[
            pltpu.VMEM(planes.shape, bf16),
            pltpu.VMEM((2, all_rows, columns), bf16),
            pltpu.VMEM((3, all_rows, hidden), bf16),
            pltpu.VMEM((all_rows, 3 * rank), bf16),
            pltpu.SemaphoreType.DMA((3,)),
            pltpu.SemaphoreType.DMA((2,)),
            pair,
            pair,
            sides,
            sides,
            pltpu.SemaphoreType.DMA((chips, 6)),
        ],
        compiler_params=pltpu.CompilerParams(
            collective_id=ident, has_side_effects=True, vmem_limit_bytes=60 << 20
        ),
        cost_estimate=busy(100),
        name="unit_rows",
    )(two, grad, planes, squeeze, widen_down, widen_gate, widen_up, narrow)


def mix_kernel(chips, *refs):
    acts_ref, planes, gate_b, up_b, down_a, o_ref = refs[:6]
    acts, held, side_buf, ring_buf, stage, mine = refs[6:12]
    held_sem, side_send, side_recv, ring_send, ring_recv = refs[12:]
    fetches = [pltpu.make_async_copy(planes.at[i], held.at[i], held_sem.at[0, i]) for i in range(3)]
    fetches += [pltpu.make_async_copy(acts_ref.at[i], acts.at[i], held_sem.at[1, i]) for i in range(3)]
    for fetch in fetches:
        fetch.start()
    core, device = ring_neighbours(chips)
    rows, columns = o_ref.shape
    reach = chips // 2
    half = columns // 2
    tile = 16
    wide = 256
    ways = (device(1, core), device(-1, core))
    side = device(0, 1 - core)
    meet((*ways, side))
    order = [(reach, 0, 0)]
    for step in range(1, reach):
        order += [(reach - step, 0, step), (chips - reach + step, 1, step)]
    order.append((0, 0, reach))

    def across(i):
        target = order[i][0]
        return pltpu.make_async_remote_copy(
            stage.at[i % 2],
            side_buf.at[target],
            side_send.at[target],
            side_recv.at[target],
            device_id={"fsdp": side},
            device_id_type=MESH,
        )

    def hop(way, step):
        target = (reach - step if way == 0 else chips - reach + step) % chips
        cols = pl.ds(way * half, half) if step == 0 else pl.ds(0, columns)
        return pltpu.make_async_remote_copy(
            side_buf.at[target, :, cols],
            ring_buf.at[way, step, :, cols],
            ring_send.at[way, step],
            ring_recv.at[way, step],
            device_id={"fsdp": ways[way]},
            device_id_type=MESH,
        )

    def make(i):
        target, slot = order[i][0], i % 2
        if i >= 2:
            across(i - 2).wait_send()
        theirs = pl.ds(pl.multiple_of(device(target, 1 - core) * rows, rows), rows)
        ours = pl.ds(pl.multiple_of(device(target, core) * rows, rows), rows)

        def block(kind):
            return jnp.concatenate([acts[kind, theirs, :], acts[kind, ours, :]], axis=0)

        def put(first, value):
            cols = pl.ds(pl.multiple_of(first, wide), wide)
            stage[slot, :, cols] = value[:rows].astype(bf16)
            mine[slot, :, cols] = value[rows:].astype(bf16)

        @pl.loop(0, MODEL_WIDTH // wide)
        def _(t):
            cols = pl.ds(pl.multiple_of(t * wide, wide), wide)
            put(
                t * wide,
                matrix_product(block(0), held[0, :, cols])
                + matrix_product(block(1), held[1, :, cols]),
            )
            put(
                MODEL_WIDTH + 2 * ADAPTER_RANK + t * wide,
                matrix_product(block(2), held[2, :, cols]),
            )

        put(MODEL_WIDTH, times_transposed(block(0), gate_b[...]))
        put(MODEL_WIDTH + ADAPTER_RANK, times_transposed(block(1), up_b[...]))
        put(2 * MODEL_WIDTH + 2 * ADAPTER_RANK, matrix_product(block(2), down_a[...]))
        across(i).start()

    def add(i):
        target, way, step = order[i]
        last = target == 0
        incoming = [(w, step - 1) for w in ((0, 1) if last else (way,))] if step else []
        across(i).wait_recv()
        for w, s in incoming:
            hop(w, s).wait_recv()

        @pl.loop(0, rows // tile)
        def _(j):
            here = pl.ds(pl.multiple_of(j * tile, tile), tile)
            for part in (0, 1):
                cols = pl.ds(part * half, half)
                total = mine[i % 2, here, cols].astype(f32) + side_buf[target, here, cols].astype(f32)
                for w, s in incoming:
                    if s or w == part:
                        total = total + ring_buf[w, s, here, cols].astype(f32)
                if last:
                    o_ref[here, cols] = total
                else:
                    side_buf[target, here, cols] = total.astype(bf16)

        if not last:
            hop(way, step).start()
            if step == 0:
                hop(1, 0).start()

    for fetch in fetches:
        fetch.wait()
    make(0)
    for i in range(len(order)):
        if i + 1 < len(order):
            make(i + 1)
        add(i)
    for i in range(len(order) - 2, len(order)):
        across(i).wait_send()
    for step in range(reach):
        for way in (0, 1):
            hop(way, step).wait_send()


def mix_rows(acts, planes, gate_b, up_b, down_a, ident):
    size = lax.axis_size("fsdp")
    if size != 16:
        gate_grad, up_grad, units = acts[0], acts[1], acts[2]
        terms = [
            matrix_product(gate_grad, planes[0]) + matrix_product(up_grad, planes[1]),
            times_transposed(gate_grad, gate_b),
            times_transposed(up_grad, up_b),
            matrix_product(units, planes[2]),
            matrix_product(units, down_a),
        ]
        return scatter_rows(jnp.concatenate(terms, axis=1))
    chips = size // 2
    rows, columns = acts.shape[1] // size, 2 * MODEL_WIDTH + 3 * ADAPTER_RANK
    pair = pltpu.SemaphoreType.DMA((2, chips // 2))
    sides = pltpu.SemaphoreType.DMA((chips,))
    return pl.pallas_call(
        functools.partial(mix_kernel, chips),
        out_shape=jax.ShapeDtypeStruct((rows, columns), f32),
        in_specs=[pl.BlockSpec(memory_space=pl.ANY)] * 2
        + [pl.BlockSpec(memory_space=pltpu.VMEM)] * 3,
        out_specs=pl.BlockSpec(memory_space=pltpu.VMEM),
        scratch_shapes=[
            pltpu.VMEM(acts.shape, bf16),
            pltpu.VMEM(planes.shape, bf16),
            pltpu.VMEM((chips, rows, columns), bf16),
            pltpu.VMEM((2, chips // 2, rows, columns), bf16),
            pltpu.VMEM((2, rows, columns), bf16),
            pltpu.VMEM((2, rows, columns), bf16),
            pltpu.SemaphoreType.DMA((2, 3)),
            sides,
            sides,
            pair,
            pair,
        ],
        compiler_params=pltpu.CompilerParams(
            collective_id=ident, has_side_effects=True, vmem_limit_bytes=60 << 20
        ),
        cost_estimate=busy(1),
        name="mix_rows",
    )(acts, planes, gate_b, up_b, down_a)


def share_kernel(size, chunk, own_count, x_ref, mid_ref, all_ref, o_ref, *sems):
    send_sem, recv_sem, own_sem = sems[5:]
    me = lax.axis_index("fsdp")
    hidden = HIDDEN_COUNT // size
    width = MODEL_WIDTH // size
    sections = (
        (0, PROJECT_COLUMNS, width),
        (width, GATE_START, hidden),
        (width + hidden, GATE_START + HIDDEN_COUNT, hidden),
    )

    def greet():
        barrier = pltpu.get_barrier_semaphore()

        def one(i, carry):
            pl.semaphore_signal(barrier, inc=1, device_id={"fsdp": (me + i) % size}, device_id_type=MESH)
            return carry

        lax.fori_loop(1, size, one, 0)
        pl.semaphore_wait(barrier, size - 1)

    def rows(ref, first):
        return ref.at[pl.ds(pl.multiple_of(first, 8), chunk)]

    def aim(start, length):
        owner = (start + me * length) // own_count
        return owner, start + me * length - owner * own_count

    def remote(source, first, owner, sent=0):
        return pltpu.make_async_remote_copy(
            source,
            rows(o_ref, first),
            send_sem.at[sent],
            recv_sem.at[first // chunk],
            device_id={"fsdp": owner},
            device_id_type=MESH,
        )

    def local(source, first):
        return pltpu.make_async_copy(source, rows(o_ref, first), own_sem.at[first // chunk])

    def send_all():
        for base, start, length in sections:

            def send(j, carry, base=base, aimed=aim(start, length)):
                over = (aimed[1] + j * chunk >= own_count).astype(jnp.int32)
                owner = aimed[0] + over
                first = aimed[1] + j * chunk - over * own_count
                source = rows(mid_ref, base + j * chunk)

                @pl.when(owner != me)
                def _():
                    remote(source, first, owner, base // chunk + j).start()

                @pl.when(owner == me)
                def _():
                    local(source, first).start()

                return carry

            lax.fori_loop(0, length // chunk, send, 0)

    gather_kernel(size // 2, x_ref, all_ref, *sems[:5], greet=greet, also=send_all)

    def arrive(j, carry):
        column = me * own_count + j * chunk
        here = rows(o_ref, j * chunk)
        away, kept = 0, 0
        for _, start, length in sections:
            mine = start + me * length
            inside = (column >= start) & (column < start + length * size)
            outside = (column < mine) | (column >= mine + length)
            away = away + (inside & outside).astype(jnp.int32)
            kept = kept + (inside & ~outside).astype(jnp.int32)

        @pl.when(away > 0)
        def _():
            remote(here, j * chunk, (me + 1) % size).wait_recv()

        @pl.when(kept > 0)
        def _():
            local(rows(mid_ref, 0), j * chunk).wait()

        return carry

    lax.fori_loop(0, own_count // chunk, arrive, 0)
    for base, start, length in sections:

        def sent(j, carry, base=base, aimed=aim(start, length)):
            over = (aimed[1] + j * chunk >= own_count).astype(jnp.int32)
            owner = aimed[0] + over
            first = aimed[1] + j * chunk - over * own_count

            @pl.when(owner != me)
            def _():
                remote(rows(mid_ref, base + j * chunk), first, owner, base // chunk + j).wait_send()

            return carry

        lax.fori_loop(0, length // chunk, sent, 0)


def share_rows(block, middle, ident):
    size = lax.axis_size("fsdp")
    rows, columns = block.shape
    own_count = ADAPTER_COLUMNS // size
    chunk = math.gcd(own_count, MODEL_WIDTH // size, HIDDEN_COUNT // size, PROJECT_COLUMNS, GATE_START)
    anywhere = pl.BlockSpec(memory_space=pl.ANY)
    pair = pltpu.SemaphoreType.DMA((2, size // 4))
    sides = pltpu.SemaphoreType.DMA((2, size // 4 + 1))
    return pl.pallas_call(
        functools.partial(share_kernel, size, chunk, own_count),
        out_shape=(
            jax.ShapeDtypeStruct((size * rows, columns), block.dtype),
            jax.ShapeDtypeStruct((own_count, ADAPTER_RANK), bf16),
        ),
        in_specs=[anywhere] * 2,
        out_specs=(anywhere, anywhere),
        scratch_shapes=[
            pltpu.SemaphoreType.DMA,
            pair,
            pair,
            sides,
            sides,
            pltpu.SemaphoreType.DMA((middle.shape[0] // chunk,)),
            pltpu.SemaphoreType.DMA((own_count // chunk,)),
            pltpu.SemaphoreType.DMA((own_count // chunk,)),
        ],
        compiler_params=pltpu.CompilerParams(collective_id=ident, has_side_effects=True),
        cost_estimate=busy(1),
        name="share_rows",
    )(block, middle)


def per_device(
    hidden_input,
    sequence_lengths,
    norm_gain_values,
    input_proj_weight,
    output_proj_weight,
    feedforward_weight,
    adapter_first,
    adapter_second,
    adapter_down_first,
    output_gradient,
):
    size = lax.axis_size("fsdp")
    place = lax.axis_index("fsdp")
    tokens_dev = hidden_input.shape[1]
    all_rows = tokens_dev * size
    hidden_own = HIDDEN_COUNT // size
    width_own = MODEL_WIDTH // size
    columns_own = ADAPTER_COLUMNS // size
    offset = place * tokens_dev
    segment_all, position_all = segment_info(sequence_lengths[0], all_rows)
    segment_own = lax.dynamic_slice_in_dim(segment_all, offset, tokens_dev)
    position_own = lax.dynamic_slice_in_dim(position_all, offset, tokens_dev)
    row_all = jnp.arange(all_rows, dtype=jnp.int32)
    row_own = offset + jnp.arange(tokens_dev, dtype=jnp.int32)
    allowed = (segment_own[:, None] == segment_all[None, :]) & (
        row_own[:, None] >= row_all[None, :]
    )
    gains = norm_gain_values.astype(f32)
    first_factor = adapter_first[0]
    second_factor = adapter_second[0]
    rank = ADAPTER_RANK
    narrow_projection = first_factor[:, : 3 * rank]
    narrow_output = first_factor[:, 3 * rank : 4 * rank]
    squeeze_gate = first_factor[:, 4 * rank : 5 * rank]
    squeeze_up = first_factor[:, 5 * rank :]
    narrow_down = lax.dynamic_slice_in_dim(adapter_down_first[0], place * hidden_own, hidden_own, 0)
    widen_query = second_factor[:, :QUERY_WIDTH]
    widen_key = second_factor[:, QUERY_WIDTH : QUERY_WIDTH + HEAD_WIDTH]
    widen_value = second_factor[:, QUERY_WIDTH + HEAD_WIDTH : PROJECT_COLUMNS]
    widen_output = second_factor[:, PROJECT_COLUMNS:GATE_START]
    widen_gate = lax.dynamic_slice_in_dim(
        second_factor, GATE_START + place * hidden_own, hidden_own, 1
    )
    widen_up = lax.dynamic_slice_in_dim(
        second_factor, GATE_START + HIDDEN_COUNT + place * hidden_own, hidden_own, 1
    )
    widen_down = second_factor[:, GATE_START + 2 * HIDDEN_COUNT :]
    scaling = HEAD_WIDTH ** (-0.5)

    hidden_state = hidden_input[0].astype(f32)
    scale_one = rms_scale(hidden_state)
    normalized = (hidden_state * scale_one * gains[0]).astype(bf16)
    proj_in = ring_gather(input_proj_weight, 0)
    proj_in, proj_out = lax.optimization_barrier((proj_in, output_proj_weight))
    proj_out = gather_rows(proj_out)
    lora_qkv = matrix_product(normalized, narrow_projection).astype(bf16)
    projected = matrix_product(normalized, proj_in)
    query_pre = projected[:, :QUERY_WIDTH] + matrix_product(lora_qkv[:, :rank], widen_query)
    key_pre = projected[:, QUERY_WIDTH : QUERY_WIDTH + HEAD_WIDTH] + matrix_product(
        lora_qkv[:, rank : 2 * rank], widen_key
    )
    value_local = (
        projected[:, QUERY_WIDTH + HEAD_WIDTH :]
        + matrix_product(lora_qkv[:, 2 * rank :], widen_value)
    ).astype(bf16)
    query_rot = rotate(query_pre, position_own, 1.0).astype(bf16)
    key_rot = rotate(key_pre, position_own, 1.0).astype(bf16)
    keys_all = ring_gather(jnp.concatenate([key_rot, value_local], axis=1), 1)
    key_rows, value_rows = keys_all[:, :HEAD_WIDTH], keys_all[:, HEAD_WIDTH:]
    query_heads = query_rot.reshape(tokens_dev, HEADS, HEAD_WIDTH)
    scores = scores_of(query_heads, key_rows, allowed, scaling)
    row_max = jnp.max(scores, axis=-1, keepdims=True)
    powered = jnp.exp(scores - row_max)
    row_sum = jnp.sum(powered, axis=-1, keepdims=True)
    probs = powered / row_sum
    probs_low = probs.astype(bf16)
    attended = (
        jnp.einsum("thu,ud->thd", probs_low, value_rows, preferred_element_type=f32)
        .reshape(tokens_dev, QUERY_WIDTH)
        .astype(bf16)
    )
    lora_out = matrix_product(attended, narrow_output).astype(bf16)
    middle = (
        hidden_state
        + times_transposed(attended, proj_out)
        + matrix_product(lora_out, widen_output)
    )
    scale_two = rms_scale(middle)
    normed_two = (middle * scale_two * gains[1]).astype(bf16)

    weight_planes = feedforward_weight.transpose(1, 0, 2)
    rows_all, acts, low_ffn = unit_rows(
        normed_two,
        output_gradient[0],
        weight_planes,
        first_factor[:, 4 * rank :],
        widen_down,
        widen_gate,
        widen_up,
        narrow_down,
        2,
    )
    two_all, grad_all = rows_all[0], rows_all[1]
    gate_grad, up_grad, units = acts[0], acts[1], acts[2]
    lora_gate, lora_up, hd_grad = low_ffn[:, :rank], low_ffn[:, rank : 2 * rank], low_ffn[:, 2 * rank :]
    ffn_shares = jnp.stack(
        [
            outer_product_rows(former, latter).astype(bf16)
            for former, latter in ((gate_grad, two_all), (up_grad, two_all), (units, grad_all))
        ]
    )
    attended_all = gather_rows(jnp.concatenate([attended, lora_qkv], axis=1))
    ffn_shares, acts, attended_all = lax.optimization_barrier((ffn_shares, acts, attended_all))
    ffn_both = loop_shares(ffn_shares)
    rows_sum = mix_rows(
        acts, weight_planes, widen_gate, widen_up, narrow_down, 3
    )
    back_own, out_own = rows_sum[:, : MODEL_WIDTH + 2 * rank], rows_sum[:, MODEL_WIDTH + 2 * rank :]
    down_own = outer_product_rows(units, hd_grad)
    gate_piece = outer_product_rows(gate_grad, lora_gate)
    up_piece = outer_product_rows(up_grad, lora_up)

    lora_hd = out_own[:, MODEL_WIDTH:].astype(bf16)
    hidden_out = (middle + out_own[:, :MODEL_WIDTH] + matrix_product(lora_hd, widen_down)).astype(bf16)

    gate_low = back_own[:, MODEL_WIDTH : MODEL_WIDTH + rank].astype(bf16)
    up_low = back_own[:, MODEL_WIDTH + rank :].astype(bf16)
    two_grad = (
        back_own[:, :MODEL_WIDTH]
        + times_transposed(gate_low, squeeze_gate)
        + times_transposed(up_low, squeeze_up)
    )
    weighted_two = gains[1] * two_grad
    middle_grad = (
        output_gradient[0].astype(f32)
        + scale_two * weighted_two
        - middle * scale_two**3 * jnp.mean(middle * weighted_two, axis=-1, keepdims=True)
    )
    gain_two = jnp.sum(two_grad * middle * scale_two, axis=0)

    branch_grad = middle_grad.astype(bf16)
    lora_out_grad = times_transposed(branch_grad, widen_output).astype(bf16)
    attended_grad = (
        matrix_product(branch_grad, proj_out) + times_transposed(lora_out_grad, narrow_output)
    ).astype(bf16)
    heads_grad = attended_grad.reshape(tokens_dev, HEADS, HEAD_WIDTH)
    prob_grad = jnp.einsum("thd,ud->thu", heads_grad, value_rows, preferred_element_type=f32)
    row_dot = jnp.sum(probs * prob_grad, axis=-1, keepdims=True)
    score_grad = (probs * (prob_grad - row_dot)).astype(bf16)
    query_rot_grad = (
        jnp.einsum("thu,ud->thd", score_grad, key_rows, preferred_element_type=f32) * scaling
    )
    key_part = (
        jnp.einsum("thu,thd->ud", score_grad, query_heads, preferred_element_type=f32) * scaling
    )
    value_part = jnp.einsum("thu,thd->ud", probs_low, heads_grad, preferred_element_type=f32)
    pair_grad = ring_scatter([key_part, value_part], 4)
    query_grad = rotate(
        query_rot_grad.reshape(tokens_dev, QUERY_WIDTH), position_own, -1.0
    ).astype(bf16)
    key_grad = rotate(pair_grad[:, :HEAD_WIDTH], position_own, -1.0).astype(bf16)
    value_grad = pair_grad[:, HEAD_WIDTH:].astype(bf16)
    proj_grad = jnp.concatenate([query_grad, key_grad, value_grad], axis=1)
    lora_qkv_grad = jnp.concatenate(
        [
            times_transposed(query_grad, widen_query),
            times_transposed(key_grad, widen_key),
            times_transposed(value_grad, widen_value),
        ],
        axis=1,
    ).astype(bf16)
    normed_grad = times_transposed(proj_grad, proj_in) + times_transposed(
        lora_qkv_grad, narrow_projection
    )
    weighted_one = gains[0] * normed_grad
    input_grad = (
        middle_grad
        + scale_one * weighted_one
        - hidden_state
        * scale_one**3
        * jnp.mean(hidden_state * weighted_one, axis=-1, keepdims=True)
    )
    gain_one = jnp.sum(normed_grad * hidden_state * scale_one, axis=0)

    lora_qkv_all = attended_all[:, QUERY_WIDTH:]
    lora_out_all = matrix_product(attended_all[:, :QUERY_WIDTH], narrow_output).astype(bf16)
    normed_turn, branch_turn = turn(normalized), turn(branch_grad)
    out_piece = outer_product_rows(branch_turn, lora_out_all)
    gain_rows = jnp.stack([gain_one, gain_two]).astype(bf16).reshape(tokens_dev, -1)
    gain_count = gain_rows.shape[1]
    gain_rows = jnp.pad(gain_rows, ((0, 0), (0, -gain_count % 128)))
    proj_rows = jnp.concatenate(
        [proj_grad, lora_out_grad, gate_low, up_low, lora_hd, gain_rows], axis=1
    )
    proj_rows, normed_turn, branch_turn = lax.optimization_barrier(
        (proj_rows, normed_turn, branch_turn)
    )
    proj_all, middle_own = share_rows(
        proj_rows, jnp.concatenate([out_piece, gate_piece, up_piece], axis=0).astype(bf16), 5
    )
    column = place * width_own
    gain_all = proj_all[:, PROJECT_COLUMNS + 4 * rank :][:, :gain_count].reshape(size, 2, MODEL_WIDTH)
    gain_all = jnp.sum(gain_all.astype(f32), axis=0)
    gain_own = lax.dynamic_slice_in_dim(gain_all, column, width_own, 1)
    gain_part = jnp.pad(gain_own, ((0, width_own - 2), (0, -width_own % 128)))
    attn_part = jnp.concatenate(
        [
            outer_product_rows(normed_turn, proj_all[:, :PROJECT_COLUMNS]),
            outer_product_rows(branch_turn, attended_all)[:, :QUERY_WIDTH],
            gain_part,
        ],
        axis=1,
    ).astype(bf16)
    attn_part, ffn_both, proj_all = lax.optimization_barrier((attn_part, ffn_both, proj_all))
    attn_sum = both_loops(loop_shares(attn_part))
    gain_column = PROJECT_COLUMNS + QUERY_WIDTH
    gain_sum = attn_sum[:2, gain_column : gain_column + width_own]
    low_all = proj_all[:, PROJECT_COLUMNS : PROJECT_COLUMNS + 4 * rank]
    proj_all = proj_all[:, :PROJECT_COLUMNS]
    qkv_low_all = jnp.concatenate(
        [
            times_transposed(proj_all[:, :QUERY_WIDTH], widen_query),
            times_transposed(proj_all[:, QUERY_WIDTH : QUERY_WIDTH + HEAD_WIDTH], widen_key),
            times_transposed(proj_all[:, QUERY_WIDTH + HEAD_WIDTH :], widen_value),
        ],
        axis=1,
    ).astype(bf16)
    attended_turn = lax.dynamic_slice_in_dim(attended_all, column, width_own, 1)
    two_turn = lax.dynamic_slice_in_dim(two_all, column, width_own, 1)
    squeeze_own = jnp.concatenate(
        [
            outer_product_rows(normed_turn, qkv_low_all),
            outer_product_rows(attended_turn, low_all[:, :rank]),
            outer_product_rows(two_turn, low_all[:, rank : 3 * rank]),
        ],
        axis=1,
    )
    near = jnp.concatenate(
        [
            outer_product_rows(proj_all[:, :QUERY_WIDTH], lora_qkv_all[:, :rank]),
            outer_product_rows(
                proj_all[:, QUERY_WIDTH : QUERY_WIDTH + HEAD_WIDTH], lora_qkv_all[:, rank : 2 * rank]
            ),
            outer_product_rows(proj_all[:, QUERY_WIDTH + HEAD_WIDTH :], lora_qkv_all[:, 2 * rank :]),
        ],
        axis=0,
    )
    far = outer_product_rows(grad_all, low_all[:, 3 * rank :])
    first = place * columns_own
    far_start = GATE_START + 2 * HIDDEN_COUNT
    near = lax.dynamic_slice_in_dim(
        jnp.pad(near.astype(bf16), ((0, columns_own), (0, 0))), jnp.minimum(first, PROJECT_COLUMNS), columns_own, 0
    )
    far = lax.dynamic_slice_in_dim(
        jnp.pad(far.astype(bf16), ((columns_own, 0), (0, 0))),
        jnp.maximum(first - far_start + columns_own, 0),
        columns_own,
        0,
    )
    owned = first + jnp.arange(columns_own, dtype=jnp.int32)[:, None]
    expand_own = jnp.where(
        owned < PROJECT_COLUMNS, near, jnp.where(owned < far_start, middle_own, far)
    ).T.astype(f32)
    ffn_sum = both_loops(ffn_both).transpose(1, 0, 2)
    return (
        hidden_out[None],
        input_grad[None],
        gain_sum,
        attn_sum[:, :PROJECT_COLUMNS],
        attn_sum[:, PROJECT_COLUMNS:gain_column],
        ffn_sum,
        squeeze_own[None],
        expand_own[None],
        down_own[None],
    )


def solution(mesh):
    return jax.shard_map(
        per_device,
        mesh=mesh,
        in_specs=(
            P("loop", "fsdp", None),
            P("loop", None),
            P(),
            P("fsdp", None),
            P("fsdp", None),
            P("fsdp", None, None),
            P("loop", None, None),
            P("loop", None, None),
            P("loop", None, None),
            P("loop", "fsdp", None),
        ),
        out_specs=(
            P("loop", "fsdp", None),
            P("loop", "fsdp", None),
            P(None, "fsdp"),
            P("fsdp", None),
            P("fsdp", None),
            P("fsdp", None, None),
            P("loop", "fsdp", None),
            P("loop", None, "fsdp"),
            P("loop", "fsdp", None),
        ),
        check_vma=False,
    )
```

```python
import functools
import math

import jax
import jax.numpy as jnp
from jax import lax
from jax.experimental import pallas as pl
from jax.experimental.pallas import tpu as pltpu
from jax.sharding import PartitionSpec as P

MODEL_WIDTH = 2048
HEADS = 8
HEAD_WIDTH = 256
HIDDEN_COUNT = 16384
ADAPTER_RANK = 256
QUERY_WIDTH = 2048
PROJECT_COLUMNS = 2560
ADAPTER_COLUMNS = 39424
GATE_START = PROJECT_COLUMNS + MODEL_WIDTH

epsilon = 1e-06
bf16 = jnp.bfloat16
f32 = jnp.float32
MESH = pl.DeviceIdType.MESH


def matrix_product(former, latter):
    return jnp.dot(former, latter, preferred_element_type=f32)


def times_transposed(former, latter):
    return lax.dot_general(former, latter, (((1,), (1,)), ((), ())), preferred_element_type=f32)


def outer_product_rows(former, latter):
    return lax.dot_general(former, latter, (((0,), (0,)), ((), ())), preferred_element_type=f32)


def segment_info(lengths, row_count):
    row_ids = jnp.arange(row_count, dtype=jnp.int32)
    count = lengths.shape[0]
    labels = jnp.arange(count, dtype=jnp.int32)
    finish = jnp.sum(jnp.where(labels[:, None] <= labels[None, :], lengths[:, None], 0), axis=0)
    starts = finish - lengths
    segment = jnp.sum((row_ids[:, None] >= finish[None, :]).astype(jnp.int32), axis=1)
    opening = jnp.sum(jnp.where(segment[:, None] == labels[None, :], starts[None, :], 0), axis=1)
    return (segment, row_ids - opening)


def rotate(values, position, direction):
    half_dim = HEAD_WIDTH // 2
    frequency = jnp.exp(
        jnp.arange(half_dim).astype(f32) * (-2.0 * math.log(10000.0) / HEAD_WIDTH)
    )
    angles = position.astype(f32)[:, None] * frequency[None, :]
    cosine = jnp.cos(angles)[:, None, :]
    sine_val = direction * jnp.sin(angles)[:, None, :]
    shaped = values.reshape(values.shape[0], -1, HEAD_WIDTH)
    former = shaped[..., :half_dim]
    latter = shaped[..., half_dim:]
    turned = jnp.concatenate(
        [former * cosine - latter * sine_val, latter * cosine + former * sine_val], axis=-1
    )
    return turned.reshape(values.shape)


def rms_scale(values):
    return lax.rsqrt(jnp.mean(values * values, axis=-1, keepdims=True) + epsilon)


def gelu_tanh(values):
    return jax.nn.gelu(values, approximate=True)


def unit_backward(gate_value, upward_activation, hidden_unit_gradient):
    activated, pullback_function = jax.vjp(gelu_tanh, gate_value)
    gate_grad = pullback_function(hidden_unit_gradient * upward_activation)[0]
    return (gate_grad.astype(bf16), (hidden_unit_gradient * activated).astype(bf16))


def scores_of(query_heads, key_rows, allowed, scaling):
    product = (
        jnp.einsum("thd,ud->thu", query_heads, key_rows, preferred_element_type=f32) * scaling
    )
    return jnp.where(allowed[:, None, :], product, -1e30)


def gather_rows(block):
    return lax.all_gather(block, "fsdp", axis=0, tiled=True)


def scatter_rows(partial):
    return lax.psum_scatter(partial.astype(bf16), "fsdp", scatter_dimension=0, tiled=True).astype(f32)


def loop_shares(partial):
    return lax.all_gather(partial.astype(bf16), "loop", axis=0)


def both_loops(shares):
    return shares[0].astype(f32) + shares[1].astype(f32)


def sum_kernel(early_ref, up_ref, o_ref):
    @pl.when(pl.program_id(0) != 1)
    def _():
        o_ref[0] = early_ref[0, 0].astype(f32) + early_ref[1, 0].astype(f32)

    @pl.when(pl.program_id(0) == 1)
    def _():
        o_ref[0] = up_ref[0].astype(f32) + up_ref[1].astype(f32)


def sum_loops(early, up):
    _, rows, columns = up.shape
    tile = min(rows, 256)
    steps = rows // tile
    return pl.pallas_call(
        sum_kernel,
        grid=(3, steps),
        out_shape=jax.ShapeDtypeStruct((3, rows, columns), f32),
        in_specs=[
            pl.BlockSpec(
                (2, 1, tile, columns),
                lambda i, j: (0, i // 2, jnp.where(i == 1, steps - 1, j), 0),
            ),
            pl.BlockSpec(
                (2, tile, columns),
                lambda i, j: (0, jnp.where(i == 1, j, jnp.where(i < 1, 0, steps - 1)), 0),
            ),
        ],
        out_specs=pl.BlockSpec((1, tile, columns), lambda i, j: (i, j, 0)),
        compiler_params=pltpu.CompilerParams(vmem_limit_bytes=32 << 20),
        cost_estimate=busy(17),
        name="sum_loops",
    )(early, up)


def turn(block):
    return lax.all_to_all(block, "fsdp", split_axis=1, concat_axis=0, tiled=True)


def chip_at(q, chips):
    return jnp.where(q < 4, 2 * q, 15 - 2 * q) if chips == 8 else q

def ring_place(chip, chips):
    return jnp.where(chip % 2 == 0, chip // 2, 7 - chip // 2) if chips == 8 else chip

def ring_neighbours(chips):
    me = lax.axis_index("fsdp")
    core = me % 2
    p = ring_place(me // 2, chips)
    def device(shift, c):
        return chip_at((p + shift + chips) % chips, chips) * 2 + c
    return core, device

def meet(devices):
    barrier = pltpu.get_barrier_semaphore()
    for d in devices:
        pl.semaphore_signal(barrier, inc=1, device_id={"fsdp": d}, device_id_type=MESH)
    pl.semaphore_wait(barrier, len(devices))

def gather_kernel(chips, x_ref, o_ref, own_sem, ring_send, ring_recv, side_send, side_recv, greet=None, also=None):
    core, device = ring_neighbours(chips)
    rows = x_ref.shape[0]
    reach = chips // 2
    ways = (device(1, core), device(-1, core))
    side = device(0, 1 - core)
    if greet is None:
        meet((*ways, side))
    else:
        greet()

    def span(way, hops):
        return (way * (rows // 2), rows // 2) if hops == reach else (0, rows)

    def at(way, hops, c, part):
        origin = device(-hops if way == 0 else hops, c)
        return o_ref.at[pl.ds(pl.multiple_of(origin * rows + part[0], 8), part[1])]

    def hop(way, hops):
        part = span(way, hops)
        here = at(way, hops - 1, core, part)
        src = x_ref.at[pl.ds(part[0], part[1])] if hops == 1 else here
        return pltpu.make_async_remote_copy(src, here, ring_send.at[way, hops - 1], ring_recv.at[way, hops - 1], device_id={"fsdp": ways[way]}, device_id_type=MESH)

    def arriving(way, hops):
        here = at(way, hops, core, span(way, hops))
        return pltpu.make_async_remote_copy(here, here, ring_send.at[way, hops - 1], ring_recv.at[way, hops - 1], device_id={"fsdp": ways[way]}, device_id_type=MESH)

    def across(way, hops, c):
        part = span(way, hops) if hops else (0, rows)
        there = at(way, hops, c, part)
        src = there if hops else x_ref
        return pltpu.make_async_remote_copy(src, there, side_send.at[way, hops], side_recv.at[way, hops], device_id={"fsdp": side}, device_id_type=MESH)

    for way in (0, 1):
        hop(way, 1).start()
    across(0, 0, core).start()
    own = pltpu.make_async_copy(x_ref, at(0, 0, core, (0, rows)), own_sem)
    own.start()
    if also is not None:
        also()
    for hops in range(1, reach + 1):
        for way in (0, 1):
            arriving(way, hops).wait_recv()
            if hops < reach:
                hop(way, hops + 1).start()
            across(way, hops, core).start()
    across(0, 0, 1 - core).wait_recv()
    across(0, 0, core).wait_send()
    for hops in range(1, reach + 1):
        for way in (0, 1):
            across(way, hops, 1 - core).wait_recv()
            across(way, hops, core).wait_send()
            hop(way, hops).wait_send()
    own.wait()

def busy(us):
    return pl.CostEstimate(flops=0, bytes_accessed=int(us * 3.0e6), transcendentals=0)


def ring_gather(block, ident):
    size = lax.axis_size("fsdp")
    chips = size // 2
    rows, columns = block.shape
    pair = pltpu.SemaphoreType.DMA((2, chips // 2))
    sides = pltpu.SemaphoreType.DMA((2, chips // 2 + 1))
    return pl.pallas_call(
        functools.partial(gather_kernel, chips),
        out_shape=jax.ShapeDtypeStruct((size * rows, columns), block.dtype),
        in_specs=[pl.BlockSpec(memory_space=pl.ANY)],
        out_specs=pl.BlockSpec(memory_space=pl.ANY),
        scratch_shapes=[pltpu.SemaphoreType.DMA, pair, pair, sides, sides],
        compiler_params=pltpu.CompilerParams(collective_id=ident, has_side_effects=True),
        cost_estimate=busy(1),
        name="ring_gather",
    )(block)

def scatter_kernel(chips, count, *refs):
    x_refs, o_ref = refs[:count], refs[count]
    side_buf, ring_buf, side_send, side_recv, ring_send, ring_recv = refs[count + 1 :]
    core, device = ring_neighbours(chips)
    rows, columns = o_ref.shape
    reach = chips // 2
    half = columns // 2
    tile = 16
    ways = (device(1, core), device(-1, core))
    side = device(0, 1 - core)
    meet((*ways, side))
    starts = [sum(x.shape[1] for x in x_refs[:i]) for i in range(count)]

    def shift(way, hops):
        return (hops if way == 0 else chips - hops) % chips

    def across(target, c, i):
        there = pl.ds(pl.multiple_of(device(target, c) * rows, tile), rows)
        return pltpu.make_async_remote_copy(
            x_refs[i].at[there],
            side_buf.at[target, :, pl.ds(starts[i], x_refs[i].shape[1])],
            side_send.at[target, i],
            side_recv.at[target, i],
            device_id={"fsdp": side},
            device_id_type=MESH,
        )

    def hop(way, step):
        cols = pl.ds(way * half, half) if step == 0 else pl.ds(0, columns)
        return pltpu.make_async_remote_copy(
            side_buf.at[shift(way, reach - step), :, cols],
            ring_buf.at[way, step, :, cols],
            ring_send.at[way, step],
            ring_recv.at[way, step],
            device_id={"fsdp": ways[way]},
            device_id_type=MESH,
        )

    order = [reach] + [shift(way, hops) for hops in range(reach - 1, 0, -1) for way in (0, 1)] + [0]
    for target in order:
        for i in range(count):
            across(target, 1 - core, i).start()

    def add(target, incoming, store):
        first = pl.multiple_of(device(target, core) * rows, tile)
        for i in range(count):
            across(target, core, i).wait_recv()

        @pl.loop(0, rows // tile)
        def _(j):
            here = pl.ds(pl.multiple_of(j * tile, tile), tile)
            mine = pl.ds(pl.multiple_of(first + j * tile, tile), tile)
            for i in range(count):
                cols = pl.ds(starts[i], x_refs[i].shape[1])
                total = x_refs[i][mine, :].astype(f32) + side_buf[target, here, cols].astype(f32)
                for way, step in incoming:
                    if step:
                        total = total + ring_buf[way, step, here, cols].astype(f32)
                store(here, cols, total)
            for way, step in incoming:
                if not step:
                    cols = pl.ds(way * half, half)
                    store(
                        here,
                        cols,
                        side_buf[target, here, cols].astype(f32) + ring_buf[way, 0, here, cols].astype(f32),
                    )

    for step in range(reach):
        for way in (0, 1):
            target = shift(way, reach - step)
            if step:
                hop(way, step - 1).wait_recv()

            def store(here, cols, total, target=target):
                side_buf[target, here, cols] = total.astype(bf16)

            if step or way == 0:
                add(target, [(way, step - 1)] if step else [], store)
            hop(way, step).start()
    for way in (0, 1):
        hop(way, reach - 1).wait_recv()

    def last(here, cols, total):
        o_ref[here, cols] = total

    add(0, [(0, reach - 1), (1, reach - 1)], last)
    for target in order:
        for i in range(count):
            across(target, 1 - core, i).wait_send()
    for step in range(reach):
        for way in (0, 1):
            hop(way, step).wait_send()


def ring_scatter(terms, ident):
    size = lax.axis_size("fsdp")
    terms = [term.astype(bf16) for term in terms]
    if size != 16:
        return scatter_rows(jnp.concatenate(terms, axis=1))
    chips, count = size // 2, len(terms)
    rows, columns = terms[0].shape[0] // size, sum(term.shape[1] for term in terms)
    pair = pltpu.SemaphoreType.DMA((2, chips // 2))
    sides = pltpu.SemaphoreType.DMA((chips, count))
    return pl.pallas_call(
        functools.partial(scatter_kernel, chips, count),
        out_shape=jax.ShapeDtypeStruct((rows, columns), f32),
        in_specs=[pl.BlockSpec(memory_space=pltpu.VMEM)] * count,
        out_specs=pl.BlockSpec(memory_space=pltpu.VMEM),
        scratch_shapes=[
            pltpu.VMEM((chips, rows, columns), bf16),
            pltpu.VMEM((2, chips // 2, rows, columns), bf16),
            sides,
            sides,
            pair,
            pair,
        ],
        compiler_params=pltpu.CompilerParams(
            collective_id=ident, has_side_effects=True, vmem_limit_bytes=56 << 20
        ),
        cost_estimate=busy(1),
        name="ring_scatter",
    )(*terms)


def unit_kernel(chips, *refs):
    sources, (planes, squeeze, widen_down, widen_gate, widen_up, narrow) = refs[:2], refs[2:8]
    two_all, grad_all, acts_all, low_all = refs[8:12]
    held, acts, low, landed = refs[12], refs[13], refs[14], refs[15:17]
    held_sem, own_sem, ring_send, ring_recv, side_send, side_recv, out_sem = refs[17:]
    core, device = ring_neighbours(chips)
    rows = sources[0].shape[0]
    reach = chips // 2
    wide = 256
    ways = (device(1, core), device(-1, core))
    side = device(0, 1 - core)
    fetches = [pltpu.make_async_copy(planes.at[i], held.at[i], held_sem.at[i]) for i in range(3)]
    for fetch in fetches:
        fetch.start()
    meet((*ways, side))

    def span(way, hops):
        return (way * (rows // 2), rows // 2) if hops == reach else (0, rows)

    def at(i, way, hops, c, part):
        origin = device(-hops if way == 0 else hops, c)
        return landed[i].at[pl.ds(pl.multiple_of(origin * rows + part[0], 16), part[1])]

    def hop(i, way, hops):
        part = span(way, hops)
        here = at(i, way, hops - 1, core, part)
        src = sources[i].at[pl.ds(part[0], part[1])] if hops == 1 else here
        return pltpu.make_async_remote_copy(
            src,
            here,
            ring_send.at[i, way, hops - 1],
            ring_recv.at[i, way, hops - 1],
            device_id={"fsdp": ways[way]},
            device_id_type=MESH,
        )

    def arriving(i, way, hops):
        here = at(i, way, hops, core, span(way, hops))
        return pltpu.make_async_remote_copy(
            here,
            here,
            ring_send.at[i, way, hops - 1],
            ring_recv.at[i, way, hops - 1],
            device_id={"fsdp": ways[way]},
            device_id_type=MESH,
        )

    def across(i, way, hops, c):
        part = span(way, hops) if hops else (0, rows)
        there = at(i, way, hops, c, part)
        return pltpu.make_async_remote_copy(
            there if hops else sources[i],
            there,
            side_send.at[i, way, hops],
            side_recv.at[i, way, hops],
            device_id={"fsdp": side},
            device_id_type=MESH,
        )

    def leaving(n, first):
        mine = pl.ds(first, 2 * rows)
        width, under = grad_all.shape[1], low.shape[1]
        pairs = [
            (landed[0].at[mine, pl.ds(0, width)], two_all.at[mine]),
            (landed[0].at[mine, pl.ds(width, ADAPTER_RANK)], low_all.at[mine, pl.ds(under, ADAPTER_RANK)]),
            (low.at[mine], low_all.at[mine, pl.ds(0, under)]),
            (landed[1].at[mine], grad_all.at[mine]),
        ]
        pairs += [(acts.at[i, mine], acts_all.at[i, mine]) for i in range(3)]
        return [pltpu.make_async_copy(a, b, out_sem.at[n, i]) for i, (a, b) in enumerate(pairs)]

    def first_row(shift):
        return pl.multiple_of(device(shift, 0) * rows, 2 * rows)

    def work(n, first):
        mine = pl.ds(first, 2 * rows)
        rank, width = ADAPTER_RANK, MODEL_WIDTH
        low[mine, : 2 * rank] = matrix_product(landed[0][mine, :width], squeeze[...]).astype(bf16)
        low[mine, 2 * rank :] = times_transposed(landed[1][mine, :], widen_down[...]).astype(bf16)

        @pl.loop(0, held.shape[1] // wide)
        def _(t):
            own = pl.ds(pl.multiple_of(t * wide, wide), wide)
            two = landed[0][mine, :width]
            gate = times_transposed(two, held[0, own, :]) + matrix_product(
                low[mine, :rank], widen_gate[:, own]
            )
            upward = times_transposed(two, held[1, own, :]) + matrix_product(
                low[mine, rank : 2 * rank], widen_up[:, own]
            )
            pull = times_transposed(landed[1][mine, :], held[2, own, :]) + times_transposed(
                low[mine, 2 * rank :], narrow[own, :]
            )
            scale = math.sqrt(2.0 / math.pi)
            square = gate * gate
            bend = jnp.tanh(scale * gate * (1.0 + 0.044715 * square))
            rise = 0.5 * (1.0 + bend)
            active = gate * rise
            slope = rise + 0.5 * gate * (1.0 - bend * bend) * (scale * (1.0 + 3 * 0.044715 * square))
            acts[0, mine, own] = (pull * upward * slope).astype(bf16)
            acts[1, mine, own] = (pull * active).astype(bf16)
            acts[2, mine, own] = (active * upward).astype(bf16)

        for copy in leaving(n, first):
            copy.start()

    for i in (0, 1):
        for way in (0, 1):
            hop(i, way, 1).start()
        across(i, 0, 0, core).start()
    keeps = [
        pltpu.make_async_copy(sources[i], at(i, 0, 0, core, (0, rows)), own_sem.at[i]) for i in (0, 1)
    ]
    for keep in keeps:
        keep.start()
    for copy in keeps + fetches:
        copy.wait()
    for i in (0, 1):
        across(i, 0, 0, 1 - core).wait_recv()
    work(0, first_row(0))
    for hops in range(1, reach + 1):
        for i in (0, 1):
            for way in (0, 1):
                arriving(i, way, hops).wait_recv()
                if hops < reach:
                    hop(i, way, hops + 1).start()
                across(i, way, hops, core).start()
        if hops < reach:
            for way in (0, 1):
                for i in (0, 1):
                    across(i, way, hops, 1 - core).wait_recv()
                work(2 * hops - 1 + way, first_row(-hops if way == 0 else hops))
    for way in (0, 1):
        for i in (0, 1):
            across(i, way, reach, 1 - core).wait_recv()
    work(2 * reach - 1, first_row(reach))
    for i in (0, 1):
        across(i, 0, 0, core).wait_send()
        for hops in range(1, reach + 1):
            for way in (0, 1):
                across(i, way, hops, core).wait_send()
                hop(i, way, hops).wait_send()
    for n in range(chips):
        if n == 0:
            shift = 0
        elif n == 2 * reach - 1:
            shift = reach
        else:
            shift = (-1 if n % 2 else 1) * ((n + 1) // 2)
        for copy in leaving(n, first_row(shift)):
            copy.wait()


def unit_rows(two, grad, planes, squeeze, widen_down, widen_gate, widen_up, narrow, ident):
    size = lax.axis_size("fsdp")
    rank = ADAPTER_RANK
    if size != 16:
        two, grad = gather_rows(two), gather_rows(grad)
        two, lora_out = two[:, :MODEL_WIDTH], two[:, MODEL_WIDTH:]
        low = matrix_product(two, squeeze).astype(bf16)
        pulled = times_transposed(grad, widen_down).astype(bf16)
        gate = times_transposed(two, planes[0]) + matrix_product(low[:, :rank], widen_gate)
        upward = times_transposed(two, planes[1]) + matrix_product(low[:, rank:], widen_up)
        units_grad = times_transposed(grad, planes[2]) + times_transposed(pulled, narrow)
        units = (gelu_tanh(gate) * upward).astype(bf16)
        gate_grad, up_grad = unit_backward(gate, upward, units_grad)
        return (
            two,
            grad,
            jnp.stack([gate_grad, up_grad, units]),
            jnp.concatenate([low, pulled, lora_out], axis=1),
        )
    chips = size // 2
    rows, columns = grad.shape
    all_rows, hidden = size * rows, planes.shape[1]
    anywhere, inside = pl.BlockSpec(memory_space=pl.ANY), pl.BlockSpec(memory_space=pltpu.VMEM)
    pair = pltpu.SemaphoreType.DMA((2, 2, chips // 2))
    sides = pltpu.SemaphoreType.DMA((2, 2, chips // 2 + 1))
    return pl.pallas_call(
        functools.partial(unit_kernel, chips),
        out_shape=(
            jax.ShapeDtypeStruct((all_rows, columns), bf16),
            jax.ShapeDtypeStruct((all_rows, columns), bf16),
            jax.ShapeDtypeStruct((3, all_rows, hidden), bf16),
            jax.ShapeDtypeStruct((all_rows, 4 * rank), bf16),
        ),
        in_specs=[anywhere] * 3 + [inside] * 5,
        out_specs=(anywhere,) * 4,
        scratch_shapes=[
            pltpu.VMEM(planes.shape, bf16),
            pltpu.VMEM((3, all_rows, hidden), bf16),
            pltpu.VMEM((all_rows, 3 * rank), bf16),
            pltpu.VMEM((all_rows, two.shape[1]), bf16),
            pltpu.VMEM((all_rows, columns), bf16),
            pltpu.SemaphoreType.DMA((3,)),
            pltpu.SemaphoreType.DMA((2,)),
            pair,
            pair,
            sides,
            sides,
            pltpu.SemaphoreType.DMA((chips, 7)),
        ],
        compiler_params=pltpu.CompilerParams(
            collective_id=ident, has_side_effects=True, vmem_limit_bytes=60 << 20
        ),
        cost_estimate=busy(100),
        name="unit_rows",
    )(two, grad, planes, squeeze, widen_down, widen_gate, widen_up, narrow)


def mix_kernel(chips, *refs):
    acts_ref, planes, gate_b, up_b, down_a, o_ref = refs[:6]
    acts, held, side_buf, ring_buf, stage, mine = refs[6:12]
    held_sem, side_send, side_recv, ring_send, ring_recv = refs[12:]
    fetches = [pltpu.make_async_copy(planes.at[i], held.at[i], held_sem.at[0, i]) for i in range(3)]
    fetches += [pltpu.make_async_copy(acts_ref.at[i], acts.at[i], held_sem.at[1, i]) for i in range(3)]
    for fetch in fetches:
        fetch.start()
    core, device = ring_neighbours(chips)
    rows, columns = o_ref.shape
    reach = chips // 2
    half = columns // 2
    tile = 16
    wide = 256
    ways = (device(1, core), device(-1, core))
    side = device(0, 1 - core)
    meet((*ways, side))
    order = [(reach, 0, 0)]
    for step in range(1, reach):
        order += [(reach - step, 0, step), (chips - reach + step, 1, step)]
    order.append((0, 0, reach))

    def across(i):
        target = order[i][0]
        return pltpu.make_async_remote_copy(
            stage.at[i % 2],
            side_buf.at[target],
            side_send.at[target],
            side_recv.at[target],
            device_id={"fsdp": side},
            device_id_type=MESH,
        )

    def hop(way, step, part):
        target = (reach - step if way == 0 else chips - reach + step) % chips
        cols = pl.ds(way * half, half) if step == 0 else pl.ds(0, columns)
        here = pl.ds(part * (rows // 2), rows // 2)
        return pltpu.make_async_remote_copy(
            side_buf.at[target, here, cols],
            ring_buf.at[way, step, here, cols],
            ring_send.at[way, step, part],
            ring_recv.at[way, step, part],
            device_id={"fsdp": ways[way]},
            device_id_type=MESH,
        )

    def make(i):
        target, slot = order[i][0], i % 2
        if i >= 2:
            across(i - 2).wait_send()
        theirs = pl.ds(pl.multiple_of(device(target, 1 - core) * rows, rows), rows)
        ours = pl.ds(pl.multiple_of(device(target, core) * rows, rows), rows)

        def block(kind):
            return jnp.concatenate([acts[kind, theirs, :], acts[kind, ours, :]], axis=0)

        def put(first, value):
            cols = pl.ds(pl.multiple_of(first, wide), wide)
            stage[slot, :, cols] = value[:rows].astype(bf16)
            mine[slot, :, cols] = value[rows:].astype(bf16)

        @pl.loop(0, MODEL_WIDTH // wide)
        def _(t):
            cols = pl.ds(pl.multiple_of(t * wide, wide), wide)
            put(
                t * wide,
                matrix_product(block(0), held[0, :, cols])
                + matrix_product(block(1), held[1, :, cols]),
            )
            put(
                MODEL_WIDTH + 2 * ADAPTER_RANK + t * wide,
                matrix_product(block(2), held[2, :, cols]),
            )

        put(MODEL_WIDTH, times_transposed(block(0), gate_b[...]))
        put(MODEL_WIDTH + ADAPTER_RANK, times_transposed(block(1), up_b[...]))
        put(2 * MODEL_WIDTH + 2 * ADAPTER_RANK, matrix_product(block(2), down_a[...]))
        across(i).start()

    def add(i):
        target, way, step = order[i]
        last = target == 0
        incoming = [(w, step - 1) for w in ((0, 1) if last else (way,))] if step else []
        across(i).wait_recv()
        for part in (0, 1):
            for w, s in incoming:
                hop(w, s, part).wait_recv()

            @pl.loop(0, rows // 2 // tile)
            def _(j, part=part):
                here = pl.ds(pl.multiple_of(part * (rows // 2) + j * tile, tile), tile)
                for side_half in (0, 1):
                    cols = pl.ds(side_half * half, half)
                    total = mine[i % 2, here, cols].astype(f32) + side_buf[target, here, cols].astype(f32)
                    for w, s in incoming:
                        if s or w == side_half:
                            total = total + ring_buf[w, s, here, cols].astype(f32)
                    if last:
                        o_ref[here, cols] = total
                    else:
                        side_buf[target, here, cols] = total.astype(bf16)

            if not last:
                hop(way, step, part).start()
                if step == 0:
                    hop(1, 0, part).start()

    for fetch in fetches:
        fetch.wait()
    make(0)
    add(0)
    make(1)
    for i in range(1, len(order)):
        if i + 1 < len(order):
            make(i + 1)
        add(i)
    for i in range(len(order) - 2, len(order)):
        across(i).wait_send()
    for step in range(reach):
        for way in (0, 1):
            for part in (0, 1):
                hop(way, step, part).wait_send()


def mix_rows(acts, planes, gate_b, up_b, down_a, ident):
    size = lax.axis_size("fsdp")
    if size != 16:
        gate_grad, up_grad, units = acts[0], acts[1], acts[2]
        terms = [
            matrix_product(gate_grad, planes[0]) + matrix_product(up_grad, planes[1]),
            times_transposed(gate_grad, gate_b),
            times_transposed(up_grad, up_b),
            matrix_product(units, planes[2]),
            matrix_product(units, down_a),
        ]
        return scatter_rows(jnp.concatenate(terms, axis=1))
    chips = size // 2
    rows, columns = acts.shape[1] // size, 2 * MODEL_WIDTH + 3 * ADAPTER_RANK
    pair = pltpu.SemaphoreType.DMA((2, chips // 2, 2))
    sides = pltpu.SemaphoreType.DMA((chips,))
    return pl.pallas_call(
        functools.partial(mix_kernel, chips),
        out_shape=jax.ShapeDtypeStruct((rows, columns), f32),
        in_specs=[pl.BlockSpec(memory_space=pl.ANY)] * 2
        + [pl.BlockSpec(memory_space=pltpu.VMEM)] * 3,
        out_specs=pl.BlockSpec(memory_space=pltpu.VMEM),
        scratch_shapes=[
            pltpu.VMEM(acts.shape, bf16),
            pltpu.VMEM(planes.shape, bf16),
            pltpu.VMEM((chips, rows, columns), bf16),
            pltpu.VMEM((2, chips // 2, rows, columns), bf16),
            pltpu.VMEM((2, rows, columns), bf16),
            pltpu.VMEM((2, rows, columns), bf16),
            pltpu.SemaphoreType.DMA((2, 3)),
            sides,
            sides,
            pair,
            pair,
        ],
        compiler_params=pltpu.CompilerParams(
            collective_id=ident, has_side_effects=True, vmem_limit_bytes=60 << 20
        ),
        cost_estimate=busy(1),
        name="mix_rows",
    )(acts, planes, gate_b, up_b, down_a)


def share_kernel(size, chunk, own_count, x_ref, mid_ref, all_ref, o_ref, *sems):
    send_sem, recv_sem, own_sem = sems[5:]
    me = lax.axis_index("fsdp")
    hidden = HIDDEN_COUNT // size
    width = MODEL_WIDTH // size
    sections = (
        (0, PROJECT_COLUMNS, width),
        (width, GATE_START, hidden),
        (width + hidden, GATE_START + HIDDEN_COUNT, hidden),
    )

    def greet():
        barrier = pltpu.get_barrier_semaphore()

        def one(i, carry):
            pl.semaphore_signal(barrier, inc=1, device_id={"fsdp": (me + i) % size}, device_id_type=MESH)
            return carry

        lax.fori_loop(1, size, one, 0)
        pl.semaphore_wait(barrier, size - 1)

    def rows(ref, first):
        return ref.at[pl.ds(pl.multiple_of(first, 8), chunk)]

    def aim(start, length):
        owner = (start + me * length) // own_count
        return owner, start + me * length - owner * own_count

    def remote(source, first, owner, sent=0):
        return pltpu.make_async_remote_copy(
            source,
            rows(o_ref, first),
            send_sem.at[sent],
            recv_sem.at[first // chunk],
            device_id={"fsdp": owner},
            device_id_type=MESH,
        )

    def local(source, first):
        return pltpu.make_async_copy(source, rows(o_ref, first), own_sem.at[first // chunk])

    def send_all():
        for base, start, length in sections:

            def send(j, carry, base=base, aimed=aim(start, length)):
                over = (aimed[1] + j * chunk >= own_count).astype(jnp.int32)
                owner = aimed[0] + over
                first = aimed[1] + j * chunk - over * own_count
                source = rows(mid_ref, base + j * chunk)

                @pl.when(owner != me)
                def _():
                    remote(source, first, owner, base // chunk + j).start()

                @pl.when(owner == me)
                def _():
                    local(source, first).start()

                return carry

            lax.fori_loop(0, length // chunk, send, 0)

    gather_kernel(size // 2, x_ref, all_ref, *sems[:5], greet=greet, also=send_all)

    def arrive(j, carry):
        column = me * own_count + j * chunk
        here = rows(o_ref, j * chunk)
        away, kept = 0, 0
        for _, start, length in sections:
            mine = start + me * length
            inside = (column >= start) & (column < start + length * size)
            outside = (column < mine) | (column >= mine + length)
            away = away + (inside & outside).astype(jnp.int32)
            kept = kept + (inside & ~outside).astype(jnp.int32)

        @pl.when(away > 0)
        def _():
            remote(here, j * chunk, (me + 1) % size).wait_recv()

        @pl.when(kept > 0)
        def _():
            local(rows(mid_ref, 0), j * chunk).wait()

        return carry

    lax.fori_loop(0, own_count // chunk, arrive, 0)
    for base, start, length in sections:

        def sent(j, carry, base=base, aimed=aim(start, length)):
            over = (aimed[1] + j * chunk >= own_count).astype(jnp.int32)
            owner = aimed[0] + over
            first = aimed[1] + j * chunk - over * own_count

            @pl.when(owner != me)
            def _():
                remote(rows(mid_ref, base + j * chunk), first, owner, base // chunk + j).wait_send()

            return carry

        lax.fori_loop(0, length // chunk, sent, 0)


def share_rows(block, middle, ident):
    size = lax.axis_size("fsdp")
    rows, columns = block.shape
    own_count = ADAPTER_COLUMNS // size
    chunk = math.gcd(own_count, MODEL_WIDTH // size, HIDDEN_COUNT // size, PROJECT_COLUMNS, GATE_START)
    anywhere = pl.BlockSpec(memory_space=pl.ANY)
    pair = pltpu.SemaphoreType.DMA((2, size // 4))
    sides = pltpu.SemaphoreType.DMA((2, size // 4 + 1))
    return pl.pallas_call(
        functools.partial(share_kernel, size, chunk, own_count),
        out_shape=(
            jax.ShapeDtypeStruct((size * rows, columns), block.dtype),
            jax.ShapeDtypeStruct((own_count, ADAPTER_RANK), bf16),
        ),
        in_specs=[anywhere] * 2,
        out_specs=(anywhere, anywhere),
        scratch_shapes=[
            pltpu.SemaphoreType.DMA,
            pair,
            pair,
            sides,
            sides,
            pltpu.SemaphoreType.DMA((middle.shape[0] // chunk,)),
            pltpu.SemaphoreType.DMA((own_count // chunk,)),
            pltpu.SemaphoreType.DMA((own_count // chunk,)),
        ],
        compiler_params=pltpu.CompilerParams(collective_id=ident, has_side_effects=True),
        cost_estimate=busy(1),
        name="share_rows",
    )(block, middle)


def per_device(
    hidden_input,
    sequence_lengths,
    norm_gain_values,
    input_proj_weight,
    output_proj_weight,
    feedforward_weight,
    adapter_first,
    adapter_second,
    adapter_down_first,
    output_gradient,
):
    size = lax.axis_size("fsdp")
    place = lax.axis_index("fsdp")
    tokens_dev = hidden_input.shape[1]
    all_rows = tokens_dev * size
    hidden_own = HIDDEN_COUNT // size
    width_own = MODEL_WIDTH // size
    columns_own = ADAPTER_COLUMNS // size
    offset = place * tokens_dev
    segment_all, position_all = segment_info(sequence_lengths[0], all_rows)
    segment_own = lax.dynamic_slice_in_dim(segment_all, offset, tokens_dev)
    position_own = lax.dynamic_slice_in_dim(position_all, offset, tokens_dev)
    row_all = jnp.arange(all_rows, dtype=jnp.int32)
    row_own = offset + jnp.arange(tokens_dev, dtype=jnp.int32)
    allowed = (segment_own[:, None] == segment_all[None, :]) & (
        row_own[:, None] >= row_all[None, :]
    )
    gains = norm_gain_values.astype(f32)
    first_factor = adapter_first[0]
    second_factor = adapter_second[0]
    rank = ADAPTER_RANK
    narrow_projection = first_factor[:, : 3 * rank]
    narrow_output = first_factor[:, 3 * rank : 4 * rank]
    squeeze_gate = first_factor[:, 4 * rank : 5 * rank]
    squeeze_up = first_factor[:, 5 * rank :]
    narrow_down = lax.dynamic_slice_in_dim(adapter_down_first[0], place * hidden_own, hidden_own, 0)
    widen_query = second_factor[:, :QUERY_WIDTH]
    widen_key = second_factor[:, QUERY_WIDTH : QUERY_WIDTH + HEAD_WIDTH]
    widen_value = second_factor[:, QUERY_WIDTH + HEAD_WIDTH : PROJECT_COLUMNS]
    widen_output = second_factor[:, PROJECT_COLUMNS:GATE_START]
    widen_gate = lax.dynamic_slice_in_dim(
        second_factor, GATE_START + place * hidden_own, hidden_own, 1
    )
    widen_up = lax.dynamic_slice_in_dim(
        second_factor, GATE_START + HIDDEN_COUNT + place * hidden_own, hidden_own, 1
    )
    widen_down = second_factor[:, GATE_START + 2 * HIDDEN_COUNT :]
    scaling = HEAD_WIDTH ** (-0.5)

    hidden_state = hidden_input[0].astype(f32)
    scale_one = rms_scale(hidden_state)
    normalized = (hidden_state * scale_one * gains[0]).astype(bf16)
    proj_in = ring_gather(input_proj_weight, 0)
    proj_in, proj_out = lax.optimization_barrier((proj_in, output_proj_weight))
    proj_out = gather_rows(proj_out)
    lora_qkv = matrix_product(normalized, narrow_projection).astype(bf16)
    projected = matrix_product(normalized, proj_in)
    query_pre = projected[:, :QUERY_WIDTH] + matrix_product(lora_qkv[:, :rank], widen_query)
    key_pre = projected[:, QUERY_WIDTH : QUERY_WIDTH + HEAD_WIDTH] + matrix_product(
        lora_qkv[:, rank : 2 * rank], widen_key
    )
    value_local = (
        projected[:, QUERY_WIDTH + HEAD_WIDTH :]
        + matrix_product(lora_qkv[:, 2 * rank :], widen_value)
    ).astype(bf16)
    query_rot = rotate(query_pre, position_own, 1.0).astype(bf16)
    key_rot = rotate(key_pre, position_own, 1.0).astype(bf16)
    keys_all = ring_gather(jnp.concatenate([key_rot, value_local], axis=1), 1)
    key_rows, value_rows = keys_all[:, :HEAD_WIDTH], keys_all[:, HEAD_WIDTH:]
    query_heads = query_rot.reshape(tokens_dev, HEADS, HEAD_WIDTH)
    scores = scores_of(query_heads, key_rows, allowed, scaling)
    row_max = jnp.max(scores, axis=-1, keepdims=True)
    powered = jnp.exp(scores - row_max)
    row_sum = jnp.sum(powered, axis=-1, keepdims=True)
    probs = powered / row_sum
    probs_low = probs.astype(bf16)
    attended = (
        jnp.einsum("thu,ud->thd", probs_low, value_rows, preferred_element_type=f32)
        .reshape(tokens_dev, QUERY_WIDTH)
        .astype(bf16)
    )
    lora_out = matrix_product(attended, narrow_output).astype(bf16)
    middle = (
        hidden_state
        + times_transposed(attended, proj_out)
        + matrix_product(lora_out, widen_output)
    )
    scale_two = rms_scale(middle)
    normed_two = (middle * scale_two * gains[1]).astype(bf16)

    weight_planes = feedforward_weight.transpose(1, 0, 2)
    two_all, grad_all, acts, low_ffn = unit_rows(
        jnp.concatenate([normed_two, lora_out], axis=1),
        output_gradient[0],
        weight_planes,
        first_factor[:, 4 * rank :],
        widen_down,
        widen_gate,
        widen_up,
        narrow_down,
        2,
    )
    gate_grad, up_grad, units = acts[0], acts[1], acts[2]
    lora_gate, lora_up = low_ffn[:, :rank], low_ffn[:, rank : 2 * rank]
    hd_grad, lora_out_all = low_ffn[:, 2 * rank : 3 * rank], low_ffn[:, 3 * rank :]
    early_shares = jnp.stack(
        [
            outer_product_rows(gate_grad, two_all).astype(bf16),
            outer_product_rows(units, grad_all).astype(bf16),
        ]
    )
    early_shares, acts = lax.optimization_barrier((early_shares, acts))
    early_both = loop_shares(early_shares)
    up_share = outer_product_rows(acts[1], two_all).astype(bf16)
    rows_sum = mix_rows(
        acts, weight_planes, widen_gate, widen_up, narrow_down, 3
    )
    back_own, out_own = rows_sum[:, : MODEL_WIDTH + 2 * rank], rows_sum[:, MODEL_WIDTH + 2 * rank :]
    down_own = outer_product_rows(units, hd_grad)
    gate_piece = outer_product_rows(gate_grad, lora_gate)
    up_piece = outer_product_rows(up_grad, lora_up)

    lora_hd = out_own[:, MODEL_WIDTH:].astype(bf16)
    hidden_out = (middle + out_own[:, :MODEL_WIDTH] + matrix_product(lora_hd, widen_down)).astype(bf16)

    gate_low = back_own[:, MODEL_WIDTH : MODEL_WIDTH + rank].astype(bf16)
    up_low = back_own[:, MODEL_WIDTH + rank :].astype(bf16)
    two_grad = (
        back_own[:, :MODEL_WIDTH]
        + times_transposed(gate_low, squeeze_gate)
        + times_transposed(up_low, squeeze_up)
    )
    weighted_two = gains[1] * two_grad
    middle_grad = (
        output_gradient[0].astype(f32)
        + scale_two * weighted_two
        - middle * scale_two**3 * jnp.mean(middle * weighted_two, axis=-1, keepdims=True)
    )
    gain_two = jnp.sum(two_grad * middle * scale_two, axis=0)

    branch_grad = middle_grad.astype(bf16)
    lora_out_grad = times_transposed(branch_grad, widen_output).astype(bf16)
    attended_grad = (
        matrix_product(branch_grad, proj_out) + times_transposed(lora_out_grad, narrow_output)
    ).astype(bf16)
    heads_grad = attended_grad.reshape(tokens_dev, HEADS, HEAD_WIDTH)
    prob_grad = jnp.einsum("thd,ud->thu", heads_grad, value_rows, preferred_element_type=f32)
    row_dot = jnp.sum(probs * prob_grad, axis=-1, keepdims=True)
    score_grad = (probs * (prob_grad - row_dot)).astype(bf16)
    query_rot_grad = (
        jnp.einsum("thu,ud->thd", score_grad, key_rows, preferred_element_type=f32) * scaling
    )
    key_part = (
        jnp.einsum("thu,thd->ud", score_grad, query_heads, preferred_element_type=f32) * scaling
    )
    value_part = jnp.einsum("thu,thd->ud", probs_low, heads_grad, preferred_element_type=f32)
    pair_grad = ring_scatter([key_part, value_part], 4)
    attended_rows, early_both, pair_grad = lax.optimization_barrier(
        (jnp.concatenate([attended, lora_qkv], axis=1), early_both, pair_grad)
    )
    attended_all = gather_rows(attended_rows)
    query_grad = rotate(
        query_rot_grad.reshape(tokens_dev, QUERY_WIDTH), position_own, -1.0
    ).astype(bf16)
    key_grad = rotate(pair_grad[:, :HEAD_WIDTH], position_own, -1.0).astype(bf16)
    value_grad = pair_grad[:, HEAD_WIDTH:].astype(bf16)
    proj_grad = jnp.concatenate([query_grad, key_grad, value_grad], axis=1)
    lora_qkv_grad = jnp.concatenate(
        [
            times_transposed(query_grad, widen_query),
            times_transposed(key_grad, widen_key),
            times_transposed(value_grad, widen_value),
        ],
        axis=1,
    ).astype(bf16)
    normed_grad = times_transposed(proj_grad, proj_in) + times_transposed(
        lora_qkv_grad, narrow_projection
    )
    weighted_one = gains[0] * normed_grad
    input_grad = (
        middle_grad
        + scale_one * weighted_one
        - hidden_state
        * scale_one**3
        * jnp.mean(hidden_state * weighted_one, axis=-1, keepdims=True)
    )
    gain_one = jnp.sum(normed_grad * hidden_state * scale_one, axis=0)

    lora_qkv_all = attended_all[:, QUERY_WIDTH:]
    normed_turn, branch_turn = turn(normalized), turn(branch_grad)
    out_piece = outer_product_rows(branch_turn, lora_out_all)
    gain_rows = jnp.stack([gain_one, gain_two]).astype(bf16).reshape(tokens_dev, -1)
    gain_count = gain_rows.shape[1]
    gain_rows = jnp.pad(gain_rows, ((0, 0), (0, -gain_count % 128)))
    proj_rows = jnp.concatenate(
        [proj_grad, lora_out_grad, gate_low, up_low, lora_hd, gain_rows], axis=1
    )
    proj_rows, normed_turn, branch_turn, up_share = lax.optimization_barrier(
        (proj_rows, normed_turn, branch_turn, up_share)
    )
    up_both = loop_shares(up_share)
    proj_all, middle_own = share_rows(
        proj_rows, jnp.concatenate([out_piece, gate_piece, up_piece], axis=0).astype(bf16), 5
    )
    column = place * width_own
    gain_all = proj_all[:, PROJECT_COLUMNS + 4 * rank :][:, :gain_count].reshape(size, 2, MODEL_WIDTH)
    gain_all = jnp.sum(gain_all.astype(f32), axis=0)
    gain_own = lax.dynamic_slice_in_dim(gain_all, column, width_own, 1)
    gain_part = jnp.pad(gain_own, ((0, width_own - 2), (0, -width_own % 128)))
    attn_part = jnp.concatenate(
        [
            outer_product_rows(normed_turn, proj_all[:, :PROJECT_COLUMNS]),
            outer_product_rows(branch_turn, attended_all)[:, :QUERY_WIDTH],
            gain_part,
        ],
        axis=1,
    ).astype(bf16)
    attn_part, up_both, proj_all = lax.optimization_barrier((attn_part, up_both, proj_all))
    attn_sum = both_loops(loop_shares(attn_part))
    gain_column = PROJECT_COLUMNS + QUERY_WIDTH
    gain_sum = attn_sum[:2, gain_column : gain_column + width_own]
    low_all = proj_all[:, PROJECT_COLUMNS : PROJECT_COLUMNS + 4 * rank]
    proj_all = proj_all[:, :PROJECT_COLUMNS]
    qkv_low_all = jnp.concatenate(
        [
            times_transposed(proj_all[:, :QUERY_WIDTH], widen_query),
            times_transposed(proj_all[:, QUERY_WIDTH : QUERY_WIDTH + HEAD_WIDTH], widen_key),
            times_transposed(proj_all[:, QUERY_WIDTH + HEAD_WIDTH :], widen_value),
        ],
        axis=1,
    ).astype(bf16)
    attended_turn = lax.dynamic_slice_in_dim(attended_all, column, width_own, 1)
    two_turn = lax.dynamic_slice_in_dim(two_all, column, width_own, 1)
    squeeze_own = jnp.concatenate(
        [
            outer_product_rows(normed_turn, qkv_low_all),
            outer_product_rows(attended_turn, low_all[:, :rank]),
            outer_product_rows(two_turn, low_all[:, rank : 3 * rank]),
        ],
        axis=1,
    )
    near = jnp.concatenate(
        [
            outer_product_rows(proj_all[:, :QUERY_WIDTH], lora_qkv_all[:, :rank]),
            outer_product_rows(
                proj_all[:, QUERY_WIDTH : QUERY_WIDTH + HEAD_WIDTH], lora_qkv_all[:, rank : 2 * rank]
            ),
            outer_product_rows(proj_all[:, QUERY_WIDTH + HEAD_WIDTH :], lora_qkv_all[:, 2 * rank :]),
        ],
        axis=0,
    )
    far = outer_product_rows(grad_all, low_all[:, 3 * rank :])
    first = place * columns_own
    far_start = GATE_START + 2 * HIDDEN_COUNT
    near = lax.dynamic_slice_in_dim(
        jnp.pad(near.astype(bf16), ((0, columns_own), (0, 0))), jnp.minimum(first, PROJECT_COLUMNS), columns_own, 0
    )
    far = lax.dynamic_slice_in_dim(
        jnp.pad(far.astype(bf16), ((columns_own, 0), (0, 0))),
        jnp.maximum(first - far_start + columns_own, 0),
        columns_own,
        0,
    )
    owned = first + jnp.arange(columns_own, dtype=jnp.int32)[:, None]
    expand_own = jnp.where(
        owned < PROJECT_COLUMNS, near, jnp.where(owned < far_start, middle_own, far)
    ).T.astype(f32)
    ffn_sum = sum_loops(early_both, up_both).transpose(1, 0, 2)
    return (
        hidden_out[None],
        input_grad[None],
        gain_sum,
        attn_sum[:, :PROJECT_COLUMNS],
        attn_sum[:, PROJECT_COLUMNS:gain_column],
        ffn_sum,
        squeeze_own[None],
        expand_own[None],
        down_own[None],
    )


def solution(mesh):
    return jax.shard_map(
        per_device,
        mesh=mesh,
        in_specs=(
            P("loop", "fsdp", None),
            P("loop", None),
            P(),
            P("fsdp", None),
            P("fsdp", None),
            P("fsdp", None, None),
            P("loop", None, None),
            P("loop", None, None),
            P("loop", None, None),
            P("loop", "fsdp", None),
        ),
        out_specs=(
            P("loop", "fsdp", None),
            P("loop", "fsdp", None),
            P(None, "fsdp"),
            P("fsdp", None),
            P("fsdp", None),
            P("fsdp", None, None),
            P("loop", "fsdp", None),
            P("loop", None, "fsdp"),
            P("loop", "fsdp", None),
        ),
        check_vma=False,
    )
```

```python
import functools
import math

import jax
import jax.numpy as jnp
from jax import lax
from jax.experimental import pallas as pl
from jax.experimental.pallas import tpu as pltpu
from jax.sharding import PartitionSpec as P

MODEL_WIDTH = 2048
HEADS = 8
HEAD_WIDTH = 256
HIDDEN_COUNT = 16384
ADAPTER_RANK = 256
QUERY_WIDTH = 2048
PROJECT_COLUMNS = 2560
ADAPTER_COLUMNS = 39424
GATE_START = PROJECT_COLUMNS + MODEL_WIDTH

epsilon = 1e-06
bf16 = jnp.bfloat16
f32 = jnp.float32
MESH = pl.DeviceIdType.MESH


def matrix_product(former, latter):
    return jnp.dot(former, latter, preferred_element_type=f32)


def times_transposed(former, latter):
    return lax.dot_general(former, latter, (((1,), (1,)), ((), ())), preferred_element_type=f32)


def outer_product_rows(former, latter):
    return lax.dot_general(former, latter, (((0,), (0,)), ((), ())), preferred_element_type=f32)


def segment_info(lengths, row_count):
    row_ids = jnp.arange(row_count, dtype=jnp.int32)
    count = lengths.shape[0]
    labels = jnp.arange(count, dtype=jnp.int32)
    finish = jnp.sum(jnp.where(labels[:, None] <= labels[None, :], lengths[:, None], 0), axis=0)
    starts = finish - lengths
    segment = jnp.sum((row_ids[:, None] >= finish[None, :]).astype(jnp.int32), axis=1)
    opening = jnp.sum(jnp.where(segment[:, None] == labels[None, :], starts[None, :], 0), axis=1)
    return (segment, row_ids - opening)


def rotate(values, position, direction):
    half_dim = HEAD_WIDTH // 2
    frequency = jnp.exp(
        jnp.arange(half_dim).astype(f32) * (-2.0 * math.log(10000.0) / HEAD_WIDTH)
    )
    angles = position.astype(f32)[:, None] * frequency[None, :]
    cosine = jnp.cos(angles)[:, None, :]
    sine_val = direction * jnp.sin(angles)[:, None, :]
    shaped = values.reshape(values.shape[0], -1, HEAD_WIDTH)
    former = shaped[..., :half_dim]
    latter = shaped[..., half_dim:]
    turned = jnp.concatenate(
        [former * cosine - latter * sine_val, latter * cosine + former * sine_val], axis=-1
    )
    return turned.reshape(values.shape)


def rms_scale(values):
    return lax.rsqrt(jnp.mean(values * values, axis=-1, keepdims=True) + epsilon)


def gelu_tanh(values):
    return jax.nn.gelu(values, approximate=True)


def unit_backward(gate_value, upward_activation, hidden_unit_gradient):
    activated, pullback_function = jax.vjp(gelu_tanh, gate_value)
    gate_grad = pullback_function(hidden_unit_gradient * upward_activation)[0]
    return (gate_grad.astype(bf16), (hidden_unit_gradient * activated).astype(bf16))


def scores_of(query_heads, key_rows, allowed, scaling):
    product = (
        jnp.einsum("thd,ud->thu", query_heads, key_rows, preferred_element_type=f32) * scaling
    )
    return jnp.where(allowed[:, None, :], product, -1e30)


def gather_rows(block):
    return lax.all_gather(block, "fsdp", axis=0, tiled=True)


def scatter_rows(partial):
    return lax.psum_scatter(partial.astype(bf16), "fsdp", scatter_dimension=0, tiled=True).astype(f32)


def loop_shares(partial):
    return lax.all_gather(partial.astype(bf16), "loop", axis=0)


def both_loops(shares):
    return shares[0].astype(f32) + shares[1].astype(f32)


def sum_kernel(early_ref, up_ref, o_ref):
    @pl.when(pl.program_id(0) != 1)
    def _():
        o_ref[0] = early_ref[0, 0].astype(f32) + early_ref[1, 0].astype(f32)

    @pl.when(pl.program_id(0) == 1)
    def _():
        o_ref[0] = up_ref[0].astype(f32) + up_ref[1].astype(f32)


def sum_loops(early, up):
    _, rows, columns = up.shape
    tile = min(rows, 256)
    steps = rows // tile
    return pl.pallas_call(
        sum_kernel,
        grid=(3, steps),
        out_shape=jax.ShapeDtypeStruct((3, rows, columns), f32),
        in_specs=[
            pl.BlockSpec(
                (2, 1, tile, columns),
                lambda i, j: (0, i // 2, jnp.where(i == 1, steps - 1, j), 0),
            ),
            pl.BlockSpec(
                (2, tile, columns),
                lambda i, j: (0, jnp.where(i == 1, j, jnp.where(i < 1, 0, steps - 1)), 0),
            ),
        ],
        out_specs=pl.BlockSpec((1, tile, columns), lambda i, j: (i, j, 0)),
        compiler_params=pltpu.CompilerParams(vmem_limit_bytes=32 << 20),
        cost_estimate=busy(17),
        name="sum_loops",
    )(early, up)


def turn(block):
    return lax.all_to_all(block, "fsdp", split_axis=1, concat_axis=0, tiled=True)


def chip_at(q, chips):
    return jnp.where(q < 4, 2 * q, 15 - 2 * q) if chips == 8 else q

def ring_place(chip, chips):
    return jnp.where(chip % 2 == 0, chip // 2, 7 - chip // 2) if chips == 8 else chip

def ring_neighbours(chips):
    me = lax.axis_index("fsdp")
    core = me % 2
    p = ring_place(me // 2, chips)
    def device(shift, c):
        return chip_at((p + shift + chips) % chips, chips) * 2 + c
    return core, device

def meet(devices):
    barrier = pltpu.get_barrier_semaphore()
    for d in devices:
        pl.semaphore_signal(barrier, inc=1, device_id={"fsdp": d}, device_id_type=MESH)
    pl.semaphore_wait(barrier, len(devices))

def gather_kernel(chips, x_ref, o_ref, own_sem, ring_send, ring_recv, side_send, side_recv, greet=None, also=None):
    core, device = ring_neighbours(chips)
    rows = x_ref.shape[0]
    reach = chips // 2
    ways = (device(1, core), device(-1, core))
    side = device(0, 1 - core)
    if greet is None:
        meet((*ways, side))
    else:
        greet()

    def span(way, hops):
        return (way * (rows // 2), rows // 2) if hops == reach else (0, rows)

    def at(way, hops, c, part):
        origin = device(-hops if way == 0 else hops, c)
        return o_ref.at[pl.ds(pl.multiple_of(origin * rows + part[0], 8), part[1])]

    def hop(way, hops):
        part = span(way, hops)
        here = at(way, hops - 1, core, part)
        src = x_ref.at[pl.ds(part[0], part[1])] if hops == 1 else here
        return pltpu.make_async_remote_copy(src, here, ring_send.at[way, hops - 1], ring_recv.at[way, hops - 1], device_id={"fsdp": ways[way]}, device_id_type=MESH)

    def arriving(way, hops):
        here = at(way, hops, core, span(way, hops))
        return pltpu.make_async_remote_copy(here, here, ring_send.at[way, hops - 1], ring_recv.at[way, hops - 1], device_id={"fsdp": ways[way]}, device_id_type=MESH)

    def across(way, hops, c):
        part = span(way, hops) if hops else (0, rows)
        there = at(way, hops, c, part)
        src = there if hops else x_ref
        return pltpu.make_async_remote_copy(src, there, side_send.at[way, hops], side_recv.at[way, hops], device_id={"fsdp": side}, device_id_type=MESH)

    for way in (0, 1):
        hop(way, 1).start()
    across(0, 0, core).start()
    own = pltpu.make_async_copy(x_ref, at(0, 0, core, (0, rows)), own_sem)
    own.start()
    if also is not None:
        also()
    for hops in range(1, reach + 1):
        for way in (0, 1):
            arriving(way, hops).wait_recv()
            if hops < reach:
                hop(way, hops + 1).start()
            across(way, hops, core).start()
    across(0, 0, 1 - core).wait_recv()
    across(0, 0, core).wait_send()
    for hops in range(1, reach + 1):
        for way in (0, 1):
            across(way, hops, 1 - core).wait_recv()
            across(way, hops, core).wait_send()
            hop(way, hops).wait_send()
    own.wait()

def busy(us):
    return pl.CostEstimate(flops=0, bytes_accessed=int(us * 3.0e6), transcendentals=0)


def ring_gather(block, ident):
    size = lax.axis_size("fsdp")
    chips = size // 2
    rows, columns = block.shape
    pair = pltpu.SemaphoreType.DMA((2, chips // 2))
    sides = pltpu.SemaphoreType.DMA((2, chips // 2 + 1))
    return pl.pallas_call(
        functools.partial(gather_kernel, chips),
        out_shape=jax.ShapeDtypeStruct((size * rows, columns), block.dtype),
        in_specs=[pl.BlockSpec(memory_space=pl.ANY)],
        out_specs=pl.BlockSpec(memory_space=pl.ANY),
        scratch_shapes=[pltpu.SemaphoreType.DMA, pair, pair, sides, sides],
        compiler_params=pltpu.CompilerParams(collective_id=ident, has_side_effects=True),
        cost_estimate=busy(1),
        name="ring_gather",
    )(block)

def scatter_kernel(chips, count, *refs):
    x_refs, o_ref = refs[:count], refs[count]
    side_buf, ring_buf, side_send, side_recv, ring_send, ring_recv = refs[count + 1 :]
    core, device = ring_neighbours(chips)
    rows, columns = o_ref.shape
    reach = chips // 2
    half = columns // 2
    tile = 16
    ways = (device(1, core), device(-1, core))
    side = device(0, 1 - core)
    meet((*ways, side))
    starts = [sum(x.shape[1] for x in x_refs[:i]) for i in range(count)]

    def shift(way, hops):
        return (hops if way == 0 else chips - hops) % chips

    def across(target, c, i):
        there = pl.ds(pl.multiple_of(device(target, c) * rows, tile), rows)
        return pltpu.make_async_remote_copy(
            x_refs[i].at[there],
            side_buf.at[target, :, pl.ds(starts[i], x_refs[i].shape[1])],
            side_send.at[target, i],
            side_recv.at[target, i],
            device_id={"fsdp": side},
            device_id_type=MESH,
        )

    def hop(way, step):
        cols = pl.ds(way * half, half) if step == 0 else pl.ds(0, columns)
        return pltpu.make_async_remote_copy(
            side_buf.at[shift(way, reach - step), :, cols],
            ring_buf.at[way, step, :, cols],
            ring_send.at[way, step],
            ring_recv.at[way, step],
            device_id={"fsdp": ways[way]},
            device_id_type=MESH,
        )

    order = [reach] + [shift(way, hops) for hops in range(reach - 1, 0, -1) for way in (0, 1)] + [0]
    for target in order:
        for i in range(count):
            across(target, 1 - core, i).start()

    def add(target, incoming, store):
        first = pl.multiple_of(device(target, core) * rows, tile)
        for i in range(count):
            across(target, core, i).wait_recv()

        @pl.loop(0, rows // tile)
        def _(j):
            here = pl.ds(pl.multiple_of(j * tile, tile), tile)
            mine = pl.ds(pl.multiple_of(first + j * tile, tile), tile)
            for i in range(count):
                cols = pl.ds(starts[i], x_refs[i].shape[1])
                total = x_refs[i][mine, :].astype(f32) + side_buf[target, here, cols].astype(f32)
                for way, step in incoming:
                    if step:
                        total = total + ring_buf[way, step, here, cols].astype(f32)
                store(here, cols, total)
            for way, step in incoming:
                if not step:
                    cols = pl.ds(way * half, half)
                    store(
                        here,
                        cols,
                        side_buf[target, here, cols].astype(f32) + ring_buf[way, 0, here, cols].astype(f32),
                    )

    for step in range(reach):
        for way in (0, 1):
            target = shift(way, reach - step)
            if step:
                hop(way, step - 1).wait_recv()

            def store(here, cols, total, target=target):
                side_buf[target, here, cols] = total.astype(bf16)

            if step or way == 0:
                add(target, [(way, step - 1)] if step else [], store)
            hop(way, step).start()
    for way in (0, 1):
        hop(way, reach - 1).wait_recv()

    def last(here, cols, total):
        o_ref[here, cols] = total

    add(0, [(0, reach - 1), (1, reach - 1)], last)
    for target in order:
        for i in range(count):
            across(target, 1 - core, i).wait_send()
    for step in range(reach):
        for way in (0, 1):
            hop(way, step).wait_send()


def ring_scatter(terms, ident):
    size = lax.axis_size("fsdp")
    terms = [term.astype(bf16) for term in terms]
    if size != 16:
        return scatter_rows(jnp.concatenate(terms, axis=1))
    chips, count = size // 2, len(terms)
    rows, columns = terms[0].shape[0] // size, sum(term.shape[1] for term in terms)
    pair = pltpu.SemaphoreType.DMA((2, chips // 2))
    sides = pltpu.SemaphoreType.DMA((chips, count))
    return pl.pallas_call(
        functools.partial(scatter_kernel, chips, count),
        out_shape=jax.ShapeDtypeStruct((rows, columns), f32),
        in_specs=[pl.BlockSpec(memory_space=pltpu.VMEM)] * count,
        out_specs=pl.BlockSpec(memory_space=pltpu.VMEM),
        scratch_shapes=[
            pltpu.VMEM((chips, rows, columns), bf16),
            pltpu.VMEM((2, chips // 2, rows, columns), bf16),
            sides,
            sides,
            pair,
            pair,
        ],
        compiler_params=pltpu.CompilerParams(
            collective_id=ident, has_side_effects=True, vmem_limit_bytes=56 << 20
        ),
        cost_estimate=busy(1),
        name="ring_scatter",
    )(*terms)


def unit_kernel(chips, *refs):
    sources, (planes, squeeze, widen_down, widen_gate, widen_up, narrow) = refs[:2], refs[2:8]
    two_all, grad_all, acts_all, low_all, early_out, up_out, piece_out, down_out = refs[8:16]
    held, turned, acts, low, tiles, landed = refs[16], refs[17], refs[18], refs[19], refs[20], refs[21:23]
    held_sem, own_sem, ring_send, ring_recv, side_send, side_recv, out_sem, acts_sem, tile_sem = refs[23:]
    core, device = ring_neighbours(chips)
    rows = sources[0].shape[0]
    reach = chips // 2
    wide = 256
    ways = (device(1, core), device(-1, core))
    side = device(0, 1 - core)
    fetches = [pltpu.make_async_copy(planes.at[i], held.at[i], held_sem.at[i]) for i in range(3)]
    for fetch in fetches:
        fetch.start()
    meet((*ways, side))

    def span(way, hops):
        return (way * (rows // 2), rows // 2) if hops == reach else (0, rows)

    def at(i, way, hops, c, part):
        origin = device(-hops if way == 0 else hops, c)
        return landed[i].at[pl.ds(pl.multiple_of(origin * rows + part[0], 16), part[1])]

    def hop(i, way, hops):
        part = span(way, hops)
        here = at(i, way, hops - 1, core, part)
        src = sources[i].at[pl.ds(part[0], part[1])] if hops == 1 else here
        return pltpu.make_async_remote_copy(
            src,
            here,
            ring_send.at[i, way, hops - 1],
            ring_recv.at[i, way, hops - 1],
            device_id={"fsdp": ways[way]},
            device_id_type=MESH,
        )

    def arriving(i, way, hops):
        here = at(i, way, hops, core, span(way, hops))
        return pltpu.make_async_remote_copy(
            here,
            here,
            ring_send.at[i, way, hops - 1],
            ring_recv.at[i, way, hops - 1],
            device_id={"fsdp": ways[way]},
            device_id_type=MESH,
        )

    def across(i, way, hops, c):
        part = span(way, hops) if hops else (0, rows)
        there = at(i, way, hops, c, part)
        return pltpu.make_async_remote_copy(
            there if hops else sources[i],
            there,
            side_send.at[i, way, hops],
            side_recv.at[i, way, hops],
            device_id={"fsdp": side},
            device_id_type=MESH,
        )

    def leaving(n, first):
        mine = pl.ds(first, 2 * rows)
        width, under = grad_all.shape[1], low.shape[1]
        pairs = [
            (landed[0].at[mine, pl.ds(0, width)], two_all.at[mine]),
            (landed[0].at[mine, pl.ds(width, ADAPTER_RANK)], low_all.at[mine, pl.ds(under, ADAPTER_RANK)]),
            (low.at[mine], low_all.at[mine, pl.ds(0, under)]),
            (landed[1].at[mine], grad_all.at[mine]),
        ]
        return [pltpu.make_async_copy(a, b, out_sem.at[n, i]) for i, (a, b) in enumerate(pairs)]

    def shown(n, first):
        mine = pl.ds(first, 2 * rows)
        return [
            pltpu.make_async_copy(acts.at[n % 2, i], acts_all.at[i, mine], acts_sem.at[n % 2, i]) for i in range(3)
        ]

    def first_row(shift):
        return pl.multiple_of(device(shift, 0) * rows, 2 * rows)

    def work(n, first):
        mine = pl.ds(first, 2 * rows)
        rank, width = ADAPTER_RANK, MODEL_WIDTH
        if n >= 2:
            for copy in shown(n, first):
                copy.wait()
        low[mine, : 2 * rank] = matrix_product(landed[0][mine, :width], squeeze[...]).astype(bf16)
        low[mine, 2 * rank :] = times_transposed(landed[1][mine, :], widen_down[...]).astype(bf16)

        @pl.loop(0, held.shape[1] // wide)
        def _(t):
            own = pl.ds(pl.multiple_of(t * wide, wide), wide)
            two = landed[0][mine, :width]
            gate = times_transposed(two, held[0, own, :]) + matrix_product(
                low[mine, :rank], widen_gate[:, own]
            )
            upward = times_transposed(two, held[1, own, :]) + matrix_product(
                low[mine, rank : 2 * rank], widen_up[:, own]
            )
            pull = times_transposed(landed[1][mine, :], held[2, own, :]) + times_transposed(
                low[mine, 2 * rank :], narrow[own, :]
            )
            scale = math.sqrt(2.0 / math.pi)
            square = gate * gate
            bend = jnp.tanh(scale * gate * (1.0 + 0.044715 * square))
            rise = 0.5 * (1.0 + bend)
            active = gate * rise
            slope = rise + 0.5 * gate * (1.0 - bend * bend) * (scale * (1.0 + 3 * 0.044715 * square))
            for i, value in enumerate((pull * upward * slope, pull * active, active * upward)):
                acts[n % 2, i, :, own] = value.astype(bf16)
                turned[i, own, mine] = value.T.astype(bf16)

        for copy in leaving(n, first) + shown(n, first):
            copy.start()

    for i in (0, 1):
        for way in (0, 1):
            hop(i, way, 1).start()
        across(i, 0, 0, core).start()
    keeps = [
        pltpu.make_async_copy(sources[i], at(i, 0, 0, core, (0, rows)), own_sem.at[i]) for i in (0, 1)
    ]
    for keep in keeps:
        keep.start()
    for copy in keeps + fetches:
        copy.wait()
    for i in (0, 1):
        across(i, 0, 0, 1 - core).wait_recv()
    work(0, first_row(0))
    for hops in range(1, reach + 1):
        for i in (0, 1):
            for way in (0, 1):
                arriving(i, way, hops).wait_recv()
                if hops < reach:
                    hop(i, way, hops + 1).start()
                across(i, way, hops, core).start()
        if hops < reach:
            for way in (0, 1):
                for i in (0, 1):
                    across(i, way, hops, 1 - core).wait_recv()
                work(2 * hops - 1 + way, first_row(-hops if way == 0 else hops))
    for way in (0, 1):
        for i in (0, 1):
            across(i, way, reach, 1 - core).wait_recv()
    work(2 * reach - 1, first_row(reach))
    rank = ADAPTER_RANK
    for kind, out in ((0, early_out.at[0]), (2, early_out.at[1]), (1, up_out)):

        def tile_copy(t, out=out):
            there = pl.ds(pl.multiple_of(t * wide, wide), wide)
            return pltpu.make_async_copy(tiles.at[t % 2], out.at[:, there], tile_sem.at[t % 2])

        @pl.loop(0, MODEL_WIDTH // wide)
        def _(t, kind=kind, tile_copy=tile_copy):
            @pl.when(t > 1)
            def _():
                tile_copy(t - 2).wait()

            cols = pl.ds(pl.multiple_of(t * wide, wide), wide)
            tiles[t % 2] = matrix_product(
                turned[kind], landed[1 if kind == 2 else 0][:, cols]
            ).astype(bf16)
            tile_copy(t).start()

        if kind == 2:
            piece_out[0] = matrix_product(turned[0], low[:, :rank]).astype(bf16)
            piece_out[1] = matrix_product(turned[1], low[:, rank : 2 * rank]).astype(bf16)
            down_out[...] = matrix_product(turned[2], low[:, 2 * rank :])
        tile_copy(MODEL_WIDTH // wide - 2).wait()
        tile_copy(MODEL_WIDTH // wide - 1).wait()
    for i in (0, 1):
        across(i, 0, 0, core).wait_send()
        for hops in range(1, reach + 1):
            for way in (0, 1):
                across(i, way, hops, core).wait_send()
                hop(i, way, hops).wait_send()
    for n in range(chips):
        if n == 0:
            shift = 0
        elif n == 2 * reach - 1:
            shift = reach
        else:
            shift = (-1 if n % 2 else 1) * ((n + 1) // 2)
        for copy in leaving(n, first_row(shift)):
            copy.wait()
        if n >= chips - 2:
            for copy in shown(n, first_row(shift)):
                copy.wait()


def unit_rows(two, grad, planes, squeeze, widen_down, widen_gate, widen_up, narrow, ident):
    size = lax.axis_size("fsdp")
    rank = ADAPTER_RANK
    if size != 16:
        two, grad = gather_rows(two), gather_rows(grad)
        two, lora_out = two[:, :MODEL_WIDTH], two[:, MODEL_WIDTH:]
        low = matrix_product(two, squeeze).astype(bf16)
        pulled = times_transposed(grad, widen_down).astype(bf16)
        gate = times_transposed(two, planes[0]) + matrix_product(low[:, :rank], widen_gate)
        upward = times_transposed(two, planes[1]) + matrix_product(low[:, rank:], widen_up)
        units_grad = times_transposed(grad, planes[2]) + times_transposed(pulled, narrow)
        units = (gelu_tanh(gate) * upward).astype(bf16)
        gate_grad, up_grad = unit_backward(gate, upward, units_grad)
        return (
            two,
            grad,
            jnp.stack([gate_grad, up_grad, units]),
            jnp.concatenate([low, pulled, lora_out], axis=1),
            jnp.stack([outer_product_rows(gate_grad, two), outer_product_rows(units, grad)]).astype(bf16),
            outer_product_rows(up_grad, two).astype(bf16),
            jnp.stack(
                [outer_product_rows(gate_grad, low[:, :rank]), outer_product_rows(up_grad, low[:, rank:])]
            ).astype(bf16),
            outer_product_rows(units, pulled),
        )
    chips = size // 2
    rows, columns = grad.shape
    all_rows, hidden = size * rows, planes.shape[1]
    anywhere, inside = pl.BlockSpec(memory_space=pl.ANY), pl.BlockSpec(memory_space=pltpu.VMEM)
    pair = pltpu.SemaphoreType.DMA((2, 2, chips // 2))
    sides = pltpu.SemaphoreType.DMA((2, 2, chips // 2 + 1))
    return pl.pallas_call(
        functools.partial(unit_kernel, chips),
        out_shape=(
            jax.ShapeDtypeStruct((all_rows, columns), bf16),
            jax.ShapeDtypeStruct((all_rows, columns), bf16),
            jax.ShapeDtypeStruct((3, all_rows, hidden), bf16),
            jax.ShapeDtypeStruct((all_rows, 4 * rank), bf16),
            jax.ShapeDtypeStruct((2, hidden, columns), bf16),
            jax.ShapeDtypeStruct((hidden, columns), bf16),
            jax.ShapeDtypeStruct((2, hidden, rank), bf16),
            jax.ShapeDtypeStruct((hidden, rank), f32),
        ),
        in_specs=[anywhere] * 3 + [inside] * 5,
        out_specs=(anywhere,) * 6 + (inside,) * 2,
        scratch_shapes=[
            pltpu.VMEM(planes.shape, bf16),
            pltpu.VMEM((3, hidden, all_rows), bf16),
            pltpu.VMEM((2, 3, 2 * rows, hidden), bf16),
            pltpu.VMEM((all_rows, 3 * rank), bf16),
            pltpu.VMEM((2, hidden, 256), bf16),
            pltpu.VMEM((all_rows, two.shape[1]), bf16),
            pltpu.VMEM((all_rows, columns), bf16),
            pltpu.SemaphoreType.DMA((3,)),
            pltpu.SemaphoreType.DMA((2,)),
            pair,
            pair,
            sides,
            sides,
            pltpu.SemaphoreType.DMA((chips, 4)),
            pltpu.SemaphoreType.DMA((2, 3)),
            pltpu.SemaphoreType.DMA((2,)),
        ],
        compiler_params=pltpu.CompilerParams(
            collective_id=ident, has_side_effects=True, vmem_limit_bytes=60 << 20
        ),
        cost_estimate=busy(100),
        name="unit_rows",
    )(two, grad, planes, squeeze, widen_down, widen_gate, widen_up, narrow)


def mix_kernel(chips, *refs):
    acts_ref, planes, gate_b, up_b, down_a, o_ref = refs[:6]
    acts, held, side_buf, ring_buf, stage, mine = refs[6:12]
    held_sem, side_send, side_recv, ring_send, ring_recv = refs[12:]
    fetches = [pltpu.make_async_copy(planes.at[i], held.at[i], held_sem.at[0, i]) for i in range(3)]
    fetches += [pltpu.make_async_copy(acts_ref.at[i], acts.at[i], held_sem.at[1, i]) for i in range(3)]
    for fetch in fetches:
        fetch.start()
    core, device = ring_neighbours(chips)
    rows, columns = o_ref.shape
    reach = chips // 2
    half = columns // 2
    tile = 16
    wide = 256
    ways = (device(1, core), device(-1, core))
    side = device(0, 1 - core)
    meet((*ways, side))
    order = [(reach, 0, 0)]
    for step in range(1, reach):
        order += [(reach - step, 0, step), (chips - reach + step, 1, step)]
    order.append((0, 0, reach))

    def across(i):
        target = order[i][0]
        return pltpu.make_async_remote_copy(
            stage.at[i % 2],
            side_buf.at[target],
            side_send.at[target],
            side_recv.at[target],
            device_id={"fsdp": side},
            device_id_type=MESH,
        )

    def hop(way, step, part):
        target = (reach - step if way == 0 else chips - reach + step) % chips
        cols = pl.ds(way * half, half) if step == 0 else pl.ds(0, columns)
        here = pl.ds(part * (rows // 2), rows // 2)
        return pltpu.make_async_remote_copy(
            side_buf.at[target, here, cols],
            ring_buf.at[way, step, here, cols],
            ring_send.at[way, step, part],
            ring_recv.at[way, step, part],
            device_id={"fsdp": ways[way]},
            device_id_type=MESH,
        )

    def make(i):
        target, slot = order[i][0], i % 2
        if i >= 2:
            across(i - 2).wait_send()
        theirs = pl.ds(pl.multiple_of(device(target, 1 - core) * rows, rows), rows)
        ours = pl.ds(pl.multiple_of(device(target, core) * rows, rows), rows)

        def block(kind):
            return jnp.concatenate([acts[kind, theirs, :], acts[kind, ours, :]], axis=0)

        def put(first, value):
            cols = pl.ds(pl.multiple_of(first, wide), wide)
            stage[slot, :, cols] = value[:rows].astype(bf16)
            mine[slot, :, cols] = value[rows:].astype(bf16)

        @pl.loop(0, MODEL_WIDTH // wide)
        def _(t):
            cols = pl.ds(pl.multiple_of(t * wide, wide), wide)
            put(
                t * wide,
                matrix_product(block(0), held[0, :, cols])
                + matrix_product(block(1), held[1, :, cols]),
            )
            put(
                MODEL_WIDTH + 2 * ADAPTER_RANK + t * wide,
                matrix_product(block(2), held[2, :, cols]),
            )

        put(MODEL_WIDTH, times_transposed(block(0), gate_b[...]))
        put(MODEL_WIDTH + ADAPTER_RANK, times_transposed(block(1), up_b[...]))
        put(2 * MODEL_WIDTH + 2 * ADAPTER_RANK, matrix_product(block(2), down_a[...]))
        across(i).start()

    def add(i):
        target, way, step = order[i]
        last = target == 0
        incoming = [(w, step - 1) for w in ((0, 1) if last else (way,))] if step else []
        across(i).wait_recv()
        for part in (0, 1):
            for w, s in incoming:
                hop(w, s, part).wait_recv()

            @pl.loop(0, rows // 2 // tile)
            def _(j, part=part):
                here = pl.ds(pl.multiple_of(part * (rows // 2) + j * tile, tile), tile)
                for side_half in (0, 1):
                    cols = pl.ds(side_half * half, half)
                    total = mine[i % 2, here, cols].astype(f32) + side_buf[target, here, cols].astype(f32)
                    for w, s in incoming:
                        if s or w == side_half:
                            total = total + ring_buf[w, s, here, cols].astype(f32)
                    if last:
                        o_ref[here, cols] = total
                    else:
                        side_buf[target, here, cols] = total.astype(bf16)

            if not last:
                hop(way, step, part).start()
                if step == 0:
                    hop(1, 0, part).start()

    for fetch in fetches:
        fetch.wait()
    make(0)
    add(0)
    make(1)
    for i in range(1, len(order)):
        if i + 1 < len(order):
            make(i + 1)
        add(i)
    for i in range(len(order) - 2, len(order)):
        across(i).wait_send()
    for step in range(reach):
        for way in (0, 1):
            for part in (0, 1):
                hop(way, step, part).wait_send()


def mix_rows(acts, planes, gate_b, up_b, down_a, ident):
    size = lax.axis_size("fsdp")
    if size != 16:
        gate_grad, up_grad, units = acts[0], acts[1], acts[2]
        terms = [
            matrix_product(gate_grad, planes[0]) + matrix_product(up_grad, planes[1]),
            times_transposed(gate_grad, gate_b),
            times_transposed(up_grad, up_b),
            matrix_product(units, planes[2]),
            matrix_product(units, down_a),
        ]
        return scatter_rows(jnp.concatenate(terms, axis=1))
    chips = size // 2
    rows, columns = acts.shape[1] // size, 2 * MODEL_WIDTH + 3 * ADAPTER_RANK
    pair = pltpu.SemaphoreType.DMA((2, chips // 2, 2))
    sides = pltpu.SemaphoreType.DMA((chips,))
    return pl.pallas_call(
        functools.partial(mix_kernel, chips),
        out_shape=jax.ShapeDtypeStruct((rows, columns), f32),
        in_specs=[pl.BlockSpec(memory_space=pl.ANY)] * 2
        + [pl.BlockSpec(memory_space=pltpu.VMEM)] * 3,
        out_specs=pl.BlockSpec(memory_space=pltpu.VMEM),
        scratch_shapes=[
            pltpu.VMEM(acts.shape, bf16),
            pltpu.VMEM(planes.shape, bf16),
            pltpu.VMEM((chips, rows, columns), bf16),
            pltpu.VMEM((2, chips // 2, rows, columns), bf16),
            pltpu.VMEM((2, rows, columns), bf16),
            pltpu.VMEM((2, rows, columns), bf16),
            pltpu.SemaphoreType.DMA((2, 3)),
            sides,
            sides,
            pair,
            pair,
        ],
        compiler_params=pltpu.CompilerParams(
            collective_id=ident, has_side_effects=True, vmem_limit_bytes=60 << 20
        ),
        cost_estimate=busy(1),
        name="mix_rows",
    )(acts, planes, gate_b, up_b, down_a)


def share_kernel(size, chunk, own_count, x_ref, mid_ref, all_ref, o_ref, *sems):
    send_sem, recv_sem, own_sem = sems[5:]
    me = lax.axis_index("fsdp")
    hidden = HIDDEN_COUNT // size
    width = MODEL_WIDTH // size
    sections = (
        (0, PROJECT_COLUMNS, width),
        (width, GATE_START, hidden),
        (width + hidden, GATE_START + HIDDEN_COUNT, hidden),
    )

    def greet():
        barrier = pltpu.get_barrier_semaphore()

        def one(i, carry):
            pl.semaphore_signal(barrier, inc=1, device_id={"fsdp": (me + i) % size}, device_id_type=MESH)
            return carry

        lax.fori_loop(1, size, one, 0)
        pl.semaphore_wait(barrier, size - 1)

    def rows(ref, first):
        return ref.at[pl.ds(pl.multiple_of(first, 8), chunk)]

    def aim(start, length):
        owner = (start + me * length) // own_count
        return owner, start + me * length - owner * own_count

    def remote(source, first, owner, sent=0):
        return pltpu.make_async_remote_copy(
            source,
            rows(o_ref, first),
            send_sem.at[sent],
            recv_sem.at[first // chunk],
            device_id={"fsdp": owner},
            device_id_type=MESH,
        )

    def local(source, first):
        return pltpu.make_async_copy(source, rows(o_ref, first), own_sem.at[first // chunk])

    def send_all():
        for base, start, length in sections:

            def send(j, carry, base=base, aimed=aim(start, length)):
                over = (aimed[1] + j * chunk >= own_count).astype(jnp.int32)
                owner = aimed[0] + over
                first = aimed[1] + j * chunk - over * own_count
                source = rows(mid_ref, base + j * chunk)

                @pl.when(owner != me)
                def _():
                    remote(source, first, owner, base // chunk + j).start()

                @pl.when(owner == me)
                def _():
                    local(source, first).start()

                return carry

            lax.fori_loop(0, length // chunk, send, 0)

    gather_kernel(size // 2, x_ref, all_ref, *sems[:5], greet=greet, also=send_all)

    def arrive(j, carry):
        column = me * own_count + j * chunk
        here = rows(o_ref, j * chunk)
        away, kept = 0, 0
        for _, start, length in sections:
            mine = start + me * length
            inside = (column >= start) & (column < start + length * size)
            outside = (column < mine) | (column >= mine + length)
            away = away + (inside & outside).astype(jnp.int32)
            kept = kept + (inside & ~outside).astype(jnp.int32)

        @pl.when(away > 0)
        def _():
            remote(here, j * chunk, (me + 1) % size).wait_recv()

        @pl.when(kept > 0)
        def _():
            local(rows(mid_ref, 0), j * chunk).wait()

        return carry

    lax.fori_loop(0, own_count // chunk, arrive, 0)
    for base, start, length in sections:

        def sent(j, carry, base=base, aimed=aim(start, length)):
            over = (aimed[1] + j * chunk >= own_count).astype(jnp.int32)
            owner = aimed[0] + over
            first = aimed[1] + j * chunk - over * own_count

            @pl.when(owner != me)
            def _():
                remote(rows(mid_ref, base + j * chunk), first, owner, base // chunk + j).wait_send()

            return carry

        lax.fori_loop(0, length // chunk, sent, 0)


def share_rows(block, middle, ident):
    size = lax.axis_size("fsdp")
    rows, columns = block.shape
    own_count = ADAPTER_COLUMNS // size
    chunk = math.gcd(own_count, MODEL_WIDTH // size, HIDDEN_COUNT // size, PROJECT_COLUMNS, GATE_START)
    anywhere = pl.BlockSpec(memory_space=pl.ANY)
    pair = pltpu.SemaphoreType.DMA((2, size // 4))
    sides = pltpu.SemaphoreType.DMA((2, size // 4 + 1))
    return pl.pallas_call(
        functools.partial(share_kernel, size, chunk, own_count),
        out_shape=(
            jax.ShapeDtypeStruct((size * rows, columns), block.dtype),
            jax.ShapeDtypeStruct((own_count, ADAPTER_RANK), bf16),
        ),
        in_specs=[anywhere] * 2,
        out_specs=(anywhere, anywhere),
        scratch_shapes=[
            pltpu.SemaphoreType.DMA,
            pair,
            pair,
            sides,
            sides,
            pltpu.SemaphoreType.DMA((middle.shape[0] // chunk,)),
            pltpu.SemaphoreType.DMA((own_count // chunk,)),
            pltpu.SemaphoreType.DMA((own_count // chunk,)),
        ],
        compiler_params=pltpu.CompilerParams(collective_id=ident, has_side_effects=True),
        cost_estimate=busy(1),
        name="share_rows",
    )(block, middle)


def per_device(
    hidden_input,
    sequence_lengths,
    norm_gain_values,
    input_proj_weight,
    output_proj_weight,
    feedforward_weight,
    adapter_first,
    adapter_second,
    adapter_down_first,
    output_gradient,
):
    size = lax.axis_size("fsdp")
    place = lax.axis_index("fsdp")
    tokens_dev = hidden_input.shape[1]
    all_rows = tokens_dev * size
    hidden_own = HIDDEN_COUNT // size
    width_own = MODEL_WIDTH // size
    columns_own = ADAPTER_COLUMNS // size
    offset = place * tokens_dev
    segment_all, position_all = segment_info(sequence_lengths[0], all_rows)
    segment_own = lax.dynamic_slice_in_dim(segment_all, offset, tokens_dev)
    position_own = lax.dynamic_slice_in_dim(position_all, offset, tokens_dev)
    row_all = jnp.arange(all_rows, dtype=jnp.int32)
    row_own = offset + jnp.arange(tokens_dev, dtype=jnp.int32)
    allowed = (segment_own[:, None] == segment_all[None, :]) & (
        row_own[:, None] >= row_all[None, :]
    )
    gains = norm_gain_values.astype(f32)
    first_factor = adapter_first[0]
    second_factor = adapter_second[0]
    rank = ADAPTER_RANK
    narrow_projection = first_factor[:, : 3 * rank]
    narrow_output = first_factor[:, 3 * rank : 4 * rank]
    squeeze_gate = first_factor[:, 4 * rank : 5 * rank]
    squeeze_up = first_factor[:, 5 * rank :]
    narrow_down = lax.dynamic_slice_in_dim(adapter_down_first[0], place * hidden_own, hidden_own, 0)
    widen_query = second_factor[:, :QUERY_WIDTH]
    widen_key = second_factor[:, QUERY_WIDTH : QUERY_WIDTH + HEAD_WIDTH]
    widen_value = second_factor[:, QUERY_WIDTH + HEAD_WIDTH : PROJECT_COLUMNS]
    widen_output = second_factor[:, PROJECT_COLUMNS:GATE_START]
    widen_gate = lax.dynamic_slice_in_dim(
        second_factor, GATE_START + place * hidden_own, hidden_own, 1
    )
    widen_up = lax.dynamic_slice_in_dim(
        second_factor, GATE_START + HIDDEN_COUNT + place * hidden_own, hidden_own, 1
    )
    widen_down = second_factor[:, GATE_START + 2 * HIDDEN_COUNT :]
    scaling = HEAD_WIDTH ** (-0.5)

    hidden_state = hidden_input[0].astype(f32)
    scale_one = rms_scale(hidden_state)
    normalized = (hidden_state * scale_one * gains[0]).astype(bf16)
    proj_in = ring_gather(input_proj_weight, 0)
    proj_in, proj_out = lax.optimization_barrier((proj_in, output_proj_weight))
    proj_out = gather_rows(proj_out)
    lora_qkv = matrix_product(normalized, narrow_projection).astype(bf16)
    projected = matrix_product(normalized, proj_in)
    query_pre = projected[:, :QUERY_WIDTH] + matrix_product(lora_qkv[:, :rank], widen_query)
    key_pre = projected[:, QUERY_WIDTH : QUERY_WIDTH + HEAD_WIDTH] + matrix_product(
        lora_qkv[:, rank : 2 * rank], widen_key
    )
    value_local = (
        projected[:, QUERY_WIDTH + HEAD_WIDTH :]
        + matrix_product(lora_qkv[:, 2 * rank :], widen_value)
    ).astype(bf16)
    query_rot = rotate(query_pre, position_own, 1.0).astype(bf16)
    key_rot = rotate(key_pre, position_own, 1.0).astype(bf16)
    keys_all = ring_gather(jnp.concatenate([key_rot, value_local], axis=1), 1)
    key_rows, value_rows = keys_all[:, :HEAD_WIDTH], keys_all[:, HEAD_WIDTH:]
    query_heads = query_rot.reshape(tokens_dev, HEADS, HEAD_WIDTH)
    scores = scores_of(query_heads, key_rows, allowed, scaling)
    row_max = jnp.max(scores, axis=-1, keepdims=True)
    powered = jnp.exp(scores - row_max)
    row_sum = jnp.sum(powered, axis=-1, keepdims=True)
    probs = powered / row_sum
    probs_low = probs.astype(bf16)
    attended = (
        jnp.einsum("thu,ud->thd", probs_low, value_rows, preferred_element_type=f32)
        .reshape(tokens_dev, QUERY_WIDTH)
        .astype(bf16)
    )
    lora_out = matrix_product(attended, narrow_output).astype(bf16)
    middle = (
        hidden_state
        + times_transposed(attended, proj_out)
        + matrix_product(lora_out, widen_output)
    )
    scale_two = rms_scale(middle)
    normed_two = (middle * scale_two * gains[1]).astype(bf16)

    weight_planes = feedforward_weight.transpose(1, 0, 2)
    two_all, grad_all, acts, low_ffn, early_shares, up_share, ffn_pieces, down_own = unit_rows(
        jnp.concatenate([normed_two, lora_out], axis=1),
        output_gradient[0],
        weight_planes,
        first_factor[:, 4 * rank :],
        widen_down,
        widen_gate,
        widen_up,
        narrow_down,
        2,
    )
    lora_out_all = low_ffn[:, 3 * rank :]
    early_shares, acts = lax.optimization_barrier((early_shares, acts))
    early_both = loop_shares(early_shares)
    rows_sum = mix_rows(
        acts, weight_planes, widen_gate, widen_up, narrow_down, 3
    )
    back_own, out_own = rows_sum[:, : MODEL_WIDTH + 2 * rank], rows_sum[:, MODEL_WIDTH + 2 * rank :]
    lora_hd = out_own[:, MODEL_WIDTH:].astype(bf16)
    hidden_out = (middle + out_own[:, :MODEL_WIDTH] + matrix_product(lora_hd, widen_down)).astype(bf16)

    gate_low = back_own[:, MODEL_WIDTH : MODEL_WIDTH + rank].astype(bf16)
    up_low = back_own[:, MODEL_WIDTH + rank :].astype(bf16)
    two_grad = (
        back_own[:, :MODEL_WIDTH]
        + times_transposed(gate_low, squeeze_gate)
        + times_transposed(up_low, squeeze_up)
    )
    weighted_two = gains[1] * two_grad
    middle_grad = (
        output_gradient[0].astype(f32)
        + scale_two * weighted_two
        - middle * scale_two**3 * jnp.mean(middle * weighted_two, axis=-1, keepdims=True)
    )
    gain_two = jnp.sum(two_grad * middle * scale_two, axis=0)

    branch_grad = middle_grad.astype(bf16)
    both = [block.reshape(tokens_dev, size, width_own) for block in (normalized, branch_grad)]
    turned = turn(jnp.concatenate(both, axis=2).reshape(tokens_dev, -1))
    normed_turn, branch_turn = turned[:, :width_own], turned[:, width_own:]
    lora_out_grad = times_transposed(branch_grad, widen_output).astype(bf16)
    attended_grad = (
        matrix_product(branch_grad, proj_out) + times_transposed(lora_out_grad, narrow_output)
    ).astype(bf16)
    heads_grad = attended_grad.reshape(tokens_dev, HEADS, HEAD_WIDTH)
    prob_grad = jnp.einsum("thd,ud->thu", heads_grad, value_rows, preferred_element_type=f32)
    row_dot = jnp.sum(probs * prob_grad, axis=-1, keepdims=True)
    score_grad = (probs * (prob_grad - row_dot)).astype(bf16)
    query_rot_grad = (
        jnp.einsum("thu,ud->thd", score_grad, key_rows, preferred_element_type=f32) * scaling
    )
    key_part = (
        jnp.einsum("thu,thd->ud", score_grad, query_heads, preferred_element_type=f32) * scaling
    )
    value_part = jnp.einsum("thu,thd->ud", probs_low, heads_grad, preferred_element_type=f32)
    pair_grad = ring_scatter([key_part, value_part], 4)
    attended_rows, early_both, pair_grad, normed_turn, branch_turn = lax.optimization_barrier(
        (jnp.concatenate([attended, lora_qkv], axis=1), early_both, pair_grad, normed_turn, branch_turn)
    )
    attended_all = gather_rows(attended_rows)
    query_grad = rotate(
        query_rot_grad.reshape(tokens_dev, QUERY_WIDTH), position_own, -1.0
    ).astype(bf16)
    key_grad = rotate(pair_grad[:, :HEAD_WIDTH], position_own, -1.0).astype(bf16)
    value_grad = pair_grad[:, HEAD_WIDTH:].astype(bf16)
    proj_grad = jnp.concatenate([query_grad, key_grad, value_grad], axis=1)
    lora_qkv_grad = jnp.concatenate(
        [
            times_transposed(query_grad, widen_query),
            times_transposed(key_grad, widen_key),
            times_transposed(value_grad, widen_value),
        ],
        axis=1,
    ).astype(bf16)
    normed_grad = times_transposed(proj_grad, proj_in) + times_transposed(
        lora_qkv_grad, narrow_projection
    )
    weighted_one = gains[0] * normed_grad
    input_grad = (
        middle_grad
        + scale_one * weighted_one
        - hidden_state
        * scale_one**3
        * jnp.mean(hidden_state * weighted_one, axis=-1, keepdims=True)
    )
    gain_one = jnp.sum(normed_grad * hidden_state * scale_one, axis=0)

    lora_qkv_all = attended_all[:, QUERY_WIDTH:]
    out_piece = outer_product_rows(branch_turn, lora_out_all)
    gain_rows = jnp.stack([gain_one, gain_two]).astype(bf16).reshape(tokens_dev, -1)
    gain_count = gain_rows.shape[1]
    gain_rows = jnp.pad(gain_rows, ((0, 0), (0, -gain_count % 128)))
    proj_rows = jnp.concatenate(
        [proj_grad, lora_out_grad, gate_low, up_low, lora_hd, gain_rows], axis=1
    )
    proj_rows, up_share = lax.optimization_barrier((proj_rows, up_share))
    up_both = loop_shares(up_share)
    proj_all, middle_own = share_rows(
        proj_rows, jnp.concatenate([out_piece.astype(bf16), ffn_pieces[0], ffn_pieces[1]], axis=0), 5
    )
    column = place * width_own
    gain_all = proj_all[:, PROJECT_COLUMNS + 4 * rank :][:, :gain_count].reshape(size, 2, MODEL_WIDTH)
    gain_all = jnp.sum(gain_all.astype(f32), axis=0)
    gain_own = lax.dynamic_slice_in_dim(gain_all, column, width_own, 1)
    gain_part = jnp.pad(gain_own, ((0, width_own - 2), (0, -width_own % 128)))
    attn_part = jnp.concatenate(
        [
            outer_product_rows(normed_turn, proj_all[:, :PROJECT_COLUMNS]),
            outer_product_rows(branch_turn, attended_all)[:, :QUERY_WIDTH],
            gain_part,
        ],
        axis=1,
    ).astype(bf16)
    attn_part, up_both, proj_all = lax.optimization_barrier((attn_part, up_both, proj_all))
    attn_sum = both_loops(loop_shares(attn_part))
    gain_column = PROJECT_COLUMNS + QUERY_WIDTH
    gain_sum = attn_sum[:2, gain_column : gain_column + width_own]
    low_all = proj_all[:, PROJECT_COLUMNS : PROJECT_COLUMNS + 4 * rank]
    proj_all = proj_all[:, :PROJECT_COLUMNS]
    qkv_low_all = jnp.concatenate(
        [
            times_transposed(proj_all[:, :QUERY_WIDTH], widen_query),
            times_transposed(proj_all[:, QUERY_WIDTH : QUERY_WIDTH + HEAD_WIDTH], widen_key),
            times_transposed(proj_all[:, QUERY_WIDTH + HEAD_WIDTH :], widen_value),
        ],
        axis=1,
    ).astype(bf16)
    attended_turn = lax.dynamic_slice_in_dim(attended_all, column, width_own, 1)
    two_turn = lax.dynamic_slice_in_dim(two_all, column, width_own, 1)
    squeeze_own = jnp.concatenate(
        [
            outer_product_rows(normed_turn, qkv_low_all),
            outer_product_rows(attended_turn, low_all[:, :rank]),
            outer_product_rows(two_turn, low_all[:, rank : 3 * rank]),
        ],
        axis=1,
    )
    near = jnp.concatenate(
        [
            outer_product_rows(proj_all[:, :QUERY_WIDTH], lora_qkv_all[:, :rank]),
            outer_product_rows(
                proj_all[:, QUERY_WIDTH : QUERY_WIDTH + HEAD_WIDTH], lora_qkv_all[:, rank : 2 * rank]
            ),
            outer_product_rows(proj_all[:, QUERY_WIDTH + HEAD_WIDTH :], lora_qkv_all[:, 2 * rank :]),
        ],
        axis=0,
    )
    far = outer_product_rows(grad_all, low_all[:, 3 * rank :])
    first = place * columns_own
    far_start = GATE_START + 2 * HIDDEN_COUNT
    near = lax.dynamic_slice_in_dim(
        jnp.pad(near.astype(bf16), ((0, columns_own), (0, 0))), jnp.minimum(first, PROJECT_COLUMNS), columns_own, 0
    )
    far = lax.dynamic_slice_in_dim(
        jnp.pad(far.astype(bf16), ((columns_own, 0), (0, 0))),
        jnp.maximum(first - far_start + columns_own, 0),
        columns_own,
        0,
    )
    owned = first + jnp.arange(columns_own, dtype=jnp.int32)[:, None]
    expand_own = jnp.where(
        owned < PROJECT_COLUMNS, near, jnp.where(owned < far_start, middle_own, far)
    ).T.astype(f32)
    ffn_sum = sum_loops(early_both, up_both).transpose(1, 0, 2)
    return (
        hidden_out[None],
        input_grad[None],
        gain_sum,
        attn_sum[:, :PROJECT_COLUMNS],
        attn_sum[:, PROJECT_COLUMNS:gain_column],
        ffn_sum,
        squeeze_own[None],
        expand_own[None],
        down_own[None],
    )


def solution(mesh):
    return jax.shard_map(
        per_device,
        mesh=mesh,
        in_specs=(
            P("loop", "fsdp", None),
            P("loop", None),
            P(),
            P("fsdp", None),
            P("fsdp", None),
            P("fsdp", None, None),
            P("loop", None, None),
            P("loop", None, None),
            P("loop", None, None),
            P("loop", "fsdp", None),
        ),
        out_specs=(
            P("loop", "fsdp", None),
            P("loop", "fsdp", None),
            P(None, "fsdp"),
            P("fsdp", None),
            P("fsdp", None),
            P("fsdp", None, None),
            P("loop", "fsdp", None),
            P("loop", None, "fsdp"),
            P("loop", "fsdp", None),
        ),
        check_vma=False,
    )
```

```python
import functools
import math

import jax
import jax.numpy as jnp
from jax import lax
from jax.experimental import pallas as pl
from jax.experimental.pallas import tpu as pltpu
from jax.sharding import PartitionSpec as P

MODEL_WIDTH = 2048
HEADS = 8
HEAD_WIDTH = 256
HIDDEN_COUNT = 16384
ADAPTER_RANK = 256
QUERY_WIDTH = 2048
PROJECT_COLUMNS = 2560
ADAPTER_COLUMNS = 39424
GATE_START = PROJECT_COLUMNS + MODEL_WIDTH

epsilon = 1e-06
bf16 = jnp.bfloat16
f32 = jnp.float32
MESH = pl.DeviceIdType.MESH


def matrix_product(former, latter):
    return jnp.dot(former, latter, preferred_element_type=f32)


def times_transposed(former, latter):
    return lax.dot_general(former, latter, (((1,), (1,)), ((), ())), preferred_element_type=f32)


def outer_product_rows(former, latter):
    return lax.dot_general(former, latter, (((0,), (0,)), ((), ())), preferred_element_type=f32)


def segment_info(lengths, row_count):
    row_ids = jnp.arange(row_count, dtype=jnp.int32)
    count = lengths.shape[0]
    labels = jnp.arange(count, dtype=jnp.int32)
    finish = jnp.sum(jnp.where(labels[:, None] <= labels[None, :], lengths[:, None], 0), axis=0)
    starts = finish - lengths
    segment = jnp.sum((row_ids[:, None] >= finish[None, :]).astype(jnp.int32), axis=1)
    opening = jnp.sum(jnp.where(segment[:, None] == labels[None, :], starts[None, :], 0), axis=1)
    return (segment, row_ids - opening)


def rotate(values, position, direction):
    half_dim = HEAD_WIDTH // 2
    frequency = jnp.exp(
        jnp.arange(half_dim).astype(f32) * (-2.0 * math.log(10000.0) / HEAD_WIDTH)
    )
    angles = position.astype(f32)[:, None] * frequency[None, :]
    cosine = jnp.cos(angles)[:, None, :]
    sine_val = direction * jnp.sin(angles)[:, None, :]
    shaped = values.reshape(values.shape[0], -1, HEAD_WIDTH)
    former = shaped[..., :half_dim]
    latter = shaped[..., half_dim:]
    turned = jnp.concatenate(
        [former * cosine - latter * sine_val, latter * cosine + former * sine_val], axis=-1
    )
    return turned.reshape(values.shape)


def rms_scale(values):
    return lax.rsqrt(jnp.mean(values * values, axis=-1, keepdims=True) + epsilon)


def gelu_tanh(values):
    return jax.nn.gelu(values, approximate=True)


def unit_backward(gate_value, upward_activation, hidden_unit_gradient):
    activated, pullback_function = jax.vjp(gelu_tanh, gate_value)
    gate_grad = pullback_function(hidden_unit_gradient * upward_activation)[0]
    return (gate_grad.astype(bf16), (hidden_unit_gradient * activated).astype(bf16))


def scores_of(query_heads, key_rows, allowed, scaling):
    product = (
        jnp.einsum("thd,ud->thu", query_heads, key_rows, preferred_element_type=f32) * scaling
    )
    return jnp.where(allowed[:, None, :], product, -1e30)


def gather_rows(block):
    return lax.all_gather(block, "fsdp", axis=0, tiled=True)


def scatter_rows(partial):
    return lax.psum_scatter(partial.astype(bf16), "fsdp", scatter_dimension=0, tiled=True).astype(f32)


def loop_shares(partial):
    return lax.all_gather(partial.astype(bf16), "loop", axis=0)


def both_loops(shares):
    return shares[0].astype(f32) + shares[1].astype(f32)


def turn(block):
    return lax.all_to_all(block, "fsdp", split_axis=1, concat_axis=0, tiled=True)


def chip_at(q, chips):
    return jnp.where(q < 4, 2 * q, 15 - 2 * q) if chips == 8 else q

def ring_place(chip, chips):
    return jnp.where(chip % 2 == 0, chip // 2, 7 - chip // 2) if chips == 8 else chip

def ring_neighbours(chips):
    me = lax.axis_index("fsdp")
    core = me % 2
    p = ring_place(me // 2, chips)
    def device(shift, c):
        return chip_at((p + shift + chips) % chips, chips) * 2 + c
    return core, device

def meet(devices):
    barrier = pltpu.get_barrier_semaphore()
    for d in devices:
        pl.semaphore_signal(barrier, inc=1, device_id={"fsdp": d}, device_id_type=MESH)
    pl.semaphore_wait(barrier, len(devices))

def gather_kernel(chips, x_ref, o_ref, own_sem, ring_send, ring_recv, side_send, side_recv, greet=None, also=None):
    core, device = ring_neighbours(chips)
    rows = x_ref.shape[0]
    reach = chips // 2
    ways = (device(1, core), device(-1, core))
    side = device(0, 1 - core)
    if greet is None:
        meet((*ways, side))
    else:
        greet()

    def span(way, hops):
        return (way * (rows // 2), rows // 2) if hops == reach else (0, rows)

    def at(way, hops, c, part):
        origin = device(-hops if way == 0 else hops, c)
        return o_ref.at[pl.ds(pl.multiple_of(origin * rows + part[0], 8), part[1])]

    def hop(way, hops):
        part = span(way, hops)
        here = at(way, hops - 1, core, part)
        src = x_ref.at[pl.ds(part[0], part[1])] if hops == 1 else here
        return pltpu.make_async_remote_copy(src, here, ring_send.at[way, hops - 1], ring_recv.at[way, hops - 1], device_id={"fsdp": ways[way]}, device_id_type=MESH)

    def arriving(way, hops):
        here = at(way, hops, core, span(way, hops))
        return pltpu.make_async_remote_copy(here, here, ring_send.at[way, hops - 1], ring_recv.at[way, hops - 1], device_id={"fsdp": ways[way]}, device_id_type=MESH)

    def across(way, hops, c):
        part = span(way, hops) if hops else (0, rows)
        there = at(way, hops, c, part)
        src = there if hops else x_ref
        return pltpu.make_async_remote_copy(src, there, side_send.at[way, hops], side_recv.at[way, hops], device_id={"fsdp": side}, device_id_type=MESH)

    for way in (0, 1):
        hop(way, 1).start()
    across(0, 0, core).start()
    own = pltpu.make_async_copy(x_ref, at(0, 0, core, (0, rows)), own_sem)
    own.start()
    if also is not None:
        also()
    for hops in range(1, reach + 1):
        for way in (0, 1):
            arriving(way, hops).wait_recv()
            if hops < reach:
                hop(way, hops + 1).start()
            across(way, hops, core).start()
    across(0, 0, 1 - core).wait_recv()
    across(0, 0, core).wait_send()
    for hops in range(1, reach + 1):
        for way in (0, 1):
            across(way, hops, 1 - core).wait_recv()
            across(way, hops, core).wait_send()
            hop(way, hops).wait_send()
    own.wait()

def busy(us):
    return pl.CostEstimate(flops=0, bytes_accessed=int(us * 3.0e6), transcendentals=0)


def ring_gather(block, ident):
    size = lax.axis_size("fsdp")
    chips = size // 2
    rows, columns = block.shape
    pair = pltpu.SemaphoreType.DMA((2, chips // 2))
    sides = pltpu.SemaphoreType.DMA((2, chips // 2 + 1))
    return pl.pallas_call(
        functools.partial(gather_kernel, chips),
        out_shape=jax.ShapeDtypeStruct((size * rows, columns), block.dtype),
        in_specs=[pl.BlockSpec(memory_space=pl.ANY)],
        out_specs=pl.BlockSpec(memory_space=pl.ANY),
        scratch_shapes=[pltpu.SemaphoreType.DMA, pair, pair, sides, sides],
        compiler_params=pltpu.CompilerParams(collective_id=ident, has_side_effects=True),
        cost_estimate=busy(1),
        name="ring_gather",
    )(block)

def scatter_kernel(chips, count, *refs):
    x_refs, o_ref = refs[:count], refs[count]
    side_buf, ring_buf, side_send, side_recv, ring_send, ring_recv = refs[count + 1 :]
    core, device = ring_neighbours(chips)
    rows, columns = o_ref.shape
    reach = chips // 2
    half = columns // 2
    tile = 16
    ways = (device(1, core), device(-1, core))
    side = device(0, 1 - core)
    meet((*ways, side))
    starts = [sum(x.shape[1] for x in x_refs[:i]) for i in range(count)]

    def shift(way, hops):
        return (hops if way == 0 else chips - hops) % chips

    def across(target, c, i):
        there = pl.ds(pl.multiple_of(device(target, c) * rows, tile), rows)
        return pltpu.make_async_remote_copy(
            x_refs[i].at[there],
            side_buf.at[target, :, pl.ds(starts[i], x_refs[i].shape[1])],
            side_send.at[target, i],
            side_recv.at[target, i],
            device_id={"fsdp": side},
            device_id_type=MESH,
        )

    def hop(way, step):
        cols = pl.ds(way * half, half) if step == 0 else pl.ds(0, columns)
        return pltpu.make_async_remote_copy(
            side_buf.at[shift(way, reach - step), :, cols],
            ring_buf.at[way, step, :, cols],
            ring_send.at[way, step],
            ring_recv.at[way, step],
            device_id={"fsdp": ways[way]},
            device_id_type=MESH,
        )

    order = [reach] + [shift(way, hops) for hops in range(reach - 1, 0, -1) for way in (0, 1)] + [0]
    for target in order:
        for i in range(count):
            across(target, 1 - core, i).start()

    def add(target, incoming, store):
        first = pl.multiple_of(device(target, core) * rows, tile)
        for i in range(count):
            across(target, core, i).wait_recv()

        @pl.loop(0, rows // tile)
        def _(j):
            here = pl.ds(pl.multiple_of(j * tile, tile), tile)
            mine = pl.ds(pl.multiple_of(first + j * tile, tile), tile)
            for i in range(count):
                cols = pl.ds(starts[i], x_refs[i].shape[1])
                total = x_refs[i][mine, :].astype(f32) + side_buf[target, here, cols].astype(f32)
                for way, step in incoming:
                    if step:
                        total = total + ring_buf[way, step, here, cols].astype(f32)
                store(here, cols, total)
            for way, step in incoming:
                if not step:
                    cols = pl.ds(way * half, half)
                    store(
                        here,
                        cols,
                        side_buf[target, here, cols].astype(f32) + ring_buf[way, 0, here, cols].astype(f32),
                    )

    for step in range(reach):
        for way in (0, 1):
            target = shift(way, reach - step)
            if step:
                hop(way, step - 1).wait_recv()

            def store(here, cols, total, target=target):
                side_buf[target, here, cols] = total.astype(bf16)

            if step or way == 0:
                add(target, [(way, step - 1)] if step else [], store)
            hop(way, step).start()
    for way in (0, 1):
        hop(way, reach - 1).wait_recv()

    def last(here, cols, total):
        o_ref[here, cols] = total

    add(0, [(0, reach - 1), (1, reach - 1)], last)
    for target in order:
        for i in range(count):
            across(target, 1 - core, i).wait_send()
    for step in range(reach):
        for way in (0, 1):
            hop(way, step).wait_send()


def ring_scatter(terms, ident):
    size = lax.axis_size("fsdp")
    terms = [term.astype(bf16) for term in terms]
    if size != 16:
        return scatter_rows(jnp.concatenate(terms, axis=1))
    chips, count = size // 2, len(terms)
    rows, columns = terms[0].shape[0] // size, sum(term.shape[1] for term in terms)
    pair = pltpu.SemaphoreType.DMA((2, chips // 2))
    sides = pltpu.SemaphoreType.DMA((chips, count))
    return pl.pallas_call(
        functools.partial(scatter_kernel, chips, count),
        out_shape=jax.ShapeDtypeStruct((rows, columns), f32),
        in_specs=[pl.BlockSpec(memory_space=pltpu.VMEM)] * count,
        out_specs=pl.BlockSpec(memory_space=pltpu.VMEM),
        scratch_shapes=[
            pltpu.VMEM((chips, rows, columns), bf16),
            pltpu.VMEM((2, chips // 2, rows, columns), bf16),
            sides,
            sides,
            pair,
            pair,
        ],
        compiler_params=pltpu.CompilerParams(
            collective_id=ident, has_side_effects=True, vmem_limit_bytes=56 << 20
        ),
        cost_estimate=busy(1),
        name="ring_scatter",
    )(*terms)


def unit_kernel(chips, *refs):
    sources, (planes, squeeze, widen_down, widen_gate, widen_up, narrow) = refs[:3], refs[3:9]
    two_all, grad_all, later_all, acts_all, low_all, share_out, piece_out, down_out = refs[9:17]
    held, turned, acts, low, tiles = refs[17:22]
    landed = (refs[22], refs[23], later_all)
    held_sem, own_sem, ring_send, ring_recv, side_send, side_recv, out_sem, acts_sem, tile_sem = refs[24:]
    core, device = ring_neighbours(chips)
    rows = sources[0].shape[0]
    reach = chips // 2
    wide = 256
    ways = (device(1, core), device(-1, core))
    side = device(0, 1 - core)
    fetches = [pltpu.make_async_copy(planes.at[i], held.at[i], held_sem.at[i]) for i in range(3)]
    for fetch in fetches:
        fetch.start()
    meet((*ways, side))

    def span(way, hops):
        return (way * (rows // 2), rows // 2) if hops == reach else (0, rows)

    def at(i, way, hops, c, part):
        origin = device(-hops if way == 0 else hops, c)
        return landed[i].at[pl.ds(pl.multiple_of(origin * rows + part[0], 16), part[1])]

    def hop(i, way, hops):
        part = span(way, hops)
        here = at(i, way, hops - 1, core, part)
        src = sources[i].at[pl.ds(part[0], part[1])] if hops == 1 else here
        return pltpu.make_async_remote_copy(
            src,
            here,
            ring_send.at[i, way, hops - 1],
            ring_recv.at[i, way, hops - 1],
            device_id={"fsdp": ways[way]},
            device_id_type=MESH,
        )

    def arriving(i, way, hops):
        here = at(i, way, hops, core, span(way, hops))
        return pltpu.make_async_remote_copy(
            here,
            here,
            ring_send.at[i, way, hops - 1],
            ring_recv.at[i, way, hops - 1],
            device_id={"fsdp": ways[way]},
            device_id_type=MESH,
        )

    def across(i, way, hops, c):
        part = span(way, hops) if hops else (0, rows)
        there = at(i, way, hops, c, part)
        return pltpu.make_async_remote_copy(
            there if hops else sources[i],
            there,
            side_send.at[i, way, hops],
            side_recv.at[i, way, hops],
            device_id={"fsdp": side},
            device_id_type=MESH,
        )

    def leaving(n, first):
        mine = pl.ds(first, 2 * rows)
        width, under = grad_all.shape[1], low.shape[1]
        pairs = [
            (landed[0].at[mine, pl.ds(0, width)], two_all.at[mine]),
            (landed[0].at[mine, pl.ds(width, ADAPTER_RANK)], low_all.at[mine, pl.ds(under, ADAPTER_RANK)]),
            (low.at[mine], low_all.at[mine, pl.ds(0, under)]),
            (landed[1].at[mine], grad_all.at[mine]),
        ]
        return [pltpu.make_async_copy(a, b, out_sem.at[n, i]) for i, (a, b) in enumerate(pairs)]

    def shown(n, first):
        mine = pl.ds(first, 2 * rows)
        return [
            pltpu.make_async_copy(acts.at[n % 2, i], acts_all.at[i, mine], acts_sem.at[n % 2, i]) for i in range(3)
        ]

    def first_row(shift):
        return pl.multiple_of(device(shift, 0) * rows, 2 * rows)

    def work(n, first):
        mine = pl.ds(first, 2 * rows)
        rank, width = ADAPTER_RANK, MODEL_WIDTH
        if n >= 2:
            for copy in shown(n, first):
                copy.wait()
        low[mine, : 2 * rank] = matrix_product(landed[0][mine, :width], squeeze[...]).astype(bf16)
        low[mine, 2 * rank :] = times_transposed(landed[1][mine, :], widen_down[...]).astype(bf16)

        @pl.loop(0, held.shape[1] // wide)
        def _(t):
            own = pl.ds(pl.multiple_of(t * wide, wide), wide)
            two = landed[0][mine, :width]
            gate = times_transposed(two, held[0, own, :]) + matrix_product(
                low[mine, :rank], widen_gate[:, own]
            )
            upward = times_transposed(two, held[1, own, :]) + matrix_product(
                low[mine, rank : 2 * rank], widen_up[:, own]
            )
            pull = times_transposed(landed[1][mine, :], held[2, own, :]) + times_transposed(
                low[mine, 2 * rank :], narrow[own, :]
            )
            scale = math.sqrt(2.0 / math.pi)
            square = gate * gate
            bend = jnp.tanh(scale * gate * (1.0 + 0.044715 * square))
            rise = 0.5 * (1.0 + bend)
            active = gate * rise
            slope = rise + 0.5 * gate * (1.0 - bend * bend) * (scale * (1.0 + 3 * 0.044715 * square))
            for i, value in enumerate((pull * upward * slope, pull * active, active * upward)):
                acts[n % 2, i, :, own] = value.astype(bf16)
                turned[i, own, mine] = value.T.astype(bf16)

        for copy in leaving(n, first) + shown(n, first):
            copy.start()

    for i in (0, 1):
        for way in (0, 1):
            hop(i, way, 1).start()
        across(i, 0, 0, core).start()
    keeps = [
        pltpu.make_async_copy(sources[i], at(i, 0, 0, core, (0, rows)), own_sem.at[i]) for i in range(3)
    ]
    for keep in keeps:
        keep.start()
    for copy in keeps + fetches:
        copy.wait()
    for i in (0, 1):
        across(i, 0, 0, 1 - core).wait_recv()
    work(0, first_row(0))
    for hops in range(1, reach + 1):
        for i in (0, 1):
            for way in (0, 1):
                arriving(i, way, hops).wait_recv()
                if hops < reach:
                    hop(i, way, hops + 1).start()
                across(i, way, hops, core).start()
        if hops == reach:
            for way in (0, 1):
                hop(2, way, 1).start()
            across(2, 0, 0, core).start()
        else:
            for way in (0, 1):
                for i in (0, 1):
                    across(i, way, hops, 1 - core).wait_recv()
                work(2 * hops - 1 + way, first_row(-hops if way == 0 else hops))
    for way in (0, 1):
        for i in (0, 1):
            across(i, way, reach, 1 - core).wait_recv()
    work(2 * reach - 1, first_row(reach))
    rank = ADAPTER_RANK

    def relay(hops):
        for way in (0, 1):
            arriving(2, way, hops).wait_recv()
            if hops < reach:
                hop(2, way, hops + 1).start()
            across(2, way, hops, core).start()

    for kind in range(3):

        def tile_copy(t, kind=kind):
            there = pl.ds(pl.multiple_of(t * wide, wide), wide)
            return pltpu.make_async_copy(
                tiles.at[t % 2], share_out.at[kind, :, there], tile_sem.at[t % 2]
            )

        @pl.loop(0, MODEL_WIDTH // wide)
        def _(t, kind=kind, tile_copy=tile_copy):
            @pl.when(t > 1)
            def _():
                tile_copy(t - 2).wait()

            cols = pl.ds(pl.multiple_of(t * wide, wide), wide)
            tiles[t % 2] = matrix_product(
                turned[kind], landed[1 if kind == 2 else 0][:, cols]
            ).astype(bf16)
            tile_copy(t).start()

        relay(kind + 1)
        if kind == 2:
            piece_out[0] = matrix_product(turned[0], low[:, :rank]).astype(bf16)
            piece_out[1] = matrix_product(turned[1], low[:, rank : 2 * rank]).astype(bf16)
            down_out[...] = matrix_product(turned[2], low[:, 2 * rank :])
        tile_copy(MODEL_WIDTH // wide - 2).wait()
        tile_copy(MODEL_WIDTH // wide - 1).wait()
    for hops in range(4, reach + 1):
        relay(hops)
    across(2, 0, 0, 1 - core).wait_recv()
    for hops in range(1, reach + 1):
        for way in (0, 1):
            across(2, way, hops, 1 - core).wait_recv()
    for i in range(3):
        across(i, 0, 0, core).wait_send()
        for hops in range(1, reach + 1):
            for way in (0, 1):
                across(i, way, hops, core).wait_send()
                hop(i, way, hops).wait_send()
    for n in range(chips):
        if n == 0:
            shift = 0
        elif n == 2 * reach - 1:
            shift = reach
        else:
            shift = (-1 if n % 2 else 1) * ((n + 1) // 2)
        for copy in leaving(n, first_row(shift)):
            copy.wait()
        if n >= chips - 2:
            for copy in shown(n, first_row(shift)):
                copy.wait()


def unit_rows(two, grad, later, planes, squeeze, widen_down, widen_gate, widen_up, narrow, ident):
    size = lax.axis_size("fsdp")
    rank = ADAPTER_RANK
    if size != 16:
        two, grad = gather_rows(two), gather_rows(grad)
        two, lora_out = two[:, :MODEL_WIDTH], two[:, MODEL_WIDTH:]
        low = matrix_product(two, squeeze).astype(bf16)
        pulled = times_transposed(grad, widen_down).astype(bf16)
        gate = times_transposed(two, planes[0]) + matrix_product(low[:, :rank], widen_gate)
        upward = times_transposed(two, planes[1]) + matrix_product(low[:, rank:], widen_up)
        units_grad = times_transposed(grad, planes[2]) + times_transposed(pulled, narrow)
        units = (gelu_tanh(gate) * upward).astype(bf16)
        gate_grad, up_grad = unit_backward(gate, upward, units_grad)
        return (
            two,
            grad,
            gather_rows(later),
            jnp.stack([gate_grad, up_grad, units]),
            jnp.concatenate([low, pulled, lora_out], axis=1),
            jnp.stack(
                [
                    outer_product_rows(gate_grad, two),
                    outer_product_rows(up_grad, two),
                    outer_product_rows(units, grad),
                ]
            ).astype(bf16),
            jnp.stack(
                [outer_product_rows(gate_grad, low[:, :rank]), outer_product_rows(up_grad, low[:, rank:])]
            ).astype(bf16),
            outer_product_rows(units, pulled),
        )
    chips = size // 2
    rows, columns = grad.shape
    all_rows, hidden = size * rows, planes.shape[1]
    anywhere, inside = pl.BlockSpec(memory_space=pl.ANY), pl.BlockSpec(memory_space=pltpu.VMEM)
    pair = pltpu.SemaphoreType.DMA((3, 2, chips // 2))
    sides = pltpu.SemaphoreType.DMA((3, 2, chips // 2 + 1))
    return pl.pallas_call(
        functools.partial(unit_kernel, chips),
        out_shape=(
            jax.ShapeDtypeStruct((all_rows, columns), bf16),
            jax.ShapeDtypeStruct((all_rows, columns), bf16),
            jax.ShapeDtypeStruct((all_rows, later.shape[1]), bf16),
            jax.ShapeDtypeStruct((3, all_rows, hidden), bf16),
            jax.ShapeDtypeStruct((all_rows, 4 * rank), bf16),
            jax.ShapeDtypeStruct((3, hidden, columns), bf16),
            jax.ShapeDtypeStruct((2, hidden, rank), bf16),
            jax.ShapeDtypeStruct((hidden, rank), f32),
        ),
        in_specs=[anywhere] * 4 + [inside] * 5,
        out_specs=(anywhere,) * 6 + (inside,) * 2,
        scratch_shapes=[
            pltpu.VMEM(planes.shape, bf16),
            pltpu.VMEM((3, hidden, all_rows), bf16),
            pltpu.VMEM((2, 3, 2 * rows, hidden), bf16),
            pltpu.VMEM((all_rows, 3 * rank), bf16),
            pltpu.VMEM((2, hidden, 256), bf16),
            pltpu.VMEM((all_rows, two.shape[1]), bf16),
            pltpu.VMEM((all_rows, columns), bf16),
            pltpu.SemaphoreType.DMA((3,)),
            pltpu.SemaphoreType.DMA((3,)),
            pair,
            pair,
            sides,
            sides,
            pltpu.SemaphoreType.DMA((chips, 4)),
            pltpu.SemaphoreType.DMA((2, 3)),
            pltpu.SemaphoreType.DMA((2,)),
        ],
        compiler_params=pltpu.CompilerParams(
            collective_id=ident, has_side_effects=True, vmem_limit_bytes=60 << 20
        ),
        cost_estimate=busy(100),
        name="unit_rows",
    )(two, grad, later, planes, squeeze, widen_down, widen_gate, widen_up, narrow)


def mix_kernel(chips, *refs):
    acts_ref, planes, gate_b, up_b, down_a, o_ref = refs[:6]
    acts, held, side_buf, ring_buf, stage, mine = refs[6:12]
    held_sem, side_send, side_recv, ring_send, ring_recv = refs[12:]
    fetches = [pltpu.make_async_copy(planes.at[i], held.at[i], held_sem.at[0, i]) for i in range(3)]
    fetches += [pltpu.make_async_copy(acts_ref.at[i], acts.at[i], held_sem.at[1, i]) for i in range(3)]
    for fetch in fetches:
        fetch.start()
    core, device = ring_neighbours(chips)
    rows, columns = o_ref.shape
    reach = chips // 2
    half = columns // 2
    tile = 16
    wide = 256
    ways = (device(1, core), device(-1, core))
    side = device(0, 1 - core)
    meet((*ways, side))
    order = [(reach, 0, 0)]
    for step in range(1, reach):
        order += [(reach - step, 0, step), (chips - reach + step, 1, step)]
    order.append((0, 0, reach))

    def across(i):
        target = order[i][0]
        return pltpu.make_async_remote_copy(
            stage.at[i % 2],
            side_buf.at[target],
            side_send.at[target],
            side_recv.at[target],
            device_id={"fsdp": side},
            device_id_type=MESH,
        )

    def hop(way, step, part):
        target = (reach - step if way == 0 else chips - reach + step) % chips
        cols = pl.ds(way * half, half) if step == 0 else pl.ds(0, columns)
        here = pl.ds(part * (rows // 2), rows // 2)
        return pltpu.make_async_remote_copy(
            side_buf.at[target, here, cols],
            ring_buf.at[way, step, here, cols],
            ring_send.at[way, step, part],
            ring_recv.at[way, step, part],
            device_id={"fsdp": ways[way]},
            device_id_type=MESH,
        )

    def make(i):
        target, slot = order[i][0], i % 2
        if i >= 2:
            across(i - 2).wait_send()
        theirs = pl.ds(pl.multiple_of(device(target, 1 - core) * rows, rows), rows)
        ours = pl.ds(pl.multiple_of(device(target, core) * rows, rows), rows)

        def block(kind):
            return jnp.concatenate([acts[kind, theirs, :], acts[kind, ours, :]], axis=0)

        def put(first, value):
            cols = pl.ds(pl.multiple_of(first, wide), wide)
            stage[slot, :, cols] = value[:rows].astype(bf16)
            mine[slot, :, cols] = value[rows:].astype(bf16)

        @pl.loop(0, MODEL_WIDTH // wide)
        def _(t):
            cols = pl.ds(pl.multiple_of(t * wide, wide), wide)
            put(
                t * wide,
                matrix_product(block(0), held[0, :, cols])
                + matrix_product(block(1), held[1, :, cols]),
            )
            put(
                MODEL_WIDTH + 2 * ADAPTER_RANK + t * wide,
                matrix_product(block(2), held[2, :, cols]),
            )

        put(MODEL_WIDTH, times_transposed(block(0), gate_b[...]))
        put(MODEL_WIDTH + ADAPTER_RANK, times_transposed(block(1), up_b[...]))
        put(2 * MODEL_WIDTH + 2 * ADAPTER_RANK, matrix_product(block(2), down_a[...]))
        across(i).start()

    def add(i):
        target, way, step = order[i]
        last = target == 0
        incoming = [(w, step - 1) for w in ((0, 1) if last else (way,))] if step else []
        across(i).wait_recv()
        for part in (0, 1):
            for w, s in incoming:
                hop(w, s, part).wait_recv()

            @pl.loop(0, rows // 2 // tile)
            def _(j, part=part):
                here = pl.ds(pl.multiple_of(part * (rows // 2) + j * tile, tile), tile)
                for side_half in (0, 1):
                    cols = pl.ds(side_half * half, half)
                    total = mine[i % 2, here, cols].astype(f32) + side_buf[target, here, cols].astype(f32)
                    for w, s in incoming:
                        if s or w == side_half:
                            total = total + ring_buf[w, s, here, cols].astype(f32)
                    if last:
                        o_ref[here, cols] = total
                    else:
                        side_buf[target, here, cols] = total.astype(bf16)

            if not last:
                hop(way, step, part).start()
                if step == 0:
                    hop(1, 0, part).start()

    for fetch in fetches:
        fetch.wait()
    make(0)
    add(0)
    make(1)
    for i in range(1, len(order)):
        if i + 1 < len(order):
            make(i + 1)
        add(i)
    for i in range(len(order) - 2, len(order)):
        across(i).wait_send()
    for step in range(reach):
        for way in (0, 1):
            for part in (0, 1):
                hop(way, step, part).wait_send()


def mix_rows(acts, planes, gate_b, up_b, down_a, ident):
    size = lax.axis_size("fsdp")
    if size != 16:
        gate_grad, up_grad, units = acts[0], acts[1], acts[2]
        terms = [
            matrix_product(gate_grad, planes[0]) + matrix_product(up_grad, planes[1]),
            times_transposed(gate_grad, gate_b),
            times_transposed(up_grad, up_b),
            matrix_product(units, planes[2]),
            matrix_product(units, down_a),
        ]
        return scatter_rows(jnp.concatenate(terms, axis=1))
    chips = size // 2
    rows, columns = acts.shape[1] // size, 2 * MODEL_WIDTH + 3 * ADAPTER_RANK
    pair = pltpu.SemaphoreType.DMA((2, chips // 2, 2))
    sides = pltpu.SemaphoreType.DMA((chips,))
    return pl.pallas_call(
        functools.partial(mix_kernel, chips),
        out_shape=jax.ShapeDtypeStruct((rows, columns), f32),
        in_specs=[pl.BlockSpec(memory_space=pl.ANY)] * 2
        + [pl.BlockSpec(memory_space=pltpu.VMEM)] * 3,
        out_specs=pl.BlockSpec(memory_space=pltpu.VMEM),
        scratch_shapes=[
            pltpu.VMEM(acts.shape, bf16),
            pltpu.VMEM(planes.shape, bf16),
            pltpu.VMEM((chips, rows, columns), bf16),
            pltpu.VMEM((2, chips // 2, rows, columns), bf16),
            pltpu.VMEM((2, rows, columns), bf16),
            pltpu.VMEM((2, rows, columns), bf16),
            pltpu.SemaphoreType.DMA((2, 3)),
            sides,
            sides,
            pair,
            pair,
        ],
        compiler_params=pltpu.CompilerParams(
            collective_id=ident, has_side_effects=True, vmem_limit_bytes=60 << 20
        ),
        cost_estimate=busy(1),
        name="mix_rows",
    )(acts, planes, gate_b, up_b, down_a)


def share_kernel(size, chunk, own_count, x_ref, mid_ref, all_ref, o_ref, *sems):
    send_sem, recv_sem, own_sem = sems[5:]
    me = lax.axis_index("fsdp")
    hidden = HIDDEN_COUNT // size
    width = MODEL_WIDTH // size
    sections = (
        (0, PROJECT_COLUMNS, width),
        (width, GATE_START, hidden),
        (width + hidden, GATE_START + HIDDEN_COUNT, hidden),
    )

    def greet():
        barrier = pltpu.get_barrier_semaphore()

        def one(i, carry):
            pl.semaphore_signal(barrier, inc=1, device_id={"fsdp": (me + i) % size}, device_id_type=MESH)
            return carry

        lax.fori_loop(1, size, one, 0)
        pl.semaphore_wait(barrier, size - 1)

    def rows(ref, first):
        return ref.at[pl.ds(pl.multiple_of(first, 8), chunk)]

    def aim(start, length):
        owner = (start + me * length) // own_count
        return owner, start + me * length - owner * own_count

    def remote(source, first, owner, sent=0):
        return pltpu.make_async_remote_copy(
            source,
            rows(o_ref, first),
            send_sem.at[sent],
            recv_sem.at[first // chunk],
            device_id={"fsdp": owner},
            device_id_type=MESH,
        )

    def local(source, first):
        return pltpu.make_async_copy(source, rows(o_ref, first), own_sem.at[first // chunk])

    def send_all():
        for base, start, length in sections:

            def send(j, carry, base=base, aimed=aim(start, length)):
                over = (aimed[1] + j * chunk >= own_count).astype(jnp.int32)
                owner = aimed[0] + over
                first = aimed[1] + j * chunk - over * own_count
                source = rows(mid_ref, base + j * chunk)

                @pl.when(owner != me)
                def _():
                    remote(source, first, owner, base // chunk + j).start()

                @pl.when(owner == me)
                def _():
                    local(source, first).start()

                return carry

            lax.fori_loop(0, length // chunk, send, 0)

    gather_kernel(size // 2, x_ref, all_ref, *sems[:5], greet=greet, also=send_all)

    def arrive(j, carry):
        column = me * own_count + j * chunk
        here = rows(o_ref, j * chunk)
        away, kept = 0, 0
        for _, start, length in sections:
            mine = start + me * length
            inside = (column >= start) & (column < start + length * size)
            outside = (column < mine) | (column >= mine + length)
            away = away + (inside & outside).astype(jnp.int32)
            kept = kept + (inside & ~outside).astype(jnp.int32)

        @pl.when(away > 0)
        def _():
            remote(here, j * chunk, (me + 1) % size).wait_recv()

        @pl.when(kept > 0)
        def _():
            local(rows(mid_ref, 0), j * chunk).wait()

        return carry

    lax.fori_loop(0, own_count // chunk, arrive, 0)
    for base, start, length in sections:

        def sent(j, carry, base=base, aimed=aim(start, length)):
            over = (aimed[1] + j * chunk >= own_count).astype(jnp.int32)
            owner = aimed[0] + over
            first = aimed[1] + j * chunk - over * own_count

            @pl.when(owner != me)
            def _():
                remote(rows(mid_ref, base + j * chunk), first, owner, base // chunk + j).wait_send()

            return carry

        lax.fori_loop(0, length // chunk, sent, 0)


def share_rows(block, middle, ident):
    size = lax.axis_size("fsdp")
    rows, columns = block.shape
    own_count = ADAPTER_COLUMNS // size
    chunk = math.gcd(own_count, MODEL_WIDTH // size, HIDDEN_COUNT // size, PROJECT_COLUMNS, GATE_START)
    anywhere = pl.BlockSpec(memory_space=pl.ANY)
    pair = pltpu.SemaphoreType.DMA((2, size // 4))
    sides = pltpu.SemaphoreType.DMA((2, size // 4 + 1))
    return pl.pallas_call(
        functools.partial(share_kernel, size, chunk, own_count),
        out_shape=(
            jax.ShapeDtypeStruct((size * rows, columns), block.dtype),
            jax.ShapeDtypeStruct((own_count, ADAPTER_RANK), bf16),
        ),
        in_specs=[anywhere] * 2,
        out_specs=(anywhere, anywhere),
        scratch_shapes=[
            pltpu.SemaphoreType.DMA,
            pair,
            pair,
            sides,
            sides,
            pltpu.SemaphoreType.DMA((middle.shape[0] // chunk,)),
            pltpu.SemaphoreType.DMA((own_count // chunk,)),
            pltpu.SemaphoreType.DMA((own_count // chunk,)),
        ],
        compiler_params=pltpu.CompilerParams(collective_id=ident, has_side_effects=True),
        cost_estimate=busy(1),
        name="share_rows",
    )(block, middle)


def per_device(
    hidden_input,
    sequence_lengths,
    norm_gain_values,
    input_proj_weight,
    output_proj_weight,
    feedforward_weight,
    adapter_first,
    adapter_second,
    adapter_down_first,
    output_gradient,
):
    size = lax.axis_size("fsdp")
    place = lax.axis_index("fsdp")
    tokens_dev = hidden_input.shape[1]
    all_rows = tokens_dev * size
    hidden_own = HIDDEN_COUNT // size
    width_own = MODEL_WIDTH // size
    columns_own = ADAPTER_COLUMNS // size
    offset = place * tokens_dev
    segment_all, position_all = segment_info(sequence_lengths[0], all_rows)
    segment_own = lax.dynamic_slice_in_dim(segment_all, offset, tokens_dev)
    position_own = lax.dynamic_slice_in_dim(position_all, offset, tokens_dev)
    row_all = jnp.arange(all_rows, dtype=jnp.int32)
    row_own = offset + jnp.arange(tokens_dev, dtype=jnp.int32)
    allowed = (segment_own[:, None] == segment_all[None, :]) & (
        row_own[:, None] >= row_all[None, :]
    )
    gains = norm_gain_values.astype(f32)
    first_factor = adapter_first[0]
    second_factor = adapter_second[0]
    rank = ADAPTER_RANK
    narrow_projection = first_factor[:, : 3 * rank]
    narrow_output = first_factor[:, 3 * rank : 4 * rank]
    squeeze_gate = first_factor[:, 4 * rank : 5 * rank]
    squeeze_up = first_factor[:, 5 * rank :]
    narrow_down = lax.dynamic_slice_in_dim(adapter_down_first[0], place * hidden_own, hidden_own, 0)
    widen_query = second_factor[:, :QUERY_WIDTH]
    widen_key = second_factor[:, QUERY_WIDTH : QUERY_WIDTH + HEAD_WIDTH]
    widen_value = second_factor[:, QUERY_WIDTH + HEAD_WIDTH : PROJECT_COLUMNS]
    widen_output = second_factor[:, PROJECT_COLUMNS:GATE_START]
    widen_gate = lax.dynamic_slice_in_dim(
        second_factor, GATE_START + place * hidden_own, hidden_own, 1
    )
    widen_up = lax.dynamic_slice_in_dim(
        second_factor, GATE_START + HIDDEN_COUNT + place * hidden_own, hidden_own, 1
    )
    widen_down = second_factor[:, GATE_START + 2 * HIDDEN_COUNT :]
    scaling = HEAD_WIDTH ** (-0.5)

    hidden_state = hidden_input[0].astype(f32)
    scale_one = rms_scale(hidden_state)
    normalized = (hidden_state * scale_one * gains[0]).astype(bf16)
    proj_in = ring_gather(input_proj_weight, 0)
    proj_in, proj_out = lax.optimization_barrier((proj_in, output_proj_weight))
    proj_out = gather_rows(proj_out)
    lora_qkv = matrix_product(normalized, narrow_projection).astype(bf16)
    projected = matrix_product(normalized, proj_in)
    query_pre = projected[:, :QUERY_WIDTH] + matrix_product(lora_qkv[:, :rank], widen_query)
    key_pre = projected[:, QUERY_WIDTH : QUERY_WIDTH + HEAD_WIDTH] + matrix_product(
        lora_qkv[:, rank : 2 * rank], widen_key
    )
    value_local = (
        projected[:, QUERY_WIDTH + HEAD_WIDTH :]
        + matrix_product(lora_qkv[:, 2 * rank :], widen_value)
    ).astype(bf16)
    query_rot = rotate(query_pre, position_own, 1.0).astype(bf16)
    key_rot = rotate(key_pre, position_own, 1.0).astype(bf16)
    keys_all = ring_gather(jnp.concatenate([key_rot, value_local], axis=1), 1)
    key_rows, value_rows = keys_all[:, :HEAD_WIDTH], keys_all[:, HEAD_WIDTH:]
    query_heads = query_rot.reshape(tokens_dev, HEADS, HEAD_WIDTH)
    scores = scores_of(query_heads, key_rows, allowed, scaling)
    row_max = jnp.max(scores, axis=-1, keepdims=True)
    powered = jnp.exp(scores - row_max)
    row_sum = jnp.sum(powered, axis=-1, keepdims=True)
    probs = powered / row_sum
    probs_low = probs.astype(bf16)
    attended = (
        jnp.einsum("thu,ud->thd", probs_low, value_rows, preferred_element_type=f32)
        .reshape(tokens_dev, QUERY_WIDTH)
        .astype(bf16)
    )
    lora_out = matrix_product(attended, narrow_output).astype(bf16)
    middle = (
        hidden_state
        + times_transposed(attended, proj_out)
        + matrix_product(lora_out, widen_output)
    )
    scale_two = rms_scale(middle)
    normed_two = (middle * scale_two * gains[1]).astype(bf16)

    weight_planes = feedforward_weight.transpose(1, 0, 2)
    two_all, grad_all, attended_all, acts, low_ffn, ffn_shares, ffn_pieces, down_own = unit_rows(
        jnp.concatenate([normed_two, lora_out], axis=1),
        output_gradient[0],
        jnp.concatenate([attended, lora_qkv], axis=1),
        weight_planes,
        first_factor[:, 4 * rank :],
        widen_down,
        widen_gate,
        widen_up,
        narrow_down,
        2,
    )
    lora_out_all = low_ffn[:, 3 * rank :]
    ffn_both = loop_shares(ffn_shares)
    rows_sum = mix_rows(
        acts, weight_planes, widen_gate, widen_up, narrow_down, 3
    )
    back_own, out_own = rows_sum[:, : MODEL_WIDTH + 2 * rank], rows_sum[:, MODEL_WIDTH + 2 * rank :]
    lora_hd = out_own[:, MODEL_WIDTH:].astype(bf16)
    hidden_out = (middle + out_own[:, :MODEL_WIDTH] + matrix_product(lora_hd, widen_down)).astype(bf16)

    gate_low = back_own[:, MODEL_WIDTH : MODEL_WIDTH + rank].astype(bf16)
    up_low = back_own[:, MODEL_WIDTH + rank :].astype(bf16)
    two_grad = (
        back_own[:, :MODEL_WIDTH]
        + times_transposed(gate_low, squeeze_gate)
        + times_transposed(up_low, squeeze_up)
    )
    weighted_two = gains[1] * two_grad
    middle_grad = (
        output_gradient[0].astype(f32)
        + scale_two * weighted_two
        - middle * scale_two**3 * jnp.mean(middle * weighted_two, axis=-1, keepdims=True)
    )
    gain_two = jnp.sum(two_grad * middle * scale_two, axis=0)

    branch_grad = middle_grad.astype(bf16)
    both = [block.reshape(tokens_dev, size, width_own) for block in (normalized, branch_grad)]
    turned = turn(jnp.concatenate(both, axis=2).reshape(tokens_dev, -1))
    normed_turn, branch_turn = turned[:, :width_own], turned[:, width_own:]
    lora_out_grad = times_transposed(branch_grad, widen_output).astype(bf16)
    attended_grad = (
        matrix_product(branch_grad, proj_out) + times_transposed(lora_out_grad, narrow_output)
    ).astype(bf16)
    heads_grad = attended_grad.reshape(tokens_dev, HEADS, HEAD_WIDTH)
    prob_grad = jnp.einsum("thd,ud->thu", heads_grad, value_rows, preferred_element_type=f32)
    row_dot = jnp.sum(probs * prob_grad, axis=-1, keepdims=True)
    score_grad = (probs * (prob_grad - row_dot)).astype(bf16)
    query_rot_grad = (
        jnp.einsum("thu,ud->thd", score_grad, key_rows, preferred_element_type=f32) * scaling
    )
    key_part = (
        jnp.einsum("thu,thd->ud", score_grad, query_heads, preferred_element_type=f32) * scaling
    )
    value_part = jnp.einsum("thu,thd->ud", probs_low, heads_grad, preferred_element_type=f32)
    pair_grad = ring_scatter([key_part, value_part], 4)
    pair_grad, normed_turn, branch_turn = lax.optimization_barrier((pair_grad, normed_turn, branch_turn))
    query_grad = rotate(
        query_rot_grad.reshape(tokens_dev, QUERY_WIDTH), position_own, -1.0
    ).astype(bf16)
    key_grad = rotate(pair_grad[:, :HEAD_WIDTH], position_own, -1.0).astype(bf16)
    value_grad = pair_grad[:, HEAD_WIDTH:].astype(bf16)
    proj_grad = jnp.concatenate([query_grad, key_grad, value_grad], axis=1)
    lora_qkv_grad = jnp.concatenate(
        [
            times_transposed(query_grad, widen_query),
            times_transposed(key_grad, widen_key),
            times_transposed(value_grad, widen_value),
        ],
        axis=1,
    ).astype(bf16)
    normed_grad = times_transposed(proj_grad, proj_in) + times_transposed(
        lora_qkv_grad, narrow_projection
    )
    weighted_one = gains[0] * normed_grad
    input_grad = (
        middle_grad
        + scale_one * weighted_one
        - hidden_state
        * scale_one**3
        * jnp.mean(hidden_state * weighted_one, axis=-1, keepdims=True)
    )
    gain_one = jnp.sum(normed_grad * hidden_state * scale_one, axis=0)

    lora_qkv_all = attended_all[:, QUERY_WIDTH:]
    out_piece = outer_product_rows(branch_turn, lora_out_all)
    gain_rows = jnp.stack([gain_one, gain_two]).astype(bf16).reshape(tokens_dev, -1)
    gain_count = gain_rows.shape[1]
    gain_rows = jnp.pad(gain_rows, ((0, 0), (0, -gain_count % 128)))
    proj_rows = jnp.concatenate(
        [proj_grad, lora_out_grad, gate_low, up_low, lora_hd, gain_rows], axis=1
    )
    proj_all, middle_own = share_rows(
        proj_rows, jnp.concatenate([out_piece.astype(bf16), ffn_pieces[0], ffn_pieces[1]], axis=0), 5
    )
    column = place * width_own
    gain_all = proj_all[:, PROJECT_COLUMNS + 4 * rank :][:, :gain_count].reshape(size, 2, MODEL_WIDTH)
    gain_all = jnp.sum(gain_all.astype(f32), axis=0)
    gain_own = lax.dynamic_slice_in_dim(gain_all, column, width_own, 1)
    gain_part = jnp.pad(gain_own, ((0, width_own - 2), (0, -width_own % 128)))
    attn_part = jnp.concatenate(
        [
            outer_product_rows(normed_turn, proj_all[:, :PROJECT_COLUMNS]),
            outer_product_rows(branch_turn, attended_all)[:, :QUERY_WIDTH],
            gain_part,
        ],
        axis=1,
    ).astype(bf16)
    attn_part, ffn_both, proj_all = lax.optimization_barrier((attn_part, ffn_both, proj_all))
    attn_sum = both_loops(loop_shares(attn_part))
    gain_column = PROJECT_COLUMNS + QUERY_WIDTH
    gain_sum = attn_sum[:2, gain_column : gain_column + width_own]
    low_all = proj_all[:, PROJECT_COLUMNS : PROJECT_COLUMNS + 4 * rank]
    proj_all = proj_all[:, :PROJECT_COLUMNS]
    qkv_low_all = jnp.concatenate(
        [
            times_transposed(proj_all[:, :QUERY_WIDTH], widen_query),
            times_transposed(proj_all[:, QUERY_WIDTH : QUERY_WIDTH + HEAD_WIDTH], widen_key),
            times_transposed(proj_all[:, QUERY_WIDTH + HEAD_WIDTH :], widen_value),
        ],
        axis=1,
    ).astype(bf16)
    attended_turn = lax.dynamic_slice_in_dim(attended_all, column, width_own, 1)
    two_turn = lax.dynamic_slice_in_dim(two_all, column, width_own, 1)
    squeeze_own = jnp.concatenate(
        [
            outer_product_rows(normed_turn, qkv_low_all),
            outer_product_rows(attended_turn, low_all[:, :rank]),
            outer_product_rows(two_turn, low_all[:, rank : 3 * rank]),
        ],
        axis=1,
    )
    near = jnp.concatenate(
        [
            outer_product_rows(proj_all[:, :QUERY_WIDTH], lora_qkv_all[:, :rank]),
            outer_product_rows(
                proj_all[:, QUERY_WIDTH : QUERY_WIDTH + HEAD_WIDTH], lora_qkv_all[:, rank : 2 * rank]
            ),
            outer_product_rows(proj_all[:, QUERY_WIDTH + HEAD_WIDTH :], lora_qkv_all[:, 2 * rank :]),
        ],
        axis=0,
    )
    far = outer_product_rows(grad_all, low_all[:, 3 * rank :])
    first = place * columns_own
    far_start = GATE_START + 2 * HIDDEN_COUNT
    near = lax.dynamic_slice_in_dim(
        jnp.pad(near.astype(bf16), ((0, columns_own), (0, 0))), jnp.minimum(first, PROJECT_COLUMNS), columns_own, 0
    )
    far = lax.dynamic_slice_in_dim(
        jnp.pad(far.astype(bf16), ((columns_own, 0), (0, 0))),
        jnp.maximum(first - far_start + columns_own, 0),
        columns_own,
        0,
    )
    owned = first + jnp.arange(columns_own, dtype=jnp.int32)[:, None]
    expand_own = jnp.where(
        owned < PROJECT_COLUMNS, near, jnp.where(owned < far_start, middle_own, far)
    ).T.astype(f32)
    ffn_sum = both_loops(ffn_both).transpose(1, 0, 2)
    return (
        hidden_out[None],
        input_grad[None],
        gain_sum,
        attn_sum[:, :PROJECT_COLUMNS],
        attn_sum[:, PROJECT_COLUMNS:gain_column],
        ffn_sum,
        squeeze_own[None],
        expand_own[None],
        down_own[None],
    )


def solution(mesh):
    return jax.shard_map(
        per_device,
        mesh=mesh,
        in_specs=(
            P("loop", "fsdp", None),
            P("loop", None),
            P(),
            P("fsdp", None),
            P("fsdp", None),
            P("fsdp", None, None),
            P("loop", None, None),
            P("loop", None, None),
            P("loop", None, None),
            P("loop", "fsdp", None),
        ),
        out_specs=(
            P("loop", "fsdp", None),
            P("loop", "fsdp", None),
            P(None, "fsdp"),
            P("fsdp", None),
            P("fsdp", None),
            P("fsdp", None, None),
            P("loop", "fsdp", None),
            P("loop", None, "fsdp"),
            P("loop", "fsdp", None),
        ),
        check_vma=False,
    )
```

```python
import functools
import math

import jax
import jax.numpy as jnp
from jax import lax
from jax.experimental import pallas as pl
from jax.experimental.pallas import tpu as pltpu
from jax.sharding import PartitionSpec as P

MODEL_WIDTH = 2048
HEADS = 8
HEAD_WIDTH = 256
HIDDEN_COUNT = 16384
ADAPTER_RANK = 256
QUERY_WIDTH = 2048
PROJECT_COLUMNS = 2560
ADAPTER_COLUMNS = 39424
GATE_START = PROJECT_COLUMNS + MODEL_WIDTH

epsilon = 1e-06
bf16 = jnp.bfloat16
f32 = jnp.float32
MESH = pl.DeviceIdType.MESH


def matrix_product(former, latter):
    return jnp.dot(former, latter, preferred_element_type=f32)


def times_transposed(former, latter):
    return lax.dot_general(former, latter, (((1,), (1,)), ((), ())), preferred_element_type=f32)


def outer_product_rows(former, latter):
    return lax.dot_general(former, latter, (((0,), (0,)), ((), ())), preferred_element_type=f32)


def segment_info(lengths, row_count):
    row_ids = jnp.arange(row_count, dtype=jnp.int32)
    count = lengths.shape[0]
    labels = jnp.arange(count, dtype=jnp.int32)
    finish = jnp.sum(jnp.where(labels[:, None] <= labels[None, :], lengths[:, None], 0), axis=0)
    starts = finish - lengths
    segment = jnp.sum((row_ids[:, None] >= finish[None, :]).astype(jnp.int32), axis=1)
    opening = jnp.sum(jnp.where(segment[:, None] == labels[None, :], starts[None, :], 0), axis=1)
    return (segment, row_ids - opening)


def rotate(values, position, direction):
    half_dim = HEAD_WIDTH // 2
    frequency = jnp.exp(
        jnp.arange(half_dim).astype(f32) * (-2.0 * math.log(10000.0) / HEAD_WIDTH)
    )
    angles = position.astype(f32)[:, None] * frequency[None, :]
    cosine = jnp.cos(angles)[:, None, :]
    sine_val = direction * jnp.sin(angles)[:, None, :]
    shaped = values.reshape(values.shape[0], -1, HEAD_WIDTH)
    former = shaped[..., :half_dim]
    latter = shaped[..., half_dim:]
    turned = jnp.concatenate(
        [former * cosine - latter * sine_val, latter * cosine + former * sine_val], axis=-1
    )
    return turned.reshape(values.shape)


def rms_scale(values):
    return lax.rsqrt(jnp.mean(values * values, axis=-1, keepdims=True) + epsilon)


def gelu_tanh(values):
    return jax.nn.gelu(values, approximate=True)


def unit_backward(gate_value, upward_activation, hidden_unit_gradient):
    activated, pullback_function = jax.vjp(gelu_tanh, gate_value)
    gate_grad = pullback_function(hidden_unit_gradient * upward_activation)[0]
    return (gate_grad.astype(bf16), (hidden_unit_gradient * activated).astype(bf16))


def scores_of(query_heads, key_rows, allowed, scaling):
    product = (
        jnp.einsum("thd,ud->thu", query_heads, key_rows, preferred_element_type=f32) * scaling
    )
    return jnp.where(allowed[:, None, :], product, -1e30)


def gather_rows(block):
    return lax.all_gather(block, "fsdp", axis=0, tiled=True)


def scatter_rows(partial):
    return lax.psum_scatter(partial.astype(bf16), "fsdp", scatter_dimension=0, tiled=True).astype(f32)


def loop_shares(partial):
    return lax.all_gather(partial.astype(bf16), "loop", axis=0)


def both_loops(shares):
    return shares[0].astype(f32) + shares[1].astype(f32)


def turn(block):
    return lax.all_to_all(block, "fsdp", split_axis=1, concat_axis=0, tiled=True)


def chip_at(q, chips):
    return jnp.where(q < 4, 2 * q, 15 - 2 * q) if chips == 8 else q

def ring_place(chip, chips):
    return jnp.where(chip % 2 == 0, chip // 2, 7 - chip // 2) if chips == 8 else chip

def ring_neighbours(chips):
    me = lax.axis_index("fsdp")
    core = me % 2
    p = ring_place(me // 2, chips)
    def device(shift, c):
        return chip_at((p + shift + chips) % chips, chips) * 2 + c
    return core, device

def meet(devices):
    barrier = pltpu.get_barrier_semaphore()
    for d in devices:
        pl.semaphore_signal(barrier, inc=1, device_id={"fsdp": d}, device_id_type=MESH)
    pl.semaphore_wait(barrier, len(devices))

def gather_kernel(chips, x_ref, o_ref, own_sem, ring_send, ring_recv, side_send, side_recv, greet, also, work):
    core, device = ring_neighbours(chips)
    rows = x_ref.shape[0]
    reach = chips // 2
    ways = (device(1, core), device(-1, core))
    side = device(0, 1 - core)
    if greet is None:
        meet((*ways, side))
    else:
        greet()

    def span(way, hops):
        return (way * (rows // 2), rows // 2) if hops == reach else (0, rows)

    def at(way, hops, c, part):
        origin = device(-hops if way == 0 else hops, c)
        return o_ref.at[pl.ds(pl.multiple_of(origin * rows + part[0], 8), part[1])]

    def hop(way, hops):
        part = span(way, hops)
        here = at(way, hops - 1, core, part)
        src = x_ref.at[pl.ds(part[0], part[1])] if hops == 1 else here
        return pltpu.make_async_remote_copy(src, here, ring_send.at[way, hops - 1], ring_recv.at[way, hops - 1], device_id={"fsdp": ways[way]}, device_id_type=MESH)

    def arriving(way, hops):
        here = at(way, hops, core, span(way, hops))
        return pltpu.make_async_remote_copy(here, here, ring_send.at[way, hops - 1], ring_recv.at[way, hops - 1], device_id={"fsdp": ways[way]}, device_id_type=MESH)

    def across(way, hops, c):
        part = span(way, hops) if hops else (0, rows)
        there = at(way, hops, c, part)
        src = there if hops else x_ref
        return pltpu.make_async_remote_copy(src, there, side_send.at[way, hops], side_recv.at[way, hops], device_id={"fsdp": side}, device_id_type=MESH)

    for way in (0, 1):
        hop(way, 1).start()
    across(0, 0, core).start()
    own = pltpu.make_async_copy(x_ref, at(0, 0, core, (0, rows)), own_sem)
    own.start()
    if also is not None:
        also()
    if work is not None:
        own.wait()
        across(0, 0, 1 - core).wait_recv()
        work(0)
    for hops in range(1, reach + 1):
        for way in (0, 1):
            arriving(way, hops).wait_recv()
            if hops < reach:
                hop(way, hops + 1).start()
            across(way, hops, core).start()
        if work is not None:
            for way in (0, 1):
                across(way, hops, 1 - core).wait_recv()
                if hops < reach:
                    work(-hops if way == 0 else hops)
                elif way:
                    work(reach)
    if work is None:
        own.wait()
        across(0, 0, 1 - core).wait_recv()
        for hops in range(1, reach + 1):
            for way in (0, 1):
                across(way, hops, 1 - core).wait_recv()
    across(0, 0, core).wait_send()
    for hops in range(1, reach + 1):
        for way in (0, 1):
            across(way, hops, core).wait_send()
            hop(way, hops).wait_send()


def busy(us):
    return pl.CostEstimate(flops=0, bytes_accessed=int(us * 3.0e6), transcendentals=0)


def ring_gather(block, ident):
    size = lax.axis_size("fsdp")
    chips = size // 2
    rows, columns = block.shape
    pair = pltpu.SemaphoreType.DMA((2, chips // 2))
    sides = pltpu.SemaphoreType.DMA((2, chips // 2 + 1))
    return pl.pallas_call(
        functools.partial(gather_kernel, chips, greet=None, also=None, work=None),
        out_shape=jax.ShapeDtypeStruct((size * rows, columns), block.dtype),
        in_specs=[pl.BlockSpec(memory_space=pl.ANY)],
        out_specs=pl.BlockSpec(memory_space=pl.ANY),
        scratch_shapes=[pltpu.SemaphoreType.DMA, pair, pair, sides, sides],
        compiler_params=pltpu.CompilerParams(collective_id=ident, has_side_effects=True),
        cost_estimate=busy(1),
        name="ring_gather",
    )(block)

def scatter_kernel(chips, count, *refs):
    x_refs, o_ref = refs[:count], refs[count]
    side_buf, ring_buf, side_send, side_recv, ring_send, ring_recv = refs[count + 1 :]
    core, device = ring_neighbours(chips)
    rows, columns = o_ref.shape
    reach = chips // 2
    half = columns // 2
    tile = 16
    ways = (device(1, core), device(-1, core))
    side = device(0, 1 - core)
    meet((*ways, side))
    starts = [sum(x.shape[1] for x in x_refs[:i]) for i in range(count)]

    def shift(way, hops):
        return (hops if way == 0 else chips - hops) % chips

    def across(target, c, i):
        there = pl.ds(pl.multiple_of(device(target, c) * rows, tile), rows)
        return pltpu.make_async_remote_copy(
            x_refs[i].at[there],
            side_buf.at[target, :, pl.ds(starts[i], x_refs[i].shape[1])],
            side_send.at[target, i],
            side_recv.at[target, i],
            device_id={"fsdp": side},
            device_id_type=MESH,
        )

    def hop(way, step):
        cols = pl.ds(way * half, half) if step == 0 else pl.ds(0, columns)
        return pltpu.make_async_remote_copy(
            side_buf.at[shift(way, reach - step), :, cols],
            ring_buf.at[way, step, :, cols],
            ring_send.at[way, step],
            ring_recv.at[way, step],
            device_id={"fsdp": ways[way]},
            device_id_type=MESH,
        )

    order = [reach] + [shift(way, hops) for hops in range(reach - 1, 0, -1) for way in (0, 1)] + [0]
    for target in order:
        for i in range(count):
            across(target, 1 - core, i).start()

    def add(target, incoming, store):
        first = pl.multiple_of(device(target, core) * rows, tile)
        for i in range(count):
            across(target, core, i).wait_recv()

        @pl.loop(0, rows // tile)
        def _(j):
            here = pl.ds(pl.multiple_of(j * tile, tile), tile)
            mine = pl.ds(pl.multiple_of(first + j * tile, tile), tile)
            for i in range(count):
                cols = pl.ds(starts[i], x_refs[i].shape[1])
                total = x_refs[i][mine, :].astype(f32) + side_buf[target, here, cols].astype(f32)
                for way, step in incoming:
                    if step:
                        total = total + ring_buf[way, step, here, cols].astype(f32)
                store(here, cols, total)
            for way, step in incoming:
                if not step:
                    cols = pl.ds(way * half, half)
                    store(
                        here,
                        cols,
                        side_buf[target, here, cols].astype(f32) + ring_buf[way, 0, here, cols].astype(f32),
                    )

    for step in range(reach):
        for way in (0, 1):
            target = shift(way, reach - step)
            if step:
                hop(way, step - 1).wait_recv()

            def store(here, cols, total, target=target):
                side_buf[target, here, cols] = total.astype(bf16)

            if step or way == 0:
                add(target, [(way, step - 1)] if step else [], store)
            hop(way, step).start()
    for way in (0, 1):
        hop(way, reach - 1).wait_recv()

    def last(here, cols, total):
        o_ref[here, cols] = total

    add(0, [(0, reach - 1), (1, reach - 1)], last)
    for target in order:
        for i in range(count):
            across(target, 1 - core, i).wait_send()
    for step in range(reach):
        for way in (0, 1):
            hop(way, step).wait_send()


def ring_scatter(terms, ident):
    size = lax.axis_size("fsdp")
    terms = [term.astype(bf16) for term in terms]
    if size != 16:
        return scatter_rows(jnp.concatenate(terms, axis=1))
    chips, count = size // 2, len(terms)
    rows, columns = terms[0].shape[0] // size, sum(term.shape[1] for term in terms)
    pair = pltpu.SemaphoreType.DMA((2, chips // 2))
    sides = pltpu.SemaphoreType.DMA((chips, count))
    return pl.pallas_call(
        functools.partial(scatter_kernel, chips, count),
        out_shape=jax.ShapeDtypeStruct((rows, columns), f32),
        in_specs=[pl.BlockSpec(memory_space=pltpu.VMEM)] * count,
        out_specs=pl.BlockSpec(memory_space=pltpu.VMEM),
        scratch_shapes=[
            pltpu.VMEM((chips, rows, columns), bf16),
            pltpu.VMEM((2, chips // 2, rows, columns), bf16),
            sides,
            sides,
            pair,
            pair,
        ],
        compiler_params=pltpu.CompilerParams(
            collective_id=ident, has_side_effects=True, vmem_limit_bytes=56 << 20
        ),
        cost_estimate=busy(1),
        name="ring_scatter",
    )(*terms)


def unit_kernel(chips, *refs):
    sources, (planes, squeeze, widen_down, widen_gate, widen_up, narrow) = refs[:3], refs[3:9]
    two_all, grad_all, later_all, acts_all, low_all, share_out, piece_out, down_out = refs[9:17]
    held, turned, acts, low, tiles = refs[17:22]
    landed = (refs[22], refs[23], later_all)
    held_sem, own_sem, ring_send, ring_recv, side_send, side_recv, out_sem, acts_sem, tile_sem = refs[24:]
    core, device = ring_neighbours(chips)
    rows = sources[0].shape[0]
    reach = chips // 2
    wide = 256
    ways = (device(1, core), device(-1, core))
    side = device(0, 1 - core)
    fetches = [pltpu.make_async_copy(planes.at[i], held.at[i], held_sem.at[i]) for i in range(3)]
    for fetch in fetches:
        fetch.start()
    meet((*ways, side))

    def span(way, hops):
        return (way * (rows // 2), rows // 2) if hops == reach else (0, rows)

    def at(i, way, hops, c, part):
        origin = device(-hops if way == 0 else hops, c)
        return landed[i].at[pl.ds(pl.multiple_of(origin * rows + part[0], 16), part[1])]

    def hop(i, way, hops):
        part = span(way, hops)
        here = at(i, way, hops - 1, core, part)
        src = sources[i].at[pl.ds(part[0], part[1])] if hops == 1 else here
        return pltpu.make_async_remote_copy(
            src,
            here,
            ring_send.at[i, way, hops - 1],
            ring_recv.at[i, way, hops - 1],
            device_id={"fsdp": ways[way]},
            device_id_type=MESH,
        )

    def arriving(i, way, hops):
        here = at(i, way, hops, core, span(way, hops))
        return pltpu.make_async_remote_copy(
            here,
            here,
            ring_send.at[i, way, hops - 1],
            ring_recv.at[i, way, hops - 1],
            device_id={"fsdp": ways[way]},
            device_id_type=MESH,
        )

    def across(i, way, hops, c):
        part = span(way, hops) if hops else (0, rows)
        there = at(i, way, hops, c, part)
        return pltpu.make_async_remote_copy(
            there if hops else sources[i],
            there,
            side_send.at[i, way, hops],
            side_recv.at[i, way, hops],
            device_id={"fsdp": side},
            device_id_type=MESH,
        )

    def leaving(n, first):
        mine = pl.ds(first, 2 * rows)
        width, under = grad_all.shape[1], low.shape[1]
        pairs = [
            (landed[0].at[mine, pl.ds(0, width)], two_all.at[mine]),
            (landed[0].at[mine, pl.ds(width, ADAPTER_RANK)], low_all.at[mine, pl.ds(under, ADAPTER_RANK)]),
            (low.at[mine], low_all.at[mine, pl.ds(0, under)]),
            (landed[1].at[mine], grad_all.at[mine]),
        ]
        return [pltpu.make_async_copy(a, b, out_sem.at[n, i]) for i, (a, b) in enumerate(pairs)]

    def shown(n, first):
        mine = pl.ds(first, 2 * rows)
        return [
            pltpu.make_async_copy(acts.at[n % 2, i], acts_all.at[i, mine], acts_sem.at[n % 2, i]) for i in range(3)
        ]

    def first_row(shift):
        return pl.multiple_of(device(shift, 0) * rows, 2 * rows)

    def work(n, first):
        mine = pl.ds(first, 2 * rows)
        rank, width = ADAPTER_RANK, MODEL_WIDTH
        if n >= 2:
            for copy in shown(n, first):
                copy.wait()
        low[mine, : 2 * rank] = matrix_product(landed[0][mine, :width], squeeze[...]).astype(bf16)
        low[mine, 2 * rank :] = times_transposed(landed[1][mine, :], widen_down[...]).astype(bf16)

        @pl.loop(0, held.shape[1] // wide)
        def _(t):
            own = pl.ds(pl.multiple_of(t * wide, wide), wide)
            two = landed[0][mine, :width]
            gate = times_transposed(two, held[0, own, :]) + matrix_product(
                low[mine, :rank], widen_gate[:, own]
            )
            upward = times_transposed(two, held[1, own, :]) + matrix_product(
                low[mine, rank : 2 * rank], widen_up[:, own]
            )
            pull = times_transposed(landed[1][mine, :], held[2, own, :]) + times_transposed(
                low[mine, 2 * rank :], narrow[own, :]
            )
            scale = math.sqrt(2.0 / math.pi)
            square = gate * gate
            bend = jnp.tanh(scale * gate * (1.0 + 0.044715 * square))
            rise = 0.5 * (1.0 + bend)
            active = gate * rise
            slope = rise + 0.5 * gate * (1.0 - bend * bend) * (scale * (1.0 + 3 * 0.044715 * square))
            for i, value in enumerate((pull * upward * slope, pull * active, active * upward)):
                acts[n % 2, i, :, own] = value.astype(bf16)
                turned[i, own, mine] = value.T.astype(bf16)

        for copy in leaving(n, first) + shown(n, first):
            copy.start()

    for i in (0, 1):
        for way in (0, 1):
            hop(i, way, 1).start()
        across(i, 0, 0, core).start()
    keeps = [
        pltpu.make_async_copy(sources[i], at(i, 0, 0, core, (0, rows)), own_sem.at[i]) for i in range(3)
    ]
    for keep in keeps:
        keep.start()
    for copy in keeps + fetches:
        copy.wait()
    for i in (0, 1):
        across(i, 0, 0, 1 - core).wait_recv()
    work(0, first_row(0))
    for hops in range(1, reach + 1):
        for i in (0, 1):
            for way in (0, 1):
                arriving(i, way, hops).wait_recv()
                if hops < reach:
                    hop(i, way, hops + 1).start()
                across(i, way, hops, core).start()
        if hops == reach:
            for way in (0, 1):
                hop(2, way, 1).start()
            across(2, 0, 0, core).start()
        else:
            for way in (0, 1):
                for i in (0, 1):
                    across(i, way, hops, 1 - core).wait_recv()
                work(2 * hops - 1 + way, first_row(-hops if way == 0 else hops))
    for way in (0, 1):
        for i in (0, 1):
            across(i, way, reach, 1 - core).wait_recv()
    work(2 * reach - 1, first_row(reach))
    rank = ADAPTER_RANK

    def relay(hops):
        for way in (0, 1):
            arriving(2, way, hops).wait_recv()
            if hops < reach:
                hop(2, way, hops + 1).start()
            across(2, way, hops, core).start()

    for kind in range(3):

        def tile_copy(t, kind=kind):
            there = pl.ds(pl.multiple_of(t * wide, wide), wide)
            return pltpu.make_async_copy(
                tiles.at[t % 2], share_out.at[kind, :, there], tile_sem.at[t % 2]
            )

        @pl.loop(0, MODEL_WIDTH // wide)
        def _(t, kind=kind, tile_copy=tile_copy):
            @pl.when(t > 1)
            def _():
                tile_copy(t - 2).wait()

            cols = pl.ds(pl.multiple_of(t * wide, wide), wide)
            tiles[t % 2] = matrix_product(
                turned[kind], landed[1 if kind == 2 else 0][:, cols]
            ).astype(bf16)
            tile_copy(t).start()

        relay(kind + 1)
        if kind == 2:
            piece_out[0] = matrix_product(turned[0], low[:, :rank]).astype(bf16)
            piece_out[1] = matrix_product(turned[1], low[:, rank : 2 * rank]).astype(bf16)
            down_out[...] = matrix_product(turned[2], low[:, 2 * rank :])
        tile_copy(MODEL_WIDTH // wide - 2).wait()
        tile_copy(MODEL_WIDTH // wide - 1).wait()
    for hops in range(4, reach + 1):
        relay(hops)
    across(2, 0, 0, 1 - core).wait_recv()
    for hops in range(1, reach + 1):
        for way in (0, 1):
            across(2, way, hops, 1 - core).wait_recv()
    for i in range(3):
        across(i, 0, 0, core).wait_send()
        for hops in range(1, reach + 1):
            for way in (0, 1):
                across(i, way, hops, core).wait_send()
                hop(i, way, hops).wait_send()
    for n in range(chips):
        if n == 0:
            shift = 0
        elif n == 2 * reach - 1:
            shift = reach
        else:
            shift = (-1 if n % 2 else 1) * ((n + 1) // 2)
        for copy in leaving(n, first_row(shift)):
            copy.wait()
        if n >= chips - 2:
            for copy in shown(n, first_row(shift)):
                copy.wait()


def unit_rows(two, grad, later, planes, squeeze, widen_down, widen_gate, widen_up, narrow, ident):
    size = lax.axis_size("fsdp")
    rank = ADAPTER_RANK
    if size != 16:
        two, grad = gather_rows(two), gather_rows(grad)
        two, lora_out = two[:, :MODEL_WIDTH], two[:, MODEL_WIDTH:]
        low = matrix_product(two, squeeze).astype(bf16)
        pulled = times_transposed(grad, widen_down).astype(bf16)
        gate = times_transposed(two, planes[0]) + matrix_product(low[:, :rank], widen_gate)
        upward = times_transposed(two, planes[1]) + matrix_product(low[:, rank:], widen_up)
        units_grad = times_transposed(grad, planes[2]) + times_transposed(pulled, narrow)
        units = (gelu_tanh(gate) * upward).astype(bf16)
        gate_grad, up_grad = unit_backward(gate, upward, units_grad)
        return (
            two,
            grad,
            gather_rows(later),
            jnp.stack([gate_grad, up_grad, units]),
            jnp.concatenate([low, pulled, lora_out], axis=1),
            jnp.stack(
                [
                    outer_product_rows(gate_grad, two),
                    outer_product_rows(up_grad, two),
                    outer_product_rows(units, grad),
                ]
            ).astype(bf16),
            jnp.stack(
                [outer_product_rows(gate_grad, low[:, :rank]), outer_product_rows(up_grad, low[:, rank:])]
            ).astype(bf16),
            outer_product_rows(units, pulled),
        )
    chips = size // 2
    rows, columns = grad.shape
    all_rows, hidden = size * rows, planes.shape[1]
    anywhere, inside = pl.BlockSpec(memory_space=pl.ANY), pl.BlockSpec(memory_space=pltpu.VMEM)
    pair = pltpu.SemaphoreType.DMA((3, 2, chips // 2))
    sides = pltpu.SemaphoreType.DMA((3, 2, chips // 2 + 1))
    return pl.pallas_call(
        functools.partial(unit_kernel, chips),
        out_shape=(
            jax.ShapeDtypeStruct((all_rows, columns), bf16),
            jax.ShapeDtypeStruct((all_rows, columns), bf16),
            jax.ShapeDtypeStruct((all_rows, later.shape[1]), bf16),
            jax.ShapeDtypeStruct((3, all_rows, hidden), bf16),
            jax.ShapeDtypeStruct((all_rows, 4 * rank), bf16),
            jax.ShapeDtypeStruct((3, hidden, columns), bf16),
            jax.ShapeDtypeStruct((2, hidden, rank), bf16),
            jax.ShapeDtypeStruct((hidden, rank), f32),
        ),
        in_specs=[anywhere] * 4 + [inside] * 5,
        out_specs=(anywhere,) * 6 + (inside,) * 2,
        scratch_shapes=[
            pltpu.VMEM(planes.shape, bf16),
            pltpu.VMEM((3, hidden, all_rows), bf16),
            pltpu.VMEM((2, 3, 2 * rows, hidden), bf16),
            pltpu.VMEM((all_rows, 3 * rank), bf16),
            pltpu.VMEM((2, hidden, 256), bf16),
            pltpu.VMEM((all_rows, two.shape[1]), bf16),
            pltpu.VMEM((all_rows, columns), bf16),
            pltpu.SemaphoreType.DMA((3,)),
            pltpu.SemaphoreType.DMA((3,)),
            pair,
            pair,
            sides,
            sides,
            pltpu.SemaphoreType.DMA((chips, 4)),
            pltpu.SemaphoreType.DMA((2, 3)),
            pltpu.SemaphoreType.DMA((2,)),
        ],
        compiler_params=pltpu.CompilerParams(
            collective_id=ident, has_side_effects=True, vmem_limit_bytes=60 << 20
        ),
        cost_estimate=busy(100),
        name="unit_rows",
    )(two, grad, later, planes, squeeze, widen_down, widen_gate, widen_up, narrow)


def mix_kernel(chips, *refs):
    acts_ref, planes, gate_b, up_b, down_a, o_ref = refs[:6]
    acts, held, side_buf, ring_buf, stage, mine = refs[6:12]
    held_sem, side_send, side_recv, ring_send, ring_recv = refs[12:]
    core, device = ring_neighbours(chips)
    rows, columns = o_ref.shape
    reach = chips // 2
    half = columns // 2
    tile = 16
    wide = 256
    ways = (device(1, core), device(-1, core))
    side = device(0, 1 - core)
    order = [(reach, 0, 0)]
    for step in range(1, reach):
        order += [(reach - step, 0, step), (chips - reach + step, 1, step)]
    order.append((0, 0, reach))
    fetches = [pltpu.make_async_copy(planes.at[i], held.at[i], held_sem.at[chips, i]) for i in range(3)]

    def fetched(i):
        here = pl.ds(pl.multiple_of(device(order[i][0], 0) * rows, 2 * rows), 2 * rows)
        return [pltpu.make_async_copy(acts_ref.at[k, here], acts.at[k, here], held_sem.at[i, k]) for k in range(3)]

    for copy in fetched(0) + fetches + [copy for i in range(1, chips) for copy in fetched(i)]:
        copy.start()
    meet((*ways, side))

    def across(i):
        target = order[i][0]
        return pltpu.make_async_remote_copy(
            stage.at[i % 2],
            side_buf.at[target],
            side_send.at[target],
            side_recv.at[target],
            device_id={"fsdp": side},
            device_id_type=MESH,
        )

    def hop(way, step, part):
        target = (reach - step if way == 0 else chips - reach + step) % chips
        cols = pl.ds(way * half, half) if step == 0 else pl.ds(0, columns)
        here = pl.ds(part * (rows // 2), rows // 2)
        return pltpu.make_async_remote_copy(
            side_buf.at[target, here, cols],
            ring_buf.at[way, step, here, cols],
            ring_send.at[way, step, part],
            ring_recv.at[way, step, part],
            device_id={"fsdp": ways[way]},
            device_id_type=MESH,
        )

    def make(i):
        target, slot = order[i][0], i % 2
        for copy in fetched(i):
            copy.wait()
        if i >= 2:
            across(i - 2).wait_send()
        theirs = pl.ds(pl.multiple_of(device(target, 1 - core) * rows, rows), rows)
        ours = pl.ds(pl.multiple_of(device(target, core) * rows, rows), rows)

        def block(kind):
            return jnp.concatenate([acts[kind, theirs, :], acts[kind, ours, :]], axis=0)

        def put(first, value):
            cols = pl.ds(pl.multiple_of(first, wide), wide)
            stage[slot, :, cols] = value[:rows].astype(bf16)
            mine[slot, :, cols] = value[rows:].astype(bf16)

        @pl.loop(0, MODEL_WIDTH // wide)
        def _(t):
            cols = pl.ds(pl.multiple_of(t * wide, wide), wide)
            put(
                t * wide,
                matrix_product(block(0), held[0, :, cols])
                + matrix_product(block(1), held[1, :, cols]),
            )
            put(
                MODEL_WIDTH + 2 * ADAPTER_RANK + t * wide,
                matrix_product(block(2), held[2, :, cols]),
            )

        put(MODEL_WIDTH, times_transposed(block(0), gate_b[...]))
        put(MODEL_WIDTH + ADAPTER_RANK, times_transposed(block(1), up_b[...]))
        put(2 * MODEL_WIDTH + 2 * ADAPTER_RANK, matrix_product(block(2), down_a[...]))
        across(i).start()

    def add(i):
        target, way, step = order[i]
        last = target == 0
        incoming = [(w, step - 1) for w in ((0, 1) if last else (way,))] if step else []
        across(i).wait_recv()
        for part in (0, 1):
            for w, s in incoming:
                hop(w, s, part).wait_recv()

            @pl.loop(0, rows // 2 // tile)
            def _(j, part=part):
                here = pl.ds(pl.multiple_of(part * (rows // 2) + j * tile, tile), tile)
                for side_half in (0, 1):
                    cols = pl.ds(side_half * half, half)
                    total = mine[i % 2, here, cols].astype(f32) + side_buf[target, here, cols].astype(f32)
                    for w, s in incoming:
                        if s or w == side_half:
                            total = total + ring_buf[w, s, here, cols].astype(f32)
                    if last:
                        o_ref[here, cols] = total
                    else:
                        side_buf[target, here, cols] = total.astype(bf16)

            if not last:
                hop(way, step, part).start()
                if step == 0:
                    hop(1, 0, part).start()

    for fetch in fetches:
        fetch.wait()
    make(0)
    add(0)
    for i in range(1, len(order), 2):
        both = range(i, min(i + 2, len(order)))
        for j in both:
            make(j)
        for j in both:
            add(j)
    for i in range(len(order) - 2, len(order)):
        across(i).wait_send()
    for step in range(reach):
        for way in (0, 1):
            for part in (0, 1):
                hop(way, step, part).wait_send()


def mix_rows(acts, planes, gate_b, up_b, down_a, ident):
    size = lax.axis_size("fsdp")
    if size != 16:
        gate_grad, up_grad, units = acts[0], acts[1], acts[2]
        terms = [
            matrix_product(gate_grad, planes[0]) + matrix_product(up_grad, planes[1]),
            times_transposed(gate_grad, gate_b),
            times_transposed(up_grad, up_b),
            matrix_product(units, planes[2]),
            matrix_product(units, down_a),
        ]
        return scatter_rows(jnp.concatenate(terms, axis=1))
    chips = size // 2
    rows, columns = acts.shape[1] // size, 2 * MODEL_WIDTH + 3 * ADAPTER_RANK
    pair = pltpu.SemaphoreType.DMA((2, chips // 2, 2))
    sides = pltpu.SemaphoreType.DMA((chips,))
    return pl.pallas_call(
        functools.partial(mix_kernel, chips),
        out_shape=jax.ShapeDtypeStruct((rows, columns), f32),
        in_specs=[pl.BlockSpec(memory_space=pl.ANY)] * 2
        + [pl.BlockSpec(memory_space=pltpu.VMEM)] * 3,
        out_specs=pl.BlockSpec(memory_space=pltpu.VMEM),
        scratch_shapes=[
            pltpu.VMEM(acts.shape, bf16),
            pltpu.VMEM(planes.shape, bf16),
            pltpu.VMEM((chips, rows, columns), bf16),
            pltpu.VMEM((2, chips // 2, rows, columns), bf16),
            pltpu.VMEM((2, rows, columns), bf16),
            pltpu.VMEM((2, rows, columns), bf16),
            pltpu.SemaphoreType.DMA((chips + 1, 3)),
            sides,
            sides,
            pair,
            pair,
        ],
        compiler_params=pltpu.CompilerParams(
            collective_id=ident, has_side_effects=True, vmem_limit_bytes=60 << 20
        ),
        cost_estimate=busy(1),
        name="mix_rows",
    )(acts, planes, gate_b, up_b, down_a)


def share_kernel(size, chunk, own_count, *refs):
    x_ref, mid_ref, turned, lora, grad, widen, o_ref, in_ref, a_ref, near_ref, far_ref, gain_ref, all_ref = refs[:13]
    sems = refs[13:]
    send_sem, recv_sem, own_sem = sems[5:]
    _, device = ring_neighbours(size // 2)
    me = lax.axis_index("fsdp")
    hidden = HIDDEN_COUNT // size
    width = MODEL_WIDTH // size
    sections = (
        (0, PROJECT_COLUMNS, width),
        (width, GATE_START, hidden),
        (width + hidden, GATE_START + HIDDEN_COUNT, hidden),
    )

    def greet():
        barrier = pltpu.get_barrier_semaphore()

        def one(i, carry):
            pl.semaphore_signal(barrier, inc=1, device_id={"fsdp": (me + i) % size}, device_id_type=MESH)
            return carry

        lax.fori_loop(1, size, one, 0)
        pl.semaphore_wait(barrier, size - 1)

    def rows(ref, first):
        return ref.at[pl.ds(pl.multiple_of(first, 8), chunk)]

    def aim(start, length):
        owner = (start + me * length) // own_count
        return owner, start + me * length - owner * own_count

    def remote(source, first, owner, sent=0):
        return pltpu.make_async_remote_copy(
            source,
            rows(o_ref, first),
            send_sem.at[sent],
            recv_sem.at[first // chunk],
            device_id={"fsdp": owner},
            device_id_type=MESH,
        )

    def local(source, first):
        return pltpu.make_async_copy(source, rows(o_ref, first), own_sem.at[first // chunk])

    def send_all():
        for base, start, length in sections:

            def send(j, carry, base=base, aimed=aim(start, length)):
                over = (aimed[1] + j * chunk >= own_count).astype(jnp.int32)
                owner = aimed[0] + over
                first = aimed[1] + j * chunk - over * own_count
                source = rows(mid_ref, base + j * chunk)

                @pl.when(owner != me)
                def _():
                    remote(source, first, owner, base // chunk + j).start()

                @pl.when(owner == me)
                def _():
                    local(source, first).start()

                return carry

            lax.fori_loop(0, length // chunk, send, 0)

    def work(shift):
        first = shift == 0
        count = 2 * x_ref.shape[0]
        here = pl.ds(pl.multiple_of(device(shift, 0) * x_ref.shape[0], count), count)
        rank = ADAPTER_RANK

        def put(ref, cols, value):
            ref[:, cols] = value if first else ref[:, cols] + value

        normed = turned[0, :, here]
        wide = PROJECT_COLUMNS // rank

        @pl.loop(0, wide)
        def _(t):
            cols = pl.ds(pl.multiple_of(t * rank, rank), rank)
            part = jnp.maximum(t - (wide - 3), 0)
            low = lora[pl.ds(pl.multiple_of(part * rank, rank), rank), here]
            total = matrix_product(jnp.concatenate([normed, low], axis=0), all_ref[here, cols])
            put(in_ref, cols, total[: normed.shape[0]])
            put(near_ref, cols, total[normed.shape[0] :])

        spans = ((0, QUERY_WIDTH), (QUERY_WIDTH, HEAD_WIDTH), (QUERY_WIDTH + HEAD_WIDTH, HEAD_WIDTH))
        for i, (start, width) in enumerate(spans):
            cols = pl.ds(start, width)
            low = times_transposed(all_ref[here, cols], widen[:, cols]).astype(bf16)
            put(a_ref, pl.ds(i * rank, rank), matrix_product(normed, low))
        lows = [all_ref[here, pl.ds(PROJECT_COLUMNS + i * rank, rank)] for i in range(4)]
        for i, kind in ((0, 1), (1, 2), (2, 2)):
            put(a_ref, pl.ds((3 + i) * rank, rank), matrix_product(turned[kind, :, here], lows[i]))
        pulled = lows[3].astype(f32).T.astype(bf16)

        @pl.loop(0, MODEL_WIDTH // rank)
        def _(t):
            cols = pl.ds(pl.multiple_of(t * rank, rank), rank)
            put(far_ref, cols, matrix_product(pulled, grad[here, cols]))

        gain_ref[here, :] = all_ref[here, pl.ds(PROJECT_COLUMNS + 4 * rank, gain_ref.shape[1])]

    gather_kernel(size // 2, x_ref, all_ref, *sems[:5], greet=greet, also=send_all, work=work)

    def arrive(j, carry):
        column = me * own_count + j * chunk
        here = rows(o_ref, j * chunk)
        away, kept = 0, 0
        for _, start, length in sections:
            mine = start + me * length
            inside = (column >= start) & (column < start + length * size)
            outside = (column < mine) | (column >= mine + length)
            away = away + (inside & outside).astype(jnp.int32)
            kept = kept + (inside & ~outside).astype(jnp.int32)

        @pl.when(away > 0)
        def _():
            remote(here, j * chunk, (me + 1) % size).wait_recv()

        @pl.when(kept > 0)
        def _():
            local(rows(mid_ref, 0), j * chunk).wait()

        return carry

    lax.fori_loop(0, own_count // chunk, arrive, 0)
    for base, start, length in sections:

        def sent(j, carry, base=base, aimed=aim(start, length)):
            over = (aimed[1] + j * chunk >= own_count).astype(jnp.int32)
            owner = aimed[0] + over
            first = aimed[1] + j * chunk - over * own_count

            @pl.when(owner != me)
            def _():
                remote(rows(mid_ref, base + j * chunk), first, owner, base // chunk + j).wait_send()

            return carry

        lax.fori_loop(0, length // chunk, sent, 0)


def share_rows(block, middle, turned, lora, grad, widen, ident):
    size = lax.axis_size("fsdp")
    rank = ADAPTER_RANK
    rows, columns = block.shape
    own_count = ADAPTER_COLUMNS // size
    gain_width = columns - PROJECT_COLUMNS - 4 * rank
    width = MODEL_WIDTH // size
    chunk = math.gcd(own_count, width, HIDDEN_COUNT // size, PROJECT_COLUMNS, GATE_START)
    if size != 16:
        every = gather_rows(block)
        spans = ((0, QUERY_WIDTH), (QUERY_WIDTH, HEAD_WIDTH), (QUERY_WIDTH + HEAD_WIDTH, HEAD_WIDTH))
        parts = [every[:, a : a + n] for a, n in spans]
        lows = [every[:, PROJECT_COLUMNS + i * rank :][:, :rank] for i in range(4)]
        squeezed = [
            matrix_product(turned[0], times_transposed(part, widen[:, a : a + n]).astype(bf16))
            for part, (a, n) in zip(parts, spans)
        ]
        squeezed += [matrix_product(turned[kind], lows[i]) for i, kind in ((0, 1), (1, 2), (2, 2))]
        near = [matrix_product(lora[i * rank : (i + 1) * rank], part) for i, part in enumerate(parts)]
        middle_all = gather_rows(middle).reshape(size, -1, rank)
        hidden = HIDDEN_COUNT // size
        cuts = ((0, width), (width, width + hidden), (width + hidden, width + 2 * hidden))
        middle_all = jnp.concatenate(
            [jnp.zeros((PROJECT_COLUMNS, rank), bf16)]
            + [middle_all[:, a:b].reshape(-1, rank) for a, b in cuts]
            + [jnp.zeros((MODEL_WIDTH, rank), bf16)],
            axis=0,
        )
        return (
            lax.dynamic_slice_in_dim(middle_all, lax.axis_index("fsdp") * own_count, own_count, 0),
            matrix_product(turned[0], every[:, :PROJECT_COLUMNS]),
            jnp.concatenate(squeezed, axis=1),
            jnp.concatenate(near, axis=1),
            outer_product_rows(lows[3], grad),
            every[:, columns - gain_width :],
        )
    anywhere, inside = pl.BlockSpec(memory_space=pl.ANY), pl.BlockSpec(memory_space=pltpu.VMEM)
    pair = pltpu.SemaphoreType.DMA((2, size // 4))
    sides = pltpu.SemaphoreType.DMA((2, size // 4 + 1))
    return pl.pallas_call(
        functools.partial(share_kernel, size, chunk, own_count),
        out_shape=(
            jax.ShapeDtypeStruct((own_count, rank), bf16),
            jax.ShapeDtypeStruct((width, PROJECT_COLUMNS), f32),
            jax.ShapeDtypeStruct((width, 6 * rank), f32),
            jax.ShapeDtypeStruct((rank, PROJECT_COLUMNS), f32),
            jax.ShapeDtypeStruct((rank, MODEL_WIDTH), f32),
            jax.ShapeDtypeStruct((size * rows, gain_width), bf16),
        ),
        in_specs=[anywhere] * 2 + [inside] * 4,
        out_specs=(anywhere,) + (inside,) * 5,
        scratch_shapes=[
            pltpu.VMEM((size * rows, columns), bf16),
            pltpu.SemaphoreType.DMA,
            pair,
            pair,
            sides,
            sides,
            pltpu.SemaphoreType.DMA((middle.shape[0] // chunk,)),
            pltpu.SemaphoreType.DMA((own_count // chunk,)),
            pltpu.SemaphoreType.DMA((own_count // chunk,)),
        ],
        compiler_params=pltpu.CompilerParams(
            collective_id=ident, has_side_effects=True, vmem_limit_bytes=56 << 20
        ),
        cost_estimate=busy(1),
        name="share_rows",
    )(block, middle, turned, lora, grad, widen)


def per_device(
    hidden_input,
    sequence_lengths,
    norm_gain_values,
    input_proj_weight,
    output_proj_weight,
    feedforward_weight,
    adapter_first,
    adapter_second,
    adapter_down_first,
    output_gradient,
):
    size = lax.axis_size("fsdp")
    place = lax.axis_index("fsdp")
    tokens_dev = hidden_input.shape[1]
    all_rows = tokens_dev * size
    hidden_own = HIDDEN_COUNT // size
    width_own = MODEL_WIDTH // size
    columns_own = ADAPTER_COLUMNS // size
    offset = place * tokens_dev
    segment_all, position_all = segment_info(sequence_lengths[0], all_rows)
    segment_own = lax.dynamic_slice_in_dim(segment_all, offset, tokens_dev)
    position_own = lax.dynamic_slice_in_dim(position_all, offset, tokens_dev)
    row_all = jnp.arange(all_rows, dtype=jnp.int32)
    row_own = offset + jnp.arange(tokens_dev, dtype=jnp.int32)
    allowed = (segment_own[:, None] == segment_all[None, :]) & (
        row_own[:, None] >= row_all[None, :]
    )
    gains = norm_gain_values.astype(f32)
    first_factor = adapter_first[0]
    second_factor = adapter_second[0]
    rank = ADAPTER_RANK
    narrow_projection = first_factor[:, : 3 * rank]
    narrow_output = first_factor[:, 3 * rank : 4 * rank]
    squeeze_gate = first_factor[:, 4 * rank : 5 * rank]
    squeeze_up = first_factor[:, 5 * rank :]
    narrow_down = lax.dynamic_slice_in_dim(adapter_down_first[0], place * hidden_own, hidden_own, 0)
    widen_query = second_factor[:, :QUERY_WIDTH]
    widen_key = second_factor[:, QUERY_WIDTH : QUERY_WIDTH + HEAD_WIDTH]
    widen_value = second_factor[:, QUERY_WIDTH + HEAD_WIDTH : PROJECT_COLUMNS]
    widen_output = second_factor[:, PROJECT_COLUMNS:GATE_START]
    widen_gate = lax.dynamic_slice_in_dim(
        second_factor, GATE_START + place * hidden_own, hidden_own, 1
    )
    widen_up = lax.dynamic_slice_in_dim(
        second_factor, GATE_START + HIDDEN_COUNT + place * hidden_own, hidden_own, 1
    )
    widen_down = second_factor[:, GATE_START + 2 * HIDDEN_COUNT :]
    scaling = HEAD_WIDTH ** (-0.5)

    hidden_state = hidden_input[0].astype(f32)
    scale_one = rms_scale(hidden_state)
    normalized = (hidden_state * scale_one * gains[0]).astype(bf16)
    proj_in = ring_gather(input_proj_weight, 0)
    proj_in, proj_out = lax.optimization_barrier((proj_in, output_proj_weight))
    proj_out = gather_rows(proj_out)
    lora_qkv = matrix_product(normalized, narrow_projection).astype(bf16)
    projected = matrix_product(normalized, proj_in)
    query_pre = projected[:, :QUERY_WIDTH] + matrix_product(lora_qkv[:, :rank], widen_query)
    key_pre = projected[:, QUERY_WIDTH : QUERY_WIDTH + HEAD_WIDTH] + matrix_product(
        lora_qkv[:, rank : 2 * rank], widen_key
    )
    value_local = (
        projected[:, QUERY_WIDTH + HEAD_WIDTH :]
        + matrix_product(lora_qkv[:, 2 * rank :], widen_value)
    ).astype(bf16)
    query_rot = rotate(query_pre, position_own, 1.0).astype(bf16)
    key_rot = rotate(key_pre, position_own, 1.0).astype(bf16)
    keys_all = ring_gather(jnp.concatenate([key_rot, value_local], axis=1), 1)
    key_rows, value_rows = keys_all[:, :HEAD_WIDTH], keys_all[:, HEAD_WIDTH:]
    query_heads = query_rot.reshape(tokens_dev, HEADS, HEAD_WIDTH)
    scores = scores_of(query_heads, key_rows, allowed, scaling)
    row_max = jnp.max(scores, axis=-1, keepdims=True)
    powered = jnp.exp(scores - row_max)
    row_sum = jnp.sum(powered, axis=-1, keepdims=True)
    probs = powered / row_sum
    probs_low = probs.astype(bf16)
    attended = (
        jnp.einsum("thu,ud->thd", probs_low, value_rows, preferred_element_type=f32)
        .reshape(tokens_dev, QUERY_WIDTH)
        .astype(bf16)
    )
    lora_out = matrix_product(attended, narrow_output).astype(bf16)
    middle = (
        hidden_state
        + times_transposed(attended, proj_out)
        + matrix_product(lora_out, widen_output)
    )
    scale_two = rms_scale(middle)
    normed_two = (middle * scale_two * gains[1]).astype(bf16)

    weight_planes = feedforward_weight.transpose(1, 0, 2)
    two_all, grad_all, attended_all, acts, low_ffn, ffn_shares, ffn_pieces, down_own = unit_rows(
        jnp.concatenate([normed_two, lora_out], axis=1),
        output_gradient[0],
        jnp.concatenate([attended, lora_qkv], axis=1),
        weight_planes,
        first_factor[:, 4 * rank :],
        widen_down,
        widen_gate,
        widen_up,
        narrow_down,
        2,
    )
    lora_out_all = low_ffn[:, 3 * rank :]
    ffn_both = loop_shares(ffn_shares)
    rows_sum = mix_rows(
        acts, weight_planes, widen_gate, widen_up, narrow_down, 3
    )
    back_own, out_own = rows_sum[:, : MODEL_WIDTH + 2 * rank], rows_sum[:, MODEL_WIDTH + 2 * rank :]
    lora_hd = out_own[:, MODEL_WIDTH:].astype(bf16)
    hidden_out = (middle + out_own[:, :MODEL_WIDTH] + matrix_product(lora_hd, widen_down)).astype(bf16)

    gate_low = back_own[:, MODEL_WIDTH : MODEL_WIDTH + rank].astype(bf16)
    up_low = back_own[:, MODEL_WIDTH + rank :].astype(bf16)
    two_grad = (
        back_own[:, :MODEL_WIDTH]
        + times_transposed(gate_low, squeeze_gate)
        + times_transposed(up_low, squeeze_up)
    )
    weighted_two = gains[1] * two_grad
    middle_grad = (
        output_gradient[0].astype(f32)
        + scale_two * weighted_two
        - middle * scale_two**3 * jnp.mean(middle * weighted_two, axis=-1, keepdims=True)
    )
    gain_two = jnp.sum(two_grad * middle * scale_two, axis=0)

    branch_grad = middle_grad.astype(bf16)
    both = [block.reshape(tokens_dev, size, width_own) for block in (normalized, branch_grad)]
    turned = turn(jnp.concatenate(both, axis=2).reshape(tokens_dev, -1))
    normed_turn, branch_turn = turned[:, :width_own], turned[:, width_own:]
    lora_out_grad = times_transposed(branch_grad, widen_output).astype(bf16)
    attended_grad = (
        matrix_product(branch_grad, proj_out) + times_transposed(lora_out_grad, narrow_output)
    ).astype(bf16)
    heads_grad = attended_grad.reshape(tokens_dev, HEADS, HEAD_WIDTH)
    prob_grad = jnp.einsum("thd,ud->thu", heads_grad, value_rows, preferred_element_type=f32)
    row_dot = jnp.sum(probs * prob_grad, axis=-1, keepdims=True)
    score_grad = (probs * (prob_grad - row_dot)).astype(bf16)
    query_rot_grad = (
        jnp.einsum("thu,ud->thd", score_grad, key_rows, preferred_element_type=f32) * scaling
    )
    key_part = (
        jnp.einsum("thu,thd->ud", score_grad, query_heads, preferred_element_type=f32) * scaling
    )
    value_part = jnp.einsum("thu,thd->ud", probs_low, heads_grad, preferred_element_type=f32)
    pair_grad = ring_scatter([key_part, value_part], 4)
    pair_grad, normed_turn, branch_turn = lax.optimization_barrier((pair_grad, normed_turn, branch_turn))
    query_grad = rotate(
        query_rot_grad.reshape(tokens_dev, QUERY_WIDTH), position_own, -1.0
    ).astype(bf16)
    key_grad = rotate(pair_grad[:, :HEAD_WIDTH], position_own, -1.0).astype(bf16)
    value_grad = pair_grad[:, HEAD_WIDTH:].astype(bf16)
    proj_grad = jnp.concatenate([query_grad, key_grad, value_grad], axis=1)
    lora_qkv_grad = jnp.concatenate(
        [
            times_transposed(query_grad, widen_query),
            times_transposed(key_grad, widen_key),
            times_transposed(value_grad, widen_value),
        ],
        axis=1,
    ).astype(bf16)
    normed_grad = times_transposed(proj_grad, proj_in) + times_transposed(
        lora_qkv_grad, narrow_projection
    )
    weighted_one = gains[0] * normed_grad
    input_grad = (
        middle_grad
        + scale_one * weighted_one
        - hidden_state
        * scale_one**3
        * jnp.mean(hidden_state * weighted_one, axis=-1, keepdims=True)
    )
    gain_one = jnp.sum(normed_grad * hidden_state * scale_one, axis=0)

    lora_qkv_all = attended_all[:, QUERY_WIDTH:]
    out_piece = outer_product_rows(branch_turn, lora_out_all)
    gain_rows = jnp.stack([gain_one, gain_two]).astype(bf16).reshape(tokens_dev, -1)
    gain_count = gain_rows.shape[1]
    gain_rows = jnp.pad(gain_rows, ((0, 0), (0, -gain_count % 128)))
    proj_rows = jnp.concatenate(
        [proj_grad, lora_out_grad, gate_low, up_low, lora_hd, gain_rows], axis=1
    )
    column = place * width_own
    attended_turn = lax.dynamic_slice_in_dim(attended_all, column, width_own, 1)
    two_turn = lax.dynamic_slice_in_dim(two_all, column, width_own, 1)
    middle_own, attn_in_part, squeeze_own, near, far, gain_all = share_rows(
        proj_rows,
        jnp.concatenate([out_piece.astype(bf16), ffn_pieces[0], ffn_pieces[1]], axis=0),
        jnp.stack([normed_turn.T, attended_turn.T, two_turn.T]),
        lora_qkv_all.T,
        grad_all,
        second_factor[:, :PROJECT_COLUMNS],
        5,
    )
    gain_all = gain_all[:, :gain_count].reshape(size, 2, MODEL_WIDTH)
    gain_all = jnp.sum(gain_all.astype(f32), axis=0)
    gain_own = lax.dynamic_slice_in_dim(gain_all, column, width_own, 1)
    gain_part = jnp.pad(gain_own, ((0, width_own - 2), (0, -width_own % 128)))
    attn_part = jnp.concatenate(
        [
            attn_in_part,
            outer_product_rows(branch_turn, attended_all)[:, :QUERY_WIDTH],
            gain_part,
        ],
        axis=1,
    ).astype(bf16)
    attn_part, ffn_both = lax.optimization_barrier((attn_part, ffn_both))
    attn_sum = both_loops(loop_shares(attn_part))
    gain_column = PROJECT_COLUMNS + QUERY_WIDTH
    gain_sum = attn_sum[:2, gain_column : gain_column + width_own]
    first = place * columns_own
    far_start = GATE_START + 2 * HIDDEN_COUNT
    near = lax.dynamic_slice_in_dim(
        jnp.pad(near.T.astype(bf16), ((0, columns_own), (0, 0))), jnp.minimum(first, PROJECT_COLUMNS), columns_own, 0
    )
    far = lax.dynamic_slice_in_dim(
        jnp.pad(far.T.astype(bf16), ((columns_own, 0), (0, 0))),
        jnp.maximum(first - far_start + columns_own, 0),
        columns_own,
        0,
    )
    owned = first + jnp.arange(columns_own, dtype=jnp.int32)[:, None]
    expand_own = jnp.where(
        owned < PROJECT_COLUMNS, near, jnp.where(owned < far_start, middle_own, far)
    ).T.astype(f32)
    ffn_sum = both_loops(ffn_both).transpose(1, 0, 2)
    return (
        hidden_out[None],
        input_grad[None],
        gain_sum,
        attn_sum[:, :PROJECT_COLUMNS],
        attn_sum[:, PROJECT_COLUMNS:gain_column],
        ffn_sum,
        squeeze_own[None],
        expand_own[None],
        down_own[None],
    )


def solution(mesh):
    return jax.shard_map(
        per_device,
        mesh=mesh,
        in_specs=(
            P("loop", "fsdp", None),
            P("loop", None),
            P(),
            P("fsdp", None),
            P("fsdp", None),
            P("fsdp", None, None),
            P("loop", None, None),
            P("loop", None, None),
            P("loop", None, None),
            P("loop", "fsdp", None),
        ),
        out_specs=(
            P("loop", "fsdp", None),
            P("loop", "fsdp", None),
            P(None, "fsdp"),
            P("fsdp", None),
            P("fsdp", None),
            P("fsdp", None, None),
            P("loop", "fsdp", None),
            P("loop", None, "fsdp"),
            P("loop", "fsdp", None),
        ),
        check_vma=False,
    )
```

```python
import functools
import math

import jax
import jax.numpy as jnp
from jax import lax
from jax.experimental import pallas as pl
from jax.experimental.pallas import tpu as pltpu
from jax.sharding import PartitionSpec as P

MODEL_WIDTH = 2048
HEADS = 8
HEAD_WIDTH = 256
HIDDEN_COUNT = 16384
ADAPTER_RANK = 256
QUERY_WIDTH = 2048
PROJECT_COLUMNS = 2560
ADAPTER_COLUMNS = 39424
GATE_START = PROJECT_COLUMNS + MODEL_WIDTH

epsilon = 1e-06
bf16 = jnp.bfloat16
f32 = jnp.float32
MESH = pl.DeviceIdType.MESH


def matrix_product(former, latter):
    return jnp.dot(former, latter, preferred_element_type=f32)


def times_transposed(former, latter):
    return lax.dot_general(former, latter, (((1,), (1,)), ((), ())), preferred_element_type=f32)


def outer_product_rows(former, latter):
    return lax.dot_general(former, latter, (((0,), (0,)), ((), ())), preferred_element_type=f32)


def segment_info(lengths, row_count):
    row_ids = jnp.arange(row_count, dtype=jnp.int32)
    count = lengths.shape[0]
    labels = jnp.arange(count, dtype=jnp.int32)
    finish = jnp.sum(jnp.where(labels[:, None] <= labels[None, :], lengths[:, None], 0), axis=0)
    starts = finish - lengths
    segment = jnp.sum((row_ids[:, None] >= finish[None, :]).astype(jnp.int32), axis=1)
    opening = jnp.sum(jnp.where(segment[:, None] == labels[None, :], starts[None, :], 0), axis=1)
    return (segment, row_ids - opening)


def rotate(values, position, direction):
    half_dim = HEAD_WIDTH // 2
    frequency = jnp.exp(
        jnp.arange(half_dim).astype(f32) * (-2.0 * math.log(10000.0) / HEAD_WIDTH)
    )
    angles = position.astype(f32)[:, None] * frequency[None, :]
    cosine = jnp.cos(angles)[:, None, :]
    sine_val = direction * jnp.sin(angles)[:, None, :]
    shaped = values.reshape(values.shape[0], -1, HEAD_WIDTH)
    former = shaped[..., :half_dim]
    latter = shaped[..., half_dim:]
    turned = jnp.concatenate(
        [former * cosine - latter * sine_val, latter * cosine + former * sine_val], axis=-1
    )
    return turned.reshape(values.shape)


def rms_scale(values):
    return lax.rsqrt(jnp.mean(values * values, axis=-1, keepdims=True) + epsilon)


def gelu_tanh(values):
    return jax.nn.gelu(values, approximate=True)


def unit_backward(gate_value, upward_activation, hidden_unit_gradient):
    activated, pullback_function = jax.vjp(gelu_tanh, gate_value)
    gate_grad = pullback_function(hidden_unit_gradient * upward_activation)[0]
    return (gate_grad.astype(bf16), (hidden_unit_gradient * activated).astype(bf16))


def scores_of(query_heads, key_rows, allowed, scaling):
    product = (
        jnp.einsum("thd,ud->thu", query_heads, key_rows, preferred_element_type=f32) * scaling
    )
    return jnp.where(allowed[:, None, :], product, -1e30)


def gather_rows(block):
    return lax.all_gather(block, "fsdp", axis=0, tiled=True)


def scatter_rows(partial):
    return lax.psum_scatter(partial.astype(bf16), "fsdp", scatter_dimension=0, tiled=True).astype(f32)


def loop_shares(partial):
    return lax.all_gather(partial.astype(bf16), "loop", axis=0)


def both_loops(shares):
    return shares[0].astype(f32) + shares[1].astype(f32)


def turn(block):
    return lax.all_to_all(block, "fsdp", split_axis=1, concat_axis=0, tiled=True)


def chip_at(q, chips):
    return jnp.where(q < 4, 2 * q, 15 - 2 * q) if chips == 8 else q

def ring_place(chip, chips):
    return jnp.where(chip % 2 == 0, chip // 2, 7 - chip // 2) if chips == 8 else chip

def ring_neighbours(chips):
    me = lax.axis_index("fsdp")
    core = me % 2
    p = ring_place(me // 2, chips)
    def device(shift, c):
        return chip_at((p + shift + chips) % chips, chips) * 2 + c
    return core, device

def meet(devices):
    barrier = pltpu.get_barrier_semaphore()
    for d in devices:
        pl.semaphore_signal(barrier, inc=1, device_id={"fsdp": d}, device_id_type=MESH)
    pl.semaphore_wait(barrier, len(devices))

def gather_kernel(chips, x_ref, o_ref, own_sem, ring_send, ring_recv, side_send, side_recv, greet, also, work):
    core, device = ring_neighbours(chips)
    rows = x_ref.shape[0]
    reach = chips // 2
    ways = (device(1, core), device(-1, core))
    side = device(0, 1 - core)
    if greet is None:
        meet((*ways, side))
    else:
        greet()

    def span(way, hops):
        return (way * (rows // 2), rows // 2) if hops == reach else (0, rows)

    def at(way, hops, c, part):
        origin = device(-hops if way == 0 else hops, c)
        return o_ref.at[pl.ds(pl.multiple_of(origin * rows + part[0], 8), part[1])]

    def hop(way, hops):
        part = span(way, hops)
        here = at(way, hops - 1, core, part)
        src = x_ref.at[pl.ds(part[0], part[1])] if hops == 1 else here
        return pltpu.make_async_remote_copy(src, here, ring_send.at[way, hops - 1], ring_recv.at[way, hops - 1], device_id={"fsdp": ways[way]}, device_id_type=MESH)

    def arriving(way, hops):
        here = at(way, hops, core, span(way, hops))
        return pltpu.make_async_remote_copy(here, here, ring_send.at[way, hops - 1], ring_recv.at[way, hops - 1], device_id={"fsdp": ways[way]}, device_id_type=MESH)

    def across(way, hops, c):
        part = span(way, hops) if hops else (0, rows)
        there = at(way, hops, c, part)
        src = there if hops else x_ref
        return pltpu.make_async_remote_copy(src, there, side_send.at[way, hops], side_recv.at[way, hops], device_id={"fsdp": side}, device_id_type=MESH)

    for way in (0, 1):
        hop(way, 1).start()
    across(0, 0, core).start()
    own = pltpu.make_async_copy(x_ref, at(0, 0, core, (0, rows)), own_sem)
    own.start()
    if also is not None:
        also()
    if work is not None:
        own.wait()
        across(0, 0, 1 - core).wait_recv()
        work(0)
    for hops in range(1, reach + 1):
        for way in (0, 1):
            arriving(way, hops).wait_recv()
            if hops < reach:
                hop(way, hops + 1).start()
            across(way, hops, core).start()
        if work is not None:
            for way in (0, 1):
                across(way, hops, 1 - core).wait_recv()
                if hops < reach:
                    work(-hops if way == 0 else hops)
                elif way:
                    work(reach)
    if work is None:
        own.wait()
        across(0, 0, 1 - core).wait_recv()
        for hops in range(1, reach + 1):
            for way in (0, 1):
                across(way, hops, 1 - core).wait_recv()
    across(0, 0, core).wait_send()
    for hops in range(1, reach + 1):
        for way in (0, 1):
            across(way, hops, core).wait_send()
            hop(way, hops).wait_send()


def busy(us):
    return pl.CostEstimate(flops=0, bytes_accessed=int(us * 3.0e6), transcendentals=0)


def ring_gather(block, ident):
    size = lax.axis_size("fsdp")
    chips = size // 2
    rows, columns = block.shape
    pair = pltpu.SemaphoreType.DMA((2, chips // 2))
    sides = pltpu.SemaphoreType.DMA((2, chips // 2 + 1))
    return pl.pallas_call(
        functools.partial(gather_kernel, chips, greet=None, also=None, work=None),
        out_shape=jax.ShapeDtypeStruct((size * rows, columns), block.dtype),
        in_specs=[pl.BlockSpec(memory_space=pl.ANY)],
        out_specs=pl.BlockSpec(memory_space=pl.ANY),
        scratch_shapes=[pltpu.SemaphoreType.DMA, pair, pair, sides, sides],
        compiler_params=pltpu.CompilerParams(collective_id=ident, has_side_effects=True),
        cost_estimate=busy(1),
        name="ring_gather",
    )(block)

def scatter_kernel(chips, count, *refs):
    x_refs, o_ref = refs[:count], refs[count]
    side_buf, ring_buf, side_send, side_recv, ring_send, ring_recv = refs[count + 1 :]
    core, device = ring_neighbours(chips)
    rows, columns = o_ref.shape
    reach = chips // 2
    half = columns // 2
    tile = 16
    ways = (device(1, core), device(-1, core))
    side = device(0, 1 - core)
    meet((*ways, side))
    starts = [sum(x.shape[1] for x in x_refs[:i]) for i in range(count)]

    def shift(way, hops):
        return (hops if way == 0 else chips - hops) % chips

    def across(target, c, i):
        there = pl.ds(pl.multiple_of(device(target, c) * rows, tile), rows)
        return pltpu.make_async_remote_copy(
            x_refs[i].at[there],
            side_buf.at[target, :, pl.ds(starts[i], x_refs[i].shape[1])],
            side_send.at[target, i],
            side_recv.at[target, i],
            device_id={"fsdp": side},
            device_id_type=MESH,
        )

    def hop(way, step):
        cols = pl.ds(way * half, half) if step == 0 else pl.ds(0, columns)
        return pltpu.make_async_remote_copy(
            side_buf.at[shift(way, reach - step), :, cols],
            ring_buf.at[way, step, :, cols],
            ring_send.at[way, step],
            ring_recv.at[way, step],
            device_id={"fsdp": ways[way]},
            device_id_type=MESH,
        )

    order = [reach] + [shift(way, hops) for hops in range(reach - 1, 0, -1) for way in (0, 1)] + [0]
    for target in order:
        for i in range(count):
            across(target, 1 - core, i).start()

    def add(target, incoming, store):
        first = pl.multiple_of(device(target, core) * rows, tile)
        for i in range(count):
            across(target, core, i).wait_recv()

        @pl.loop(0, rows // tile)
        def _(j):
            here = pl.ds(pl.multiple_of(j * tile, tile), tile)
            mine = pl.ds(pl.multiple_of(first + j * tile, tile), tile)
            for i in range(count):
                cols = pl.ds(starts[i], x_refs[i].shape[1])
                total = x_refs[i][mine, :].astype(f32) + side_buf[target, here, cols].astype(f32)
                for way, step in incoming:
                    if step:
                        total = total + ring_buf[way, step, here, cols].astype(f32)
                store(here, cols, total)
            for way, step in incoming:
                if not step:
                    cols = pl.ds(way * half, half)
                    store(
                        here,
                        cols,
                        side_buf[target, here, cols].astype(f32) + ring_buf[way, 0, here, cols].astype(f32),
                    )

    for step in range(reach):
        for way in (0, 1):
            target = shift(way, reach - step)
            if step:
                hop(way, step - 1).wait_recv()

            def store(here, cols, total, target=target):
                side_buf[target, here, cols] = total.astype(bf16)

            if step or way == 0:
                add(target, [(way, step - 1)] if step else [], store)
            hop(way, step).start()
    for way in (0, 1):
        hop(way, reach - 1).wait_recv()

    def last(here, cols, total):
        o_ref[here, cols] = total

    add(0, [(0, reach - 1), (1, reach - 1)], last)
    for target in order:
        for i in range(count):
            across(target, 1 - core, i).wait_send()
    for step in range(reach):
        for way in (0, 1):
            hop(way, step).wait_send()


def ring_scatter(terms, ident):
    size = lax.axis_size("fsdp")
    terms = [term.astype(bf16) for term in terms]
    if size != 16:
        return scatter_rows(jnp.concatenate(terms, axis=1))
    chips, count = size // 2, len(terms)
    rows, columns = terms[0].shape[0] // size, sum(term.shape[1] for term in terms)
    pair = pltpu.SemaphoreType.DMA((2, chips // 2))
    sides = pltpu.SemaphoreType.DMA((chips, count))
    return pl.pallas_call(
        functools.partial(scatter_kernel, chips, count),
        out_shape=jax.ShapeDtypeStruct((rows, columns), f32),
        in_specs=[pl.BlockSpec(memory_space=pltpu.VMEM)] * count,
        out_specs=pl.BlockSpec(memory_space=pltpu.VMEM),
        scratch_shapes=[
            pltpu.VMEM((chips, rows, columns), bf16),
            pltpu.VMEM((2, chips // 2, rows, columns), bf16),
            sides,
            sides,
            pair,
            pair,
        ],
        compiler_params=pltpu.CompilerParams(
            collective_id=ident, has_side_effects=True, vmem_limit_bytes=56 << 20
        ),
        cost_estimate=busy(1),
        name="ring_scatter",
    )(*terms)


def unit_kernel(chips, *refs):
    sources, (planes, squeeze, widen_down, widen_gate, widen_up, narrow) = refs[:3], refs[3:9]
    two_all, grad_all, later_all, acts_all, low_all, share_out, piece_out, down_out = refs[9:17]
    held, turned, acts, low, tiles = refs[17:22]
    landed = (refs[22], refs[23], later_all)
    held_sem, own_sem, ring_send, ring_recv, side_send, side_recv, out_sem, acts_sem, tile_sem = refs[24:]
    core, device = ring_neighbours(chips)
    rows = sources[0].shape[0]
    reach = chips // 2
    wide = 256
    ways = (device(1, core), device(-1, core))
    side = device(0, 1 - core)
    fetches = [pltpu.make_async_copy(planes.at[i], held.at[i], held_sem.at[i]) for i in range(3)]
    for fetch in fetches:
        fetch.start()
    meet((*ways, side))

    def span(way, hops):
        return (way * (rows // 2), rows // 2) if hops == reach else (0, rows)

    def at(i, way, hops, c, part):
        origin = device(-hops if way == 0 else hops, c)
        return landed[i].at[pl.ds(pl.multiple_of(origin * rows + part[0], 16), part[1])]

    def hop(i, way, hops):
        part = span(way, hops)
        here = at(i, way, hops - 1, core, part)
        src = sources[i].at[pl.ds(part[0], part[1])] if hops == 1 else here
        return pltpu.make_async_remote_copy(
            src,
            here,
            ring_send.at[i, way, hops - 1],
            ring_recv.at[i, way, hops - 1],
            device_id={"fsdp": ways[way]},
            device_id_type=MESH,
        )

    def arriving(i, way, hops):
        here = at(i, way, hops, core, span(way, hops))
        return pltpu.make_async_remote_copy(
            here,
            here,
            ring_send.at[i, way, hops - 1],
            ring_recv.at[i, way, hops - 1],
            device_id={"fsdp": ways[way]},
            device_id_type=MESH,
        )

    def across(i, way, hops, c):
        part = span(way, hops) if hops else (0, rows)
        there = at(i, way, hops, c, part)
        return pltpu.make_async_remote_copy(
            there if hops else sources[i],
            there,
            side_send.at[i, way, hops],
            side_recv.at[i, way, hops],
            device_id={"fsdp": side},
            device_id_type=MESH,
        )

    def leaving(n, first):
        mine = pl.ds(first, 2 * rows)
        width, under = grad_all.shape[1], low.shape[1]
        pairs = [
            (landed[0].at[mine, pl.ds(0, width)], two_all.at[mine]),
            (landed[0].at[mine, pl.ds(width, ADAPTER_RANK)], low_all.at[mine, pl.ds(under, ADAPTER_RANK)]),
            (low.at[mine], low_all.at[mine, pl.ds(0, under)]),
            (landed[1].at[mine], grad_all.at[mine]),
        ]
        return [pltpu.make_async_copy(a, b, out_sem.at[n, i]) for i, (a, b) in enumerate(pairs)]

    def shown(n, first):
        mine = pl.ds(first, 2 * rows)
        return [
            pltpu.make_async_copy(acts.at[n % 2, i], acts_all.at[i, mine], acts_sem.at[n % 2, i]) for i in range(3)
        ]

    def first_row(shift):
        return pl.multiple_of(device(shift, 0) * rows, 2 * rows)

    def work(n, first):
        mine = pl.ds(first, 2 * rows)
        rank, width = ADAPTER_RANK, MODEL_WIDTH
        if n >= 2:
            for copy in shown(n, first):
                copy.wait()
        low[mine, : 2 * rank] = matrix_product(landed[0][mine, :width], squeeze[...]).astype(bf16)
        low[mine, 2 * rank :] = times_transposed(landed[1][mine, :], widen_down[...]).astype(bf16)

        @pl.loop(0, held.shape[1] // wide)
        def _(t):
            own = pl.ds(pl.multiple_of(t * wide, wide), wide)
            two = landed[0][mine, :width]
            gate = times_transposed(two, held[0, own, :]) + matrix_product(
                low[mine, :rank], widen_gate[:, own]
            )
            upward = times_transposed(two, held[1, own, :]) + matrix_product(
                low[mine, rank : 2 * rank], widen_up[:, own]
            )
            pull = times_transposed(landed[1][mine, :], held[2, own, :]) + times_transposed(
                low[mine, 2 * rank :], narrow[own, :]
            )
            scale = math.sqrt(2.0 / math.pi)
            square = gate * gate
            bend = jnp.tanh(scale * gate * (1.0 + 0.044715 * square))
            rise = 0.5 * (1.0 + bend)
            active = gate * rise
            slope = rise + 0.5 * gate * (1.0 - bend * bend) * (scale * (1.0 + 3 * 0.044715 * square))
            for i, value in enumerate((pull * upward * slope, pull * active, active * upward)):
                acts[n % 2, i, :, own] = value.astype(bf16)
                turned[i, own, mine] = value.T.astype(bf16)

        for copy in leaving(n, first) + shown(n, first):
            copy.start()

    for i in (0, 1):
        for way in (0, 1):
            hop(i, way, 1).start()
        across(i, 0, 0, core).start()
    keeps = [
        pltpu.make_async_copy(sources[i], at(i, 0, 0, core, (0, rows)), own_sem.at[i]) for i in range(3)
    ]
    for keep in keeps:
        keep.start()
    for copy in keeps + fetches:
        copy.wait()
    for i in (0, 1):
        across(i, 0, 0, 1 - core).wait_recv()
    work(0, first_row(0))
    for hops in range(1, reach + 1):
        for i in (0, 1):
            for way in (0, 1):
                arriving(i, way, hops).wait_recv()
                if hops < reach:
                    hop(i, way, hops + 1).start()
                across(i, way, hops, core).start()
        if hops == reach:
            for way in (0, 1):
                hop(2, way, 1).start()
            across(2, 0, 0, core).start()
        else:
            for way in (0, 1):
                for i in (0, 1):
                    across(i, way, hops, 1 - core).wait_recv()
                work(2 * hops - 1 + way, first_row(-hops if way == 0 else hops))
    for way in (0, 1):
        for i in (0, 1):
            across(i, way, reach, 1 - core).wait_recv()
    work(2 * reach - 1, first_row(reach))
    rank = ADAPTER_RANK

    def relay(hops):
        for way in (0, 1):
            arriving(2, way, hops).wait_recv()
            if hops < reach:
                hop(2, way, hops + 1).start()
            across(2, way, hops, core).start()

    for kind in range(3):

        def tile_copy(t, kind=kind):
            there = pl.ds(pl.multiple_of(t * wide, wide), wide)
            return pltpu.make_async_copy(
                tiles.at[t % 2], share_out.at[kind, :, there], tile_sem.at[t % 2]
            )

        @pl.loop(0, MODEL_WIDTH // wide)
        def _(t, kind=kind, tile_copy=tile_copy):
            @pl.when(t > 1)
            def _():
                tile_copy(t - 2).wait()

            cols = pl.ds(pl.multiple_of(t * wide, wide), wide)
            tiles[t % 2] = matrix_product(
                turned[kind], landed[1 if kind == 2 else 0][:, cols]
            ).astype(bf16)
            tile_copy(t).start()

        relay(kind + 1)
        if kind == 2:
            piece_out[0] = matrix_product(turned[0], low[:, :rank]).astype(bf16)
            piece_out[1] = matrix_product(turned[1], low[:, rank : 2 * rank]).astype(bf16)
            down_out[...] = matrix_product(turned[2], low[:, 2 * rank :])
        tile_copy(MODEL_WIDTH // wide - 2).wait()
        tile_copy(MODEL_WIDTH // wide - 1).wait()
    for hops in range(4, reach + 1):
        relay(hops)
    across(2, 0, 0, 1 - core).wait_recv()
    for hops in range(1, reach + 1):
        for way in (0, 1):
            across(2, way, hops, 1 - core).wait_recv()
    for i in range(3):
        across(i, 0, 0, core).wait_send()
        for hops in range(1, reach + 1):
            for way in (0, 1):
                across(i, way, hops, core).wait_send()
                hop(i, way, hops).wait_send()
    for n in range(chips):
        if n == 0:
            shift = 0
        elif n == 2 * reach - 1:
            shift = reach
        else:
            shift = (-1 if n % 2 else 1) * ((n + 1) // 2)
        for copy in leaving(n, first_row(shift)):
            copy.wait()
        if n >= chips - 2:
            for copy in shown(n, first_row(shift)):
                copy.wait()


def unit_rows(two, grad, later, planes, squeeze, widen_down, widen_gate, widen_up, narrow, ident):
    size = lax.axis_size("fsdp")
    rank = ADAPTER_RANK
    if size != 16:
        two, grad = gather_rows(two), gather_rows(grad)
        two, lora_out = two[:, :MODEL_WIDTH], two[:, MODEL_WIDTH:]
        low = matrix_product(two, squeeze).astype(bf16)
        pulled = times_transposed(grad, widen_down).astype(bf16)
        gate = times_transposed(two, planes[0]) + matrix_product(low[:, :rank], widen_gate)
        upward = times_transposed(two, planes[1]) + matrix_product(low[:, rank:], widen_up)
        units_grad = times_transposed(grad, planes[2]) + times_transposed(pulled, narrow)
        units = (gelu_tanh(gate) * upward).astype(bf16)
        gate_grad, up_grad = unit_backward(gate, upward, units_grad)
        return (
            two,
            grad,
            gather_rows(later),
            jnp.stack([gate_grad, up_grad, units]),
            jnp.concatenate([low, pulled, lora_out], axis=1),
            jnp.stack(
                [
                    outer_product_rows(gate_grad, two),
                    outer_product_rows(up_grad, two),
                    outer_product_rows(units, grad),
                ]
            ).astype(bf16),
            jnp.stack(
                [outer_product_rows(gate_grad, low[:, :rank]), outer_product_rows(up_grad, low[:, rank:])]
            ).astype(bf16),
            outer_product_rows(units, pulled),
        )
    chips = size // 2
    rows, columns = grad.shape
    all_rows, hidden = size * rows, planes.shape[1]
    anywhere, inside = pl.BlockSpec(memory_space=pl.ANY), pl.BlockSpec(memory_space=pltpu.VMEM)
    pair = pltpu.SemaphoreType.DMA((3, 2, chips // 2))
    sides = pltpu.SemaphoreType.DMA((3, 2, chips // 2 + 1))
    return pl.pallas_call(
        functools.partial(unit_kernel, chips),
        out_shape=(
            jax.ShapeDtypeStruct((all_rows, columns), bf16),
            jax.ShapeDtypeStruct((all_rows, columns), bf16),
            jax.ShapeDtypeStruct((all_rows, later.shape[1]), bf16),
            jax.ShapeDtypeStruct((3, all_rows, hidden), bf16),
            jax.ShapeDtypeStruct((all_rows, 4 * rank), bf16),
            jax.ShapeDtypeStruct((3, hidden, columns), bf16),
            jax.ShapeDtypeStruct((2, hidden, rank), bf16),
            jax.ShapeDtypeStruct((hidden, rank), f32),
        ),
        in_specs=[anywhere] * 4 + [inside] * 5,
        out_specs=(anywhere,) * 6 + (inside,) * 2,
        scratch_shapes=[
            pltpu.VMEM(planes.shape, bf16),
            pltpu.VMEM((3, hidden, all_rows), bf16),
            pltpu.VMEM((2, 3, 2 * rows, hidden), bf16),
            pltpu.VMEM((all_rows, 3 * rank), bf16),
            pltpu.VMEM((2, hidden, 256), bf16),
            pltpu.VMEM((all_rows, two.shape[1]), bf16),
            pltpu.VMEM((all_rows, columns), bf16),
            pltpu.SemaphoreType.DMA((3,)),
            pltpu.SemaphoreType.DMA((3,)),
            pair,
            pair,
            sides,
            sides,
            pltpu.SemaphoreType.DMA((chips, 4)),
            pltpu.SemaphoreType.DMA((2, 3)),
            pltpu.SemaphoreType.DMA((2,)),
        ],
        compiler_params=pltpu.CompilerParams(
            collective_id=ident, has_side_effects=True, vmem_limit_bytes=60 << 20
        ),
        cost_estimate=busy(100),
        name="unit_rows",
    )(two, grad, later, planes, squeeze, widen_down, widen_gate, widen_up, narrow)


def mix_kernel(chips, *refs):
    acts_ref, planes, gate_b, up_b, down_a, o_ref = refs[:6]
    acts, held, side_buf, ring_buf, stage, mine = refs[6:12]
    held_sem, side_send, side_recv, ring_send, ring_recv = refs[12:]
    core, device = ring_neighbours(chips)
    rows, columns = o_ref.shape
    reach = chips // 2
    half = columns // 2
    tile = 16
    wide = 256
    ways = (device(1, core), device(-1, core))
    side = device(0, 1 - core)
    order = [(reach, 0, 0)]
    for step in range(1, reach):
        order += [(reach - step, 0, step), (chips - reach + step, 1, step)]
    order.append((0, 0, reach))
    fetches = [pltpu.make_async_copy(planes.at[i], held.at[i], held_sem.at[chips, i]) for i in range(3)]

    def fetched(i):
        here = pl.ds(pl.multiple_of(device(order[i][0], 0) * rows, 2 * rows), 2 * rows)
        return [pltpu.make_async_copy(acts_ref.at[k, here], acts.at[k, here], held_sem.at[i, k]) for k in range(3)]

    for copy in fetched(0) + fetches + [copy for i in range(1, chips) for copy in fetched(i)]:
        copy.start()
    meet((*ways, side))

    def across(i):
        target = order[i][0]
        return pltpu.make_async_remote_copy(
            stage.at[i % 2],
            side_buf.at[target],
            side_send.at[target],
            side_recv.at[target],
            device_id={"fsdp": side},
            device_id_type=MESH,
        )

    def hop(way, step, part):
        target = (reach - step if way == 0 else chips - reach + step) % chips
        cols = pl.ds(way * half, half) if step == 0 else pl.ds(0, columns)
        here = pl.ds(part * (rows // 2), rows // 2)
        return pltpu.make_async_remote_copy(
            side_buf.at[target, here, cols],
            ring_buf.at[way, step, here, cols],
            ring_send.at[way, step, part],
            ring_recv.at[way, step, part],
            device_id={"fsdp": ways[way]},
            device_id_type=MESH,
        )

    def make(i):
        target, slot = order[i][0], i % 2
        for copy in fetched(i):
            copy.wait()
        if i >= 2:
            across(i - 2).wait_send()
        theirs = pl.ds(pl.multiple_of(device(target, 1 - core) * rows, rows), rows)
        ours = pl.ds(pl.multiple_of(device(target, core) * rows, rows), rows)

        def block(kind):
            return jnp.concatenate([acts[kind, theirs, :], acts[kind, ours, :]], axis=0)

        def put(first, value):
            cols = pl.ds(pl.multiple_of(first, wide), wide)
            stage[slot, :, cols] = value[:rows].astype(bf16)
            mine[slot, :, cols] = value[rows:].astype(bf16)

        @pl.loop(0, MODEL_WIDTH // wide)
        def _(t):
            cols = pl.ds(pl.multiple_of(t * wide, wide), wide)
            put(
                t * wide,
                matrix_product(block(0), held[0, :, cols])
                + matrix_product(block(1), held[1, :, cols]),
            )
            put(
                MODEL_WIDTH + 2 * ADAPTER_RANK + t * wide,
                matrix_product(block(2), held[2, :, cols]),
            )

        put(MODEL_WIDTH, times_transposed(block(0), gate_b[...]))
        put(MODEL_WIDTH + ADAPTER_RANK, times_transposed(block(1), up_b[...]))
        put(2 * MODEL_WIDTH + 2 * ADAPTER_RANK, matrix_product(block(2), down_a[...]))
        across(i).start()

    def add(i):
        target, way, step = order[i]
        last = target == 0
        incoming = [(w, step - 1) for w in ((0, 1) if last else (way,))] if step else []
        across(i).wait_recv()
        for part in (0, 1):
            for w, s in incoming:
                hop(w, s, part).wait_recv()

            @pl.loop(0, rows // 2 // tile)
            def _(j, part=part):
                here = pl.ds(pl.multiple_of(part * (rows // 2) + j * tile, tile), tile)
                for side_half in (0, 1):
                    cols = pl.ds(side_half * half, half)
                    total = mine[i % 2, here, cols].astype(f32) + side_buf[target, here, cols].astype(f32)
                    for w, s in incoming:
                        if s or w == side_half:
                            total = total + ring_buf[w, s, here, cols].astype(f32)
                    if last:
                        o_ref[here, cols] = total
                    else:
                        side_buf[target, here, cols] = total.astype(bf16)

            if not last:
                hop(way, step, part).start()
                if step == 0:
                    hop(1, 0, part).start()

    for fetch in fetches:
        fetch.wait()
    make(0)
    add(0)
    for i in range(1, len(order), 2):
        both = range(i, min(i + 2, len(order)))
        for j in both:
            make(j)
        for j in both:
            add(j)
    for i in range(len(order) - 2, len(order)):
        across(i).wait_send()
    for step in range(reach):
        for way in (0, 1):
            for part in (0, 1):
                hop(way, step, part).wait_send()


def mix_rows(acts, planes, gate_b, up_b, down_a, ident):
    size = lax.axis_size("fsdp")
    if size != 16:
        gate_grad, up_grad, units = acts[0], acts[1], acts[2]
        terms = [
            matrix_product(gate_grad, planes[0]) + matrix_product(up_grad, planes[1]),
            times_transposed(gate_grad, gate_b),
            times_transposed(up_grad, up_b),
            matrix_product(units, planes[2]),
            matrix_product(units, down_a),
        ]
        return scatter_rows(jnp.concatenate(terms, axis=1))
    chips = size // 2
    rows, columns = acts.shape[1] // size, 2 * MODEL_WIDTH + 3 * ADAPTER_RANK
    pair = pltpu.SemaphoreType.DMA((2, chips // 2, 2))
    sides = pltpu.SemaphoreType.DMA((chips,))
    return pl.pallas_call(
        functools.partial(mix_kernel, chips),
        out_shape=jax.ShapeDtypeStruct((rows, columns), f32),
        in_specs=[pl.BlockSpec(memory_space=pl.ANY)] * 2
        + [pl.BlockSpec(memory_space=pltpu.VMEM)] * 3,
        out_specs=pl.BlockSpec(memory_space=pltpu.VMEM),
        scratch_shapes=[
            pltpu.VMEM(acts.shape, bf16),
            pltpu.VMEM(planes.shape, bf16),
            pltpu.VMEM((chips, rows, columns), bf16),
            pltpu.VMEM((2, chips // 2, rows, columns), bf16),
            pltpu.VMEM((2, rows, columns), bf16),
            pltpu.VMEM((2, rows, columns), bf16),
            pltpu.SemaphoreType.DMA((chips + 1, 3)),
            sides,
            sides,
            pair,
            pair,
        ],
        compiler_params=pltpu.CompilerParams(
            collective_id=ident, has_side_effects=True, vmem_limit_bytes=60 << 20
        ),
        cost_estimate=busy(1),
        name="mix_rows",
    )(acts, planes, gate_b, up_b, down_a)


def share_kernel(size, chunk, own_count, *refs):
    x_ref, mid_ref, turned, lora, grad, widen, o_ref, in_ref, a_ref, near_ref, far_ref, gain_ref, all_ref, low_t = refs[:14]
    sems = refs[14:]
    send_sem, recv_sem, own_sem = sems[5:]
    _, device = ring_neighbours(size // 2)
    me = lax.axis_index("fsdp")
    hidden = HIDDEN_COUNT // size
    width = MODEL_WIDTH // size
    sections = (
        (0, PROJECT_COLUMNS, width),
        (width, GATE_START, hidden),
        (width + hidden, GATE_START + HIDDEN_COUNT, hidden),
    )

    def greet():
        barrier = pltpu.get_barrier_semaphore()

        def one(i, carry):
            pl.semaphore_signal(barrier, inc=1, device_id={"fsdp": (me + i) % size}, device_id_type=MESH)
            return carry

        lax.fori_loop(1, size, one, 0)
        pl.semaphore_wait(barrier, size - 1)

    def rows(ref, first):
        return ref.at[pl.ds(pl.multiple_of(first, 8), chunk)]

    def aim(start, length):
        owner = (start + me * length) // own_count
        return owner, start + me * length - owner * own_count

    def remote(source, first, owner, sent=0):
        return pltpu.make_async_remote_copy(
            source,
            rows(o_ref, first),
            send_sem.at[sent],
            recv_sem.at[first // chunk],
            device_id={"fsdp": owner},
            device_id_type=MESH,
        )

    def local(source, first):
        return pltpu.make_async_copy(source, rows(o_ref, first), own_sem.at[first // chunk])

    def send_all():
        for base, start, length in sections:

            def send(j, carry, base=base, aimed=aim(start, length)):
                over = (aimed[1] + j * chunk >= own_count).astype(jnp.int32)
                owner = aimed[0] + over
                first = aimed[1] + j * chunk - over * own_count
                source = rows(mid_ref, base + j * chunk)

                @pl.when(owner != me)
                def _():
                    remote(source, first, owner, base // chunk + j).start()

                @pl.when(owner == me)
                def _():
                    local(source, first).start()

                return carry

            lax.fori_loop(0, length // chunk, send, 0)

    def work(shift):
        first = shift == 0
        count = 2 * x_ref.shape[0]
        here = pl.ds(pl.multiple_of(device(shift, 0) * x_ref.shape[0], count), count)
        rank = ADAPTER_RANK

        def put(ref, cols, value):
            ref[:, cols] = value if first else ref[:, cols] + value

        def flip(block):
            return block.astype(f32).T.astype(bf16)

        normed = flip(turned[0, here, :])
        wide = PROJECT_COLUMNS // rank
        for i in range(3):
            low_t[i] = flip(lora[here, pl.ds(i * rank, rank)])

        @pl.loop(0, wide)
        def _(t):
            cols = pl.ds(pl.multiple_of(t * rank, rank), rank)
            part = jnp.maximum(t - (wide - 3), 0)
            total = matrix_product(jnp.concatenate([normed, low_t[part]], axis=0), all_ref[here, cols])
            put(in_ref, cols, total[: normed.shape[0]])
            put(near_ref, cols, total[normed.shape[0] :])

        spans = ((0, QUERY_WIDTH), (QUERY_WIDTH, HEAD_WIDTH), (QUERY_WIDTH + HEAD_WIDTH, HEAD_WIDTH))
        for i, (start, width) in enumerate(spans):
            cols = pl.ds(start, width)
            low = times_transposed(all_ref[here, cols], widen[:, cols]).astype(bf16)
            put(a_ref, pl.ds(i * rank, rank), matrix_product(normed, low))
        lows = [all_ref[here, pl.ds(PROJECT_COLUMNS + i * rank, rank)] for i in range(4)]
        for i, kind in ((0, 1), (1, 2), (2, 2)):
            put(a_ref, pl.ds((3 + i) * rank, rank), matrix_product(flip(turned[kind, here, :]), lows[i]))
        pulled = flip(lows[3])

        @pl.loop(0, MODEL_WIDTH // rank)
        def _(t):
            cols = pl.ds(pl.multiple_of(t * rank, rank), rank)
            put(far_ref, cols, matrix_product(pulled, grad[here, cols]))

        gain_ref[here, :] = all_ref[here, pl.ds(PROJECT_COLUMNS + 4 * rank, gain_ref.shape[1])]

    gather_kernel(size // 2, x_ref, all_ref, *sems[:5], greet=greet, also=send_all, work=work)

    def arrive(j, carry):
        column = me * own_count + j * chunk
        here = rows(o_ref, j * chunk)
        away, kept = 0, 0
        for _, start, length in sections:
            mine = start + me * length
            inside = (column >= start) & (column < start + length * size)
            outside = (column < mine) | (column >= mine + length)
            away = away + (inside & outside).astype(jnp.int32)
            kept = kept + (inside & ~outside).astype(jnp.int32)

        @pl.when(away > 0)
        def _():
            remote(here, j * chunk, (me + 1) % size).wait_recv()

        @pl.when(kept > 0)
        def _():
            local(rows(mid_ref, 0), j * chunk).wait()

        return carry

    lax.fori_loop(0, own_count // chunk, arrive, 0)
    for base, start, length in sections:

        def sent(j, carry, base=base, aimed=aim(start, length)):
            over = (aimed[1] + j * chunk >= own_count).astype(jnp.int32)
            owner = aimed[0] + over
            first = aimed[1] + j * chunk - over * own_count

            @pl.when(owner != me)
            def _():
                remote(rows(mid_ref, base + j * chunk), first, owner, base // chunk + j).wait_send()

            return carry

        lax.fori_loop(0, length // chunk, sent, 0)


def share_rows(block, middle, turned, lora, grad, widen, ident):
    size = lax.axis_size("fsdp")
    rank = ADAPTER_RANK
    rows, columns = block.shape
    own_count = ADAPTER_COLUMNS // size
    gain_width = columns - PROJECT_COLUMNS - 4 * rank
    width = MODEL_WIDTH // size
    chunk = math.gcd(own_count, width, HIDDEN_COUNT // size, PROJECT_COLUMNS, GATE_START)
    if size != 16:
        every = gather_rows(block)
        spans = ((0, QUERY_WIDTH), (QUERY_WIDTH, HEAD_WIDTH), (QUERY_WIDTH + HEAD_WIDTH, HEAD_WIDTH))
        parts = [every[:, a : a + n] for a, n in spans]
        lows = [every[:, PROJECT_COLUMNS + i * rank :][:, :rank] for i in range(4)]
        squeezed = [
            outer_product_rows(turned[0], times_transposed(part, widen[:, a : a + n]).astype(bf16))
            for part, (a, n) in zip(parts, spans)
        ]
        squeezed += [outer_product_rows(turned[kind], lows[i]) for i, kind in ((0, 1), (1, 2), (2, 2))]
        near = [outer_product_rows(lora[:, i * rank :][:, :rank], part) for i, part in enumerate(parts)]
        middle_all = gather_rows(middle).reshape(size, -1, rank)
        hidden = HIDDEN_COUNT // size
        cuts = ((0, width), (width, width + hidden), (width + hidden, width + 2 * hidden))
        middle_all = jnp.concatenate(
            [jnp.zeros((PROJECT_COLUMNS, rank), bf16)]
            + [middle_all[:, a:b].reshape(-1, rank) for a, b in cuts]
            + [jnp.zeros((MODEL_WIDTH, rank), bf16)],
            axis=0,
        )
        return (
            lax.dynamic_slice_in_dim(middle_all, lax.axis_index("fsdp") * own_count, own_count, 0),
            outer_product_rows(turned[0], every[:, :PROJECT_COLUMNS]),
            jnp.concatenate(squeezed, axis=1),
            jnp.concatenate(near, axis=1),
            outer_product_rows(lows[3], grad),
            every[:, columns - gain_width :],
        )
    anywhere, inside = pl.BlockSpec(memory_space=pl.ANY), pl.BlockSpec(memory_space=pltpu.VMEM)
    pair = pltpu.SemaphoreType.DMA((2, size // 4))
    sides = pltpu.SemaphoreType.DMA((2, size // 4 + 1))
    return pl.pallas_call(
        functools.partial(share_kernel, size, chunk, own_count),
        out_shape=(
            jax.ShapeDtypeStruct((own_count, rank), bf16),
            jax.ShapeDtypeStruct((width, PROJECT_COLUMNS), f32),
            jax.ShapeDtypeStruct((width, 6 * rank), f32),
            jax.ShapeDtypeStruct((rank, PROJECT_COLUMNS), f32),
            jax.ShapeDtypeStruct((rank, MODEL_WIDTH), f32),
            jax.ShapeDtypeStruct((size * rows, gain_width), bf16),
        ),
        in_specs=[anywhere] * 2 + [inside] * 4,
        out_specs=(anywhere,) + (inside,) * 5,
        scratch_shapes=[
            pltpu.VMEM((size * rows, columns), bf16),
            pltpu.VMEM((3, rank, rank), bf16),
            pltpu.SemaphoreType.DMA,
            pair,
            pair,
            sides,
            sides,
            pltpu.SemaphoreType.DMA((middle.shape[0] // chunk,)),
            pltpu.SemaphoreType.DMA((own_count // chunk,)),
            pltpu.SemaphoreType.DMA((own_count // chunk,)),
        ],
        compiler_params=pltpu.CompilerParams(
            collective_id=ident, has_side_effects=True, vmem_limit_bytes=56 << 20
        ),
        cost_estimate=busy(1),
        name="share_rows",
    )(block, middle, turned, lora, grad, widen)


def per_device(
    hidden_input,
    sequence_lengths,
    norm_gain_values,
    input_proj_weight,
    output_proj_weight,
    feedforward_weight,
    adapter_first,
    adapter_second,
    adapter_down_first,
    output_gradient,
):
    size = lax.axis_size("fsdp")
    place = lax.axis_index("fsdp")
    tokens_dev = hidden_input.shape[1]
    all_rows = tokens_dev * size
    hidden_own = HIDDEN_COUNT // size
    width_own = MODEL_WIDTH // size
    columns_own = ADAPTER_COLUMNS // size
    offset = place * tokens_dev
    segment_all, position_all = segment_info(sequence_lengths[0], all_rows)
    segment_own = lax.dynamic_slice_in_dim(segment_all, offset, tokens_dev)
    position_own = lax.dynamic_slice_in_dim(position_all, offset, tokens_dev)
    row_all = jnp.arange(all_rows, dtype=jnp.int32)
    row_own = offset + jnp.arange(tokens_dev, dtype=jnp.int32)
    allowed = (segment_own[:, None] == segment_all[None, :]) & (
        row_own[:, None] >= row_all[None, :]
    )
    gains = norm_gain_values.astype(f32)
    first_factor = adapter_first[0]
    second_factor = adapter_second[0]
    rank = ADAPTER_RANK
    narrow_projection = first_factor[:, : 3 * rank]
    narrow_output = first_factor[:, 3 * rank : 4 * rank]
    squeeze_gate = first_factor[:, 4 * rank : 5 * rank]
    squeeze_up = first_factor[:, 5 * rank :]
    narrow_down = lax.dynamic_slice_in_dim(adapter_down_first[0], place * hidden_own, hidden_own, 0)
    widen_query = second_factor[:, :QUERY_WIDTH]
    widen_key = second_factor[:, QUERY_WIDTH : QUERY_WIDTH + HEAD_WIDTH]
    widen_value = second_factor[:, QUERY_WIDTH + HEAD_WIDTH : PROJECT_COLUMNS]
    widen_output = second_factor[:, PROJECT_COLUMNS:GATE_START]
    widen_gate = lax.dynamic_slice_in_dim(
        second_factor, GATE_START + place * hidden_own, hidden_own, 1
    )
    widen_up = lax.dynamic_slice_in_dim(
        second_factor, GATE_START + HIDDEN_COUNT + place * hidden_own, hidden_own, 1
    )
    widen_down = second_factor[:, GATE_START + 2 * HIDDEN_COUNT :]
    scaling = HEAD_WIDTH ** (-0.5)

    hidden_state = hidden_input[0].astype(f32)
    scale_one = rms_scale(hidden_state)
    normalized = (hidden_state * scale_one * gains[0]).astype(bf16)
    proj_in = ring_gather(input_proj_weight, 0)
    proj_in, proj_out = lax.optimization_barrier((proj_in, output_proj_weight))
    proj_out = gather_rows(proj_out)
    lora_qkv = matrix_product(normalized, narrow_projection).astype(bf16)
    projected = matrix_product(normalized, proj_in)
    query_pre = projected[:, :QUERY_WIDTH] + matrix_product(lora_qkv[:, :rank], widen_query)
    key_pre = projected[:, QUERY_WIDTH : QUERY_WIDTH + HEAD_WIDTH] + matrix_product(
        lora_qkv[:, rank : 2 * rank], widen_key
    )
    value_local = (
        projected[:, QUERY_WIDTH + HEAD_WIDTH :]
        + matrix_product(lora_qkv[:, 2 * rank :], widen_value)
    ).astype(bf16)
    query_rot = rotate(query_pre, position_own, 1.0).astype(bf16)
    key_rot = rotate(key_pre, position_own, 1.0).astype(bf16)
    keys_all = ring_gather(jnp.concatenate([key_rot, value_local], axis=1), 1)
    key_rows, value_rows = keys_all[:, :HEAD_WIDTH], keys_all[:, HEAD_WIDTH:]
    query_heads = query_rot.reshape(tokens_dev, HEADS, HEAD_WIDTH)
    scores = scores_of(query_heads, key_rows, allowed, scaling)
    row_max = jnp.max(scores, axis=-1, keepdims=True)
    powered = jnp.exp(scores - row_max)
    row_sum = jnp.sum(powered, axis=-1, keepdims=True)
    probs = powered / row_sum
    probs_low = probs.astype(bf16)
    attended = (
        jnp.einsum("thu,ud->thd", probs_low, value_rows, preferred_element_type=f32)
        .reshape(tokens_dev, QUERY_WIDTH)
        .astype(bf16)
    )
    lora_out = matrix_product(attended, narrow_output).astype(bf16)
    middle = (
        hidden_state
        + times_transposed(attended, proj_out)
        + matrix_product(lora_out, widen_output)
    )
    scale_two = rms_scale(middle)
    normed_two = (middle * scale_two * gains[1]).astype(bf16)

    weight_planes = feedforward_weight.transpose(1, 0, 2)
    two_all, grad_all, attended_all, acts, low_ffn, ffn_shares, ffn_pieces, down_own = unit_rows(
        jnp.concatenate([normed_two, lora_out], axis=1),
        output_gradient[0],
        jnp.concatenate([attended, lora_qkv], axis=1),
        weight_planes,
        first_factor[:, 4 * rank :],
        widen_down,
        widen_gate,
        widen_up,
        narrow_down,
        2,
    )
    lora_out_all = low_ffn[:, 3 * rank :]
    ffn_both = loop_shares(ffn_shares)
    rows_sum = mix_rows(
        acts, weight_planes, widen_gate, widen_up, narrow_down, 3
    )
    back_own, out_own = rows_sum[:, : MODEL_WIDTH + 2 * rank], rows_sum[:, MODEL_WIDTH + 2 * rank :]
    lora_hd = out_own[:, MODEL_WIDTH:].astype(bf16)

    gate_low = back_own[:, MODEL_WIDTH : MODEL_WIDTH + rank].astype(bf16)
    up_low = back_own[:, MODEL_WIDTH + rank :].astype(bf16)
    two_grad = (
        back_own[:, :MODEL_WIDTH]
        + times_transposed(gate_low, squeeze_gate)
        + times_transposed(up_low, squeeze_up)
    )
    weighted_two = gains[1] * two_grad
    middle_grad = (
        output_gradient[0].astype(f32)
        + scale_two * weighted_two
        - middle * scale_two**3 * jnp.mean(middle * weighted_two, axis=-1, keepdims=True)
    )
    gain_two = jnp.sum(two_grad * middle * scale_two, axis=0)

    branch_grad = middle_grad.astype(bf16)
    both = [block.reshape(tokens_dev, size, width_own) for block in (normalized, branch_grad)]
    turned = turn(jnp.concatenate(both, axis=2).reshape(tokens_dev, -1))
    normed_turn, branch_turn = turned[:, :width_own], turned[:, width_own:]
    lora_out_grad = times_transposed(branch_grad, widen_output).astype(bf16)
    attended_grad = (
        matrix_product(branch_grad, proj_out) + times_transposed(lora_out_grad, narrow_output)
    ).astype(bf16)
    heads_grad = attended_grad.reshape(tokens_dev, HEADS, HEAD_WIDTH)
    prob_grad = jnp.einsum("thd,ud->thu", heads_grad, value_rows, preferred_element_type=f32)
    row_dot = jnp.sum(probs * prob_grad, axis=-1, keepdims=True)
    score_grad = (probs * (prob_grad - row_dot)).astype(bf16)
    query_rot_grad = (
        jnp.einsum("thu,ud->thd", score_grad, key_rows, preferred_element_type=f32) * scaling
    )
    key_part = (
        jnp.einsum("thu,thd->ud", score_grad, query_heads, preferred_element_type=f32) * scaling
    )
    value_part = jnp.einsum("thu,thd->ud", probs_low, heads_grad, preferred_element_type=f32)
    pair_grad = ring_scatter([key_part, value_part], 4)
    pair_grad, normed_turn, branch_turn = lax.optimization_barrier((pair_grad, normed_turn, branch_turn))
    query_grad = rotate(
        query_rot_grad.reshape(tokens_dev, QUERY_WIDTH), position_own, -1.0
    ).astype(bf16)
    key_grad = rotate(pair_grad[:, :HEAD_WIDTH], position_own, -1.0).astype(bf16)
    value_grad = pair_grad[:, HEAD_WIDTH:].astype(bf16)
    proj_grad = jnp.concatenate([query_grad, key_grad, value_grad], axis=1)
    lora_qkv_grad = jnp.concatenate(
        [
            times_transposed(query_grad, widen_query),
            times_transposed(key_grad, widen_key),
            times_transposed(value_grad, widen_value),
        ],
        axis=1,
    ).astype(bf16)
    normed_grad = times_transposed(proj_grad, proj_in) + times_transposed(
        lora_qkv_grad, narrow_projection
    )
    weighted_one = gains[0] * normed_grad
    input_grad = (
        middle_grad
        + scale_one * weighted_one
        - hidden_state
        * scale_one**3
        * jnp.mean(hidden_state * weighted_one, axis=-1, keepdims=True)
    )
    gain_one = jnp.sum(normed_grad * hidden_state * scale_one, axis=0)

    lora_qkv_all = attended_all[:, QUERY_WIDTH:]
    out_piece = outer_product_rows(branch_turn, lora_out_all)
    gain_rows = jnp.stack([gain_one, gain_two]).astype(bf16).reshape(tokens_dev, -1)
    gain_count = gain_rows.shape[1]
    gain_rows = jnp.pad(gain_rows, ((0, 0), (0, -gain_count % 128)))
    proj_rows = jnp.concatenate(
        [proj_grad, lora_out_grad, gate_low, up_low, lora_hd, gain_rows], axis=1
    )
    column = place * width_own
    attended_turn, two_turn, attn_out_part, lora_qkv_all, proj_rows = lax.optimization_barrier(
        (
            lax.dynamic_slice_in_dim(attended_all, column, width_own, 1),
            lax.dynamic_slice_in_dim(two_all, column, width_own, 1),
            outer_product_rows(branch_turn, attended_all)[:, :QUERY_WIDTH],
            lora_qkv_all,
            proj_rows,
        )
    )
    middle_own, attn_in_part, squeeze_own, near, far, gain_all = share_rows(
        proj_rows,
        jnp.concatenate([out_piece.astype(bf16), ffn_pieces[0], ffn_pieces[1]], axis=0),
        jnp.stack([normed_turn, attended_turn, two_turn]),
        lora_qkv_all,
        grad_all,
        second_factor[:, :PROJECT_COLUMNS],
        5,
    )
    gain_all = gain_all[:, :gain_count].reshape(size, 2, MODEL_WIDTH)
    gain_all = jnp.sum(gain_all.astype(f32), axis=0)
    gain_own = lax.dynamic_slice_in_dim(gain_all, column, width_own, 1)
    gain_part = jnp.pad(gain_own, ((0, width_own - 2), (0, -width_own % 128)))
    attn_part = jnp.concatenate(
        [
            attn_in_part,
            attn_out_part,
            gain_part,
        ],
        axis=1,
    ).astype(bf16)
    attn_part, ffn_both, near, far, middle_own, out_own = lax.optimization_barrier(
        (attn_part, ffn_both, near, far, middle_own, out_own)
    )
    attn_sum = both_loops(loop_shares(attn_part))
    gain_column = PROJECT_COLUMNS + QUERY_WIDTH
    gain_sum = attn_sum[:2, gain_column : gain_column + width_own]
    first = place * columns_own
    far_start = GATE_START + 2 * HIDDEN_COUNT
    near = lax.dynamic_slice_in_dim(
        jnp.pad(near.T.astype(bf16), ((0, columns_own), (0, 0))), jnp.minimum(first, PROJECT_COLUMNS), columns_own, 0
    )
    far = lax.dynamic_slice_in_dim(
        jnp.pad(far.T.astype(bf16), ((columns_own, 0), (0, 0))),
        jnp.maximum(first - far_start + columns_own, 0),
        columns_own,
        0,
    )
    owned = first + jnp.arange(columns_own, dtype=jnp.int32)[:, None]
    expand_own = jnp.where(
        owned < PROJECT_COLUMNS, near, jnp.where(owned < far_start, middle_own, far)
    ).T.astype(f32)
    hidden_out = (middle + out_own[:, :MODEL_WIDTH] + matrix_product(lora_hd, widen_down)).astype(bf16)
    ffn_sum = both_loops(ffn_both).transpose(1, 0, 2)
    return (
        hidden_out[None],
        input_grad[None],
        gain_sum,
        attn_sum[:, :PROJECT_COLUMNS],
        attn_sum[:, PROJECT_COLUMNS:gain_column],
        ffn_sum,
        squeeze_own[None],
        expand_own[None],
        down_own[None],
    )


def solution(mesh):
    return jax.shard_map(
        per_device,
        mesh=mesh,
        in_specs=(
            P("loop", "fsdp", None),
            P("loop", None),
            P(),
            P("fsdp", None),
            P("fsdp", None),
            P("fsdp", None, None),
            P("loop", None, None),
            P("loop", None, None),
            P("loop", None, None),
            P("loop", "fsdp", None),
        ),
        out_specs=(
            P("loop", "fsdp", None),
            P("loop", "fsdp", None),
            P(None, "fsdp"),
            P("fsdp", None),
            P("fsdp", None),
            P("fsdp", None, None),
            P("loop", "fsdp", None),
            P("loop", None, "fsdp"),
            P("loop", "fsdp", None),
        ),
        check_vma=False,
    )
```

```python
import functools
import math

import jax
import jax.numpy as jnp
from jax import lax
from jax.experimental import pallas as pl
from jax.experimental.pallas import tpu as pltpu
from jax.sharding import PartitionSpec as P

MODEL_WIDTH = 2048
HEADS = 8
HEAD_WIDTH = 256
HIDDEN_COUNT = 16384
ADAPTER_RANK = 256
QUERY_WIDTH = 2048
PROJECT_COLUMNS = 2560
ADAPTER_COLUMNS = 39424
GATE_START = PROJECT_COLUMNS + MODEL_WIDTH

epsilon = 1e-06
bf16 = jnp.bfloat16
f32 = jnp.float32
MESH = pl.DeviceIdType.MESH


def matrix_product(former, latter):
    return jnp.dot(former, latter, preferred_element_type=f32)


def times_transposed(former, latter):
    return lax.dot_general(former, latter, (((1,), (1,)), ((), ())), preferred_element_type=f32)


def outer_product_rows(former, latter):
    return lax.dot_general(former, latter, (((0,), (0,)), ((), ())), preferred_element_type=f32)


def segment_info(lengths, row_count):
    row_ids = jnp.arange(row_count, dtype=jnp.int32)
    count = lengths.shape[0]
    labels = jnp.arange(count, dtype=jnp.int32)
    finish = jnp.sum(jnp.where(labels[:, None] <= labels[None, :], lengths[:, None], 0), axis=0)
    starts = finish - lengths
    segment = jnp.sum((row_ids[:, None] >= finish[None, :]).astype(jnp.int32), axis=1)
    opening = jnp.sum(jnp.where(segment[:, None] == labels[None, :], starts[None, :], 0), axis=1)
    return (segment, row_ids - opening)


def rotate(values, position, direction):
    half_dim = HEAD_WIDTH // 2
    frequency = jnp.exp(
        jnp.arange(half_dim).astype(f32) * (-2.0 * math.log(10000.0) / HEAD_WIDTH)
    )
    angles = position.astype(f32)[:, None] * frequency[None, :]
    cosine = jnp.cos(angles)[:, None, :]
    sine_val = direction * jnp.sin(angles)[:, None, :]
    shaped = values.reshape(values.shape[0], -1, HEAD_WIDTH)
    former = shaped[..., :half_dim]
    latter = shaped[..., half_dim:]
    turned = jnp.concatenate(
        [former * cosine - latter * sine_val, latter * cosine + former * sine_val], axis=-1
    )
    return turned.reshape(values.shape)


def rms_scale(values):
    return lax.rsqrt(jnp.mean(values * values, axis=-1, keepdims=True) + epsilon)


def gelu_tanh(values):
    return jax.nn.gelu(values, approximate=True)


def unit_backward(gate_value, upward_activation, hidden_unit_gradient):
    activated, pullback_function = jax.vjp(gelu_tanh, gate_value)
    gate_grad = pullback_function(hidden_unit_gradient * upward_activation)[0]
    return (gate_grad.astype(bf16), (hidden_unit_gradient * activated).astype(bf16))


def scores_of(query_heads, key_rows, allowed, scaling):
    product = (
        jnp.einsum("thd,ud->thu", query_heads, key_rows, preferred_element_type=f32) * scaling
    )
    return jnp.where(allowed[:, None, :], product, -1e30)


def gather_rows(block):
    return lax.all_gather(block, "fsdp", axis=0, tiled=True)


def scatter_rows(partial):
    return lax.psum_scatter(partial.astype(bf16), "fsdp", scatter_dimension=0, tiled=True).astype(f32)


def loop_shares(partial):
    return lax.all_gather(partial.astype(bf16), "loop", axis=0)


def both_loops(shares):
    return shares[0].astype(f32) + shares[1].astype(f32)


def sum_kernel(x_ref, o_ref):
    o_ref[...] = x_ref[0].astype(f32) + x_ref[1].astype(f32)


def sum_loops(shares):
    _, planes, rows, columns = shares.shape
    tile = min(rows, 256)
    return pl.pallas_call(
        sum_kernel,
        grid=(planes, rows // tile),
        out_shape=jax.ShapeDtypeStruct((planes, rows, columns), f32),
        in_specs=[pl.BlockSpec((2, 1, tile, columns), lambda i, j: (0, i, j, 0))],
        out_specs=pl.BlockSpec((1, tile, columns), lambda i, j: (i, j, 0)),
        compiler_params=pltpu.CompilerParams(vmem_limit_bytes=32 << 20),
        cost_estimate=busy(1),
        name="sum_loops",
    )(shares)


def turn(block):
    return lax.all_to_all(block, "fsdp", split_axis=1, concat_axis=0, tiled=True)


def chip_at(q, chips):
    return jnp.where(q < 4, 2 * q, 15 - 2 * q) if chips == 8 else q

def ring_place(chip, chips):
    return jnp.where(chip % 2 == 0, chip // 2, 7 - chip // 2) if chips == 8 else chip

def ring_neighbours(chips):
    me = lax.axis_index("fsdp")
    core = me % 2
    p = ring_place(me // 2, chips)
    def device(shift, c):
        return chip_at((p + shift + chips) % chips, chips) * 2 + c
    return core, device

def meet(devices):
    barrier = pltpu.get_barrier_semaphore()
    for d in devices:
        pl.semaphore_signal(barrier, inc=1, device_id={"fsdp": d}, device_id_type=MESH)
    pl.semaphore_wait(barrier, len(devices))

def gather_kernel(chips, x_ref, o_ref, own_sem, ring_send, ring_recv, side_send, side_recv, greet, also, work):
    core, device = ring_neighbours(chips)
    rows = x_ref.shape[0]
    reach = chips // 2
    ways = (device(1, core), device(-1, core))
    side = device(0, 1 - core)
    if greet is None:
        meet((*ways, side))
    else:
        greet()

    def span(way, hops):
        return (way * (rows // 2), rows // 2) if hops == reach else (0, rows)

    def at(way, hops, c, part):
        origin = device(-hops if way == 0 else hops, c)
        return o_ref.at[pl.ds(pl.multiple_of(origin * rows + part[0], 8), part[1])]

    def hop(way, hops):
        part = span(way, hops)
        here = at(way, hops - 1, core, part)
        src = x_ref.at[pl.ds(part[0], part[1])] if hops == 1 else here
        return pltpu.make_async_remote_copy(src, here, ring_send.at[way, hops - 1], ring_recv.at[way, hops - 1], device_id={"fsdp": ways[way]}, device_id_type=MESH)

    def arriving(way, hops):
        here = at(way, hops, core, span(way, hops))
        return pltpu.make_async_remote_copy(here, here, ring_send.at[way, hops - 1], ring_recv.at[way, hops - 1], device_id={"fsdp": ways[way]}, device_id_type=MESH)

    def across(way, hops, c):
        part = span(way, hops) if hops else (0, rows)
        there = at(way, hops, c, part)
        src = there if hops else x_ref
        return pltpu.make_async_remote_copy(src, there, side_send.at[way, hops], side_recv.at[way, hops], device_id={"fsdp": side}, device_id_type=MESH)

    for way in (0, 1):
        hop(way, 1).start()
    across(0, 0, core).start()
    own = pltpu.make_async_copy(x_ref, at(0, 0, core, (0, rows)), own_sem)
    own.start()
    if also is not None:
        also()
    if work is not None:
        own.wait()
        across(0, 0, 1 - core).wait_recv()
        work(0)
    for hops in range(1, reach + 1):
        for way in (0, 1):
            arriving(way, hops).wait_recv()
            if hops < reach:
                hop(way, hops + 1).start()
            across(way, hops, core).start()
        if work is not None:
            for way in (0, 1):
                across(way, hops, 1 - core).wait_recv()
                if hops < reach:
                    work(-hops if way == 0 else hops)
                elif way:
                    work(reach)
    if work is None:
        own.wait()
        across(0, 0, 1 - core).wait_recv()
        for hops in range(1, reach + 1):
            for way in (0, 1):
                across(way, hops, 1 - core).wait_recv()
    across(0, 0, core).wait_send()
    for hops in range(1, reach + 1):
        for way in (0, 1):
            across(way, hops, core).wait_send()
            hop(way, hops).wait_send()


def busy(us):
    return pl.CostEstimate(flops=0, bytes_accessed=int(us * 3.0e6), transcendentals=0)


def ring_gather(block, ident):
    size = lax.axis_size("fsdp")
    chips = size // 2
    rows, columns = block.shape
    pair = pltpu.SemaphoreType.DMA((2, chips // 2))
    sides = pltpu.SemaphoreType.DMA((2, chips // 2 + 1))
    return pl.pallas_call(
        functools.partial(gather_kernel, chips, greet=None, also=None, work=None),
        out_shape=jax.ShapeDtypeStruct((size * rows, columns), block.dtype),
        in_specs=[pl.BlockSpec(memory_space=pl.ANY)],
        out_specs=pl.BlockSpec(memory_space=pl.ANY),
        scratch_shapes=[pltpu.SemaphoreType.DMA, pair, pair, sides, sides],
        compiler_params=pltpu.CompilerParams(collective_id=ident, has_side_effects=True),
        cost_estimate=busy(1),
        name="ring_gather",
    )(block)

def scatter_kernel(chips, count, *refs):
    x_refs, o_ref = refs[:count], refs[count]
    side_buf, ring_buf, side_send, side_recv, ring_send, ring_recv = refs[count + 1 :]
    core, device = ring_neighbours(chips)
    rows, columns = o_ref.shape
    reach = chips // 2
    half = columns // 2
    tile = 16
    ways = (device(1, core), device(-1, core))
    side = device(0, 1 - core)
    meet((*ways, side))
    starts = [sum(x.shape[1] for x in x_refs[:i]) for i in range(count)]

    def shift(way, hops):
        return (hops if way == 0 else chips - hops) % chips

    def across(target, c, i):
        there = pl.ds(pl.multiple_of(device(target, c) * rows, tile), rows)
        return pltpu.make_async_remote_copy(
            x_refs[i].at[there],
            side_buf.at[target, :, pl.ds(starts[i], x_refs[i].shape[1])],
            side_send.at[target, i],
            side_recv.at[target, i],
            device_id={"fsdp": side},
            device_id_type=MESH,
        )

    def hop(way, step):
        cols = pl.ds(way * half, half) if step == 0 else pl.ds(0, columns)
        return pltpu.make_async_remote_copy(
            side_buf.at[shift(way, reach - step), :, cols],
            ring_buf.at[way, step, :, cols],
            ring_send.at[way, step],
            ring_recv.at[way, step],
            device_id={"fsdp": ways[way]},
            device_id_type=MESH,
        )

    order = [reach] + [shift(way, hops) for hops in range(reach - 1, 0, -1) for way in (0, 1)] + [0]
    for target in order:
        for i in range(count):
            across(target, 1 - core, i).start()

    def add(target, incoming, store):
        first = pl.multiple_of(device(target, core) * rows, tile)
        for i in range(count):
            across(target, core, i).wait_recv()

        @pl.loop(0, rows // tile)
        def _(j):
            here = pl.ds(pl.multiple_of(j * tile, tile), tile)
            mine = pl.ds(pl.multiple_of(first + j * tile, tile), tile)
            for i in range(count):
                cols = pl.ds(starts[i], x_refs[i].shape[1])
                total = x_refs[i][mine, :].astype(f32) + side_buf[target, here, cols].astype(f32)
                for way, step in incoming:
                    if step:
                        total = total + ring_buf[way, step, here, cols].astype(f32)
                store(here, cols, total)
            for way, step in incoming:
                if not step:
                    cols = pl.ds(way * half, half)
                    store(
                        here,
                        cols,
                        side_buf[target, here, cols].astype(f32) + ring_buf[way, 0, here, cols].astype(f32),
                    )

    for step in range(reach):
        for way in (0, 1):
            target = shift(way, reach - step)
            if step:
                hop(way, step - 1).wait_recv()

            def store(here, cols, total, target=target):
                side_buf[target, here, cols] = total.astype(bf16)

            if step or way == 0:
                add(target, [(way, step - 1)] if step else [], store)
            hop(way, step).start()
    for way in (0, 1):
        hop(way, reach - 1).wait_recv()

    def last(here, cols, total):
        o_ref[here, cols] = total

    add(0, [(0, reach - 1), (1, reach - 1)], last)
    for target in order:
        for i in range(count):
            across(target, 1 - core, i).wait_send()
    for step in range(reach):
        for way in (0, 1):
            hop(way, step).wait_send()


def ring_scatter(terms, ident):
    size = lax.axis_size("fsdp")
    terms = [term.astype(bf16) for term in terms]
    if size != 16:
        return scatter_rows(jnp.concatenate(terms, axis=1))
    chips, count = size // 2, len(terms)
    rows, columns = terms[0].shape[0] // size, sum(term.shape[1] for term in terms)
    pair = pltpu.SemaphoreType.DMA((2, chips // 2))
    sides = pltpu.SemaphoreType.DMA((chips, count))
    return pl.pallas_call(
        functools.partial(scatter_kernel, chips, count),
        out_shape=jax.ShapeDtypeStruct((rows, columns), f32),
        in_specs=[pl.BlockSpec(memory_space=pltpu.VMEM)] * count,
        out_specs=pl.BlockSpec(memory_space=pltpu.VMEM),
        scratch_shapes=[
            pltpu.VMEM((chips, rows, columns), bf16),
            pltpu.VMEM((2, chips // 2, rows, columns), bf16),
            sides,
            sides,
            pair,
            pair,
        ],
        compiler_params=pltpu.CompilerParams(
            collective_id=ident, has_side_effects=True, vmem_limit_bytes=56 << 20
        ),
        cost_estimate=busy(1),
        name="ring_scatter",
    )(*terms)


def adapter_parts(first_factor, second_factor, down_first):
    own = HIDDEN_COUNT // lax.axis_size("fsdp")
    start = lax.axis_index("fsdp") * own
    return (
        first_factor[:, 4 * ADAPTER_RANK :],
        second_factor[:, GATE_START + 2 * HIDDEN_COUNT :],
        lax.dynamic_slice_in_dim(second_factor, GATE_START + start, own, 1),
        lax.dynamic_slice_in_dim(second_factor, GATE_START + HIDDEN_COUNT + start, own, 1),
        lax.dynamic_slice_in_dim(down_first, start, own, 0),
    )


def part_copies(first_ref, second_ref, down_ref, parts, sems):
    own = parts[4].shape[0]
    start = pl.multiple_of(lax.axis_index("fsdp") * own, own)
    sources = (
        lambda: first_ref.at[:, pl.ds(4 * ADAPTER_RANK, 2 * ADAPTER_RANK)],
        lambda: second_ref.at[:, pl.ds(GATE_START + 2 * HIDDEN_COUNT, MODEL_WIDTH)],
        lambda: second_ref.at[:, pl.ds(pl.multiple_of(GATE_START + start, 128), own)],
        lambda: second_ref.at[:, pl.ds(pl.multiple_of(GATE_START + HIDDEN_COUNT + start, 128), own)],
        lambda: down_ref.at[pl.ds(start, own)],
    )
    return [
        pltpu.make_async_copy(source(), part, sems.at[i])
        for i, (source, part) in enumerate(zip(sources, parts))
        if part is not None
    ]


def unit_kernel(chips, *refs):
    sources, planes, adapters = refs[:3], refs[3], refs[4:7]
    two_all, grad_all, later_all, acts_all, low_all, share_out, piece_out, down_out = refs[7:15]
    held, turned, acts, low, tiles = refs[15:20]
    landed = (refs[20], refs[21], later_all)
    parts, part_sem = refs[22:27], refs[27]
    squeeze, widen_down, widen_gate, widen_up, narrow = parts
    held_sem, own_sem, ring_send, ring_recv, side_send, side_recv, out_sem, acts_sem, tile_sem = refs[28:]
    core, device = ring_neighbours(chips)
    rows = sources[0].shape[0]
    reach = chips // 2
    wide = 256
    ways = (device(1, core), device(-1, core))
    side = device(0, 1 - core)
    fetches = [pltpu.make_async_copy(planes.at[i], held.at[i], held_sem.at[i]) for i in range(3)]
    fetches += part_copies(*adapters, parts, part_sem)
    for fetch in fetches:
        fetch.start()
    meet((*ways, side))

    def span(way, hops):
        return (way * (rows // 2), rows // 2) if hops == reach else (0, rows)

    def at(i, way, hops, c, part):
        origin = device(-hops if way == 0 else hops, c)
        return landed[i].at[pl.ds(pl.multiple_of(origin * rows + part[0], 16), part[1])]

    def hop(i, way, hops):
        part = span(way, hops)
        here = at(i, way, hops - 1, core, part)
        src = sources[i].at[pl.ds(part[0], part[1])] if hops == 1 else here
        return pltpu.make_async_remote_copy(
            src,
            here,
            ring_send.at[i, way, hops - 1],
            ring_recv.at[i, way, hops - 1],
            device_id={"fsdp": ways[way]},
            device_id_type=MESH,
        )

    def arriving(i, way, hops):
        here = at(i, way, hops, core, span(way, hops))
        return pltpu.make_async_remote_copy(
            here,
            here,
            ring_send.at[i, way, hops - 1],
            ring_recv.at[i, way, hops - 1],
            device_id={"fsdp": ways[way]},
            device_id_type=MESH,
        )

    def across(i, way, hops, c):
        part = span(way, hops) if hops else (0, rows)
        there = at(i, way, hops, c, part)
        return pltpu.make_async_remote_copy(
            there if hops else sources[i],
            there,
            side_send.at[i, way, hops],
            side_recv.at[i, way, hops],
            device_id={"fsdp": side},
            device_id_type=MESH,
        )

    def leaving(n, first):
        mine = pl.ds(first, 2 * rows)
        width, under = grad_all.shape[1], low.shape[1]
        pairs = [
            (landed[0].at[mine, pl.ds(0, width)], two_all.at[mine]),
            (landed[0].at[mine, pl.ds(width, ADAPTER_RANK)], low_all.at[mine, pl.ds(under, ADAPTER_RANK)]),
            (low.at[mine], low_all.at[mine, pl.ds(0, under)]),
            (landed[1].at[mine], grad_all.at[mine]),
        ]
        return [pltpu.make_async_copy(a, b, out_sem.at[n, i]) for i, (a, b) in enumerate(pairs)]

    def shown(n, first):
        mine = pl.ds(first, 2 * rows)
        return [
            pltpu.make_async_copy(acts.at[n % 2, i], acts_all.at[i, mine], acts_sem.at[n % 2, i]) for i in range(3)
        ]

    def first_row(shift):
        return pl.multiple_of(device(shift, 0) * rows, 2 * rows)

    def work(n, first):
        mine = pl.ds(first, 2 * rows)
        rank, width = ADAPTER_RANK, MODEL_WIDTH
        if n >= 2:
            for copy in shown(n, first):
                copy.wait()
        low[mine, : 2 * rank] = matrix_product(landed[0][mine, :width], squeeze[...]).astype(bf16)
        low[mine, 2 * rank :] = times_transposed(landed[1][mine, :], widen_down[...]).astype(bf16)

        @pl.loop(0, held.shape[1] // wide)
        def _(t):
            own = pl.ds(pl.multiple_of(t * wide, wide), wide)
            two = landed[0][mine, :width]
            gate = times_transposed(two, held[0, own, :]) + matrix_product(
                low[mine, :rank], widen_gate[:, own]
            )
            upward = times_transposed(two, held[1, own, :]) + matrix_product(
                low[mine, rank : 2 * rank], widen_up[:, own]
            )
            pull = times_transposed(landed[1][mine, :], held[2, own, :]) + times_transposed(
                low[mine, 2 * rank :], narrow[own, :]
            )
            scale = math.sqrt(2.0 / math.pi)
            square = gate * gate
            bend = jnp.tanh(scale * gate * (1.0 + 0.044715 * square))
            rise = 0.5 * (1.0 + bend)
            active = gate * rise
            slope = rise + 0.5 * gate * (1.0 - bend * bend) * (scale * (1.0 + 3 * 0.044715 * square))
            for i, value in enumerate((pull * upward * slope, pull * active, active * upward)):
                acts[n % 2, i, :, own] = value.astype(bf16)
                turned[i, own, mine] = value.T.astype(bf16)

        for copy in leaving(n, first) + shown(n, first):
            copy.start()

    for i in (0, 1):
        for way in (0, 1):
            hop(i, way, 1).start()
        across(i, 0, 0, core).start()
    keeps = [
        pltpu.make_async_copy(sources[i], at(i, 0, 0, core, (0, rows)), own_sem.at[i]) for i in range(3)
    ]
    for keep in keeps:
        keep.start()
    for copy in keeps + fetches:
        copy.wait()
    for i in (0, 1):
        across(i, 0, 0, 1 - core).wait_recv()
    work(0, first_row(0))
    for hops in range(1, reach + 1):
        for i in (0, 1):
            for way in (0, 1):
                arriving(i, way, hops).wait_recv()
                if hops < reach:
                    hop(i, way, hops + 1).start()
                across(i, way, hops, core).start()
        if hops == reach:
            for way in (0, 1):
                hop(2, way, 1).start()
            across(2, 0, 0, core).start()
        else:
            for way in (0, 1):
                for i in (0, 1):
                    across(i, way, hops, 1 - core).wait_recv()
                work(2 * hops - 1 + way, first_row(-hops if way == 0 else hops))
    for way in (0, 1):
        for i in (0, 1):
            across(i, way, reach, 1 - core).wait_recv()
    work(2 * reach - 1, first_row(reach))
    rank = ADAPTER_RANK

    def relay(hops):
        for way in (0, 1):
            arriving(2, way, hops).wait_recv()
            if hops < reach:
                hop(2, way, hops + 1).start()
            across(2, way, hops, core).start()

    for kind in range(3):

        def tile_copy(t, kind=kind):
            there = pl.ds(pl.multiple_of(t * wide, wide), wide)
            return pltpu.make_async_copy(
                tiles.at[t % 2], share_out.at[kind, :, there], tile_sem.at[t % 2]
            )

        @pl.loop(0, MODEL_WIDTH // wide)
        def _(t, kind=kind, tile_copy=tile_copy):
            @pl.when(t > 1)
            def _():
                tile_copy(t - 2).wait()

            cols = pl.ds(pl.multiple_of(t * wide, wide), wide)
            tiles[t % 2] = matrix_product(
                turned[kind], landed[1 if kind == 2 else 0][:, cols]
            ).astype(bf16)
            tile_copy(t).start()

        relay(kind + 1)
        if kind == 2:
            piece_out[0] = matrix_product(turned[0], low[:, :rank]).astype(bf16)
            piece_out[1] = matrix_product(turned[1], low[:, rank : 2 * rank]).astype(bf16)
            down_out[...] = matrix_product(turned[2], low[:, 2 * rank :])
        tile_copy(MODEL_WIDTH // wide - 2).wait()
        tile_copy(MODEL_WIDTH // wide - 1).wait()
    for hops in range(4, reach + 1):
        relay(hops)
    across(2, 0, 0, 1 - core).wait_recv()
    for hops in range(1, reach + 1):
        for way in (0, 1):
            across(2, way, hops, 1 - core).wait_recv()
    for i in range(3):
        across(i, 0, 0, core).wait_send()
        for hops in range(1, reach + 1):
            for way in (0, 1):
                across(i, way, hops, core).wait_send()
                hop(i, way, hops).wait_send()
    for n in range(chips):
        if n == 0:
            shift = 0
        elif n == 2 * reach - 1:
            shift = reach
        else:
            shift = (-1 if n % 2 else 1) * ((n + 1) // 2)
        for copy in leaving(n, first_row(shift)):
            copy.wait()
        if n >= chips - 2:
            for copy in shown(n, first_row(shift)):
                copy.wait()


def unit_rows(two, grad, later, planes, adapters, ident):
    size = lax.axis_size("fsdp")
    rank = ADAPTER_RANK
    if size != 16:
        squeeze, widen_down, widen_gate, widen_up, narrow = adapter_parts(*adapters)
        two, grad = gather_rows(two), gather_rows(grad)
        two, lora_out = two[:, :MODEL_WIDTH], two[:, MODEL_WIDTH:]
        low = matrix_product(two, squeeze).astype(bf16)
        pulled = times_transposed(grad, widen_down).astype(bf16)
        gate = times_transposed(two, planes[0]) + matrix_product(low[:, :rank], widen_gate)
        upward = times_transposed(two, planes[1]) + matrix_product(low[:, rank:], widen_up)
        units_grad = times_transposed(grad, planes[2]) + times_transposed(pulled, narrow)
        units = (gelu_tanh(gate) * upward).astype(bf16)
        gate_grad, up_grad = unit_backward(gate, upward, units_grad)
        return (
            two,
            grad,
            gather_rows(later),
            jnp.stack([gate_grad, up_grad, units]),
            jnp.concatenate([low, pulled, lora_out], axis=1),
            jnp.stack(
                [
                    outer_product_rows(gate_grad, two),
                    outer_product_rows(up_grad, two),
                    outer_product_rows(units, grad),
                ]
            ).astype(bf16),
            jnp.stack(
                [outer_product_rows(gate_grad, low[:, :rank]), outer_product_rows(up_grad, low[:, rank:])]
            ).astype(bf16),
            outer_product_rows(units, pulled),
        )
    chips = size // 2
    rows, columns = grad.shape
    all_rows, hidden = size * rows, planes.shape[1]
    anywhere, inside = pl.BlockSpec(memory_space=pl.ANY), pl.BlockSpec(memory_space=pltpu.VMEM)
    pair = pltpu.SemaphoreType.DMA((3, 2, chips // 2))
    sides = pltpu.SemaphoreType.DMA((3, 2, chips // 2 + 1))
    return pl.pallas_call(
        functools.partial(unit_kernel, chips),
        out_shape=(
            jax.ShapeDtypeStruct((all_rows, columns), bf16),
            jax.ShapeDtypeStruct((all_rows, columns), bf16),
            jax.ShapeDtypeStruct((all_rows, later.shape[1]), bf16),
            jax.ShapeDtypeStruct((3, all_rows, hidden), bf16),
            jax.ShapeDtypeStruct((all_rows, 4 * rank), bf16),
            jax.ShapeDtypeStruct((3, hidden, columns), bf16),
            jax.ShapeDtypeStruct((2, hidden, rank), bf16),
            jax.ShapeDtypeStruct((hidden, rank), f32),
        ),
        in_specs=[anywhere] * 7,
        out_specs=(anywhere,) * 6 + (inside,) * 2,
        scratch_shapes=[
            pltpu.VMEM(planes.shape, bf16),
            pltpu.VMEM((3, hidden, all_rows), bf16),
            pltpu.VMEM((2, 3, 2 * rows, hidden), bf16),
            pltpu.VMEM((all_rows, 3 * rank), bf16),
            pltpu.VMEM((2, hidden, 256), bf16),
            pltpu.VMEM((all_rows, two.shape[1]), bf16),
            pltpu.VMEM((all_rows, columns), bf16),
            pltpu.VMEM((columns, 2 * rank), bf16),
            pltpu.VMEM((rank, columns), bf16),
            pltpu.VMEM((rank, hidden), bf16),
            pltpu.VMEM((rank, hidden), bf16),
            pltpu.VMEM((hidden, rank), bf16),
            pltpu.SemaphoreType.DMA((5,)),
            pltpu.SemaphoreType.DMA((3,)),
            pltpu.SemaphoreType.DMA((3,)),
            pair,
            pair,
            sides,
            sides,
            pltpu.SemaphoreType.DMA((chips, 4)),
            pltpu.SemaphoreType.DMA((2, 3)),
            pltpu.SemaphoreType.DMA((2,)),
        ],
        compiler_params=pltpu.CompilerParams(
            collective_id=ident, has_side_effects=True, vmem_limit_bytes=60 << 20
        ),
        cost_estimate=busy(100),
        name="unit_rows",
    )(two, grad, later, planes, *adapters)


def mix_kernel(chips, *refs):
    acts_ref, planes, adapters, o_ref = refs[0], refs[1], refs[2:5], refs[5]
    acts, held, gate_b, up_b, down_a, side_buf, ring_buf, stage, mine = refs[6:15]
    part_sem, held_sem, side_send, side_recv, ring_send, ring_recv = refs[15:]
    core, device = ring_neighbours(chips)
    rows, columns = o_ref.shape
    reach = chips // 2
    half = columns // 2
    tile = 16
    wide = 256
    ways = (device(1, core), device(-1, core))
    side = device(0, 1 - core)
    order = [(reach, 0, 0)]
    for step in range(1, reach):
        order += [(reach - step, 0, step), (chips - reach + step, 1, step)]
    order.append((0, 0, reach))
    fetches = [pltpu.make_async_copy(planes.at[i], held.at[i], held_sem.at[chips, i]) for i in range(3)]
    fetches += part_copies(*adapters, (None, None, gate_b, up_b, down_a), part_sem)

    def fetched(i):
        here = pl.ds(pl.multiple_of(device(order[i][0], 0) * rows, 2 * rows), 2 * rows)
        return [pltpu.make_async_copy(acts_ref.at[k, here], acts.at[k, here], held_sem.at[i, k]) for k in range(3)]

    for copy in fetched(0) + fetches + [copy for i in range(1, chips) for copy in fetched(i)]:
        copy.start()
    meet((*ways, side))

    def across(i):
        target = order[i][0]
        return pltpu.make_async_remote_copy(
            stage.at[i % 2],
            side_buf.at[target],
            side_send.at[target],
            side_recv.at[target],
            device_id={"fsdp": side},
            device_id_type=MESH,
        )

    def hop(way, step, part):
        target = (reach - step if way == 0 else chips - reach + step) % chips
        cols = pl.ds(way * half, half) if step == 0 else pl.ds(0, columns)
        here = pl.ds(part * (rows // 2), rows // 2)
        return pltpu.make_async_remote_copy(
            side_buf.at[target, here, cols],
            ring_buf.at[way, step, here, cols],
            ring_send.at[way, step, part],
            ring_recv.at[way, step, part],
            device_id={"fsdp": ways[way]},
            device_id_type=MESH,
        )

    def make(i):
        target, slot = order[i][0], i % 2
        for copy in fetched(i):
            copy.wait()
        if i >= 2:
            across(i - 2).wait_send()
        theirs = pl.ds(pl.multiple_of(device(target, 1 - core) * rows, rows), rows)
        ours = pl.ds(pl.multiple_of(device(target, core) * rows, rows), rows)

        def block(kind):
            return jnp.concatenate([acts[kind, theirs, :], acts[kind, ours, :]], axis=0)

        def put(first, value):
            cols = pl.ds(pl.multiple_of(first, wide), wide)
            stage[slot, :, cols] = value[:rows].astype(bf16)
            mine[slot, :, cols] = value[rows:].astype(bf16)

        @pl.loop(0, MODEL_WIDTH // wide)
        def _(t):
            cols = pl.ds(pl.multiple_of(t * wide, wide), wide)
            put(
                t * wide,
                matrix_product(block(0), held[0, :, cols])
                + matrix_product(block(1), held[1, :, cols]),
            )
            put(
                MODEL_WIDTH + 2 * ADAPTER_RANK + t * wide,
                matrix_product(block(2), held[2, :, cols]),
            )

        put(MODEL_WIDTH, times_transposed(block(0), gate_b[...]))
        put(MODEL_WIDTH + ADAPTER_RANK, times_transposed(block(1), up_b[...]))
        put(2 * MODEL_WIDTH + 2 * ADAPTER_RANK, matrix_product(block(2), down_a[...]))
        across(i).start()

    def add(i):
        target, way, step = order[i]
        last = target == 0
        incoming = [(w, step - 1) for w in ((0, 1) if last else (way,))] if step else []
        across(i).wait_recv()
        for part in (0, 1):
            for w, s in incoming:
                hop(w, s, part).wait_recv()

            @pl.loop(0, rows // 2 // tile)
            def _(j, part=part):
                here = pl.ds(pl.multiple_of(part * (rows // 2) + j * tile, tile), tile)
                for side_half in (0, 1):
                    cols = pl.ds(side_half * half, half)
                    total = mine[i % 2, here, cols].astype(f32) + side_buf[target, here, cols].astype(f32)
                    for w, s in incoming:
                        if s or w == side_half:
                            total = total + ring_buf[w, s, here, cols].astype(f32)
                    if last:
                        o_ref[here, cols] = total
                    else:
                        side_buf[target, here, cols] = total.astype(bf16)

            if not last:
                hop(way, step, part).start()
                if step == 0:
                    hop(1, 0, part).start()

    for fetch in fetches:
        fetch.wait()
    make(0)
    add(0)
    for i in range(1, len(order), 2):
        both = range(i, min(i + 2, len(order)))
        for j in both:
            make(j)
        for j in both:
            add(j)
    for i in range(len(order) - 2, len(order)):
        across(i).wait_send()
    for step in range(reach):
        for way in (0, 1):
            for part in (0, 1):
                hop(way, step, part).wait_send()


def mix_rows(acts, planes, adapters, ident):
    size = lax.axis_size("fsdp")
    if size != 16:
        gate_grad, up_grad, units = acts[0], acts[1], acts[2]
        gate_b, up_b, down_a = adapter_parts(*adapters)[2:]
        terms = [
            matrix_product(gate_grad, planes[0]) + matrix_product(up_grad, planes[1]),
            times_transposed(gate_grad, gate_b),
            times_transposed(up_grad, up_b),
            matrix_product(units, planes[2]),
            matrix_product(units, down_a),
        ]
        return scatter_rows(jnp.concatenate(terms, axis=1))
    chips = size // 2
    rows, columns = acts.shape[1] // size, 2 * MODEL_WIDTH + 3 * ADAPTER_RANK
    pair = pltpu.SemaphoreType.DMA((2, chips // 2, 2))
    sides = pltpu.SemaphoreType.DMA((chips,))
    return pl.pallas_call(
        functools.partial(mix_kernel, chips),
        out_shape=jax.ShapeDtypeStruct((rows, columns), f32),
        in_specs=[pl.BlockSpec(memory_space=pl.ANY)] * 5,
        out_specs=pl.BlockSpec(memory_space=pltpu.VMEM),
        scratch_shapes=[
            pltpu.VMEM(acts.shape, bf16),
            pltpu.VMEM(planes.shape, bf16),
            pltpu.VMEM((ADAPTER_RANK, planes.shape[1]), bf16),
            pltpu.VMEM((ADAPTER_RANK, planes.shape[1]), bf16),
            pltpu.VMEM((planes.shape[1], ADAPTER_RANK), bf16),
            pltpu.VMEM((chips, rows, columns), bf16),
            pltpu.VMEM((2, chips // 2, rows, columns), bf16),
            pltpu.VMEM((2, rows, columns), bf16),
            pltpu.VMEM((2, rows, columns), bf16),
            pltpu.SemaphoreType.DMA((5,)),
            pltpu.SemaphoreType.DMA((chips + 1, 3)),
            sides,
            sides,
            pair,
            pair,
        ],
        compiler_params=pltpu.CompilerParams(
            collective_id=ident, has_side_effects=True, vmem_limit_bytes=60 << 20
        ),
        cost_estimate=busy(1),
        name="mix_rows",
    )(acts, planes, *adapters)


def share_kernel(size, chunk, own_count, *refs):
    x_ref, mid_ref, turned, later_ref, grad, second_ref = refs[:6]
    o_ref, in_ref, a_ref, near_ref, far_ref, gain_ref, all_ref, low_t, lora, widen, load_sem = refs[6:17]
    sems = refs[17:]
    loads = [
        pltpu.make_async_copy(
            later_ref.at[:, pl.ds(QUERY_WIDTH, 3 * ADAPTER_RANK)], lora, load_sem.at[0]
        ),
        pltpu.make_async_copy(second_ref.at[:, pl.ds(0, PROJECT_COLUMNS)], widen, load_sem.at[1]),
    ]
    for load in loads:
        load.start()
    send_sem, recv_sem, own_sem = sems[5:]
    _, device = ring_neighbours(size // 2)
    me = lax.axis_index("fsdp")
    hidden = HIDDEN_COUNT // size
    width = MODEL_WIDTH // size
    sections = (
        (0, PROJECT_COLUMNS, width),
        (width, GATE_START, hidden),
        (width + hidden, GATE_START + HIDDEN_COUNT, hidden),
    )

    def greet():
        barrier = pltpu.get_barrier_semaphore()

        def one(i, carry):
            pl.semaphore_signal(barrier, inc=1, device_id={"fsdp": (me + i) % size}, device_id_type=MESH)
            return carry

        lax.fori_loop(1, size, one, 0)
        pl.semaphore_wait(barrier, size - 1)

    def rows(ref, first):
        return ref.at[pl.ds(pl.multiple_of(first, 8), chunk)]

    def aim(start, length):
        owner = (start + me * length) // own_count
        return owner, start + me * length - owner * own_count

    def remote(source, first, owner, sent=0):
        return pltpu.make_async_remote_copy(
            source,
            rows(o_ref, first),
            send_sem.at[sent],
            recv_sem.at[first // chunk],
            device_id={"fsdp": owner},
            device_id_type=MESH,
        )

    def local(source, first):
        return pltpu.make_async_copy(source, rows(o_ref, first), own_sem.at[first // chunk])

    def send_all():
        for base, start, length in sections:

            def send(j, carry, base=base, aimed=aim(start, length)):
                over = (aimed[1] + j * chunk >= own_count).astype(jnp.int32)
                owner = aimed[0] + over
                first = aimed[1] + j * chunk - over * own_count
                source = rows(mid_ref, base + j * chunk)

                @pl.when(owner != me)
                def _():
                    remote(source, first, owner, base // chunk + j).start()

                @pl.when(owner == me)
                def _():
                    local(source, first).start()

                return carry

            lax.fori_loop(0, length // chunk, send, 0)

    def work(shift):
        first = shift == 0
        if first:
            for load in loads:
                load.wait()
        count = 2 * x_ref.shape[0]
        here = pl.ds(pl.multiple_of(device(shift, 0) * x_ref.shape[0], count), count)
        rank = ADAPTER_RANK

        def put(ref, cols, value):
            ref[:, cols] = value if first else ref[:, cols] + value

        def flip(block):
            return block.astype(f32).T.astype(bf16)

        normed = flip(turned[0, here, :])
        wide = PROJECT_COLUMNS // rank
        for i in range(3):
            low_t[i] = flip(lora[here, pl.ds(i * rank, rank)])

        @pl.loop(0, wide)
        def _(t):
            cols = pl.ds(pl.multiple_of(t * rank, rank), rank)
            part = jnp.maximum(t - (wide - 3), 0)
            total = matrix_product(jnp.concatenate([normed, low_t[part]], axis=0), all_ref[here, cols])
            put(in_ref, cols, total[: normed.shape[0]])
            put(near_ref, cols, total[normed.shape[0] :])

        spans = ((0, QUERY_WIDTH), (QUERY_WIDTH, HEAD_WIDTH), (QUERY_WIDTH + HEAD_WIDTH, HEAD_WIDTH))
        for i, (start, width) in enumerate(spans):
            cols = pl.ds(start, width)
            low = times_transposed(all_ref[here, cols], widen[:, cols]).astype(bf16)
            put(a_ref, pl.ds(i * rank, rank), matrix_product(normed, low))
        lows = [all_ref[here, pl.ds(PROJECT_COLUMNS + i * rank, rank)] for i in range(4)]
        for i, kind in ((0, 1), (1, 2), (2, 2)):
            put(a_ref, pl.ds((3 + i) * rank, rank), matrix_product(flip(turned[kind, here, :]), lows[i]))
        pulled = flip(lows[3])

        @pl.loop(0, MODEL_WIDTH // rank)
        def _(t):
            cols = pl.ds(pl.multiple_of(t * rank, rank), rank)
            put(far_ref, cols, matrix_product(pulled, grad[here, cols]))

        gain_ref[here, :] = all_ref[here, pl.ds(PROJECT_COLUMNS + 4 * rank, gain_ref.shape[1])]

    gather_kernel(size // 2, x_ref, all_ref, *sems[:5], greet=greet, also=send_all, work=work)

    def arrive(j, carry):
        column = me * own_count + j * chunk
        here = rows(o_ref, j * chunk)
        away, kept = 0, 0
        for _, start, length in sections:
            mine = start + me * length
            inside = (column >= start) & (column < start + length * size)
            outside = (column < mine) | (column >= mine + length)
            away = away + (inside & outside).astype(jnp.int32)
            kept = kept + (inside & ~outside).astype(jnp.int32)

        @pl.when(away > 0)
        def _():
            remote(here, j * chunk, (me + 1) % size).wait_recv()

        @pl.when(kept > 0)
        def _():
            local(rows(mid_ref, 0), j * chunk).wait()

        return carry

    lax.fori_loop(0, own_count // chunk, arrive, 0)
    for base, start, length in sections:

        def sent(j, carry, base=base, aimed=aim(start, length)):
            over = (aimed[1] + j * chunk >= own_count).astype(jnp.int32)
            owner = aimed[0] + over
            first = aimed[1] + j * chunk - over * own_count

            @pl.when(owner != me)
            def _():
                remote(rows(mid_ref, base + j * chunk), first, owner, base // chunk + j).wait_send()

            return carry

        lax.fori_loop(0, length // chunk, sent, 0)


def share_rows(block, middle, turned, later, grad, second_factor, ident):
    size = lax.axis_size("fsdp")
    rank = ADAPTER_RANK
    rows, columns = block.shape
    own_count = ADAPTER_COLUMNS // size
    gain_width = columns - PROJECT_COLUMNS - 4 * rank
    width = MODEL_WIDTH // size
    chunk = math.gcd(own_count, width, HIDDEN_COUNT // size, PROJECT_COLUMNS, GATE_START)
    if size != 16:
        every = gather_rows(block)
        lora, widen = later[:, QUERY_WIDTH:], second_factor[:, :PROJECT_COLUMNS]
        spans = ((0, QUERY_WIDTH), (QUERY_WIDTH, HEAD_WIDTH), (QUERY_WIDTH + HEAD_WIDTH, HEAD_WIDTH))
        parts = [every[:, a : a + n] for a, n in spans]
        lows = [every[:, PROJECT_COLUMNS + i * rank :][:, :rank] for i in range(4)]
        squeezed = [
            outer_product_rows(turned[0], times_transposed(part, widen[:, a : a + n]).astype(bf16))
            for part, (a, n) in zip(parts, spans)
        ]
        squeezed += [outer_product_rows(turned[kind], lows[i]) for i, kind in ((0, 1), (1, 2), (2, 2))]
        near = [outer_product_rows(lora[:, i * rank :][:, :rank], part) for i, part in enumerate(parts)]
        middle_all = gather_rows(middle).reshape(size, -1, rank)
        hidden = HIDDEN_COUNT // size
        cuts = ((0, width), (width, width + hidden), (width + hidden, width + 2 * hidden))
        middle_all = jnp.concatenate(
            [jnp.zeros((PROJECT_COLUMNS, rank), bf16)]
            + [middle_all[:, a:b].reshape(-1, rank) for a, b in cuts]
            + [jnp.zeros((MODEL_WIDTH, rank), bf16)],
            axis=0,
        )
        return (
            lax.dynamic_slice_in_dim(middle_all, lax.axis_index("fsdp") * own_count, own_count, 0),
            outer_product_rows(turned[0], every[:, :PROJECT_COLUMNS]),
            jnp.concatenate(squeezed, axis=1),
            jnp.concatenate(near, axis=1),
            outer_product_rows(lows[3], grad),
            every[:, columns - gain_width :],
        )
    anywhere, inside = pl.BlockSpec(memory_space=pl.ANY), pl.BlockSpec(memory_space=pltpu.VMEM)
    pair = pltpu.SemaphoreType.DMA((2, size // 4))
    sides = pltpu.SemaphoreType.DMA((2, size // 4 + 1))
    return pl.pallas_call(
        functools.partial(share_kernel, size, chunk, own_count),
        out_shape=(
            jax.ShapeDtypeStruct((own_count, rank), bf16),
            jax.ShapeDtypeStruct((width, PROJECT_COLUMNS), f32),
            jax.ShapeDtypeStruct((width, 6 * rank), f32),
            jax.ShapeDtypeStruct((rank, PROJECT_COLUMNS), f32),
            jax.ShapeDtypeStruct((rank, MODEL_WIDTH), f32),
            jax.ShapeDtypeStruct((size * rows, gain_width), bf16),
        ),
        in_specs=[anywhere] * 2 + [inside, anywhere, inside, anywhere],
        out_specs=(anywhere,) + (inside,) * 5,
        scratch_shapes=[
            pltpu.VMEM((size * rows, columns), bf16),
            pltpu.VMEM((3, rank, rank), bf16),
            pltpu.VMEM((size * rows, 3 * rank), bf16),
            pltpu.VMEM((rank, PROJECT_COLUMNS), bf16),
            pltpu.SemaphoreType.DMA((2,)),
            pltpu.SemaphoreType.DMA,
            pair,
            pair,
            sides,
            sides,
            pltpu.SemaphoreType.DMA((middle.shape[0] // chunk,)),
            pltpu.SemaphoreType.DMA((own_count // chunk,)),
            pltpu.SemaphoreType.DMA((own_count // chunk,)),
        ],
        compiler_params=pltpu.CompilerParams(
            collective_id=ident, has_side_effects=True, vmem_limit_bytes=56 << 20
        ),
        cost_estimate=busy(1),
        name="share_rows",
    )(block, middle, turned, later, grad, second_factor)


def per_device(
    hidden_input,
    sequence_lengths,
    norm_gain_values,
    input_proj_weight,
    output_proj_weight,
    feedforward_weight,
    adapter_first,
    adapter_second,
    adapter_down_first,
    output_gradient,
):
    size = lax.axis_size("fsdp")
    place = lax.axis_index("fsdp")
    tokens_dev = hidden_input.shape[1]
    all_rows = tokens_dev * size
    hidden_own = HIDDEN_COUNT // size
    width_own = MODEL_WIDTH // size
    columns_own = ADAPTER_COLUMNS // size
    offset = place * tokens_dev
    segment_all, position_all = segment_info(sequence_lengths[0], all_rows)
    segment_own = lax.dynamic_slice_in_dim(segment_all, offset, tokens_dev)
    position_own = lax.dynamic_slice_in_dim(position_all, offset, tokens_dev)
    row_all = jnp.arange(all_rows, dtype=jnp.int32)
    row_own = offset + jnp.arange(tokens_dev, dtype=jnp.int32)
    allowed = (segment_own[:, None] == segment_all[None, :]) & (
        row_own[:, None] >= row_all[None, :]
    )
    gains = norm_gain_values.astype(f32)
    first_factor = adapter_first[0]
    second_factor = adapter_second[0]
    rank = ADAPTER_RANK
    narrow_projection = first_factor[:, : 3 * rank]
    narrow_output = first_factor[:, 3 * rank : 4 * rank]
    squeeze_gate = first_factor[:, 4 * rank : 5 * rank]
    squeeze_up = first_factor[:, 5 * rank :]
    adapters = (first_factor, second_factor, adapter_down_first[0])
    widen_query = second_factor[:, :QUERY_WIDTH]
    widen_key = second_factor[:, QUERY_WIDTH : QUERY_WIDTH + HEAD_WIDTH]
    widen_value = second_factor[:, QUERY_WIDTH + HEAD_WIDTH : PROJECT_COLUMNS]
    widen_output = second_factor[:, PROJECT_COLUMNS:GATE_START]
    widen_down = second_factor[:, GATE_START + 2 * HIDDEN_COUNT :]
    scaling = HEAD_WIDTH ** (-0.5)

    hidden_state = hidden_input[0].astype(f32)
    scale_one = rms_scale(hidden_state)
    normalized = (hidden_state * scale_one * gains[0]).astype(bf16)
    proj_in = ring_gather(input_proj_weight, 0)
    proj_in, proj_out = lax.optimization_barrier((proj_in, output_proj_weight))
    proj_out = gather_rows(proj_out)
    lora_qkv = matrix_product(normalized, narrow_projection).astype(bf16)
    projected = matrix_product(normalized, proj_in)
    query_pre = projected[:, :QUERY_WIDTH] + matrix_product(lora_qkv[:, :rank], widen_query)
    key_pre = projected[:, QUERY_WIDTH : QUERY_WIDTH + HEAD_WIDTH] + matrix_product(
        lora_qkv[:, rank : 2 * rank], widen_key
    )
    value_local = (
        projected[:, QUERY_WIDTH + HEAD_WIDTH :]
        + matrix_product(lora_qkv[:, 2 * rank :], widen_value)
    ).astype(bf16)
    query_rot = rotate(query_pre, position_own, 1.0).astype(bf16)
    key_rot = rotate(key_pre, position_own, 1.0).astype(bf16)
    keys_all = ring_gather(jnp.concatenate([key_rot, value_local], axis=1), 1)
    key_rows, value_rows = keys_all[:, :HEAD_WIDTH], keys_all[:, HEAD_WIDTH:]
    query_heads = query_rot.reshape(tokens_dev, HEADS, HEAD_WIDTH)
    scores = scores_of(query_heads, key_rows, allowed, scaling)
    row_max = jnp.max(scores, axis=-1, keepdims=True)
    powered = jnp.exp(scores - row_max)
    row_sum = jnp.sum(powered, axis=-1, keepdims=True)
    probs = powered / row_sum
    probs_low = probs.astype(bf16)
    attended = (
        jnp.einsum("thu,ud->thd", probs_low, value_rows, preferred_element_type=f32)
        .reshape(tokens_dev, QUERY_WIDTH)
        .astype(bf16)
    )
    lora_out = matrix_product(attended, narrow_output).astype(bf16)
    middle = (
        hidden_state
        + times_transposed(attended, proj_out)
        + matrix_product(lora_out, widen_output)
    )
    scale_two = rms_scale(middle)
    normed_two = (middle * scale_two * gains[1]).astype(bf16)

    weight_planes = feedforward_weight.transpose(1, 0, 2)
    two_all, grad_all, attended_all, acts, low_ffn, ffn_shares, ffn_pieces, down_own = unit_rows(
        jnp.concatenate([normed_two, lora_out], axis=1),
        output_gradient[0],
        jnp.concatenate([attended, lora_qkv], axis=1),
        weight_planes,
        adapters,
        2,
    )
    lora_out_all = low_ffn[:, 3 * rank :]
    ffn_both = loop_shares(ffn_shares)
    rows_sum = mix_rows(
        acts, weight_planes, adapters, 3
    )
    back_own, out_own = rows_sum[:, : MODEL_WIDTH + 2 * rank], rows_sum[:, MODEL_WIDTH + 2 * rank :]
    lora_hd = out_own[:, MODEL_WIDTH:].astype(bf16)

    gate_low = back_own[:, MODEL_WIDTH : MODEL_WIDTH + rank].astype(bf16)
    up_low = back_own[:, MODEL_WIDTH + rank :].astype(bf16)
    two_grad = (
        back_own[:, :MODEL_WIDTH]
        + times_transposed(gate_low, squeeze_gate)
        + times_transposed(up_low, squeeze_up)
    )
    weighted_two = gains[1] * two_grad
    middle_grad = (
        output_gradient[0].astype(f32)
        + scale_two * weighted_two
        - middle * scale_two**3 * jnp.mean(middle * weighted_two, axis=-1, keepdims=True)
    )
    gain_two = jnp.sum(two_grad * middle * scale_two, axis=0)

    branch_grad = middle_grad.astype(bf16)
    both = [block.reshape(tokens_dev, size, width_own) for block in (normalized, branch_grad)]
    turned = turn(jnp.concatenate(both, axis=2).reshape(tokens_dev, -1))
    normed_turn, branch_turn = turned[:, :width_own], turned[:, width_own:]
    lora_out_grad = times_transposed(branch_grad, widen_output).astype(bf16)
    attended_grad = (
        matrix_product(branch_grad, proj_out) + times_transposed(lora_out_grad, narrow_output)
    ).astype(bf16)
    heads_grad = attended_grad.reshape(tokens_dev, HEADS, HEAD_WIDTH)
    prob_grad = jnp.einsum("thd,ud->thu", heads_grad, value_rows, preferred_element_type=f32)
    row_dot = jnp.sum(probs * prob_grad, axis=-1, keepdims=True)
    score_grad = (probs * (prob_grad - row_dot)).astype(bf16)
    query_rot_grad = (
        jnp.einsum("thu,ud->thd", score_grad, key_rows, preferred_element_type=f32) * scaling
    )
    key_part = (
        jnp.einsum("thu,thd->ud", score_grad, query_heads, preferred_element_type=f32) * scaling
    )
    value_part = jnp.einsum("thu,thd->ud", probs_low, heads_grad, preferred_element_type=f32)
    pair_grad = ring_scatter([key_part, value_part], 4)
    pair_grad, normed_turn, branch_turn = lax.optimization_barrier((pair_grad, normed_turn, branch_turn))
    query_grad = rotate(
        query_rot_grad.reshape(tokens_dev, QUERY_WIDTH), position_own, -1.0
    ).astype(bf16)
    key_grad = rotate(pair_grad[:, :HEAD_WIDTH], position_own, -1.0).astype(bf16)
    value_grad = pair_grad[:, HEAD_WIDTH:].astype(bf16)
    proj_grad = jnp.concatenate([query_grad, key_grad, value_grad], axis=1)
    lora_qkv_grad = jnp.concatenate(
        [
            times_transposed(query_grad, widen_query),
            times_transposed(key_grad, widen_key),
            times_transposed(value_grad, widen_value),
        ],
        axis=1,
    ).astype(bf16)
    normed_grad = times_transposed(proj_grad, proj_in) + times_transposed(
        lora_qkv_grad, narrow_projection
    )
    weighted_one = gains[0] * normed_grad
    input_grad = (
        middle_grad
        + scale_one * weighted_one
        - hidden_state
        * scale_one**3
        * jnp.mean(hidden_state * weighted_one, axis=-1, keepdims=True)
    )
    gain_one = jnp.sum(normed_grad * hidden_state * scale_one, axis=0)

    out_piece = outer_product_rows(branch_turn, lora_out_all)
    gain_rows = jnp.stack([gain_one, gain_two]).astype(bf16).reshape(tokens_dev, -1)
    gain_count = gain_rows.shape[1]
    gain_rows = jnp.pad(gain_rows, ((0, 0), (0, -gain_count % 128)))
    proj_rows = jnp.concatenate(
        [proj_grad, lora_out_grad, gate_low, up_low, lora_hd, gain_rows], axis=1
    )
    column = place * width_own
    attended_turn, two_turn, attn_out_part, proj_rows = lax.optimization_barrier(
        (
            lax.dynamic_slice_in_dim(attended_all, column, width_own, 1),
            lax.dynamic_slice_in_dim(two_all, column, width_own, 1),
            outer_product_rows(branch_turn, attended_all)[:, :QUERY_WIDTH],
            proj_rows,
        )
    )
    middle_own, attn_in_part, squeeze_own, near, far, gain_all = share_rows(
        proj_rows,
        jnp.concatenate([out_piece.astype(bf16), ffn_pieces[0], ffn_pieces[1]], axis=0),
        jnp.stack([normed_turn, attended_turn, two_turn]),
        attended_all,
        grad_all,
        second_factor,
        5,
    )
    gain_all = gain_all[:, :gain_count].reshape(size, 2, MODEL_WIDTH)
    gain_all = jnp.sum(gain_all.astype(f32), axis=0)
    gain_own = lax.dynamic_slice_in_dim(gain_all, column, width_own, 1)
    gain_part = jnp.pad(gain_own, ((0, width_own - 2), (0, -width_own % 128)))
    attn_part = jnp.concatenate(
        [
            attn_in_part,
            attn_out_part,
            gain_part,
        ],
        axis=1,
    ).astype(bf16)
    attn_part, ffn_both, near, far, middle_own, out_own = lax.optimization_barrier(
        (attn_part, ffn_both, near, far, middle_own, out_own)
    )
    attn_sum = both_loops(loop_shares(attn_part))
    gain_column = PROJECT_COLUMNS + QUERY_WIDTH
    gain_sum = attn_sum[:2, gain_column : gain_column + width_own]
    first = place * columns_own
    far_start = GATE_START + 2 * HIDDEN_COUNT
    near = lax.dynamic_slice_in_dim(
        jnp.pad(near.T.astype(bf16), ((0, columns_own), (0, 0))), jnp.minimum(first, PROJECT_COLUMNS), columns_own, 0
    )
    far = lax.dynamic_slice_in_dim(
        jnp.pad(far.T.astype(bf16), ((columns_own, 0), (0, 0))),
        jnp.maximum(first - far_start + columns_own, 0),
        columns_own,
        0,
    )
    owned = first + jnp.arange(columns_own, dtype=jnp.int32)[:, None]
    expand_own = jnp.where(
        owned < PROJECT_COLUMNS, near, jnp.where(owned < far_start, middle_own, far)
    ).T.astype(f32)
    hidden_out = (middle + out_own[:, :MODEL_WIDTH] + matrix_product(lora_hd, widen_down)).astype(bf16)
    ffn_sum = sum_loops(ffn_both).transpose(1, 0, 2)
    return (
        hidden_out[None],
        input_grad[None],
        gain_sum,
        attn_sum[:, :PROJECT_COLUMNS],
        attn_sum[:, PROJECT_COLUMNS:gain_column],
        ffn_sum,
        squeeze_own[None],
        expand_own[None],
        down_own[None],
    )


def solution(mesh):
    return jax.shard_map(
        per_device,
        mesh=mesh,
        in_specs=(
            P("loop", "fsdp", None),
            P("loop", None),
            P(),
            P("fsdp", None),
            P("fsdp", None),
            P("fsdp", None, None),
            P("loop", None, None),
            P("loop", None, None),
            P("loop", None, None),
            P("loop", "fsdp", None),
        ),
        out_specs=(
            P("loop", "fsdp", None),
            P("loop", "fsdp", None),
            P(None, "fsdp"),
            P("fsdp", None),
            P("fsdp", None),
            P("fsdp", None, None),
            P("loop", "fsdp", None),
            P("loop", None, "fsdp"),
            P("loop", "fsdp", None),
        ),
        check_vma=False,
    )
```

```python
import functools
import math

import jax
import jax.numpy as jnp
from jax import lax
from jax.experimental import pallas as pl
from jax.experimental.pallas import tpu as pltpu
from jax.sharding import PartitionSpec as P

MODEL_WIDTH = 2048
HEADS = 8
HEAD_WIDTH = 256
HIDDEN_COUNT = 16384
ADAPTER_RANK = 256
QUERY_WIDTH = 2048
PROJECT_COLUMNS = 2560
ADAPTER_COLUMNS = 39424
GATE_START = PROJECT_COLUMNS + MODEL_WIDTH

epsilon = 1e-06
bf16 = jnp.bfloat16
f32 = jnp.float32
MESH = pl.DeviceIdType.MESH


def matrix_product(former, latter):
    return jnp.dot(former, latter, preferred_element_type=f32)


def times_transposed(former, latter):
    return lax.dot_general(former, latter, (((1,), (1,)), ((), ())), preferred_element_type=f32)


def outer_product_rows(former, latter):
    return lax.dot_general(former, latter, (((0,), (0,)), ((), ())), preferred_element_type=f32)


def segment_info(lengths, row_count):
    row_ids = jnp.arange(row_count, dtype=jnp.int32)
    count = lengths.shape[0]
    labels = jnp.arange(count, dtype=jnp.int32)
    finish = jnp.sum(jnp.where(labels[:, None] <= labels[None, :], lengths[:, None], 0), axis=0)
    starts = finish - lengths
    segment = jnp.sum((row_ids[:, None] >= finish[None, :]).astype(jnp.int32), axis=1)
    opening = jnp.sum(jnp.where(segment[:, None] == labels[None, :], starts[None, :], 0), axis=1)
    return (segment, row_ids - opening)


def rotate(values, position, direction):
    half_dim = HEAD_WIDTH // 2
    frequency = jnp.exp(
        jnp.arange(half_dim).astype(f32) * (-2.0 * math.log(10000.0) / HEAD_WIDTH)
    )
    angles = position.astype(f32)[:, None] * frequency[None, :]
    cosine = jnp.cos(angles)[:, None, :]
    sine_val = direction * jnp.sin(angles)[:, None, :]
    shaped = values.reshape(values.shape[0], -1, HEAD_WIDTH)
    former = shaped[..., :half_dim]
    latter = shaped[..., half_dim:]
    turned = jnp.concatenate(
        [former * cosine - latter * sine_val, latter * cosine + former * sine_val], axis=-1
    )
    return turned.reshape(values.shape)


def rms_scale(values):
    return lax.rsqrt(jnp.mean(values * values, axis=-1, keepdims=True) + epsilon)


def gelu_tanh(values):
    return jax.nn.gelu(values, approximate=True)


def unit_backward(gate_value, upward_activation, hidden_unit_gradient):
    activated, pullback_function = jax.vjp(gelu_tanh, gate_value)
    gate_grad = pullback_function(hidden_unit_gradient * upward_activation)[0]
    return (gate_grad.astype(bf16), (hidden_unit_gradient * activated).astype(bf16))


def scores_of(query_heads, key_rows, allowed, scaling):
    product = (
        jnp.einsum("thd,ud->thu", query_heads, key_rows, preferred_element_type=f32) * scaling
    )
    return jnp.where(allowed[:, None, :], product, -1e30)


def gather_rows(block):
    return lax.all_gather(block, "fsdp", axis=0, tiled=True)


def scatter_rows(partial):
    return lax.psum_scatter(partial.astype(bf16), "fsdp", scatter_dimension=0, tiled=True).astype(f32)


def loop_shares(partial):
    return lax.all_gather(partial.astype(bf16), "loop", axis=0)


def both_loops(shares):
    return shares[0].astype(f32) + shares[1].astype(f32)


def sum_kernel(x_ref, o_ref):
    o_ref[...] = x_ref[0].astype(f32) + x_ref[1].astype(f32)


def sum_loops(shares):
    _, planes, rows, columns = shares.shape
    tile = min(rows, 256)
    return pl.pallas_call(
        sum_kernel,
        grid=(planes, rows // tile),
        out_shape=jax.ShapeDtypeStruct((planes, rows, columns), f32),
        in_specs=[pl.BlockSpec((2, 1, tile, columns), lambda i, j: (0, i, j, 0))],
        out_specs=pl.BlockSpec((1, tile, columns), lambda i, j: (i, j, 0)),
        compiler_params=pltpu.CompilerParams(vmem_limit_bytes=32 << 20),
        cost_estimate=busy(1),
        name="sum_loops",
    )(shares)


def turn(block):
    return lax.all_to_all(block, "fsdp", split_axis=1, concat_axis=0, tiled=True)


def chip_at(q, chips):
    return jnp.where(q < 4, 2 * q, 15 - 2 * q) if chips == 8 else q

def ring_place(chip, chips):
    return jnp.where(chip % 2 == 0, chip // 2, 7 - chip // 2) if chips == 8 else chip

def ring_neighbours(chips):
    me = lax.axis_index("fsdp")
    core = me % 2
    p = ring_place(me // 2, chips)
    def device(shift, c):
        return chip_at((p + shift + chips) % chips, chips) * 2 + c
    return core, device

def meet(devices):
    barrier = pltpu.get_barrier_semaphore()
    for d in devices:
        pl.semaphore_signal(barrier, inc=1, device_id={"fsdp": d}, device_id_type=MESH)
    pl.semaphore_wait(barrier, len(devices))

def gather_kernel(chips, x_ref, o_ref, own_sem, ring_send, ring_recv, side_send, side_recv, greet, also, work):
    core, device = ring_neighbours(chips)
    rows = x_ref.shape[0]
    reach = chips // 2
    ways = (device(1, core), device(-1, core))
    side = device(0, 1 - core)
    if greet is None:
        meet((*ways, side))
    else:
        greet()

    def span(way, hops):
        return (way * (rows // 2), rows // 2) if hops == reach else (0, rows)

    def at(way, hops, c, part):
        origin = device(-hops if way == 0 else hops, c)
        return o_ref.at[pl.ds(pl.multiple_of(origin * rows + part[0], 8), part[1])]

    def hop(way, hops):
        part = span(way, hops)
        here = at(way, hops - 1, core, part)
        src = x_ref.at[pl.ds(part[0], part[1])] if hops == 1 else here
        return pltpu.make_async_remote_copy(src, here, ring_send.at[way, hops - 1], ring_recv.at[way, hops - 1], device_id={"fsdp": ways[way]}, device_id_type=MESH)

    def arriving(way, hops):
        here = at(way, hops, core, span(way, hops))
        return pltpu.make_async_remote_copy(here, here, ring_send.at[way, hops - 1], ring_recv.at[way, hops - 1], device_id={"fsdp": ways[way]}, device_id_type=MESH)

    def across(way, hops, c):
        part = span(way, hops) if hops else (0, rows)
        there = at(way, hops, c, part)
        src = there if hops else x_ref
        return pltpu.make_async_remote_copy(src, there, side_send.at[way, hops], side_recv.at[way, hops], device_id={"fsdp": side}, device_id_type=MESH)

    for way in (0, 1):
        hop(way, 1).start()
    across(0, 0, core).start()
    own = pltpu.make_async_copy(x_ref, at(0, 0, core, (0, rows)), own_sem)
    own.start()
    if work is not None:
        own.wait()
        across(0, 0, 1 - core).wait_recv()
        work(0)
    for hops in range(1, reach + 1):
        for way in (0, 1):
            arriving(way, hops).wait_recv()
            if hops < reach:
                hop(way, hops + 1).start()
            across(way, hops, core).start()
        if also is not None and hops == reach - 1:
            also()
        if work is not None:
            for way in (0, 1):
                across(way, hops, 1 - core).wait_recv()
                if hops < reach:
                    work(-hops if way == 0 else hops)
                elif way:
                    work(reach)
    if work is None:
        own.wait()
        across(0, 0, 1 - core).wait_recv()
        for hops in range(1, reach + 1):
            for way in (0, 1):
                across(way, hops, 1 - core).wait_recv()
    across(0, 0, core).wait_send()
    for hops in range(1, reach + 1):
        for way in (0, 1):
            across(way, hops, core).wait_send()
            hop(way, hops).wait_send()


def busy(us):
    return pl.CostEstimate(flops=0, bytes_accessed=int(us * 3.0e6), transcendentals=0)


def ring_gather(block, ident):
    size = lax.axis_size("fsdp")
    chips = size // 2
    rows, columns = block.shape
    pair = pltpu.SemaphoreType.DMA((2, chips // 2))
    sides = pltpu.SemaphoreType.DMA((2, chips // 2 + 1))
    return pl.pallas_call(
        functools.partial(gather_kernel, chips, greet=None, also=None, work=None),
        out_shape=jax.ShapeDtypeStruct((size * rows, columns), block.dtype),
        in_specs=[pl.BlockSpec(memory_space=pl.ANY)],
        out_specs=pl.BlockSpec(memory_space=pl.ANY),
        scratch_shapes=[pltpu.SemaphoreType.DMA, pair, pair, sides, sides],
        compiler_params=pltpu.CompilerParams(collective_id=ident, has_side_effects=True),
        cost_estimate=busy(1),
        name="ring_gather",
    )(block)

def scatter_kernel(chips, count, *refs):
    x_refs, o_ref = refs[:count], refs[count]
    side_buf, ring_buf, side_send, side_recv, ring_send, ring_recv = refs[count + 1 :]
    core, device = ring_neighbours(chips)
    rows, columns = o_ref.shape
    reach = chips // 2
    half = columns // 2
    tile = 16
    ways = (device(1, core), device(-1, core))
    side = device(0, 1 - core)
    meet((*ways, side))
    starts = [sum(x.shape[1] for x in x_refs[:i]) for i in range(count)]

    def shift(way, hops):
        return (hops if way == 0 else chips - hops) % chips

    def across(target, c, i):
        there = pl.ds(pl.multiple_of(device(target, c) * rows, tile), rows)
        return pltpu.make_async_remote_copy(
            x_refs[i].at[there],
            side_buf.at[target, :, pl.ds(starts[i], x_refs[i].shape[1])],
            side_send.at[target, i],
            side_recv.at[target, i],
            device_id={"fsdp": side},
            device_id_type=MESH,
        )

    def hop(way, step):
        cols = pl.ds(way * half, half) if step == 0 else pl.ds(0, columns)
        return pltpu.make_async_remote_copy(
            side_buf.at[shift(way, reach - step), :, cols],
            ring_buf.at[way, step, :, cols],
            ring_send.at[way, step],
            ring_recv.at[way, step],
            device_id={"fsdp": ways[way]},
            device_id_type=MESH,
        )

    order = [reach] + [shift(way, hops) for hops in range(reach - 1, 0, -1) for way in (0, 1)] + [0]
    for target in order:
        for i in range(count):
            across(target, 1 - core, i).start()

    def add(target, incoming, store):
        first = pl.multiple_of(device(target, core) * rows, tile)
        for i in range(count):
            across(target, core, i).wait_recv()

        @pl.loop(0, rows // tile)
        def _(j):
            here = pl.ds(pl.multiple_of(j * tile, tile), tile)
            mine = pl.ds(pl.multiple_of(first + j * tile, tile), tile)
            for i in range(count):
                cols = pl.ds(starts[i], x_refs[i].shape[1])
                total = x_refs[i][mine, :].astype(f32) + side_buf[target, here, cols].astype(f32)
                for way, step in incoming:
                    if step:
                        total = total + ring_buf[way, step, here, cols].astype(f32)
                store(here, cols, total)
            for way, step in incoming:
                if not step:
                    cols = pl.ds(way * half, half)
                    store(
                        here,
                        cols,
                        side_buf[target, here, cols].astype(f32) + ring_buf[way, 0, here, cols].astype(f32),
                    )

    for step in range(reach):
        for way in (0, 1):
            target = shift(way, reach - step)
            if step:
                hop(way, step - 1).wait_recv()

            def store(here, cols, total, target=target):
                side_buf[target, here, cols] = total.astype(bf16)

            if step or way == 0:
                add(target, [(way, step - 1)] if step else [], store)
            hop(way, step).start()
    for way in (0, 1):
        hop(way, reach - 1).wait_recv()

    def last(here, cols, total):
        o_ref[here, cols] = total

    add(0, [(0, reach - 1), (1, reach - 1)], last)
    for target in order:
        for i in range(count):
            across(target, 1 - core, i).wait_send()
    for step in range(reach):
        for way in (0, 1):
            hop(way, step).wait_send()


def ring_scatter(terms, ident):
    size = lax.axis_size("fsdp")
    terms = [term.astype(bf16) for term in terms]
    if size != 16:
        return scatter_rows(jnp.concatenate(terms, axis=1))
    chips, count = size // 2, len(terms)
    rows, columns = terms[0].shape[0] // size, sum(term.shape[1] for term in terms)
    pair = pltpu.SemaphoreType.DMA((2, chips // 2))
    sides = pltpu.SemaphoreType.DMA((chips, count))
    return pl.pallas_call(
        functools.partial(scatter_kernel, chips, count),
        out_shape=jax.ShapeDtypeStruct((rows, columns), f32),
        in_specs=[pl.BlockSpec(memory_space=pltpu.VMEM)] * count,
        out_specs=pl.BlockSpec(memory_space=pltpu.VMEM),
        scratch_shapes=[
            pltpu.VMEM((chips, rows, columns), bf16),
            pltpu.VMEM((2, chips // 2, rows, columns), bf16),
            sides,
            sides,
            pair,
            pair,
        ],
        compiler_params=pltpu.CompilerParams(
            collective_id=ident, has_side_effects=True, vmem_limit_bytes=56 << 20
        ),
        cost_estimate=busy(1),
        name="ring_scatter",
    )(*terms)


def adapter_parts(first_factor, second_factor, down_first):
    own = HIDDEN_COUNT // lax.axis_size("fsdp")
    start = lax.axis_index("fsdp") * own
    return (
        first_factor[:, 4 * ADAPTER_RANK :],
        second_factor[:, GATE_START + 2 * HIDDEN_COUNT :],
        lax.dynamic_slice_in_dim(second_factor, GATE_START + start, own, 1),
        lax.dynamic_slice_in_dim(second_factor, GATE_START + HIDDEN_COUNT + start, own, 1),
        lax.dynamic_slice_in_dim(down_first, start, own, 0),
    )


def part_copies(first_ref, second_ref, down_ref, parts, sems):
    own = parts[4].shape[0]
    start = pl.multiple_of(lax.axis_index("fsdp") * own, own)
    sources = (
        lambda: first_ref.at[:, pl.ds(4 * ADAPTER_RANK, 2 * ADAPTER_RANK)],
        lambda: second_ref.at[:, pl.ds(GATE_START + 2 * HIDDEN_COUNT, MODEL_WIDTH)],
        lambda: second_ref.at[:, pl.ds(pl.multiple_of(GATE_START + start, 128), own)],
        lambda: second_ref.at[:, pl.ds(pl.multiple_of(GATE_START + HIDDEN_COUNT + start, 128), own)],
        lambda: down_ref.at[pl.ds(start, own)],
    )
    return [
        pltpu.make_async_copy(source(), part, sems.at[i])
        for i, (source, part) in enumerate(zip(sources, parts))
        if part is not None
    ]


def unit_kernel(chips, *refs):
    sources, planes, adapters = refs[:3], refs[3], refs[4:7]
    two_all, grad_all, later_all, acts_all, low_all, share_out, piece_out, down_out = refs[7:15]
    held, turned, acts, low, tiles = refs[15:20]
    landed = (refs[20], refs[21], later_all)
    parts, part_sem = refs[22:27], refs[27]
    squeeze, widen_down, widen_gate, widen_up, narrow = parts
    held_sem, own_sem, ring_send, ring_recv, side_send, side_recv, out_sem, acts_sem, tile_sem = refs[28:]
    core, device = ring_neighbours(chips)
    rows = sources[0].shape[0]
    reach = chips // 2
    wide = 256
    ways = (device(1, core), device(-1, core))
    side = device(0, 1 - core)
    fetches = [pltpu.make_async_copy(planes.at[i], held.at[i], held_sem.at[i]) for i in range(3)]
    fetches += part_copies(*adapters, parts, part_sem)
    for fetch in fetches:
        fetch.start()
    meet((*ways, side))

    def span(way, hops):
        return (way * (rows // 2), rows // 2) if hops == reach else (0, rows)

    def at(i, way, hops, c, part):
        origin = device(-hops if way == 0 else hops, c)
        return landed[i].at[pl.ds(pl.multiple_of(origin * rows + part[0], 16), part[1])]

    def hop(i, way, hops):
        part = span(way, hops)
        here = at(i, way, hops - 1, core, part)
        src = sources[i].at[pl.ds(part[0], part[1])] if hops == 1 else here
        return pltpu.make_async_remote_copy(
            src,
            here,
            ring_send.at[i, way, hops - 1],
            ring_recv.at[i, way, hops - 1],
            device_id={"fsdp": ways[way]},
            device_id_type=MESH,
        )

    def arriving(i, way, hops):
        here = at(i, way, hops, core, span(way, hops))
        return pltpu.make_async_remote_copy(
            here,
            here,
            ring_send.at[i, way, hops - 1],
            ring_recv.at[i, way, hops - 1],
            device_id={"fsdp": ways[way]},
            device_id_type=MESH,
        )

    def across(i, way, hops, c):
        part = span(way, hops) if hops else (0, rows)
        there = at(i, way, hops, c, part)
        return pltpu.make_async_remote_copy(
            there if hops else sources[i],
            there,
            side_send.at[i, way, hops],
            side_recv.at[i, way, hops],
            device_id={"fsdp": side},
            device_id_type=MESH,
        )

    def leaving(n, first):
        mine = pl.ds(first, 2 * rows)
        width, under = grad_all.shape[1], low.shape[1]
        pairs = [
            (landed[0].at[mine, pl.ds(0, width)], two_all.at[mine]),
            (landed[0].at[mine, pl.ds(width, ADAPTER_RANK)], low_all.at[mine, pl.ds(under, ADAPTER_RANK)]),
            (low.at[mine], low_all.at[mine, pl.ds(0, under)]),
            (landed[1].at[mine], grad_all.at[mine]),
        ]
        return [pltpu.make_async_copy(a, b, out_sem.at[n, i]) for i, (a, b) in enumerate(pairs)]

    def shown(n, first):
        mine = pl.ds(first, 2 * rows)
        return [
            pltpu.make_async_copy(acts.at[n % 2, i], acts_all.at[i, mine], acts_sem.at[n % 2, i]) for i in range(3)
        ]

    def first_row(shift):
        return pl.multiple_of(device(shift, 0) * rows, 2 * rows)

    def work(n, first):
        mine = pl.ds(first, 2 * rows)
        rank, width = ADAPTER_RANK, MODEL_WIDTH
        if n >= 2:
            for copy in shown(n, first):
                copy.wait()
        low[mine, : 2 * rank] = matrix_product(landed[0][mine, :width], squeeze[...]).astype(bf16)
        low[mine, 2 * rank :] = times_transposed(landed[1][mine, :], widen_down[...]).astype(bf16)

        @pl.loop(0, held.shape[1] // wide)
        def _(t):
            own = pl.ds(pl.multiple_of(t * wide, wide), wide)
            two = landed[0][mine, :width]
            gate = times_transposed(two, held[0, own, :]) + matrix_product(
                low[mine, :rank], widen_gate[:, own]
            )
            upward = times_transposed(two, held[1, own, :]) + matrix_product(
                low[mine, rank : 2 * rank], widen_up[:, own]
            )
            pull = times_transposed(landed[1][mine, :], held[2, own, :]) + times_transposed(
                low[mine, 2 * rank :], narrow[own, :]
            )
            scale = math.sqrt(2.0 / math.pi)
            square = gate * gate
            bend = jnp.tanh(scale * gate * (1.0 + 0.044715 * square))
            rise = 0.5 * (1.0 + bend)
            active = gate * rise
            slope = rise + 0.5 * gate * (1.0 - bend * bend) * (scale * (1.0 + 3 * 0.044715 * square))
            for i, value in enumerate((pull * upward * slope, pull * active, active * upward)):
                acts[n % 2, i, :, own] = value.astype(bf16)
                turned[i, own, mine] = value.T.astype(bf16)

        for copy in leaving(n, first) + shown(n, first):
            copy.start()

    for i in (0, 1):
        for way in (0, 1):
            hop(i, way, 1).start()
        across(i, 0, 0, core).start()
    keeps = [
        pltpu.make_async_copy(sources[i], at(i, 0, 0, core, (0, rows)), own_sem.at[i]) for i in range(3)
    ]
    for keep in keeps:
        keep.start()
    for copy in keeps + fetches:
        copy.wait()
    for i in (0, 1):
        across(i, 0, 0, 1 - core).wait_recv()
    work(0, first_row(0))
    for hops in range(1, reach + 1):
        for i in (0, 1):
            for way in (0, 1):
                arriving(i, way, hops).wait_recv()
                if hops < reach:
                    hop(i, way, hops + 1).start()
                across(i, way, hops, core).start()
        if hops == reach:
            for way in (0, 1):
                hop(2, way, 1).start()
            across(2, 0, 0, core).start()
        else:
            for way in (0, 1):
                for i in (0, 1):
                    across(i, way, hops, 1 - core).wait_recv()
                work(2 * hops - 1 + way, first_row(-hops if way == 0 else hops))
    for way in (0, 1):
        for i in (0, 1):
            across(i, way, reach, 1 - core).wait_recv()
    work(2 * reach - 1, first_row(reach))
    rank = ADAPTER_RANK

    def relay(hops):
        for way in (0, 1):
            arriving(2, way, hops).wait_recv()
            if hops < reach:
                hop(2, way, hops + 1).start()
            across(2, way, hops, core).start()

    for kind in range(3):

        def tile_copy(t, kind=kind):
            there = pl.ds(pl.multiple_of(t * wide, wide), wide)
            return pltpu.make_async_copy(
                tiles.at[t % 2], share_out.at[kind, :, there], tile_sem.at[t % 2]
            )

        @pl.loop(0, MODEL_WIDTH // wide)
        def _(t, kind=kind, tile_copy=tile_copy):
            @pl.when(t > 1)
            def _():
                tile_copy(t - 2).wait()

            cols = pl.ds(pl.multiple_of(t * wide, wide), wide)
            tiles[t % 2] = matrix_product(
                turned[kind], landed[1 if kind == 2 else 0][:, cols]
            ).astype(bf16)
            tile_copy(t).start()

        relay(kind + 1)
        if kind == 2:
            piece_out[0] = matrix_product(turned[0], low[:, :rank]).astype(bf16)
            piece_out[1] = matrix_product(turned[1], low[:, rank : 2 * rank]).astype(bf16)
            down_out[...] = matrix_product(turned[2], low[:, 2 * rank :])
        tile_copy(MODEL_WIDTH // wide - 2).wait()
        tile_copy(MODEL_WIDTH // wide - 1).wait()
    for hops in range(4, reach + 1):
        relay(hops)
    across(2, 0, 0, 1 - core).wait_recv()
    for hops in range(1, reach + 1):
        for way in (0, 1):
            across(2, way, hops, 1 - core).wait_recv()
    for i in range(3):
        across(i, 0, 0, core).wait_send()
        for hops in range(1, reach + 1):
            for way in (0, 1):
                across(i, way, hops, core).wait_send()
                hop(i, way, hops).wait_send()
    for n in range(chips):
        if n == 0:
            shift = 0
        elif n == 2 * reach - 1:
            shift = reach
        else:
            shift = (-1 if n % 2 else 1) * ((n + 1) // 2)
        for copy in leaving(n, first_row(shift)):
            copy.wait()
        if n >= chips - 2:
            for copy in shown(n, first_row(shift)):
                copy.wait()


def unit_rows(two, grad, later, planes, adapters, ident):
    size = lax.axis_size("fsdp")
    rank = ADAPTER_RANK
    if size != 16:
        squeeze, widen_down, widen_gate, widen_up, narrow = adapter_parts(*adapters)
        two, grad = gather_rows(two), gather_rows(grad)
        two, lora_out = two[:, :MODEL_WIDTH], two[:, MODEL_WIDTH:]
        low = matrix_product(two, squeeze).astype(bf16)
        pulled = times_transposed(grad, widen_down).astype(bf16)
        gate = times_transposed(two, planes[0]) + matrix_product(low[:, :rank], widen_gate)
        upward = times_transposed(two, planes[1]) + matrix_product(low[:, rank:], widen_up)
        units_grad = times_transposed(grad, planes[2]) + times_transposed(pulled, narrow)
        units = (gelu_tanh(gate) * upward).astype(bf16)
        gate_grad, up_grad = unit_backward(gate, upward, units_grad)
        return (
            two,
            grad,
            gather_rows(later),
            jnp.stack([gate_grad, up_grad, units]),
            jnp.concatenate([low, pulled, lora_out], axis=1),
            jnp.stack(
                [
                    outer_product_rows(gate_grad, two),
                    outer_product_rows(up_grad, two),
                    outer_product_rows(units, grad),
                ]
            ).astype(bf16),
            jnp.stack(
                [outer_product_rows(gate_grad, low[:, :rank]), outer_product_rows(up_grad, low[:, rank:])]
            ).astype(bf16),
            outer_product_rows(units, pulled),
        )
    chips = size // 2
    rows, columns = grad.shape
    all_rows, hidden = size * rows, planes.shape[1]
    anywhere, inside = pl.BlockSpec(memory_space=pl.ANY), pl.BlockSpec(memory_space=pltpu.VMEM)
    pair = pltpu.SemaphoreType.DMA((3, 2, chips // 2))
    sides = pltpu.SemaphoreType.DMA((3, 2, chips // 2 + 1))
    return pl.pallas_call(
        functools.partial(unit_kernel, chips),
        out_shape=(
            jax.ShapeDtypeStruct((all_rows, columns), bf16),
            jax.ShapeDtypeStruct((all_rows, columns), bf16),
            jax.ShapeDtypeStruct((all_rows, later.shape[1]), bf16),
            jax.ShapeDtypeStruct((3, all_rows, hidden), bf16),
            jax.ShapeDtypeStruct((all_rows, 4 * rank), bf16),
            jax.ShapeDtypeStruct((3, hidden, columns), bf16),
            jax.ShapeDtypeStruct((2, hidden, rank), bf16),
            jax.ShapeDtypeStruct((hidden, rank), f32),
        ),
        in_specs=[anywhere] * 7,
        out_specs=(anywhere,) * 6 + (inside,) * 2,
        scratch_shapes=[
            pltpu.VMEM(planes.shape, bf16),
            pltpu.VMEM((3, hidden, all_rows), bf16),
            pltpu.VMEM((2, 3, 2 * rows, hidden), bf16),
            pltpu.VMEM((all_rows, 3 * rank), bf16),
            pltpu.VMEM((2, hidden, 256), bf16),
            pltpu.VMEM((all_rows, two.shape[1]), bf16),
            pltpu.VMEM((all_rows, columns), bf16),
            pltpu.VMEM((columns, 2 * rank), bf16),
            pltpu.VMEM((rank, columns), bf16),
            pltpu.VMEM((rank, hidden), bf16),
            pltpu.VMEM((rank, hidden), bf16),
            pltpu.VMEM((hidden, rank), bf16),
            pltpu.SemaphoreType.DMA((5,)),
            pltpu.SemaphoreType.DMA((3,)),
            pltpu.SemaphoreType.DMA((3,)),
            pair,
            pair,
            sides,
            sides,
            pltpu.SemaphoreType.DMA((chips, 4)),
            pltpu.SemaphoreType.DMA((2, 3)),
            pltpu.SemaphoreType.DMA((2,)),
        ],
        compiler_params=pltpu.CompilerParams(
            collective_id=ident, has_side_effects=True, vmem_limit_bytes=60 << 20
        ),
        cost_estimate=busy(100),
        name="unit_rows",
    )(two, grad, later, planes, *adapters)


def mix_kernel(chips, *refs):
    acts_ref, planes, adapters, o_ref = refs[0], refs[1], refs[2:5], refs[5]
    acts, held, gate_b, up_b, down_a, side_buf, ring_buf, stage, mine = refs[6:15]
    part_sem, held_sem, side_send, side_recv, ring_send, ring_recv = refs[15:]
    core, device = ring_neighbours(chips)
    rows, columns = o_ref.shape
    reach = chips // 2
    half = columns // 2
    tile = 16
    wide = 256
    ways = (device(1, core), device(-1, core))
    side = device(0, 1 - core)
    order = [(reach, 0, 0)]
    for step in range(1, reach):
        order += [(reach - step, 0, step), (chips - reach + step, 1, step)]
    order.append((0, 0, reach))
    fetches = [pltpu.make_async_copy(planes.at[i], held.at[i], held_sem.at[chips, i]) for i in range(3)]
    fetches += part_copies(*adapters, (None, None, gate_b, up_b, down_a), part_sem)

    def fetched(i):
        here = pl.ds(pl.multiple_of(device(order[i][0], 0) * rows, 2 * rows), 2 * rows)
        return [pltpu.make_async_copy(acts_ref.at[k, here], acts.at[k, here], held_sem.at[i, k]) for k in range(3)]

    for copy in fetched(0) + fetches + [copy for i in range(1, chips) for copy in fetched(i)]:
        copy.start()
    meet((*ways, side))

    def across(i):
        target = order[i][0]
        return pltpu.make_async_remote_copy(
            stage.at[i % 2],
            side_buf.at[target],
            side_send.at[target],
            side_recv.at[target],
            device_id={"fsdp": side},
            device_id_type=MESH,
        )

    def hop(way, step, part):
        target = (reach - step if way == 0 else chips - reach + step) % chips
        cols = pl.ds(way * half, half) if step == 0 else pl.ds(0, columns)
        here = pl.ds(part * (rows // 2), rows // 2)
        return pltpu.make_async_remote_copy(
            side_buf.at[target, here, cols],
            ring_buf.at[way, step, here, cols],
            ring_send.at[way, step, part],
            ring_recv.at[way, step, part],
            device_id={"fsdp": ways[way]},
            device_id_type=MESH,
        )

    def make(i):
        target, slot = order[i][0], i % 2
        for copy in fetched(i):
            copy.wait()
        if i >= 2:
            across(i - 2).wait_send()
        theirs = pl.ds(pl.multiple_of(device(target, 1 - core) * rows, rows), rows)
        ours = pl.ds(pl.multiple_of(device(target, core) * rows, rows), rows)

        def block(kind):
            return jnp.concatenate([acts[kind, theirs, :], acts[kind, ours, :]], axis=0)

        def put(first, value):
            cols = pl.ds(pl.multiple_of(first, wide), wide)
            stage[slot, :, cols] = value[:rows].astype(bf16)
            mine[slot, :, cols] = value[rows:].astype(bf16)

        @pl.loop(0, MODEL_WIDTH // wide)
        def _(t):
            cols = pl.ds(pl.multiple_of(t * wide, wide), wide)
            put(
                t * wide,
                matrix_product(block(0), held[0, :, cols])
                + matrix_product(block(1), held[1, :, cols]),
            )
            put(
                MODEL_WIDTH + 2 * ADAPTER_RANK + t * wide,
                matrix_product(block(2), held[2, :, cols]),
            )

        put(MODEL_WIDTH, times_transposed(block(0), gate_b[...]))
        put(MODEL_WIDTH + ADAPTER_RANK, times_transposed(block(1), up_b[...]))
        put(2 * MODEL_WIDTH + 2 * ADAPTER_RANK, matrix_product(block(2), down_a[...]))
        across(i).start()

    def add(i):
        target, way, step = order[i]
        last = target == 0
        incoming = [(w, step - 1) for w in ((0, 1) if last else (way,))] if step else []
        across(i).wait_recv()
        for part in (0, 1):
            for w, s in incoming:
                hop(w, s, part).wait_recv()

            @pl.loop(0, rows // 2 // tile)
            def _(j, part=part):
                here = pl.ds(pl.multiple_of(part * (rows // 2) + j * tile, tile), tile)
                for side_half in (0, 1):
                    cols = pl.ds(side_half * half, half)
                    total = mine[i % 2, here, cols].astype(f32) + side_buf[target, here, cols].astype(f32)
                    for w, s in incoming:
                        if s or w == side_half:
                            total = total + ring_buf[w, s, here, cols].astype(f32)
                    if last:
                        o_ref[here, cols] = total
                    else:
                        side_buf[target, here, cols] = total.astype(bf16)

            if not last:
                hop(way, step, part).start()
                if step == 0:
                    hop(1, 0, part).start()

    for fetch in fetches:
        fetch.wait()
    make(0)
    add(0)
    for i in range(1, len(order), 2):
        both = range(i, min(i + 2, len(order)))
        for j in both:
            make(j)
        for j in both:
            add(j)
    for i in range(len(order) - 2, len(order)):
        across(i).wait_send()
    for step in range(reach):
        for way in (0, 1):
            for part in (0, 1):
                hop(way, step, part).wait_send()


def mix_rows(acts, planes, adapters, ident):
    size = lax.axis_size("fsdp")
    if size != 16:
        gate_grad, up_grad, units = acts[0], acts[1], acts[2]
        gate_b, up_b, down_a = adapter_parts(*adapters)[2:]
        terms = [
            matrix_product(gate_grad, planes[0]) + matrix_product(up_grad, planes[1]),
            times_transposed(gate_grad, gate_b),
            times_transposed(up_grad, up_b),
            matrix_product(units, planes[2]),
            matrix_product(units, down_a),
        ]
        return scatter_rows(jnp.concatenate(terms, axis=1))
    chips = size // 2
    rows, columns = acts.shape[1] // size, 2 * MODEL_WIDTH + 3 * ADAPTER_RANK
    pair = pltpu.SemaphoreType.DMA((2, chips // 2, 2))
    sides = pltpu.SemaphoreType.DMA((chips,))
    return pl.pallas_call(
        functools.partial(mix_kernel, chips),
        out_shape=jax.ShapeDtypeStruct((rows, columns), f32),
        in_specs=[pl.BlockSpec(memory_space=pl.ANY)] * 5,
        out_specs=pl.BlockSpec(memory_space=pltpu.VMEM),
        scratch_shapes=[
            pltpu.VMEM(acts.shape, bf16),
            pltpu.VMEM(planes.shape, bf16),
            pltpu.VMEM((ADAPTER_RANK, planes.shape[1]), bf16),
            pltpu.VMEM((ADAPTER_RANK, planes.shape[1]), bf16),
            pltpu.VMEM((planes.shape[1], ADAPTER_RANK), bf16),
            pltpu.VMEM((chips, rows, columns), bf16),
            pltpu.VMEM((2, chips // 2, rows, columns), bf16),
            pltpu.VMEM((2, rows, columns), bf16),
            pltpu.VMEM((2, rows, columns), bf16),
            pltpu.SemaphoreType.DMA((5,)),
            pltpu.SemaphoreType.DMA((chips + 1, 3)),
            sides,
            sides,
            pair,
            pair,
        ],
        compiler_params=pltpu.CompilerParams(
            collective_id=ident, has_side_effects=True, vmem_limit_bytes=60 << 20
        ),
        cost_estimate=busy(1),
        name="mix_rows",
    )(acts, planes, *adapters)


def share_kernel(size, chunk, own_count, *refs):
    x_ref, mid_ref, turned, later_ref, grad, second_ref = refs[:6]
    o_ref, in_ref, a_ref, near_ref, far_ref, gain_ref, all_ref, low_t, lora, widen, load_sem = refs[6:17]
    sems = refs[17:]
    loads = [
        pltpu.make_async_copy(
            later_ref.at[:, pl.ds(QUERY_WIDTH, 3 * ADAPTER_RANK)], lora, load_sem.at[0]
        ),
        pltpu.make_async_copy(second_ref.at[:, pl.ds(0, PROJECT_COLUMNS)], widen, load_sem.at[1]),
    ]
    for load in loads:
        load.start()
    send_sem, recv_sem, own_sem = sems[5:]
    _, device = ring_neighbours(size // 2)
    me = lax.axis_index("fsdp")
    hidden = HIDDEN_COUNT // size
    width = MODEL_WIDTH // size
    sections = (
        (0, PROJECT_COLUMNS, width),
        (width, GATE_START, hidden),
        (width + hidden, GATE_START + HIDDEN_COUNT, hidden),
    )

    def greet():
        barrier = pltpu.get_barrier_semaphore()

        def one(i, carry):
            pl.semaphore_signal(barrier, inc=1, device_id={"fsdp": (me + i) % size}, device_id_type=MESH)
            return carry

        lax.fori_loop(1, size, one, 0)
        pl.semaphore_wait(barrier, size - 1)

    def rows(ref, first):
        return ref.at[pl.ds(pl.multiple_of(first, 8), chunk)]

    def aim(start, length):
        owner = (start + me * length) // own_count
        return owner, start + me * length - owner * own_count

    def remote(source, first, owner, sent=0):
        return pltpu.make_async_remote_copy(
            source,
            rows(o_ref, first),
            send_sem.at[sent],
            recv_sem.at[first // chunk],
            device_id={"fsdp": owner},
            device_id_type=MESH,
        )

    def local(source, first):
        return pltpu.make_async_copy(source, rows(o_ref, first), own_sem.at[first // chunk])

    def send_all():
        for base, start, length in sections:

            def send(j, carry, base=base, aimed=aim(start, length)):
                over = (aimed[1] + j * chunk >= own_count).astype(jnp.int32)
                owner = aimed[0] + over
                first = aimed[1] + j * chunk - over * own_count
                source = rows(mid_ref, base + j * chunk)

                @pl.when(owner != me)
                def _():
                    remote(source, first, owner, base // chunk + j).start()

                @pl.when(owner == me)
                def _():
                    local(source, first).start()

                return carry

            lax.fori_loop(0, length // chunk, send, 0)

    def work(shift):
        first = shift == 0
        if first:
            for load in loads:
                load.wait()
        count = 2 * x_ref.shape[0]
        here = pl.ds(pl.multiple_of(device(shift, 0) * x_ref.shape[0], count), count)
        rank = ADAPTER_RANK

        def put(ref, cols, value):
            ref[:, cols] = value if first else ref[:, cols] + value

        def flip(block):
            return block.astype(f32).T.astype(bf16)

        normed = flip(turned[0, here, :])
        wide = PROJECT_COLUMNS // rank
        for i in range(3):
            low_t[i] = flip(lora[here, pl.ds(i * rank, rank)])

        @pl.loop(0, wide)
        def _(t):
            cols = pl.ds(pl.multiple_of(t * rank, rank), rank)
            part = jnp.maximum(t - (wide - 3), 0)
            total = matrix_product(jnp.concatenate([normed, low_t[part]], axis=0), all_ref[here, cols])
            put(in_ref, cols, total[: normed.shape[0]])
            put(near_ref, cols, total[normed.shape[0] :])

        spans = ((0, QUERY_WIDTH), (QUERY_WIDTH, HEAD_WIDTH), (QUERY_WIDTH + HEAD_WIDTH, HEAD_WIDTH))
        for i, (start, width) in enumerate(spans):
            cols = pl.ds(start, width)
            low = times_transposed(all_ref[here, cols], widen[:, cols]).astype(bf16)
            put(a_ref, pl.ds(i * rank, rank), matrix_product(normed, low))
        lows = [all_ref[here, pl.ds(PROJECT_COLUMNS + i * rank, rank)] for i in range(4)]
        for i, kind in ((0, 1), (1, 2), (2, 2)):
            put(a_ref, pl.ds((3 + i) * rank, rank), matrix_product(flip(turned[kind, here, :]), lows[i]))
        pulled = flip(lows[3])

        @pl.loop(0, MODEL_WIDTH // rank)
        def _(t):
            cols = pl.ds(pl.multiple_of(t * rank, rank), rank)
            put(far_ref, cols, matrix_product(pulled, grad[here, cols]))

        gain_ref[here, :] = all_ref[here, pl.ds(PROJECT_COLUMNS + 4 * rank, gain_ref.shape[1])]

    gather_kernel(size // 2, x_ref, all_ref, *sems[:5], greet=greet, also=send_all, work=work)

    def arrive(j, carry):
        column = me * own_count + j * chunk
        here = rows(o_ref, j * chunk)
        away, kept = 0, 0
        for _, start, length in sections:
            mine = start + me * length
            inside = (column >= start) & (column < start + length * size)
            outside = (column < mine) | (column >= mine + length)
            away = away + (inside & outside).astype(jnp.int32)
            kept = kept + (inside & ~outside).astype(jnp.int32)

        @pl.when(away > 0)
        def _():
            remote(here, j * chunk, (me + 1) % size).wait_recv()

        @pl.when(kept > 0)
        def _():
            local(rows(mid_ref, 0), j * chunk).wait()

        return carry

    lax.fori_loop(0, own_count // chunk, arrive, 0)
    for base, start, length in sections:

        def sent(j, carry, base=base, aimed=aim(start, length)):
            over = (aimed[1] + j * chunk >= own_count).astype(jnp.int32)
            owner = aimed[0] + over
            first = aimed[1] + j * chunk - over * own_count

            @pl.when(owner != me)
            def _():
                remote(rows(mid_ref, base + j * chunk), first, owner, base // chunk + j).wait_send()

            return carry

        lax.fori_loop(0, length // chunk, sent, 0)


def share_rows(block, middle, turned, later, grad, second_factor, ident):
    size = lax.axis_size("fsdp")
    rank = ADAPTER_RANK
    rows, columns = block.shape
    own_count = ADAPTER_COLUMNS // size
    gain_width = columns - PROJECT_COLUMNS - 4 * rank
    width = MODEL_WIDTH // size
    chunk = math.gcd(own_count, width, HIDDEN_COUNT // size, PROJECT_COLUMNS, GATE_START)
    if size != 16:
        every = gather_rows(block)
        lora, widen = later[:, QUERY_WIDTH:], second_factor[:, :PROJECT_COLUMNS]
        spans = ((0, QUERY_WIDTH), (QUERY_WIDTH, HEAD_WIDTH), (QUERY_WIDTH + HEAD_WIDTH, HEAD_WIDTH))
        parts = [every[:, a : a + n] for a, n in spans]
        lows = [every[:, PROJECT_COLUMNS + i * rank :][:, :rank] for i in range(4)]
        squeezed = [
            outer_product_rows(turned[0], times_transposed(part, widen[:, a : a + n]).astype(bf16))
            for part, (a, n) in zip(parts, spans)
        ]
        squeezed += [outer_product_rows(turned[kind], lows[i]) for i, kind in ((0, 1), (1, 2), (2, 2))]
        near = [outer_product_rows(lora[:, i * rank :][:, :rank], part) for i, part in enumerate(parts)]
        middle_all = gather_rows(middle).reshape(size, -1, rank)
        hidden = HIDDEN_COUNT // size
        cuts = ((0, width), (width, width + hidden), (width + hidden, width + 2 * hidden))
        middle_all = jnp.concatenate(
            [jnp.zeros((PROJECT_COLUMNS, rank), bf16)]
            + [middle_all[:, a:b].reshape(-1, rank) for a, b in cuts]
            + [jnp.zeros((MODEL_WIDTH, rank), bf16)],
            axis=0,
        )
        return (
            lax.dynamic_slice_in_dim(middle_all, lax.axis_index("fsdp") * own_count, own_count, 0),
            outer_product_rows(turned[0], every[:, :PROJECT_COLUMNS]),
            jnp.concatenate(squeezed, axis=1),
            jnp.concatenate(near, axis=1),
            outer_product_rows(lows[3], grad),
            every[:, columns - gain_width :],
        )
    anywhere, inside = pl.BlockSpec(memory_space=pl.ANY), pl.BlockSpec(memory_space=pltpu.VMEM)
    pair = pltpu.SemaphoreType.DMA((2, size // 4))
    sides = pltpu.SemaphoreType.DMA((2, size // 4 + 1))
    return pl.pallas_call(
        functools.partial(share_kernel, size, chunk, own_count),
        out_shape=(
            jax.ShapeDtypeStruct((own_count, rank), bf16),
            jax.ShapeDtypeStruct((width, PROJECT_COLUMNS), f32),
            jax.ShapeDtypeStruct((width, 6 * rank), f32),
            jax.ShapeDtypeStruct((rank, PROJECT_COLUMNS), f32),
            jax.ShapeDtypeStruct((rank, MODEL_WIDTH), f32),
            jax.ShapeDtypeStruct((size * rows, gain_width), bf16),
        ),
        in_specs=[anywhere] * 2 + [inside, anywhere, inside, anywhere],
        out_specs=(anywhere,) + (inside,) * 5,
        scratch_shapes=[
            pltpu.VMEM((size * rows, columns), bf16),
            pltpu.VMEM((3, rank, rank), bf16),
            pltpu.VMEM((size * rows, 3 * rank), bf16),
            pltpu.VMEM((rank, PROJECT_COLUMNS), bf16),
            pltpu.SemaphoreType.DMA((2,)),
            pltpu.SemaphoreType.DMA,
            pair,
            pair,
            sides,
            sides,
            pltpu.SemaphoreType.DMA((middle.shape[0] // chunk,)),
            pltpu.SemaphoreType.DMA((own_count // chunk,)),
            pltpu.SemaphoreType.DMA((own_count // chunk,)),
        ],
        compiler_params=pltpu.CompilerParams(
            collective_id=ident, has_side_effects=True, vmem_limit_bytes=56 << 20
        ),
        cost_estimate=busy(1),
        name="share_rows",
    )(block, middle, turned, later, grad, second_factor)


def per_device(
    hidden_input,
    sequence_lengths,
    norm_gain_values,
    input_proj_weight,
    output_proj_weight,
    feedforward_weight,
    adapter_first,
    adapter_second,
    adapter_down_first,
    output_gradient,
):
    size = lax.axis_size("fsdp")
    place = lax.axis_index("fsdp")
    tokens_dev = hidden_input.shape[1]
    all_rows = tokens_dev * size
    hidden_own = HIDDEN_COUNT // size
    width_own = MODEL_WIDTH // size
    columns_own = ADAPTER_COLUMNS // size
    offset = place * tokens_dev
    segment_all, position_all = segment_info(sequence_lengths[0], all_rows)
    segment_own = lax.dynamic_slice_in_dim(segment_all, offset, tokens_dev)
    position_own = lax.dynamic_slice_in_dim(position_all, offset, tokens_dev)
    row_all = jnp.arange(all_rows, dtype=jnp.int32)
    row_own = offset + jnp.arange(tokens_dev, dtype=jnp.int32)
    allowed = (segment_own[:, None] == segment_all[None, :]) & (
        row_own[:, None] >= row_all[None, :]
    )
    gains = norm_gain_values.astype(f32)
    first_factor = adapter_first[0]
    second_factor = adapter_second[0]
    rank = ADAPTER_RANK
    narrow_projection = first_factor[:, : 3 * rank]
    narrow_output = first_factor[:, 3 * rank : 4 * rank]
    squeeze_gate = first_factor[:, 4 * rank : 5 * rank]
    squeeze_up = first_factor[:, 5 * rank :]
    adapters = (first_factor, second_factor, adapter_down_first[0])
    widen_query = second_factor[:, :QUERY_WIDTH]
    widen_key = second_factor[:, QUERY_WIDTH : QUERY_WIDTH + HEAD_WIDTH]
    widen_value = second_factor[:, QUERY_WIDTH + HEAD_WIDTH : PROJECT_COLUMNS]
    widen_output = second_factor[:, PROJECT_COLUMNS:GATE_START]
    widen_down = second_factor[:, GATE_START + 2 * HIDDEN_COUNT :]
    scaling = HEAD_WIDTH ** (-0.5)

    hidden_state = hidden_input[0].astype(f32)
    scale_one = rms_scale(hidden_state)
    normalized = (hidden_state * scale_one * gains[0]).astype(bf16)
    proj_in = ring_gather(input_proj_weight, 0)
    proj_in, proj_out = lax.optimization_barrier((proj_in, output_proj_weight))
    proj_out = gather_rows(proj_out)
    lora_qkv = matrix_product(normalized, narrow_projection).astype(bf16)
    projected = matrix_product(normalized, proj_in)
    query_pre = projected[:, :QUERY_WIDTH] + matrix_product(lora_qkv[:, :rank], widen_query)
    key_pre = projected[:, QUERY_WIDTH : QUERY_WIDTH + HEAD_WIDTH] + matrix_product(
        lora_qkv[:, rank : 2 * rank], widen_key
    )
    value_local = (
        projected[:, QUERY_WIDTH + HEAD_WIDTH :]
        + matrix_product(lora_qkv[:, 2 * rank :], widen_value)
    ).astype(bf16)
    query_rot = rotate(query_pre, position_own, 1.0).astype(bf16)
    key_rot = rotate(key_pre, position_own, 1.0).astype(bf16)
    keys_all = ring_gather(jnp.concatenate([key_rot, value_local], axis=1), 1)
    key_rows, value_rows = keys_all[:, :HEAD_WIDTH], keys_all[:, HEAD_WIDTH:]
    query_heads = query_rot.reshape(tokens_dev, HEADS, HEAD_WIDTH)
    scores = scores_of(query_heads, key_rows, allowed, scaling)
    row_max = jnp.max(scores, axis=-1, keepdims=True)
    powered = jnp.exp(scores - row_max)
    row_sum = jnp.sum(powered, axis=-1, keepdims=True)
    probs = powered / row_sum
    probs_low = probs.astype(bf16)
    attended = (
        jnp.einsum("thu,ud->thd", probs_low, value_rows, preferred_element_type=f32)
        .reshape(tokens_dev, QUERY_WIDTH)
        .astype(bf16)
    )
    lora_out = matrix_product(attended, narrow_output).astype(bf16)
    middle = (
        hidden_state
        + times_transposed(attended, proj_out)
        + matrix_product(lora_out, widen_output)
    )
    scale_two = rms_scale(middle)
    normed_two = (middle * scale_two * gains[1]).astype(bf16)

    weight_planes = feedforward_weight.transpose(1, 0, 2)
    two_all, grad_all, attended_all, acts, low_ffn, ffn_shares, ffn_pieces, down_own = unit_rows(
        jnp.concatenate([normed_two, lora_out], axis=1),
        output_gradient[0],
        jnp.concatenate([attended, lora_qkv], axis=1),
        weight_planes,
        adapters,
        2,
    )
    lora_out_all = low_ffn[:, 3 * rank :]
    ffn_both = loop_shares(ffn_shares)
    rows_sum = mix_rows(
        acts, weight_planes, adapters, 3
    )
    back_own, out_own = rows_sum[:, : MODEL_WIDTH + 2 * rank], rows_sum[:, MODEL_WIDTH + 2 * rank :]
    lora_hd = out_own[:, MODEL_WIDTH:].astype(bf16)

    gate_low = back_own[:, MODEL_WIDTH : MODEL_WIDTH + rank].astype(bf16)
    up_low = back_own[:, MODEL_WIDTH + rank :].astype(bf16)
    two_grad = (
        back_own[:, :MODEL_WIDTH]
        + times_transposed(gate_low, squeeze_gate)
        + times_transposed(up_low, squeeze_up)
    )
    weighted_two = gains[1] * two_grad
    middle_grad = (
        output_gradient[0].astype(f32)
        + scale_two * weighted_two
        - middle * scale_two**3 * jnp.mean(middle * weighted_two, axis=-1, keepdims=True)
    )
    gain_two = jnp.sum(two_grad * middle * scale_two, axis=0)

    branch_grad = middle_grad.astype(bf16)
    both = [block.reshape(tokens_dev, size, width_own) for block in (normalized, branch_grad)]
    turned = turn(jnp.concatenate(both, axis=2).reshape(tokens_dev, -1))
    normed_turn, branch_turn = turned[:, :width_own], turned[:, width_own:]
    lora_out_grad = times_transposed(branch_grad, widen_output).astype(bf16)
    attended_grad = (
        matrix_product(branch_grad, proj_out) + times_transposed(lora_out_grad, narrow_output)
    ).astype(bf16)
    heads_grad = attended_grad.reshape(tokens_dev, HEADS, HEAD_WIDTH)
    prob_grad = jnp.einsum("thd,ud->thu", heads_grad, value_rows, preferred_element_type=f32)
    row_dot = jnp.sum(probs * prob_grad, axis=-1, keepdims=True)
    score_grad = (probs * (prob_grad - row_dot)).astype(bf16)
    query_rot_grad = (
        jnp.einsum("thu,ud->thd", score_grad, key_rows, preferred_element_type=f32) * scaling
    )
    key_part = (
        jnp.einsum("thu,thd->ud", score_grad, query_heads, preferred_element_type=f32) * scaling
    )
    value_part = jnp.einsum("thu,thd->ud", probs_low, heads_grad, preferred_element_type=f32)
    pair_grad = ring_scatter([key_part, value_part], 4)
    pair_grad, normed_turn, branch_turn = lax.optimization_barrier((pair_grad, normed_turn, branch_turn))
    query_grad = rotate(
        query_rot_grad.reshape(tokens_dev, QUERY_WIDTH), position_own, -1.0
    ).astype(bf16)
    key_grad = rotate(pair_grad[:, :HEAD_WIDTH], position_own, -1.0).astype(bf16)
    value_grad = pair_grad[:, HEAD_WIDTH:].astype(bf16)
    proj_grad = jnp.concatenate([query_grad, key_grad, value_grad], axis=1)
    lora_qkv_grad = jnp.concatenate(
        [
            times_transposed(query_grad, widen_query),
            times_transposed(key_grad, widen_key),
            times_transposed(value_grad, widen_value),
        ],
        axis=1,
    ).astype(bf16)
    normed_grad = times_transposed(proj_grad, proj_in) + times_transposed(
        lora_qkv_grad, narrow_projection
    )
    weighted_one = gains[0] * normed_grad
    input_grad = (
        middle_grad
        + scale_one * weighted_one
        - hidden_state
        * scale_one**3
        * jnp.mean(hidden_state * weighted_one, axis=-1, keepdims=True)
    )
    gain_one = jnp.sum(normed_grad * hidden_state * scale_one, axis=0)

    out_piece = outer_product_rows(branch_turn, lora_out_all)
    gain_rows = jnp.stack([gain_one, gain_two]).astype(bf16).reshape(tokens_dev, -1)
    gain_count = gain_rows.shape[1]
    gain_rows = jnp.pad(gain_rows, ((0, 0), (0, -gain_count % 128)))
    proj_rows = jnp.concatenate(
        [proj_grad, lora_out_grad, gate_low, up_low, lora_hd, gain_rows], axis=1
    )
    column = place * width_own
    attended_turn, two_turn, attn_out_part, proj_rows = lax.optimization_barrier(
        (
            lax.dynamic_slice_in_dim(attended_all, column, width_own, 1),
            lax.dynamic_slice_in_dim(two_all, column, width_own, 1),
            outer_product_rows(branch_turn, attended_all)[:, :QUERY_WIDTH],
            proj_rows,
        )
    )
    middle_own, attn_in_part, squeeze_own, near, far, gain_all = share_rows(
        proj_rows,
        jnp.concatenate([out_piece.astype(bf16), ffn_pieces[0], ffn_pieces[1]], axis=0),
        jnp.stack([normed_turn, attended_turn, two_turn]),
        attended_all,
        grad_all,
        second_factor,
        5,
    )
    gain_all = gain_all[:, :gain_count].reshape(size, 2, MODEL_WIDTH)
    gain_all = jnp.sum(gain_all.astype(f32), axis=0)
    gain_own = lax.dynamic_slice_in_dim(gain_all, column, width_own, 1)
    gain_part = jnp.pad(gain_own, ((0, width_own - 2), (0, -width_own % 128)))
    attn_part = jnp.concatenate(
        [
            attn_in_part,
            attn_out_part,
            gain_part,
        ],
        axis=1,
    ).astype(bf16)
    attn_part, ffn_both, near, far, middle_own, out_own = lax.optimization_barrier(
        (attn_part, ffn_both, near, far, middle_own, out_own)
    )
    attn_sum = both_loops(loop_shares(attn_part))
    gain_column = PROJECT_COLUMNS + QUERY_WIDTH
    gain_sum = attn_sum[:2, gain_column : gain_column + width_own]
    first = place * columns_own
    far_start = GATE_START + 2 * HIDDEN_COUNT
    near = lax.dynamic_slice_in_dim(
        jnp.pad(near.T.astype(bf16), ((0, columns_own), (0, 0))), jnp.minimum(first, PROJECT_COLUMNS), columns_own, 0
    )
    far = lax.dynamic_slice_in_dim(
        jnp.pad(far.T.astype(bf16), ((columns_own, 0), (0, 0))),
        jnp.maximum(first - far_start + columns_own, 0),
        columns_own,
        0,
    )
    owned = first + jnp.arange(columns_own, dtype=jnp.int32)[:, None]
    expand_own = jnp.where(
        owned < PROJECT_COLUMNS, near, jnp.where(owned < far_start, middle_own, far)
    ).T.astype(f32)
    hidden_out = (middle + out_own[:, :MODEL_WIDTH] + matrix_product(lora_hd, widen_down)).astype(bf16)
    ffn_sum = sum_loops(ffn_both).transpose(1, 0, 2)
    return (
        hidden_out[None],
        input_grad[None],
        gain_sum,
        attn_sum[:, :PROJECT_COLUMNS],
        attn_sum[:, PROJECT_COLUMNS:gain_column],
        ffn_sum,
        squeeze_own[None],
        expand_own[None],
        down_own[None],
    )


def solution(mesh):
    return jax.shard_map(
        per_device,
        mesh=mesh,
        in_specs=(
            P("loop", "fsdp", None),
            P("loop", None),
            P(),
            P("fsdp", None),
            P("fsdp", None),
            P("fsdp", None, None),
            P("loop", None, None),
            P("loop", None, None),
            P("loop", None, None),
            P("loop", "fsdp", None),
        ),
        out_specs=(
            P("loop", "fsdp", None),
            P("loop", "fsdp", None),
            P(None, "fsdp"),
            P("fsdp", None),
            P("fsdp", None),
            P("fsdp", None, None),
            P("loop", "fsdp", None),
            P("loop", None, "fsdp"),
            P("loop", "fsdp", None),
        ),
        check_vma=False,
    )
```
